32 devices in a mesh: dp: 16 (over z, y, x), seq: 2 (over core).
Axes of the slice: x: 2, y: 2, z: 4, core: 2. Of those that a mesh axis runs over, the one named last changes fastest.
Arguments:
- latents: float32 [16, 256, 48], P('dp', 'seq'), may hold values from -6 to 6
- valid: int32 [16, 256], P('dp', 'seq'), may hold values 0 or 1
- class_labels: int32 [16], replicated, may hold values from 0 to 447
- group_perm: int32 [16], P('dp'), may hold values from 0 to 15, as said below
- patch_weight: bfloat16 [48, 768], replicated, may hold values from -0.875 to 0.875
- pos_table: bfloat16 [256, 768], P('seq'), may hold values from -3 to 3
- class_table: bfloat16 [1024, 768], replicated, may hold values from -3 to 3
- ln1_gain: bfloat16 [1, 768], replicated, may hold values from 0.25 to 1.75
- ln1_bias: bfloat16 [1, 768], replicated, may hold values from -1.5 to 1.5
- qkv_weight: bfloat16 [1, 768, 2304], replicated, may hold values from -0.21875 to 0.21875
- out_weight: bfloat16 [1, 768, 768], replicated, may hold values from -0.875 to 0.875
- ln2_gain: bfloat16 [1, 768], replicated, may hold values from 0.25 to 1.75
- ln2_bias: bfloat16 [1, 768], replicated, may hold values from -1.5 to 1.5
- up_weight: bfloat16 [1, 768, 3072], replicated, may hold values from -0.21875 to 0.21875
- up_bias: bfloat16 [1, 3072], replicated, may hold values from -1.5 to 1.5
- down_weight: bfloat16 [1, 3072, 768], replicated, may hold values from -0.109375 to 0.109375
- head_weight: bfloat16 [768, 96], replicated, may hold values from -0.109375 to 0.109375
- head_bias: bfloat16 [96], replicated, may hold values from -1 to 1
- cot_latents: float32 [16, 256, 48], P('dp', 'seq'), may hold values from -6 to 6
- cot_logdet: float32 [16], P('dp'), may hold values from -4 to 4
Outputs:
- new_latents: float32 [16, 256, 48], P('dp', 'seq')
- logdet: float32 [16], P('dp')
- latents_grad: float32 [16, 256, 48], P('dp', 'seq')
- patch_weight_grad: float32 [48, 768], replicated
- pos_grad: float32 [256, 768], P('seq')
- class_grad: float32 [1024, 768], P('dp')
- ln1_gain_grad: float32 [1, 768], replicated
- ln1_bias_grad: float32 [1, 768], replicated
- qkv_grad: float32 [1, 768, 2304], replicated
- out_grad: float32 [1, 768, 768], replicated
- ln2_gain_grad: float32 [1, 768], replicated
- ln2_bias_grad: float32 [1, 768], replicated
- up_grad: float32 [1, 768, 3072], replicated
- up_bias_grad: float32 [1, 3072], replicated
- down_grad: float32 [1, 3072, 768], replicated
- head_weight_grad: float32 [768, 96], replicated
- head_bias_grad: float32 [96], replicated
The draws below stay inside these ranges and needn't reach their ends.
Inputs may be any that keep to these rules, and one draw needn't show every extreme that they name: Each of 0 to 15 once; class_labels[group_perm] never falls.
All inputs are finite; a program needn't handle non-finite values. No bound on the sum of `valid` on one device may be relied on, other than what follows from the above.
Results may differ from the reference program's by a relative error of at most 0.023.
Values may be sent and summed in bfloat16 or wider, within the bound.
A program may use at most 320 MiB of HBM per device.

```python
import math
import jax
import jax.numpy as jnp
from jax import lax

D = 768
HEAD_DIM = 64
FF = 3072
CHAN = 48
CLASSES = 1000
CLS_PAD = 1024
PATCHES = 256
LAYERS = 1
OUTS = 96
IMAGES = 16
N_DP = 16


def label_pair(key):
    label_top = min(CLASSES, CLS_PAD // 2 - CLS_PAD // N_DP)
    labels = jax.random.randint(jax.random.fold_in(key, 7), (IMAGES,), 0, label_top, dtype=jnp.int32)
    labels = labels.at[0].set(label_top - 1).at[1].set(0)
    ranking = labels * IMAGES + lax.iota(jnp.int32, IMAGES)
    ordering = jnp.argsort(ranking, stable=True).astype(jnp.int32)
    return (labels, ordering)


def draw_class_labels(key, part):
    return label_pair(key)[0]


def draw_group_perm(key, part):
    return label_pair(key)[1]


def place_ends(drawn, stream_key, least, largest):
    shape = drawn.shape
    place = [jax.random.randint(jax.random.fold_in(stream_key, axis), (), 0, shape[axis]) for axis in range(len(shape))]
    drawn = drawn.at[tuple(place)].set(least)
    longest = shape.index(max(shape))
    place[longest] = (place[longest] + 1) % shape[longest]
    return drawn.at[tuple(place)].set(largest)


def block_levels(key, dims, split, least, top_value):
    loudness = 1.0
    for position, parts in split:
        draws = jax.random.uniform(jax.random.fold_in(jax.random.fold_in(key, 6), position), (parts,), jnp.float32, least / len(split), top_value / len(split))
        loudness = loudness * jnp.repeat(jnp.exp(draws), dims[position] // parts).reshape((-1,) + (1,) * (len(dims) - 1 - position))
    return loudness


def bell_draw(stream_key, extent, width, limit, shards=(), held_as=jnp.bfloat16):
    factor_of = block_levels(stream_key, extent, shards, -0.22, 0.18) if shards else 1.0
    result = jax.random.normal(stream_key, extent, jnp.float32) * width * factor_of
    return jnp.minimum(jnp.maximum(result, -limit), limit).astype(held_as)


def setup_inputs(seed: int = 0) -> dict:
    seeds = jax.random.split(jax.random.key(seed), 21)
    return {
        "latents": bell_draw(seeds[0], (IMAGES, PATCHES, CHAN), 1.0, 6.0, ((0, 16), (1, 2)), jnp.float32),
        "valid": place_ends((jax.random.randint(seeds[1], (IMAGES, PATCHES), 0, 4) < 3).astype(jnp.int32), jax.random.fold_in(seeds[1], 1), 0, 1),
        "class_labels": draw_class_labels(jax.random.fold_in(seeds[20], 71), 0),
        "group_perm": draw_group_perm(jax.random.fold_in(seeds[20], 71), 0),
        "patch_weight": bell_draw(seeds[4], (CHAN, D), CHAN ** -0.5, 0.875),
        "pos_table": bell_draw(seeds[5], (PATCHES, D), 0.5, 3.0, ((0, 2),)),
        "class_table": bell_draw(seeds[6], (CLS_PAD, D), 0.5, 3.0),
        "ln1_gain": jnp.clip(1.0 + 0.15 * jax.random.normal(seeds[7], (LAYERS, D), jnp.float32), 0.25, 1.75).astype(jnp.bfloat16),
        "ln1_bias": bell_draw(seeds[8], (LAYERS, D), 0.3, 1.5),
        "qkv_weight": bell_draw(seeds[9], (LAYERS, D, 3 * D), D ** -0.5, 0.21875),
        "out_weight": bell_draw(seeds[10], (LAYERS, D, D), (D // 16) ** -0.5, 0.875),
        "ln2_gain": jnp.clip(1.0 + 0.15 * jax.random.normal(seeds[11], (LAYERS, D), jnp.float32), 0.25, 1.75).astype(jnp.bfloat16),
        "ln2_bias": bell_draw(seeds[12], (LAYERS, D), 0.3, 1.5),
        "up_weight": bell_draw(seeds[13], (LAYERS, D, FF), D ** -0.5, 0.21875),
        "up_bias": bell_draw(seeds[14], (LAYERS, FF), 0.3, 1.5),
        "down_weight": bell_draw(seeds[15], (LAYERS, FF, D), FF ** -0.5, 0.109375),
        "head_weight": bell_draw(seeds[16], (D, OUTS), (4 * D) ** -0.5, 0.109375),
        "head_bias": bell_draw(seeds[17], (OUTS,), 0.2, 1.0),
        "cot_latents": bell_draw(seeds[18], (IMAGES, PATCHES, CHAN), 1.0, 6.0, ((0, 16), (1, 2)), jnp.float32),
        "cot_logdet": bell_draw(seeds[19], (IMAGES,), 1.0, 4.0, ((0, 16),), jnp.float32),
    }


precise = lax.Precision.HIGHEST
norm_eps = 1e-05

@jax.custom_vjp
def low(v):
    return lax.optimization_barrier(v.astype(jnp.bfloat16)).astype(jnp.float32)

@jax.custom_vjp
def low_back(v):
    return v

def low_keep(v):
    return (low(v), None)

def low_pass(kept, grad):
    return (grad,)

def back_keep(v):
    return (v, None)

def back_low(kept, grad):
    return (low(grad),)
low.defvjp(low_keep, low_pass)
low_back.defvjp(back_keep, back_low)

def rounded_both(values):
    return low(low_back(values))

def layer_norm(values, norm_gain, norm_bias):
    center = values - lax.optimization_barrier(jnp.mean(values, -1, keepdims=True))
    spread = lax.optimization_barrier(jnp.mean(center * center, -1, keepdims=True))
    return center * lax.rsqrt(spread + norm_eps) * norm_gain + norm_bias

def matmul(left_side, weight_mat):
    return jnp.einsum('gpd,de->gpe', left_side, weight_mat, precision=precise)

def flow_block(params, latent_in, valid_in, label_in):
    patch_weight, pos_table, class_table, ln1_gain, ln1_bias, qkv_weight, out_weight, ln2_gain, ln2_bias, up_weight, up_bias, down_weight, head_weight, head_bias = params
    images, patch_count, channels = latent_in.shape
    model_width = qkv_weight.shape[1]
    head_count = model_width // HEAD_DIM
    score_scale = HEAD_DIM ** (-0.5)
    latent_low = low(latent_in)
    hidden = low_back(matmul(latent_low, patch_weight)) + pos_table[None] + class_table[label_in][:, None, :]
    places = jnp.arange(patch_count)
    earlier = (places[None, :] < places[:, None])[None] & (valid_in[:, None, :] == 1)
    allowed = earlier | (places[None, :] == places[:, None])[None]
    for layer_index in range(qkv_weight.shape[0]):
        normed = low(layer_norm(hidden, ln1_gain[layer_index], ln1_bias[layer_index]))
        packed = matmul(normed, qkv_weight[layer_index])
        query = rounded_both(packed[..., :model_width]).reshape(images, patch_count, head_count, HEAD_DIM)
        keys = rounded_both(packed[..., model_width:2 * model_width]).reshape(images, patch_count, head_count, HEAD_DIM)
        values = rounded_both(packed[..., 2 * model_width:]).reshape(images, patch_count, head_count, HEAD_DIM)
        logits = low_back(jnp.einsum('gqhd,gkhd->ghqk', query, keys, precision=precise) * score_scale)
        logits = jnp.where(allowed[:, None], logits, -1e+30)
        weights_soft = low(jax.nn.softmax(logits, -1))
        attended = rounded_both(jnp.einsum('ghqk,gkhd->gqhd', weights_soft, values, precision=precise))
        attended = attended.reshape(images, patch_count, model_width)
        hidden = hidden + low_back(matmul(attended, out_weight[layer_index]))
        second = low(layer_norm(hidden, ln2_gain[layer_index], ln2_bias[layer_index]))
        preact = low_back(matmul(second, up_weight[layer_index]) + up_bias[layer_index])
        activated = low(jax.nn.gelu(preact, approximate=True))
        hidden = hidden + low_back(matmul(activated, down_weight[layer_index]))
    head_out = low_back(matmul(low(hidden), head_weight) + head_bias)
    shifted = jnp.concatenate((jnp.zeros_like(head_out[:, :1]), head_out[:, :-1]), 1)
    shifted = shifted * valid_in.astype(head_out.dtype)[..., None]
    alpha = shifted[..., :channels]
    shift_mean = shifted[..., channels:]
    new_latents = (latent_in - shift_mean) * jnp.exp(-alpha)
    logdet = -lax.optimization_barrier(jnp.sum(alpha, (1, 2)))
    return (new_latents, logdet)

def reference(latents, valid, class_labels, group_perm, patch_weight, pos_table, class_table, ln1_gain, ln1_bias, qkv_weight, out_weight, ln2_gain, ln2_bias, up_weight, up_bias, down_weight, head_weight, head_bias, cot_latents, cot_logdet):
    params = tuple((arr.astype(jnp.float32) for arr in (patch_weight, pos_table, class_table, ln1_gain, ln1_bias, qkv_weight, out_weight, ln2_gain, ln2_bias, up_weight, up_bias, down_weight, head_weight, head_bias)))
    image_labels = class_labels[group_perm].astype(jnp.int32)
    group_size = math.gcd(IMAGES, max(1, 4096 // PATCHES))
    group_count = IMAGES // group_size
    sliced_inputs = (latents.reshape(group_count, group_size, PATCHES, CHAN), valid.reshape(group_count, group_size, PATCHES), image_labels.reshape(group_count, group_size), cot_latents.reshape(group_count, group_size, PATCHES, CHAN), cot_logdet.reshape(group_count, group_size))

    def group_step(carried, sliced):
        latent_in, valid_in, label_in, cot_in, cot_det = sliced

        def flow_of(prm, lat_in):
            return flow_block(prm, lat_in, valid_in, label_in)
        outputs, pull = jax.vjp(flow_of, params, latent_in)
        param_grads, latent_grad = pull((cot_in, cot_det))
        carried = jax.tree.map(lambda first, second: first + second, carried, param_grads)
        return (carried, (outputs[0], outputs[1], latent_grad))
    zeros_tree = jax.tree.map(jnp.zeros_like, params)
    totals, (new_latents, logdet, latents_grad) = lax.scan(group_step, zeros_tree, sliced_inputs)
    new_latents = new_latents.reshape(IMAGES, PATCHES, CHAN)
    logdet = logdet.reshape(IMAGES)
    latents_grad = latents_grad.reshape(IMAGES, PATCHES, CHAN)
    return (new_latents, logdet, latents_grad, totals[0], totals[1], totals[2], totals[3], totals[4], totals[5], totals[6], totals[7], totals[8], totals[9], totals[10], totals[11], totals[12], totals[13])
```

```python
import jax
import jax.numpy as jnp
from jax import lax
from jax.experimental import pallas as pl
from jax.experimental.pallas import tpu as pltpu
from jax.sharding import PartitionSpec as P

HEAD_DIM = 64


precise = lax.Precision.HIGHEST
norm_eps = 1e-05


def shifted_2(shard, axis, by):
    size = lax.axis_size(axis)
    pairs = [(i, i + by) for i in range(size) if 0 <= i + by < size]
    return lax.ppermute(shard, axis, pairs)


def layer_norm(values, norm_gain, norm_bias):
    center = values - jnp.mean(values, -1, keepdims=True)
    spread = jnp.mean(center * center, -1, keepdims=True)
    return center * lax.rsqrt(spread + norm_eps) * norm_gain + norm_bias


def matmul(left_side, weight_mat):
    return jnp.dot(left_side, weight_mat, preferred_element_type=jnp.float32)


def outer_sum(left_side, grad_side):
    left_flat = left_side.reshape(-1, left_side.shape[-1])
    grad_flat = grad_side.reshape(-1, grad_side.shape[-1])
    return lax.dot_general(
        left_flat, grad_flat, (((0,), (0,)), ((), ())), preferred_element_type=jnp.float32
    )


def transposed(grad_side, weight_mat):
    return lax.dot_general(
        grad_side,
        weight_mat,
        (((grad_side.ndim - 1,), (1,)), ((), ())),
        preferred_element_type=jnp.float32,
    )


def eight_rows(matrix):
    return matrix.reshape(8, -1)


def attention_mask(key_valid, patch_rows, seq_place):
    query_pos = seq_place * patch_rows + lax.iota(jnp.int32, patch_rows)
    key_pos = (seq_place - 1) * patch_rows + lax.iota(jnp.int32, 2 * patch_rows)
    earlier = (key_pos[None, :] < query_pos[:, None])[None] & (key_valid[:, None, :] > 0)
    return earlier | (key_pos[None, :] == query_pos[:, None])[None]


def masked_scores(query, keys, allowed):
    logits = jnp.einsum(
        "bqhd,bkhd->bhqk", query, keys, preferred_element_type=jnp.float32
    ) * HEAD_DIM ** (-0.5)
    return jnp.where(allowed[:, None], logits, -1e30)


MESH = pl.DeviceIdType.MESH
UNITS = 12
ROWS = 256
COLS = 384
STAGES = 3
f32 = jnp.float32
bf16 = jnp.bfloat16


def grads_kernel(
    lt_ref, r_ref, pos_ref, small_ref,
    down_hbm, up_hbm, out_hbm, qkv_hbm, pos_hbm, small_hbm,
    stage, part, full, core_in, ab_in, c_in, send_sem, recv_sem, local_sem,
):
    dp = lax.axis_index("dp")
    core = lax.axis_index("seq")
    x, y, z = dp % 2, (dp // 2) % 2, dp // 4
    side = z // 2
    inner = ((z + 1) // 2) % 2 == 1
    outer = ((z + 1) // 2) % 2 == 0
    to_core = (dp, 1 - core)
    to_x = (dp + 1 - 2 * x, core)
    to_y = (dp + 2 - 4 * y, core)
    to_mate = (dp + 4 - 8 * (z % 2), core)
    to_inner = ((dp + 12 - 8 * z + 16) % 16, core)

    def rows_at(start, count):
        return pl.ds(pl.multiple_of(start, 16), count)

    barrier = pltpu.get_barrier_semaphore()
    for target in (to_core, to_x, to_y, to_mate):
        pl.semaphore_signal(barrier, inc=1, device_id=target, device_id_type=MESH)

    @pl.when(inner)
    def _():
        pl.semaphore_signal(barrier, inc=1, device_id=to_inner, device_id_type=MESH)
        pl.semaphore_wait(barrier, 5)

    @pl.when(outer)
    def _():
        pl.semaphore_wait(barrier, 4)

    def copy(u, k, src, dst, target):
        return pltpu.make_async_remote_copy(
            src_ref=src, dst_ref=dst, send_sem=send_sem.at[u, k], recv_sem=recv_sem.at[u, k],
            device_id=target, device_id_type=MESH,
        )

    def arrived(u, k, dst):
        copy(u, k, dst, dst, to_core).wait_recv()

    def added(dst, left, right):
        dst[...] = (left[...].astype(f32) + right[...].astype(f32)).astype(bf16)

    first = (x, y)
    second = (y, x)
    to_first = (to_x, to_y)
    to_second = (to_y, to_x)

    def out_rows(u, t, start, count):
        return full.at[u, rows_at(t * ROWS + start, count)]

    def part_rows(u, t, start, count):
        return part.at[u, rows_at(t * ROWS + start, count)]

    def left_index(u):
        return jnp.minimum(u, 4) + jnp.minimum(jnp.maximum(u - 7, 0), 2)

    def right_index(u):
        return jnp.maximum(u - 3, 0)

    small_rows = (slice(128, 256), slice(384, 512))

    def core_first(u):
        return copy(u, 0, stage.at[u % STAGES], core_in.at[u], to_core)

    def small_first(t):
        return copy(UNITS, 25 + t, small_ref.at[1 - core, t], core_in.at[UNITS, small_rows[t]], to_core)

    def produce(u):
        @pl.when(jnp.logical_and(u >= STAGES, u < UNITS))
        def _():
            core_first(u - STAGES).wait_send()

        @pl.when(u < UNITS)
        def _():
            right = r_ref[right_index(u), 1 - core]
            for t in range(3):
                product = jnp.dot(
                    lt_ref[left_index(u), t * ROWS : (t + 1) * ROWS], right, preferred_element_type=f32
                )
                stage[u % STAGES, t * ROWS : (t + 1) * ROWS] = product.astype(bf16)
            core_first(u).start()

        @pl.when(u == UNITS)
        def _():
            for t in range(2):
                small_first(t).start()

    def begin(u):
        @pl.when(u < UNITS)
        def _():
            arrived(u, 0, core_in.at[u])
            right = r_ref[right_index(u), core]
            for t in range(3):
                rows = slice(t * ROWS, (t + 1) * ROWS)
                product = jnp.dot(lt_ref[left_index(u), rows], right, preferred_element_type=f32)
                part[u, rows] = (product + core_in[u, rows].astype(f32)).astype(bf16)
                if t < 2:
                    ab_first(u, t).start()

            @pl.when(outer)
            def _():
                c_z1(u).start()

        @pl.when(u == UNITS)
        def _():
            for t in range(2):
                arrived(UNITS, 25 + t, core_in.at[UNITS, small_rows[t]])
                part[UNITS, t * ROWS : t * ROWS + 128] = pos_ref[t]
                part[UNITS, small_rows[t]] = (
                    small_ref[core, t].astype(f32) + core_in[UNITS, small_rows[t]].astype(f32)
                ).astype(bf16)
                ab_first(u, t).start()

    def ab_first(u, t):
        return copy(u, 1 + t, part_rows(u, t, (1 - first[t]) * 128, 128), ab_in.at[u, t, 0:128], to_first[t])

    def ab_second(u, t):
        row = first[t] * 128 + (1 - second[t]) * 64
        return copy(u, 3 + t, part_rows(u, t, row, 64), ab_in.at[u, t, 128:192], to_second[t])

    def ab_base(t):
        return first[t] * 128 + second[t] * 64

    def ab_z1(u, t):
        return copy(u, 5 + t, part_rows(u, t, ab_base(t), 64), ab_in.at[u, t, 192:256], to_mate)

    def ab_z2(u, t):
        return copy(
            u, 7 + t, part_rows(u, t, ab_base(t) + (2 - z) * 32, 32), ab_in.at[u, t, 256:288], to_inner
        )

    def ab_z3(u, t, row):
        block = out_rows(u, t, row, 32)
        return copy(u, 9 + t, block, block, to_inner)

    def ab_z4(u, t):
        block = out_rows(u, t, ab_base(t), 64)
        return copy(u, 11 + t, block, block, to_mate)

    def ab_back2(u, t, row):
        block = out_rows(u, t, row, 64)
        return copy(u, 13 + t, block, block, to_second[t])

    def ab_back1(u, t, row):
        block = out_rows(u, t, row, 128)
        return copy(u, 15 + t, block, block, to_first[t])

    def ab1(u):
        for t in range(2):
            arrived(u, 1 + t, ab_in.at[u, t, 0:128])
            kept = part_rows(u, t, first[t] * 128, 128)
            added(kept, kept, ab_in.at[u, t, 0:128])
            ab_second(u, t).start()

    def ab2(u):
        for t in range(2):
            arrived(u, 3 + t, ab_in.at[u, t, 128:192])
            kept = part_rows(u, t, ab_base(t), 64)
            added(kept, kept, ab_in.at[u, t, 128:192])

        @pl.when(outer)
        def _():
            for t in range(2):
                ab_z1(u, t).start()

    def ab3_inner(u):
        for t in range(2):
            arrived(u, 5 + t, ab_in.at[u, t, 192:256])
            kept = part_rows(u, t, ab_base(t), 64)
            added(kept, kept, ab_in.at[u, t, 192:256])
            ab_z2(u, t).start()

    def ab4_inner(u):
        for t in range(2):
            arrived(u, 7 + t, ab_in.at[u, t, 256:288])
            row = ab_base(t) + (z - 1) * 32
            added(out_rows(u, t, row, 32), part_rows(u, t, row, 32), ab_in.at[u, t, 256:288])
            ab_z3(u, t, row).start()

    def ab5_inner(u):
        for t in range(2):
            arrived(u, 9 + t, out_rows(u, t, ab_base(t) + (2 - z) * 32, 32))
            ab_z4(u, t).start()
            ab_back2(u, t, ab_base(t)).start()

    def ab5_outer(u):
        for t in range(2):
            arrived(u, 11 + t, out_rows(u, t, ab_base(t), 64))
            ab_back2(u, t, ab_base(t)).start()

    def ab6(u):
        for t in range(2):
            arrived(u, 13 + t, out_rows(u, t, first[t] * 128 + (1 - second[t]) * 64, 64))
            ab_back1(u, t, first[t] * 128).start()

    def place(u, h, row, count, act):
        def columns(base):
            return pl.ds(pl.multiple_of(base + h * COLS, 128), COLS)

        @pl.when(u < 4)
        def _():
            act(down_hbm.at[pl.ds(pl.multiple_of(u * 768 + row, 16), count), columns(0)])

        @pl.when(jnp.logical_and(u >= 4, u < 8))
        def _():
            act(up_hbm.at[row : row + count, columns((u - 4) * 768)])

        @pl.when(u == 8)
        def _():
            act(out_hbm.at[row : row + count, columns(0)])

        @pl.when(jnp.logical_and(u >= 9, u < UNITS))
        def _():
            act(qkv_hbm.at[row : row + count, columns((u - 9) * 768)])

    def to_other(u, k, row, count):
        return lambda dst: copy(u, k, full.at[u, row : row + count], dst, to_core)

    def to_own(u, k, row, count):
        return lambda dst: pltpu.make_async_copy(full.at[u, row : row + count], dst, local_sem.at[u, k])

    def spread_ab(u):
        place(u, core, 0, 512, lambda dst: to_other(u, 27, 0, 512)(dst).start())
        place(u, core, 0, 512, lambda dst: to_own(u, 0, 0, 512)(dst).start())

    def spread_c(u):
        place(u, core, 512, 256, lambda dst: to_other(u, 28, 512, 256)(dst).start())
        place(u, core, 512, 256, lambda dst: to_own(u, 1, 512, 256)(dst).start())

    def small_out(h, t):
        return small_hbm.at[pl.ds(pl.multiple_of(h * 128, 128), 128), t * COLS : (t + 1) * COLS]

    def small_other(t):
        return copy(UNITS, 27 + t, full.at[UNITS, small_rows[t]], small_out(core, t), to_core)

    def small_own(t):
        return pltpu.make_async_copy(
            full.at[UNITS, small_rows[t]], small_out(core, t), local_sem.at[UNITS, t]
        )

    def pos_own(t):
        return pltpu.make_async_copy(
            full.at[UNITS, t * ROWS : t * ROWS + 128],
            pos_hbm.at[:, t * COLS : (t + 1) * COLS],
            local_sem.at[UNITS, 2 + t],
        )

    def ab7(u):
        for t in range(2):
            arrived(u, 15 + t, out_rows(u, t, (1 - first[t]) * 128, 128))
        spread_ab(u)

        @pl.when(u == UNITS)
        def _():
            for t in range(2):
                small_other(t).start()
                small_own(t).start()
                pos_own(t).start()

    far = 64 * (1 - side)
    own_end = 192 * side
    shard = z * 64
    half = shard + x * 32
    mine = half + y * 16

    def c_z1(u):
        return copy(u, 17, part_rows(u, 2, far, 192), c_in.at[u, 0:192], to_mate)

    def c_z2(u):
        return copy(u, 18, part_rows(u, 2, (1 - side) * 128, 128), c_in.at[u, 192:320], to_inner)

    def c_z3(u):
        return copy(u, 19, part_rows(u, 2, own_end, 64), c_in.at[u, 320:384], to_mate)

    def c_x(u):
        return copy(u, 20, part_rows(u, 2, shard + (1 - x) * 32, 32), c_in.at[u, 384:416], to_x)

    def c_y(u):
        return copy(u, 21, part_rows(u, 2, half + (1 - y) * 16, 16), c_in.at[u, 416:432], to_y)

    def c_back_y(u, row):
        block = out_rows(u, 2, row, 16)
        return copy(u, 22, block, block, to_y)

    def c_back_x(u, row):
        block = out_rows(u, 2, row, 32)
        return copy(u, 23, block, block, to_x)

    def c_z4(u):
        block = out_rows(u, 2, own_end, 64)
        return copy(u, 24, block, block, to_mate)

    def c_z5(u, row):
        block = out_rows(u, 2, row, 128)
        return copy(u, 25, block, block, to_inner)

    def c_z6(u):
        block = out_rows(u, 2, far, 192)
        return copy(u, 26, block, block, to_mate)

    def c1_inner(u):
        arrived(u, 17, c_in.at[u, 0:192])
        kept = part_rows(u, 2, far, 192)
        added(kept, kept, c_in.at[u, 0:192])
        c_z2(u).start()

    def c2_inner(u):
        arrived(u, 18, c_in.at[u, 192:320])
        kept = part_rows(u, 2, side * 128, 128)
        added(kept, kept, c_in.at[u, 192:320])
        c_z3(u).start()
        c_x(u).start()

    def c3_outer(u):
        arrived(u, 19, c_in.at[u, 320:384])
        kept = part_rows(u, 2, shard, 64)
        added(kept, kept, c_in.at[u, 320:384])
        c_x(u).start()

    def c4(u):
        arrived(u, 20, c_in.at[u, 384:416])
        kept = part_rows(u, 2, half, 32)
        added(kept, kept, c_in.at[u, 384:416])
        c_y(u).start()

    def c5(u):
        arrived(u, 21, c_in.at[u, 416:432])
        added(out_rows(u, 2, mine, 16), part_rows(u, 2, mine, 16), c_in.at[u, 416:432])
        c_back_y(u, mine).start()

    def c6(u):
        arrived(u, 22, out_rows(u, 2, half + (1 - y) * 16, 16))
        c_back_x(u, half).start()

    def c7(u):
        arrived(u, 23, out_rows(u, 2, shard + (1 - x) * 32, 32))

    def c7_outer(u):
        c7(u)
        c_z4(u).start()

    def c8_inner(u):
        arrived(u, 24, out_rows(u, 2, own_end, 64))
        c_z5(u, side * 128).start()

    def c9_inner(u):
        arrived(u, 25, out_rows(u, 2, (1 - side) * 128, 128))
        c_z6(u).start()
        spread_c(u)

    def c10_outer(u):
        arrived(u, 26, out_rows(u, 2, far, 192))
        spread_c(u)

    everyone, inners, outers = None, inner, outer
    events = [
        (0, UNITS + 1, everyone, produce),
        (1, UNITS + 1, everyone, begin),
        (2, UNITS + 1, everyone, ab1),
        (2, UNITS, inners, c1_inner),
        (3, UNITS, inners, c2_inner),
        (3, UNITS + 1, everyone, ab2),
        (4, UNITS, outers, c3_outer),
        (4, UNITS + 1, inners, ab3_inner),
        (4, UNITS, inners, c4),
        (5, UNITS, outers, c4),
        (5, UNITS + 1, inners, ab4_inner),
        (5, UNITS, inners, c5),
        (6, UNITS, outers, c5),
        (6, UNITS + 1, inners, ab5_inner),
        (6, UNITS, inners, c6),
        (7, UNITS, outers, c6),
        (7, UNITS + 1, outers, ab5_outer),
        (7, UNITS, inners, c7),
        (8, UNITS, outers, c7_outer),
        (8, UNITS + 1, everyone, ab6),
        (9, UNITS, inners, c8_inner),
        (9, UNITS + 1, everyone, ab7),
        (10, UNITS, inners, c9_inner),
        (11, UNITS, outers, c10_outer),
    ]

    def step(t, carried):
        for lag, count, who, event in events:
            u = t - lag
            now = jnp.logical_and(u >= 0, u < count)
            if who is not None:
                now = jnp.logical_and(now, who)
            pl.when(now)(lambda event=event, u=u: event(u))
        return carried

    lax.fori_loop(0, UNITS + 11, step, 0)

    def drain(u, carried):
        @pl.when(u < UNITS)
        def _():
            place(u, core, 0, 512, lambda dst: to_other(u, 27, 0, 512)(dst).wait_send())
            place(u, core, 0, 512, lambda dst: to_own(u, 0, 0, 512)(dst).wait())
            place(u, 1 - core, 0, 512, lambda dst: to_other(u, 27, 0, 512)(dst).wait_recv())
            place(u, core, 512, 256, lambda dst: to_other(u, 28, 512, 256)(dst).wait_send())
            place(u, core, 512, 256, lambda dst: to_own(u, 1, 512, 256)(dst).wait())
            place(u, 1 - core, 512, 256, lambda dst: to_other(u, 28, 512, 256)(dst).wait_recv())
            c_x(u).wait_send()
            c_y(u).wait_send()
            c_back_y(u, mine).wait_send()
            c_back_x(u, half).wait_send()

            @pl.when(outer)
            def _():
                c_z1(u).wait_send()
                c_z4(u).wait_send()

            @pl.when(inner)
            def _():
                c_z2(u).wait_send()
                c_z3(u).wait_send()
                c_z5(u, side * 128).wait_send()
                c_z6(u).wait_send()

        for t in range(2):
            ab_first(u, t).wait_send()
            ab_second(u, t).wait_send()
            ab_back2(u, t, ab_base(t)).wait_send()
            ab_back1(u, t, first[t] * 128).wait_send()

        @pl.when(outer)
        def _():
            for t in range(2):
                ab_z1(u, t).wait_send()

        @pl.when(inner)
        def _():
            for t in range(2):
                ab_z2(u, t).wait_send()
                ab_z3(u, t, ab_base(t) + (z - 1) * 32).wait_send()
                ab_z4(u, t).wait_send()

        return carried

    lax.fori_loop(0, UNITS + 1, drain, 0)
    for u in range(UNITS - STAGES, UNITS):
        core_first(u).wait_send()
    for t in range(2):
        small_first(t).wait_send()
        small_other(t).wait_send()
        arrived(UNITS, 27 + t, small_out(1 - core, t))
        small_own(t).wait()
        pos_own(t).wait()


def summed_grads(lt, r, pos, small):
    vmem = pl.BlockSpec(memory_space=pltpu.VMEM)
    hbm = pl.BlockSpec(memory_space=pl.ANY)
    return pl.pallas_call(
        grads_kernel,
        out_shape=(
            jax.ShapeDtypeStruct((3072, 768), bf16),
            jax.ShapeDtypeStruct((768, 3072), bf16),
            jax.ShapeDtypeStruct((768, 768), bf16),
            jax.ShapeDtypeStruct((768, 2304), bf16),
            jax.ShapeDtypeStruct((128, 768), bf16),
            jax.ShapeDtypeStruct((256, 768), bf16),
        ),
        in_specs=[vmem] * 4,
        out_specs=(hbm,) * 6,
        scratch_shapes=[
            pltpu.VMEM((STAGES, 3 * ROWS, COLS), bf16),
            pltpu.VMEM((UNITS + 1, 3 * ROWS, COLS), bf16),
            pltpu.VMEM((UNITS + 1, 3 * ROWS, COLS), bf16),
            pltpu.VMEM((UNITS + 1, 3 * ROWS, COLS), bf16),
            pltpu.VMEM((UNITS + 1, 2, 288, COLS), bf16),
            pltpu.VMEM((UNITS, 432, COLS), bf16),
            pltpu.SemaphoreType.DMA((UNITS + 1, 29)),
            pltpu.SemaphoreType.DMA((UNITS + 1, 29)),
            pltpu.SemaphoreType.DMA((UNITS + 1, 4)),
        ],
        compiler_params=pltpu.CompilerParams(
            collective_id=0, has_side_effects=True, vmem_limit_bytes=58 << 20
        ),
        name="grads",
    )(lt, r, pos, small)


def forward(latents, valid, class_rows, seq_place, weights):
    (
        patch_weight,
        pos_table,
        qkv_weight,
        out_weight,
        ln1_gain,
        ln1_bias,
        ln2_gain,
        ln2_bias,
        up_weight,
        up_bias,
        down_weight,
        head_weight,
        head_bias,
    ) = weights
    images, patch_rows, channels = latents.shape
    model_width = qkv_weight.shape[1]
    head_count = model_width // HEAD_DIM
    latent_low = latents.astype(jnp.bfloat16)
    hidden = (
        matmul(latent_low, patch_weight)
        + pos_table.astype(jnp.float32)[None]
        + class_rows[:, None, :]
    )
    own_mask = valid.astype(jnp.bfloat16)
    normed = layer_norm(
        hidden, ln1_gain[0].astype(jnp.float32), ln1_bias[0].astype(jnp.float32)
    ).astype(jnp.bfloat16)
    packed = matmul(normed, qkv_weight[0]).astype(jnp.bfloat16)
    query = packed[..., :model_width].reshape(images, patch_rows, head_count, HEAD_DIM)
    keys_own = packed[..., model_width : 2 * model_width]
    values_own = packed[..., 2 * model_width :]
    prior_keys, prior_values, prior_mask = shifted_2((keys_own, values_own, own_mask), "seq", 1)
    keys = jnp.concatenate((prior_keys, keys_own), 1).reshape(
        images, 2 * patch_rows, head_count, HEAD_DIM
    )
    values = jnp.concatenate((prior_values, values_own), 1).reshape(
        images, 2 * patch_rows, head_count, HEAD_DIM
    )
    allowed = attention_mask(jnp.concatenate((prior_mask, own_mask), 1), patch_rows, seq_place)
    logits = masked_scores(query, keys, allowed)
    row_peak = jnp.max(logits, -1, keepdims=True)
    log_total = row_peak + jnp.log(jnp.sum(jnp.exp(logits - row_peak), -1, keepdims=True))
    weights_soft = jnp.exp(logits - log_total).astype(jnp.bfloat16)
    attended = jnp.einsum(
        "bhqk,bkhd->bqhd", weights_soft, values, preferred_element_type=jnp.float32
    )
    attended = attended.astype(jnp.bfloat16).reshape(images, patch_rows, model_width)
    mid = hidden + matmul(attended, out_weight[0])
    second = layer_norm(
        mid, ln2_gain[0].astype(jnp.float32), ln2_bias[0].astype(jnp.float32)
    ).astype(jnp.bfloat16)
    preact = matmul(second, up_weight[0]) + up_bias[0].astype(jnp.float32)
    activated = jax.nn.gelu(preact, approximate=True).astype(jnp.bfloat16)
    saved = [
        (
            hidden,
            normed,
            query,
            keys,
            values,
            allowed,
            log_total,
            attended,
            mid,
            second,
            preact,
            activated,
        )
    ]
    hidden = mid + matmul(activated, down_weight[0])
    top_low = hidden.astype(jnp.bfloat16)
    head_out = matmul(top_low, head_weight) + head_bias.astype(jnp.float32)
    prior_row = shifted_2(head_out[:, patch_rows - 1, :], "seq", 1)
    shifted = jnp.concatenate((prior_row[:, None, :], head_out[:, : patch_rows - 1, :]), 1)
    shifted = shifted * valid.astype(jnp.float32)[..., None]
    alpha = shifted[..., :channels]
    shift_mean = shifted[..., channels:]
    factor = jnp.exp(-alpha)
    new_latents = (latents - shift_mean) * factor
    logdet_part = -jnp.sum(alpha, (1, 2))
    return (new_latents, logdet_part, factor, top_low, saved)


def local(
    latents,
    valid,
    class_labels,
    group_perm,
    patch_weight,
    pos_table,
    class_table,
    ln1_gain,
    ln1_bias,
    qkv_weight,
    out_weight,
    ln2_gain,
    ln2_bias,
    up_weight,
    up_bias,
    down_weight,
    head_weight,
    head_bias,
    cot_latents,
    cot_logdet,
):
    images, patch_rows, channels = latents.shape
    model_width = qkv_weight.shape[1]
    head_count = model_width // HEAD_DIM
    layer_total = qkv_weight.shape[0]
    seq_place = lax.axis_index("seq")
    picks = group_perm[:, None] == lax.iota(jnp.int32, class_labels.shape[0])[None, :]
    image_labels = jnp.sum(jnp.where(picks, class_labels[None, :], 0), 1)
    label_hot = image_labels[:, None] == lax.iota(jnp.int32, class_table.shape[0])[None, :]
    class_rows = matmul(label_hot.astype(jnp.bfloat16), class_table)
    weights = (
        patch_weight,
        pos_table,
        qkv_weight,
        out_weight,
        ln1_gain,
        ln1_bias,
        ln2_gain,
        ln2_bias,
        up_weight,
        up_bias,
        down_weight,
        head_weight,
        head_bias,
    )
    new_latents, logdet_part, factor, top_low, saved = forward(
        latents, valid, class_rows, seq_place, weights
    )
    valid_float = valid.astype(jnp.float32)
    d_alpha = -cot_latents * new_latents - cot_logdet[:, None, None]
    d_mean = -cot_latents * factor
    d_shifted = jnp.concatenate((d_alpha, d_mean), -1) * valid_float[..., None]
    next_row = shifted_2(d_shifted[:, 0, :], "seq", -1)
    d_head = jnp.concatenate((d_shifted[:, 1:, :], next_row[:, None, :]), 1).astype(jnp.bfloat16)
    head_weight_grad = outer_sum(top_low, d_head)
    head_bias_grad = jnp.sum(d_head.astype(jnp.float32), (0, 1))
    d_hidden = transposed(d_head, head_weight)
    grads_qkv, grads_out, grads_up, grads_down = ([], [], [], [])
    grads_g1, grads_b1, grads_g2, grads_b2, grads_ub = ([], [], [], [], [])
    for layer_index in reversed(range(layer_total)):
        (
            hidden,
            normed,
            query,
            keys,
            values,
            allowed,
            log_total,
            attended,
            mid,
            second,
            preact,
            activated,
        ) = saved[layer_index]
        d_down = d_hidden.astype(jnp.bfloat16)
        down_grad = (activated, d_down)
        d_act = transposed(d_down, down_weight[layer_index])
        unused_gelu, gelu_pull = jax.vjp(lambda inner: jax.nn.gelu(inner, approximate=True), preact)
        d_pre = gelu_pull(d_act)[0].astype(jnp.bfloat16)
        up_bias_grad = jnp.sum(d_pre.astype(jnp.float32), (0, 1))
        up_grad = (second, d_pre)
        d_second = transposed(d_pre, up_weight[layer_index])
        unused_norm, norm_pull = jax.vjp(
            layer_norm,
            mid,
            ln2_gain[layer_index].astype(jnp.float32),
            ln2_bias[layer_index].astype(jnp.float32),
        )
        d_mid_norm, ln2_gain_part, ln2_bias_part = norm_pull(d_second)
        d_mid = d_hidden + d_mid_norm
        d_proj = d_mid.astype(jnp.bfloat16)
        out_grad = (attended, d_proj)
        d_attended = transposed(d_proj, out_weight[layer_index]).astype(jnp.bfloat16)
        d_attended = d_attended.reshape(images, patch_rows, head_count, HEAD_DIM)
        logits = masked_scores(query, keys, allowed)
        probs = jnp.exp(logits - log_total)
        d_probs = jnp.einsum(
            "bqhd,bkhd->bhqk", d_attended, values, preferred_element_type=jnp.float32
        )
        d_scores = (probs * (d_probs - jnp.sum(d_probs * probs, -1, keepdims=True))).astype(
            jnp.bfloat16
        )
        d_query = jnp.einsum(
            "bhqk,bkhd->bqhd", d_scores, keys, preferred_element_type=jnp.float32
        ) * HEAD_DIM ** (-0.5)
        d_keys = jnp.einsum(
            "bhqk,bqhd->bkhd", d_scores, query, preferred_element_type=jnp.float32
        ) * HEAD_DIM ** (-0.5)
        d_values = jnp.einsum(
            "bhqk,bqhd->bkhd",
            probs.astype(jnp.bfloat16),
            d_attended,
            preferred_element_type=jnp.float32,
        )
        d_keys = d_keys.reshape(images, 2 * patch_rows, model_width)
        d_values = d_values.reshape(images, 2 * patch_rows, model_width)
        back_keys, back_values = (
            shifted_2(d_keys[:, :patch_rows].astype(jnp.bfloat16), "seq", -1).astype(jnp.float32),
            shifted_2(d_values[:, :patch_rows].astype(jnp.bfloat16), "seq", -1).astype(jnp.float32),
        )
        d_packed = jnp.concatenate(
            (
                d_query.reshape(images, patch_rows, model_width),
                d_keys[:, patch_rows:] + back_keys,
                d_values[:, patch_rows:] + back_values,
            ),
            -1,
        ).astype(jnp.bfloat16)
        qkv_grad = (normed, d_packed)
        d_normed = transposed(d_packed, qkv_weight[layer_index])
        unused_norm, norm_pull = jax.vjp(
            layer_norm,
            hidden,
            ln1_gain[layer_index].astype(jnp.float32),
            ln1_bias[layer_index].astype(jnp.float32),
        )
        d_input, ln1_gain_part, ln1_bias_part = norm_pull(d_normed)
        d_hidden = d_mid + d_input
        grads_qkv.insert(0, qkv_grad)
        grads_out.insert(0, out_grad)
        grads_up.insert(0, up_grad)
        grads_down.insert(0, down_grad)
        grads_g1.insert(0, ln1_gain_part)
        grads_b1.insert(0, ln1_bias_part)
        grads_g2.insert(0, ln2_gain_part)
        grads_b2.insert(0, ln2_bias_part)
        grads_ub.insert(0, up_bias_grad)
    d_embed_low = d_hidden.astype(jnp.bfloat16)
    patch_grad_part = outer_sum(latents.astype(jnp.bfloat16), d_embed_low)
    latents_grad = cot_latents * factor + transposed(d_embed_low, patch_weight)
    pos_part = jnp.sum(d_hidden, 0)
    class_part = jnp.sum(d_hidden, 1)
    small_parts = (
        patch_grad_part,
        head_weight_grad,
        head_bias_grad,
        grads_g1[0],
        grads_b1[0],
        grads_g2[0],
        grads_b2[0],
        grads_ub[0],
    )
    if lax.axis_size("dp") == 16 and lax.axis_size("seq") == 2:
        return (new_latents,) + kernel_sums(
            logdet_part, latents_grad, pos_part, class_part, label_hot, class_labels, small_parts,
            grads_qkv[0], grads_out[0], grads_up[0], grads_down[0],
        )
    return (new_latents,) + plain_sums(
        logdet_part, latents_grad, pos_part, class_part, label_hot, small_parts,
        grads_qkv[0], grads_out[0], grads_up[0], grads_down[0],
    )


def kernel_sums(
    logdet_part, latents_grad, pos_part, class_part, label_hot, class_labels, small_parts, qkv, out, up, down
):
    dp = lax.axis_index("dp")
    count = lax.axis_size("dp")
    patch, head, head_bias, g1, b1, g2, b2, ub = small_parts
    model_width = 768

    def columns(matrix):
        width = matrix.shape[-1] // model_width
        return matrix.reshape(128, width, model_width).transpose(1, 0, 2)

    lefts = jnp.concatenate(
        (columns(down[0][0]), columns(up[0][0]), columns(out[0][0]), columns(qkv[0][0]))
    ).transpose(0, 2, 1)
    rights = jnp.concatenate(
        (columns(down[1][0]), columns(up[1][0]), columns(out[1][0]), columns(qkv[1][0]))
    )
    rights = rights.reshape(9, 128, 2, COLS).transpose(0, 2, 1, 3)
    slot = (lax.iota(jnp.int32, count) == dp).astype(f32)
    misc = jnp.concatenate(
        (head_bias, slot * logdet_part[0], jnp.zeros((model_width - head_bias.shape[0] - count,), f32))
    )
    small = jnp.concatenate(
        (
            patch,
            head.T,
            slot[:, None] * class_part,
            g1[None],
            b1[None],
            g2[None],
            b2[None],
            ub.reshape(4, model_width),
            misc[None],
            jnp.zeros((256 - 169, model_width), f32),
        )
    ).astype(bf16)
    small = small.reshape(2, 128, 2, COLS).transpose(0, 2, 1, 3)
    pos = pos_part.astype(bf16).reshape(128, 2, COLS).transpose(1, 0, 2)
    down_sum, up_sum, out_sum, qkv_sum, pos_sum, small_sum = summed_grads(lefts, rights, pos, small)
    pos_grad = pos_sum.astype(f32)
    sums = small_sum.astype(f32)
    class_rows = sums[144:160]
    misc = sums[168]
    owned = label_hot.shape[1] // count
    own_rows = dp * owned + lax.iota(jnp.int32, owned)
    own = (stored_labels(class_labels)[:, None] == own_rows[None, :]).astype(f32)
    class_grad = lax.dot_general(
        own, class_rows, (((0,), (0,)), ((), ())), precision=precise, preferred_element_type=f32
    )
    logdet = lax.dynamic_slice_in_dim(misc, head_bias.shape[0] + dp, 1)

    return (
        logdet,
        latents_grad,
        sums[:48],
        pos_grad,
        class_grad,
        sums[160:161],
        sums[161:162],
        qkv_sum.astype(f32)[None],
        out_sum.astype(f32)[None],
        sums[162:163],
        sums[163:164],
        up_sum.astype(f32)[None],
        sums[164:168].reshape(1, -1),
        down_sum.astype(f32)[None],
        sums[48:144].T,
        misc[: head_bias.shape[0]],
    )


def stored_labels(class_labels):
    place = lax.iota(jnp.int32, class_labels.shape[0])
    less = class_labels[:, None] < class_labels[None, :]
    tie = (class_labels[:, None] == class_labels[None, :]) & (place[:, None] < place[None, :])
    rank = jnp.sum((less | tie).astype(jnp.int32), 0)
    return jnp.sum(jnp.where(rank[:, None] == place[None, :], class_labels[:, None], 0), 0)


def plain_sums(
    logdet_part, latents_grad, pos_part, class_part, label_hot, small_parts, qkv, out, up, down
):
    logdet, class_sums = lax.psum((logdet_part, class_part), "seq")
    class_term = lax.dot_general(
        label_hot.astype(jnp.float32),
        class_sums,
        (((0,), (0,)), ((), ())),
        precision=precise,
        preferred_element_type=jnp.float32,
    )
    class_grad = lax.psum_scatter(class_term, "dp", scatter_dimension=0, tiled=True)
    pos_grad = lax.psum(pos_part, "dp")
    patch, head, head_bias, g1, b1, g2, b2, ub = lax.psum(small_parts, ("dp", "seq"))

    def gathered(pair):
        grad = outer_sum(*pair)
        share = lax.psum_scatter(eight_rows(grad), ("dp", "seq"), scatter_dimension=1, tiled=True)
        every = lax.all_gather(share.astype(jnp.bfloat16), ("dp", "seq"), axis=1, tiled=True)
        return every.astype(jnp.float32).reshape((1,) + grad.shape)

    return (
        logdet,
        latents_grad,
        patch,
        pos_grad,
        class_grad,
        g1[None],
        b1[None],
        gathered(qkv),
        gathered(out),
        g2[None],
        b2[None],
        gathered(up),
        ub[None],
        gathered(down),
        head,
        head_bias,
    )


def solution(mesh):
    in_specs = (
        P("dp", "seq", None),
        P("dp", "seq"),
        P(),
        P("dp"),
        P(),
        P("seq", None),
        P(),
        P(),
        P(),
        P(),
        P(),
        P(),
        P(),
        P(),
        P(),
        P(),
        P(),
        P(),
        P("dp", "seq", None),
        P("dp"),
    )
    out_specs = (
        P("dp", "seq", None),
        P("dp"),
        P("dp", "seq", None),
        P(),
        P("seq", None),
        P("dp", None),
        P(),
        P(),
        P(),
        P(),
        P(),
        P(),
        P(),
        P(),
        P(),
        P(),
        P(),
    )
    return jax.shard_map(local, mesh=mesh, in_specs=in_specs, out_specs=out_specs, check_vma=False)
```

```python
import jax
import jax.numpy as jnp
from jax import lax
from jax.experimental import pallas as pl
from jax.experimental.pallas import tpu as pltpu
from jax.sharding import PartitionSpec as P

HEAD_DIM = 64


precise = lax.Precision.HIGHEST
norm_eps = 1e-05


def shifted_2(shard, axis, by):
    size = lax.axis_size(axis)
    pairs = [(i, i + by) for i in range(size) if 0 <= i + by < size]
    return lax.ppermute(shard, axis, pairs)


def layer_norm(values, norm_gain, norm_bias):
    center = values - jnp.mean(values, -1, keepdims=True)
    spread = jnp.mean(center * center, -1, keepdims=True)
    return center * lax.rsqrt(spread + norm_eps) * norm_gain + norm_bias


def matmul(left_side, weight_mat):
    return jnp.dot(left_side, weight_mat, preferred_element_type=jnp.float32)


def outer_sum(left_side, grad_side):
    left_flat = left_side.reshape(-1, left_side.shape[-1])
    grad_flat = grad_side.reshape(-1, grad_side.shape[-1])
    return lax.dot_general(
        left_flat, grad_flat, (((0,), (0,)), ((), ())), preferred_element_type=jnp.float32
    )


def transposed(grad_side, weight_mat):
    return lax.dot_general(
        grad_side,
        weight_mat,
        (((grad_side.ndim - 1,), (1,)), ((), ())),
        preferred_element_type=jnp.float32,
    )


def eight_rows(matrix):
    return matrix.reshape(8, -1)


def attention_mask(key_valid, patch_rows, seq_place):
    query_pos = seq_place * patch_rows + lax.iota(jnp.int32, patch_rows)
    key_pos = (seq_place - 1) * patch_rows + lax.iota(jnp.int32, 2 * patch_rows)
    earlier = (key_pos[None, :] < query_pos[:, None])[None] & (key_valid[:, None, :] > 0)
    return earlier | (key_pos[None, :] == query_pos[:, None])[None]


def masked_scores(query, keys, allowed):
    logits = jnp.einsum(
        "bqhd,bkhd->bhqk", query, keys, preferred_element_type=jnp.float32
    ) * HEAD_DIM ** (-0.5)
    return jnp.where(allowed[:, None], logits, -1e30)


MESH = pl.DeviceIdType.MESH
UNITS = 12
ROWS = 256
COLS = 384
STAGES = 3
CHUNK = 32
GELU_A = (2.0 / 3.141592653589793) ** 0.5
GELU_B = 0.044715
f32 = jnp.float32
bf16 = jnp.bfloat16


def flow_kernel(
    labels_sm, perm_sm, cot_logdet_sm,
    latents_ref, valid_ref, patch_ref, pos_table_ref, g1_ref, b1_ref, g2_ref, b2_ref,
    up_bias_ref, head_w_ref, head_b_ref, cot_ref,
    class_hbm, qkv_any, out_any, up_any, down_any,
    down_hbm, up_hbm, out_hbm, qkv_hbm, pos_hbm, small_hbm, latents_hbm,
    stage, part, full, core_in, ab_in, c_in, send_sem, recv_sem, local_sem,
    qkv_w, out_w, up_w, down_w, load_sem,
    lat_pad, cot_pad, patch_pad, head_pad, hidden, mid, xhat1, xhat2, scale1, scale2,
    keys, values, query, attended, bias, prior_mask, mask_row, probs, slope, d_hidden, d_second, d_att, d_keys, d_values,
    d_prior, d_back, row_out, row_in, grad_out, grad_in, lat_out,
    lt_ref, r_ref, pos_ref, small_ref, ub_grad, low_top, exch_send, exch_recv, lat_sem,
):
    dp = lax.axis_index("dp")
    core = lax.axis_index("seq")
    x, y, z = dp % 2, (dp // 2) % 2, dp // 4
    side = z // 2
    inner = ((z + 1) // 2) % 2 == 1
    outer = ((z + 1) // 2) % 2 == 0
    to_core = (dp, 1 - core)
    to_x = (dp + 1 - 2 * x, core)
    to_y = (dp + 2 - 4 * y, core)
    to_mate = (dp + 4 - 8 * (z % 2), core)
    to_inner = ((dp + 12 - 8 * z + 16) % 16, core)

    def rows_at(start, count):
        return pl.ds(pl.multiple_of(start, 16), count)

    sources = [class_hbm.at[r : r + n, h * COLS : (h + 1) * COLS] for h in range(2) for r, n in ((0, 768), (768, 256))]
    targets = [part.at[2 * h + i, 0:n] for h in range(2) for i, n in ((0, 768), (1, 256))]
    sources += [qkv_any.at[0], out_any.at[0], up_any.at[0], down_any.at[0]]
    targets += [qkv_w, out_w, up_w, down_w]

    def load(i):
        return pltpu.make_async_copy(sources[i], targets[i], load_sem.at[i])

    for i in range(8):
        load(i).start()

    barrier = pltpu.get_barrier_semaphore()
    for target in (to_core, to_x, to_y, to_mate):
        pl.semaphore_signal(barrier, inc=1, device_id=target, device_id_type=MESH)

    @pl.when(inner)
    def _():
        pl.semaphore_signal(barrier, inc=1, device_id=to_inner, device_id_type=MESH)
        pl.semaphore_wait(barrier, 5)

    @pl.when(outer)
    def _():
        pl.semaphore_wait(barrier, 4)

    def copy(u, k, src, dst, target):
        return pltpu.make_async_remote_copy(
            src_ref=src, dst_ref=dst, send_sem=send_sem.at[u, k], recv_sem=recv_sem.at[u, k],
            device_id=target, device_id_type=MESH,
        )

    def arrived(u, k, dst):
        copy(u, k, dst, dst, to_core).wait_recv()

    def added(dst, left, right):
        dst[...] = (left[...].astype(f32) + right[...].astype(f32)).astype(bf16)

    first = (x, y)
    second = (y, x)
    to_first = (to_x, to_y)
    to_second = (to_y, to_x)

    def out_rows(u, t, start, count):
        return full.at[u, rows_at(t * ROWS + start, count)]

    def part_rows(u, t, start, count):
        return part.at[u, rows_at(t * ROWS + start, count)]

    def left_index(u):
        return jnp.minimum(u, 4) + jnp.minimum(jnp.maximum(u - 7, 0), 2)

    def right_index(u):
        return jnp.maximum(u - 3, 0)

    small_rows = (slice(128, 256), slice(384, 512))

    def core_first(u):
        return copy(u, 0, stage.at[u % STAGES], core_in.at[u], to_core)

    def small_first(t):
        return copy(UNITS, 25 + t, small_ref.at[1 - core, t], core_in.at[UNITS, small_rows[t]], to_core)

    def produce(u):
        @pl.when(jnp.logical_and(u >= STAGES, u < UNITS))
        def _():
            core_first(u - STAGES).wait_send()

        @pl.when(u < UNITS)
        def _():
            right = r_ref[right_index(u), 1 - core]
            for t in range(3):
                product = jnp.dot(
                    lt_ref[left_index(u), t * ROWS : (t + 1) * ROWS], right, preferred_element_type=f32
                )
                stage[u % STAGES, t * ROWS : (t + 1) * ROWS] = product.astype(bf16)
            core_first(u).start()

        @pl.when(u == UNITS)
        def _():
            for t in range(2):
                small_first(t).start()

    def begin(u):
        @pl.when(u < UNITS)
        def _():
            arrived(u, 0, core_in.at[u])
            right = r_ref[right_index(u), core]
            for t in range(3):
                rows = slice(t * ROWS, (t + 1) * ROWS)
                product = jnp.dot(lt_ref[left_index(u), rows], right, preferred_element_type=f32)
                part[u, rows] = (product + core_in[u, rows].astype(f32)).astype(bf16)
                if t < 2:
                    ab_first(u, t).start()

            @pl.when(outer)
            def _():
                c_z1(u).start()

        @pl.when(u == UNITS)
        def _():
            for t in range(2):
                arrived(UNITS, 25 + t, core_in.at[UNITS, small_rows[t]])
                part[UNITS, t * ROWS : t * ROWS + 128] = pos_ref[t]
                part[UNITS, small_rows[t]] = (
                    small_ref[core, t].astype(f32) + core_in[UNITS, small_rows[t]].astype(f32)
                ).astype(bf16)
                ab_first(u, t).start()

    def ab_first(u, t):
        return copy(u, 1 + t, part_rows(u, t, (1 - first[t]) * 128, 128), ab_in.at[u, t, 0:128], to_first[t])

    def ab_second(u, t):
        row = first[t] * 128 + (1 - second[t]) * 64
        return copy(u, 3 + t, part_rows(u, t, row, 64), ab_in.at[u, t, 128:192], to_second[t])

    def ab_base(t):
        return first[t] * 128 + second[t] * 64

    def ab_z1(u, t):
        return copy(u, 5 + t, part_rows(u, t, ab_base(t), 64), ab_in.at[u, t, 192:256], to_mate)

    def ab_z2(u, t):
        return copy(
            u, 7 + t, part_rows(u, t, ab_base(t) + (2 - z) * 32, 32), ab_in.at[u, t, 256:288], to_inner
        )

    def ab_z3(u, t, row):
        block = out_rows(u, t, row, 32)
        return copy(u, 9 + t, block, block, to_inner)

    def ab_z4(u, t):
        block = out_rows(u, t, ab_base(t), 64)
        return copy(u, 11 + t, block, block, to_mate)

    def ab_back2(u, t, row):
        block = out_rows(u, t, row, 64)
        return copy(u, 13 + t, block, block, to_second[t])

    def ab_back1(u, t, row):
        block = out_rows(u, t, row, 128)
        return copy(u, 15 + t, block, block, to_first[t])

    def ab1(u):
        for t in range(2):
            arrived(u, 1 + t, ab_in.at[u, t, 0:128])
            kept = part_rows(u, t, first[t] * 128, 128)
            added(kept, kept, ab_in.at[u, t, 0:128])
            ab_second(u, t).start()

    def ab2(u):
        for t in range(2):
            arrived(u, 3 + t, ab_in.at[u, t, 128:192])
            kept = part_rows(u, t, ab_base(t), 64)
            added(kept, kept, ab_in.at[u, t, 128:192])

        @pl.when(outer)
        def _():
            for t in range(2):
                ab_z1(u, t).start()

    def ab3_inner(u):
        for t in range(2):
            arrived(u, 5 + t, ab_in.at[u, t, 192:256])
            kept = part_rows(u, t, ab_base(t), 64)
            added(kept, kept, ab_in.at[u, t, 192:256])
            ab_z2(u, t).start()

    def ab4_inner(u):
        for t in range(2):
            arrived(u, 7 + t, ab_in.at[u, t, 256:288])
            row = ab_base(t) + (z - 1) * 32
            added(out_rows(u, t, row, 32), part_rows(u, t, row, 32), ab_in.at[u, t, 256:288])
            ab_z3(u, t, row).start()

    def ab5_inner(u):
        for t in range(2):
            arrived(u, 9 + t, out_rows(u, t, ab_base(t) + (2 - z) * 32, 32))
            ab_z4(u, t).start()
            ab_back2(u, t, ab_base(t)).start()

    def ab5_outer(u):
        for t in range(2):
            arrived(u, 11 + t, out_rows(u, t, ab_base(t), 64))
            ab_back2(u, t, ab_base(t)).start()

    def ab6(u):
        for t in range(2):
            arrived(u, 13 + t, out_rows(u, t, first[t] * 128 + (1 - second[t]) * 64, 64))
            ab_back1(u, t, first[t] * 128).start()

    def place(u, h, row, count, act):
        def columns(base):
            return pl.ds(pl.multiple_of(base + h * COLS, 128), COLS)

        @pl.when(u < 4)
        def _():
            act(down_hbm.at[pl.ds(pl.multiple_of(u * 768 + row, 16), count), columns(0)])

        @pl.when(jnp.logical_and(u >= 4, u < 8))
        def _():
            act(up_hbm.at[row : row + count, columns((u - 4) * 768)])

        @pl.when(u == 8)
        def _():
            act(out_hbm.at[row : row + count, columns(0)])

        @pl.when(jnp.logical_and(u >= 9, u < UNITS))
        def _():
            act(qkv_hbm.at[row : row + count, columns((u - 9) * 768)])

    def to_other(u, k, row, count):
        return lambda dst: copy(u, k, full.at[u, row : row + count], dst, to_core)

    def to_own(u, k, row, count):
        return lambda dst: pltpu.make_async_copy(full.at[u, row : row + count], dst, local_sem.at[u, k])

    def spread_ab(u):
        place(u, core, 0, 512, lambda dst: to_other(u, 27, 0, 512)(dst).start())
        place(u, core, 0, 512, lambda dst: to_own(u, 0, 0, 512)(dst).start())

    def spread_c(u):
        place(u, core, 512, 256, lambda dst: to_other(u, 28, 512, 256)(dst).start())
        place(u, core, 512, 256, lambda dst: to_own(u, 1, 512, 256)(dst).start())

    def small_out(h, t):
        return small_hbm.at[pl.ds(pl.multiple_of(h * 128, 128), 128), t * COLS : (t + 1) * COLS]

    def small_other(t):
        return copy(UNITS, 27 + t, full.at[UNITS, small_rows[t]], small_out(core, t), to_core)

    def small_own(t):
        return pltpu.make_async_copy(
            full.at[UNITS, small_rows[t]], small_out(core, t), local_sem.at[UNITS, t]
        )

    def pos_own(t):
        return pltpu.make_async_copy(
            full.at[UNITS, t * ROWS : t * ROWS + 128],
            pos_hbm.at[:, t * COLS : (t + 1) * COLS],
            local_sem.at[UNITS, 2 + t],
        )

    def ab7(u):
        for t in range(2):
            arrived(u, 15 + t, out_rows(u, t, (1 - first[t]) * 128, 128))
        spread_ab(u)

        @pl.when(u == UNITS)
        def _():
            for t in range(2):
                small_other(t).start()
                small_own(t).start()
                pos_own(t).start()

    far = 64 * (1 - side)
    own_end = 192 * side
    shard = z * 64
    half = shard + x * 32
    mine = half + y * 16

    def c_z1(u):
        return copy(u, 17, part_rows(u, 2, far, 192), c_in.at[u, 0:192], to_mate)

    def c_z2(u):
        return copy(u, 18, part_rows(u, 2, (1 - side) * 128, 128), c_in.at[u, 192:320], to_inner)

    def c_z3(u):
        return copy(u, 19, part_rows(u, 2, own_end, 64), c_in.at[u, 320:384], to_mate)

    def c_x(u):
        return copy(u, 20, part_rows(u, 2, shard + (1 - x) * 32, 32), c_in.at[u, 384:416], to_x)

    def c_y(u):
        return copy(u, 21, part_rows(u, 2, half + (1 - y) * 16, 16), c_in.at[u, 416:432], to_y)

    def c_back_y(u, row):
        block = out_rows(u, 2, row, 16)
        return copy(u, 22, block, block, to_y)

    def c_back_x(u, row):
        block = out_rows(u, 2, row, 32)
        return copy(u, 23, block, block, to_x)

    def c_z4(u):
        block = out_rows(u, 2, own_end, 64)
        return copy(u, 24, block, block, to_mate)

    def c_z5(u, row):
        block = out_rows(u, 2, row, 128)
        return copy(u, 25, block, block, to_inner)

    def c_z6(u):
        block = out_rows(u, 2, far, 192)
        return copy(u, 26, block, block, to_mate)

    def c1_inner(u):
        arrived(u, 17, c_in.at[u, 0:192])
        kept = part_rows(u, 2, far, 192)
        added(kept, kept, c_in.at[u, 0:192])
        c_z2(u).start()

    def c2_inner(u):
        arrived(u, 18, c_in.at[u, 192:320])
        kept = part_rows(u, 2, side * 128, 128)
        added(kept, kept, c_in.at[u, 192:320])
        c_z3(u).start()
        c_x(u).start()

    def c3_outer(u):
        arrived(u, 19, c_in.at[u, 320:384])
        kept = part_rows(u, 2, shard, 64)
        added(kept, kept, c_in.at[u, 320:384])
        c_x(u).start()

    def c4(u):
        arrived(u, 20, c_in.at[u, 384:416])
        kept = part_rows(u, 2, half, 32)
        added(kept, kept, c_in.at[u, 384:416])
        c_y(u).start()

    def c5(u):
        arrived(u, 21, c_in.at[u, 416:432])
        added(out_rows(u, 2, mine, 16), part_rows(u, 2, mine, 16), c_in.at[u, 416:432])
        c_back_y(u, mine).start()

    def c6(u):
        arrived(u, 22, out_rows(u, 2, half + (1 - y) * 16, 16))
        c_back_x(u, half).start()

    def c7(u):
        arrived(u, 23, out_rows(u, 2, shard + (1 - x) * 32, 32))

    def c7_outer(u):
        c7(u)
        c_z4(u).start()

    def c8_inner(u):
        arrived(u, 24, out_rows(u, 2, own_end, 64))
        c_z5(u, side * 128).start()

    def c9_inner(u):
        arrived(u, 25, out_rows(u, 2, (1 - side) * 128, 128))
        c_z6(u).start()
        spread_c(u)

    def c10_outer(u):
        arrived(u, 26, out_rows(u, 2, far, 192))
        spread_c(u)

    everyone, inners, outers = None, inner, outer
    events = [
        (0, UNITS + 1, everyone, produce),
        (1, UNITS + 1, everyone, begin),
        (2, UNITS + 1, everyone, ab1),
        (2, UNITS, inners, c1_inner),
        (3, UNITS, inners, c2_inner),
        (3, UNITS + 1, everyone, ab2),
        (4, UNITS, outers, c3_outer),
        (4, UNITS + 1, inners, ab3_inner),
        (4, UNITS, inners, c4),
        (5, UNITS, outers, c4),
        (5, UNITS + 1, inners, ab4_inner),
        (5, UNITS, inners, c5),
        (6, UNITS, outers, c5),
        (6, UNITS + 1, inners, ab5_inner),
        (6, UNITS, inners, c6),
        (7, UNITS, outers, c6),
        (7, UNITS + 1, outers, ab5_outer),
        (7, UNITS, inners, c7),
        (8, UNITS, outers, c7_outer),
        (8, UNITS + 1, everyone, ab6),
        (9, UNITS, inners, c8_inner),
        (9, UNITS + 1, everyone, ab7),
        (10, UNITS, inners, c9_inner),
        (11, UNITS, outers, c10_outer),
    ]

    def step(t, carried):
        for lag, count, who, event in events:
            u = t - lag
            now = jnp.logical_and(u >= 0, u < count)
            if who is not None:
                now = jnp.logical_and(now, who)
            pl.when(now)(lambda event=event, u=u: event(u))
        return carried

    mm_nt = (((1,), (1,)), ((), ()))
    mm_tn = (((0,), (0,)), ((), ()))

    def nt(left, right):
        return lax.dot_general(left, right, mm_nt, preferred_element_type=f32)

    def tn(left, right):
        return lax.dot_general(left, right, mm_tn, preferred_element_type=f32)

    def nn(left, right):
        return jnp.dot(left, right, preferred_element_type=f32)

    def exchange(k, src, dst):
        return pltpu.make_async_remote_copy(
            src_ref=src, dst_ref=dst, send_sem=exch_send.at[k], recv_sem=exch_recv.at[k],
            device_id=to_core, device_id_type=MESH,
        )

    chunks = [slice(r, r + CHUNK) for r in range(0, 128, CHUNK)]
    lane = lax.broadcasted_iota(jnp.int32, (128, 128), 1)
    row = lax.broadcasted_iota(jnp.int32, (128, 128), 0)
    eye = row == lane
    low_half = lane < 64
    valid_row = valid_ref[...].astype(f32)
    valid_col = jnp.sum(jnp.where(eye, valid_row, 0.0), axis=1, keepdims=True)
    mask_row[...] = jnp.broadcast_to(valid_row, (8, 128))
    lat_pad[...] = jnp.zeros((128, 128), f32)
    lat_pad[:, 0:48] = latents_ref[0]
    cot_pad[...] = jnp.zeros((128, 128), f32)
    cot_pad[:, 0:48] = cot_ref[0]
    patch_pad[...] = jnp.zeros((128, 768), bf16)
    patch_pad[0:48] = patch_ref[...]
    head_pad[...] = jnp.zeros((768, 128), bf16)
    head_pad[:, 0:96] = head_w_ref[...]
    head_bias = jnp.concatenate((head_b_ref[...].astype(f32), jnp.zeros((1, 32), f32)), 1)

    @pl.when(core == 0)
    def _():
        keys[0:128] = jnp.zeros((128, 768), bf16)
        values[0:128] = jnp.zeros((128, 768), bf16)
        prior_mask[...] = jnp.zeros((8, 128), f32)
        row_in[...] = jnp.zeros((8, 128), f32)

    @pl.when(core == 1)
    def _():
        grad_in[...] = jnp.zeros((8, 128), f32)
        d_back[...] = jnp.zeros((2, 128, 768), bf16)

    @pl.when(core == 0)
    def _():
        exchange(2, mask_row, prior_mask).start()

    def normalize(src, hat, scale, gain, shift, put):
        for r in chunks:
            v = src[r]
            center = v - jnp.mean(v, -1, keepdims=True)
            inv = lax.rsqrt(jnp.mean(center * center, -1, keepdims=True) + norm_eps)
            scaled = center * inv
            hat[r] = scaled
            scale[r] = inv
            put(r, scaled * gain + shift)

    label = labels_sm[perm_sm[0]]
    hot = jnp.where(lax.broadcasted_iota(jnp.int32, (16, 1024), 1) == label, 1.0, 0.0).astype(bf16)
    for i in range(4):
        load(i).wait()
    class_row = jnp.concatenate(
        [nn(hot[:, 0:768], part[2 * h]) + nn(hot[:, 768:1024], part[2 * h + 1, 0:256]) for h in range(2)], 1
    )[0:1]
    hidden[...] = (
        nn(lat_pad[...].astype(bf16), patch_pad[...]) + pos_table_ref[...].astype(f32) + class_row
    )

    def put_low(r, v):
        low_top[r] = v.astype(bf16)

    normalize(hidden, xhat1, scale1, g1_ref[...].astype(f32), b1_ref[...].astype(f32), put_low)
    load(4).wait()
    normed = low_top[...]
    keys[128:256] = nn(normed, qkv_w[:, 768:1536]).astype(bf16)

    @pl.when(core == 0)
    def _():
        exchange(0, keys.at[128:256], keys.at[0:128]).start()

    values[128:256] = nn(normed, qkv_w[:, 1536:2304]).astype(bf16)

    @pl.when(core == 0)
    def _():
        exchange(1, values.at[128:256], values.at[0:128]).start()

    query[...] = nn(normed, qkv_w[:, 0:768]).astype(bf16)
    lt_ref[6] = normed.astype(f32).T.astype(bf16)

    @pl.when(core == 1)
    def _():
        exchange(2, mask_row, prior_mask).wait_recv()
        exchange(0, keys.at[128:256], keys.at[0:128]).wait_recv()
        exchange(1, values.at[128:256], values.at[0:128]).wait_recv()

    bias[:, 0:128] = jnp.where(jnp.broadcast_to(prior_mask[0:1], (128, 128)) > 0.5, 0.0, -1e30)
    bias[:, 128:256] = jnp.where(((lane < row) & (valid_row > 0.5)) | eye, 0.0, -1e30)

    def columns128(p):
        return pl.ds(pl.multiple_of(p * 128, 128), 128)

    def attend(p, carried):
        cols = columns128(p)
        q_pair = query[:, cols]
        k_pair = keys[:, cols]
        v_pair = values[:, cols]
        outs = []
        for i in range(2):
            q_one = jnp.where(low_half if i == 0 else lane >= 64, q_pair, jnp.zeros_like(q_pair))
            scores = nt(q_one, k_pair) * 0.125 + bias[...]
            top = jnp.max(scores, -1, keepdims=True)
            powers = jnp.exp(scores - top)
            soft = powers * (1.0 / jnp.sum(powers, -1, keepdims=True))
            probs[2 * p + i] = soft
            outs.append(nn(soft.astype(bf16), v_pair))
        attended[:, cols] = jnp.where(low_half, outs[0], outs[1]).astype(bf16)
        return carried

    lax.fori_loop(0, 6, attend, 0)
    load(5).wait()
    mid[...] = hidden[...] + nn(attended[...], out_w[...])
    lt_ref[5] = attended[...].astype(f32).T.astype(bf16)
    normalize(mid, xhat2, scale2, g2_ref[...].astype(f32), b2_ref[...].astype(f32), put_low)
    lt_ref[4] = low_top[...].astype(f32).T.astype(bf16)
    load(6).wait()
    load(7).wait()
    d_hidden[...] = mid[...]

    def rows768(j):
        return pl.ds(pl.multiple_of(j * 768, 128), 768)

    def feed(j, carried):
        d_second[...] = nn(low_top[...], up_w[:, rows768(j)])
        shift = up_bias_ref[:, rows768(j)].astype(f32)
        for r in chunks:
            pre = d_second[r] + shift
            square = pre * pre
            bend = jnp.tanh(pre * (GELU_A + (GELU_A * GELU_B) * square))
            left = 0.5 * (1.0 + bend)
            slope[j, r] = left + 0.5 * pre * (1.0 - bend * bend) * (GELU_A + (3.0 * GELU_A * GELU_B) * square)
            d_second[r] = pre * left
        act = d_second[...]
        lt_ref[j] = act.T.astype(bf16)
        d_hidden[...] += nn(act.astype(bf16), down_w[rows768(j)])
        return carried

    lax.fori_loop(0, 4, feed, 0)
    low_top[...] = d_hidden[...].astype(bf16)
    row_out[...] = nn(low_top[...], head_pad[...]) + head_bias

    @pl.when(core == 0)
    def _():
        exchange(3, row_out.at[120:128], row_in).start()

    rolled = pltpu.roll(row_out[...], 1, 0)

    @pl.when(core == 1)
    def _():
        exchange(3, row_out.at[120:128], row_in).wait_recv()

    shifted = jnp.where(row == 0, jnp.broadcast_to(row_in[7:8], (128, 128)), rolled) * valid_col
    inside = lane < 48
    alpha = jnp.where(inside, shifted, 0.0)
    shift_mean = jnp.where(inside, pltpu.roll(shifted, 80, 1), 0.0)
    factor = jnp.exp(-alpha)
    new_latents = (lat_pad[...] - shift_mean) * factor
    lat_out[0] = new_latents
    logdet = -jnp.sum(jnp.sum(alpha, 1, keepdims=True), 0, keepdims=True)
    d_alpha = -cot_pad[...] * new_latents - cot_logdet_sm[0]
    direct = cot_pad[...] * factor
    lat_out[1] = direct
    grad_out[...] = (
        jnp.where(inside, d_alpha, pltpu.roll(jnp.where(inside, -direct, 0.0), 48, 1)) * valid_col
    )

    @pl.when(core == 1)
    def _():
        exchange(4, grad_out.at[0:8], grad_in).start()

    rolled_back = pltpu.roll(grad_out[...], 127, 0)

    @pl.when(core == 0)
    def _():
        exchange(4, grad_out.at[0:8], grad_in).wait_recv()

    d_head = jnp.where(row == 127, jnp.broadcast_to(grad_in[0:1], (128, 128)), rolled_back).astype(bf16)
    head_grad = tn(d_head, low_top[...])
    head_bias_grad = jnp.sum(d_head.astype(f32), 0, keepdims=True)
    d_hidden[...] = nt(d_head, head_pad[...])
    low_top[...] = d_hidden[...].astype(bf16)
    for h in range(2):
        r_ref[0, h] = low_top[:, h * COLS : (h + 1) * COLS]

    def put(first_row, value):
        h, r = first_row // 128, first_row % 128
        for t in range(2):
            small_ref[h, t, r : r + value.shape[0]] = value[:, t * COLS : (t + 1) * COLS].astype(bf16)

    put(0, head_grad[0:96])

    d_second[...] = jnp.zeros((128, 768), f32)

    def feed_back(j, carried):
        d_keys[...] = nt(low_top[...], down_w[rows768(j)])
        total = jnp.zeros((1, 768), f32)
        for r in chunks:
            d_pre = (slope[j, r] * d_keys[r]).astype(bf16)
            d_att[r] = d_pre
            total += jnp.sum(d_pre.astype(f32), 0, keepdims=True)
            for h in range(2):
                r_ref[1 + j, h, r] = d_pre[:, h * COLS : (h + 1) * COLS]
        ub_grad[pl.ds(j, 1)] = total
        d_second[...] += nt(d_att[...], up_w[:, rows768(j)])
        return carried

    lax.fori_loop(0, 4, feed_back, 0)

    def norm_back(grad, hat, scale, gain, base, out):
        gain_total = jnp.zeros((1, 768), f32)
        shift_total = jnp.zeros((1, 768), f32)
        for r in chunks:
            d = grad[r]
            scaled = hat[r]
            e = d * gain
            v = e - jnp.mean(e, -1, keepdims=True) - scaled * jnp.mean(e * scaled, -1, keepdims=True)
            out[r] = base[r] + scale[r] * v
            gain_total += jnp.sum(d * scaled, 0, keepdims=True)
            shift_total += jnp.sum(d, 0, keepdims=True)
        return gain_total, shift_total

    g2_grad, b2_grad = norm_back(d_second, xhat2, scale2, g2_ref[...].astype(f32), d_hidden, mid)
    low_top[...] = mid[...].astype(bf16)
    for h in range(2):
        r_ref[5, h] = low_top[:, h * COLS : (h + 1) * COLS]
    d_att[...] = nt(low_top[...], out_w[...]).astype(bf16)

    def attend_back(p, carried):
        cols = columns128(p)
        q_pair = query[:, cols]
        k_pair = keys[:, cols]
        v_pair = values[:, cols]
        a_pair = d_att[:, cols]
        dq, dk, dv = [], [], []
        for i in range(2):
            own = low_half if i == 0 else lane >= 64
            a_one = jnp.where(own, a_pair, jnp.zeros_like(a_pair))
            q_one = jnp.where(own, q_pair, jnp.zeros_like(q_pair))
            soft = probs[2 * p + i]
            d_soft = nt(a_one, v_pair)
            weighted = d_soft * soft
            d_score = weighted - soft * jnp.sum(weighted, -1, keepdims=True)
            d_low = d_score.astype(bf16)
            dq.append(nn(d_low, k_pair))
            dk.append(tn(d_low, q_one))
            dv.append(tn(soft.astype(bf16), a_one))
        h, local = p // 3, pl.ds(pl.multiple_of((p % 3) * 128, 128), 128)
        r_ref[6, h, :, local] = (jnp.where(low_half, dq[0], dq[1]) * 0.125).astype(bf16)
        dk_pair = (dk[0] + dk[1]) * 0.125
        dv_pair = dv[0] + dv[1]
        d_prior[0, :, cols] = dk_pair[0:128].astype(bf16)
        d_prior[1, :, cols] = dv_pair[0:128].astype(bf16)
        d_keys[:, cols] = dk_pair[128:256]
        d_values[:, cols] = dv_pair[128:256]
        return carried

    lax.fori_loop(0, 6, attend_back, 0)

    @pl.when(core == 1)
    def _():
        exchange(5, d_prior, d_back).start()

    @pl.when(core == 0)
    def _():
        exchange(5, d_prior, d_back).wait_recv()

    for h in range(2):
        cols = slice(h * COLS, (h + 1) * COLS)
        r_ref[7, h] = (d_keys[:, cols] + d_back[0, :, cols].astype(f32)).astype(bf16)
        r_ref[8, h] = (d_values[:, cols] + d_back[1, :, cols].astype(f32)).astype(bf16)
    d_second[...] = sum(
        nt(r_ref[6 + j, h], qkv_w[:, j * 768 + h * COLS : j * 768 + (h + 1) * COLS])
        for j in range(3)
        for h in range(2)
    )
    g1_grad, b1_grad = norm_back(d_second, xhat1, scale1, g1_ref[...].astype(f32), mid, d_hidden)
    low_top[...] = d_hidden[...].astype(bf16)
    for t in range(2):
        pos_ref[t] = low_top[:, t * COLS : (t + 1) * COLS]
    patch_grad = tn(lat_pad[...].astype(bf16), low_top[...])
    lat_out[1] += nt(low_top[...], patch_pad[...])
    lat_copy = pltpu.make_async_copy(lat_out, latents_hbm, lat_sem)
    lat_copy.start()
    class_grad = jnp.sum(d_hidden[...], 0, keepdims=True)
    put(96, patch_grad[0:32])
    put(128, patch_grad[32:48])
    line = lax.broadcasted_iota(jnp.int32, (16, 768), 0)
    put(144, jnp.where(line == dp, class_grad, 0.0))
    lane1 = lax.broadcasted_iota(jnp.int32, (1, 128), 1)
    high = logdet.astype(bf16).astype(f32)
    slot = lane1 == core * 16 + dp
    misc = jnp.concatenate(
        (
            head_bias_grad,
            jnp.where(slot, high, 0.0),
            jnp.where(slot, logdet - high, 0.0),
            jnp.zeros((1, 384), f32),
        ),
        1,
    )
    lines = [g1_grad, b1_grad, g2_grad, b2_grad] + [ub_grad[j : j + 1] for j in range(4)] + [misc]
    block = jnp.zeros((16, 768), f32)
    for i, one in enumerate(lines):
        block = jnp.where(line == i, one, block)
    put(160, block)
    put(176, jnp.zeros((80, 768), f32))
    lax.fori_loop(0, UNITS + 11, step, 0)


    def drain(u, carried):
        @pl.when(u < UNITS)
        def _():
            place(u, core, 0, 512, lambda dst: to_other(u, 27, 0, 512)(dst).wait_send())
            place(u, core, 0, 512, lambda dst: to_own(u, 0, 0, 512)(dst).wait())
            place(u, 1 - core, 0, 512, lambda dst: to_other(u, 27, 0, 512)(dst).wait_recv())
            place(u, core, 512, 256, lambda dst: to_other(u, 28, 512, 256)(dst).wait_send())
            place(u, core, 512, 256, lambda dst: to_own(u, 1, 512, 256)(dst).wait())
            place(u, 1 - core, 512, 256, lambda dst: to_other(u, 28, 512, 256)(dst).wait_recv())
            c_x(u).wait_send()
            c_y(u).wait_send()
            c_back_y(u, mine).wait_send()
            c_back_x(u, half).wait_send()

            @pl.when(outer)
            def _():
                c_z1(u).wait_send()
                c_z4(u).wait_send()

            @pl.when(inner)
            def _():
                c_z2(u).wait_send()
                c_z3(u).wait_send()
                c_z5(u, side * 128).wait_send()
                c_z6(u).wait_send()

        for t in range(2):
            ab_first(u, t).wait_send()
            ab_second(u, t).wait_send()
            ab_back2(u, t, ab_base(t)).wait_send()
            ab_back1(u, t, first[t] * 128).wait_send()

        @pl.when(outer)
        def _():
            for t in range(2):
                ab_z1(u, t).wait_send()

        @pl.when(inner)
        def _():
            for t in range(2):
                ab_z2(u, t).wait_send()
                ab_z3(u, t, ab_base(t) + (z - 1) * 32).wait_send()
                ab_z4(u, t).wait_send()

        return carried

    lax.fori_loop(0, UNITS + 1, drain, 0)
    for u in range(UNITS - STAGES, UNITS):
        core_first(u).wait_send()
    for t in range(2):
        small_first(t).wait_send()
        small_other(t).wait_send()
        arrived(UNITS, 27 + t, small_out(1 - core, t))
        small_own(t).wait()
        pos_own(t).wait()
    lat_copy.wait()

    @pl.when(core == 0)
    def _():
        exchange(2, mask_row, prior_mask).wait_send()
        exchange(0, keys.at[128:256], keys.at[0:128]).wait_send()
        exchange(1, values.at[128:256], values.at[0:128]).wait_send()
        exchange(3, row_out.at[120:128], row_in).wait_send()

    @pl.when(core == 1)
    def _():
        exchange(4, grad_out.at[0:8], grad_in).wait_send()
        exchange(5, d_prior, d_back).wait_send()


def flow(
    class_labels, group_perm, cot_logdet, latents, valid, patch_weight, pos_table, ln1_gain, ln1_bias,
    ln2_gain, ln2_bias, up_bias, head_weight, head_bias, cot_latents, class_table,
    qkv_weight, out_weight, up_weight, down_weight,
):
    smem = pl.BlockSpec(memory_space=pltpu.SMEM)
    vmem = pl.BlockSpec(memory_space=pltpu.VMEM)
    hbm = pl.BlockSpec(memory_space=pl.ANY)
    wide = (128, 768)
    return pl.pallas_call(
        flow_kernel,
        out_shape=(
            jax.ShapeDtypeStruct((3072, 768), bf16),
            jax.ShapeDtypeStruct((768, 3072), bf16),
            jax.ShapeDtypeStruct((768, 768), bf16),
            jax.ShapeDtypeStruct((768, 2304), bf16),
            jax.ShapeDtypeStruct((128, 768), bf16),
            jax.ShapeDtypeStruct((256, 768), bf16),
            jax.ShapeDtypeStruct((2, 128, 128), f32),
        ),
        in_specs=[smem] * 3 + [vmem] * 12 + [hbm] * 5,
        out_specs=(hbm,) * 7,
        scratch_shapes=[
            pltpu.VMEM((STAGES, 3 * ROWS, COLS), bf16),
            pltpu.VMEM((UNITS + 1, 3 * ROWS, COLS), bf16),
            pltpu.VMEM((UNITS + 1, 3 * ROWS, COLS), bf16),
            pltpu.VMEM((UNITS + 1, 3 * ROWS, COLS), bf16),
            pltpu.VMEM((UNITS + 1, 2, 288, COLS), bf16),
            pltpu.VMEM((UNITS, 432, COLS), bf16),
            pltpu.SemaphoreType.DMA((UNITS + 1, 29)),
            pltpu.SemaphoreType.DMA((UNITS + 1, 29)),
            pltpu.SemaphoreType.DMA((UNITS + 1, 4)),
            pltpu.VMEM((768, 2304), bf16),
            pltpu.VMEM((768, 768), bf16),
            pltpu.VMEM((768, 3072), bf16),
            pltpu.VMEM((3072, 768), bf16),
            pltpu.SemaphoreType.DMA((8,)),
            pltpu.VMEM((128, 128), f32),
            pltpu.VMEM((128, 128), f32),
            pltpu.VMEM(wide, bf16),
            pltpu.VMEM((768, 128), bf16),
            pltpu.VMEM(wide, f32),
            pltpu.VMEM(wide, f32),
            pltpu.VMEM(wide, f32),
            pltpu.VMEM(wide, f32),
            pltpu.VMEM((128, 1), f32),
            pltpu.VMEM((128, 1), f32),
            pltpu.VMEM((256, 768), bf16),
            pltpu.VMEM((256, 768), bf16),
            pltpu.VMEM(wide, bf16),
            pltpu.VMEM(wide, bf16),
            pltpu.VMEM((128, 256), f32),
            pltpu.VMEM((8, 128), f32),
            pltpu.VMEM((8, 128), f32),
            pltpu.VMEM((12, 128, 256), f32),
            pltpu.VMEM((4, 128, 768), f32),
            pltpu.VMEM(wide, f32),
            pltpu.VMEM(wide, f32),
            pltpu.VMEM(wide, bf16),
            pltpu.VMEM(wide, f32),
            pltpu.VMEM(wide, f32),
            pltpu.VMEM((2, 128, 768), bf16),
            pltpu.VMEM((2, 128, 768), bf16),
            pltpu.VMEM((128, 128), f32),
            pltpu.VMEM((8, 128), f32),
            pltpu.VMEM((128, 128), f32),
            pltpu.VMEM((8, 128), f32),
            pltpu.VMEM((2, 128, 128), f32),
            pltpu.VMEM((7, 768, 128), bf16),
            pltpu.VMEM((9, 2, 128, COLS), bf16),
            pltpu.VMEM((2, 128, COLS), bf16),
            pltpu.VMEM((2, 2, 128, COLS), bf16),
            pltpu.VMEM((8, 768), f32),
            pltpu.VMEM(wide, bf16),
            pltpu.SemaphoreType.DMA((6,)),
            pltpu.SemaphoreType.DMA((6,)),
            pltpu.SemaphoreType.DMA,
        ],
        compiler_params=pltpu.CompilerParams(
            collective_id=0, has_side_effects=True, vmem_limit_bytes=62 << 20
        ),
        name="flow",
    )(
        class_labels, group_perm, cot_logdet, latents, valid, patch_weight, pos_table, ln1_gain, ln1_bias,
        ln2_gain, ln2_bias, up_bias, head_weight, head_bias, cot_latents, class_table,
        qkv_weight, out_weight, up_weight, down_weight,
    )


def finish_kernel(
    labels_ref, down_ref, up_ref, out_ref, qkv_ref, pos_ref, small_ref, lat_ref,
    new_latents, logdet, latents_grad, patch, pos, classes, g1, b1, qkv, out, g2, b2, up, ub, down, head, hb,
):
    dp = lax.axis_index("dp")
    down[0] = down_ref[...].astype(f32)
    up[0] = up_ref[...].astype(f32)
    out[0] = out_ref[...].astype(f32)
    qkv[0] = qkv_ref[...].astype(f32)

    @pl.when(pl.program_id(0) == 0)
    def _():
        new_latents[0] = lat_ref[0, :, 0:48]
        latents_grad[0] = lat_ref[1, :, 0:48]
        pos[...] = pos_ref[...].astype(f32)
        patch[...] = small_ref[96:144].astype(f32)
        head[...] = small_ref[0:128].astype(f32).T[:, 0:96]
        block = small_ref[160:176].astype(f32)
        for i, one in enumerate((g1, b1, g2, b2)):
            one[...] = block[i : i + 1]
        for i in range(4):
            ub[:, i * 768 : (i + 1) * 768] = block[4 + i : 5 + i]
        hb[...] = block[8:9, 0:96]
        count = labels_ref.shape[1]
        terms = block[8:9, 128:256] + block[8:9, 256:384]
        lane = lax.broadcasted_iota(jnp.int32, (1, 128), 1)
        mine = jnp.logical_or(lane == dp, lane == count + dp)
        logdet[...] = jnp.sum(jnp.where(mine, terms, 0.0), 1, keepdims=True)
        by_lane = jnp.broadcast_to(labels_ref[...], (count, count)).astype(f32)
        first = lax.broadcasted_iota(jnp.int32, (count, count), 0)
        second = lax.broadcasted_iota(jnp.int32, (count, count), 1)
        by_row = jnp.sum(jnp.where(first == second, by_lane, 0.0), 1, keepdims=True)
        before = (by_lane < by_row) | ((by_lane == by_row) & (second < first))
        rank = jnp.sum(jnp.where(before, 1.0, 0.0), 1, keepdims=True)
        stored = jnp.sum(jnp.where(rank == second.astype(f32), by_row, 0.0), 0, keepdims=True)
        owned = classes.shape[0]
        wanted = (dp * owned + lax.broadcasted_iota(jnp.int32, (owned, count), 0)).astype(f32)
        hot = jnp.where(stored == wanted, 1.0, 0.0).astype(bf16)
        classes[...] = jnp.dot(hot, small_ref[144:160], preferred_element_type=f32)


def finish(class_labels, down, up, out, qkv, pos, small, lat):
    steps = 16

    def blocked(rows, width):
        return pl.BlockSpec((rows // steps, width), lambda i: (i, 0))

    def blocked_out(rows, width):
        return pl.BlockSpec((1, rows // steps, width), lambda i: (0, i, 0))

    def kept(*shape):
        return pl.BlockSpec(shape, lambda i: (0,) * len(shape))

    count = class_labels.shape[1]
    owned = 1024 // count
    shapes = [
        (1, 128, 48), (1, 1), (1, 128, 48), (48, 768), (128, 768), (owned, 768), (1, 768), (1, 768),
        (1, 768, 2304), (1, 768, 768), (1, 768), (1, 768), (1, 768, 3072), (1, 3072), (1, 3072, 768),
        (768, 96), (1, 96),
    ]
    specs = [kept(*shape) for shape in shapes]
    specs[8], specs[9] = blocked_out(768, 2304), blocked_out(768, 768)
    specs[12], specs[14] = blocked_out(768, 3072), blocked_out(3072, 768)
    return pl.pallas_call(
        finish_kernel,
        grid=(steps,),
        out_shape=[jax.ShapeDtypeStruct(shape, f32) for shape in shapes],
        in_specs=[
            kept(1, count), blocked(3072, 768), blocked(768, 3072), blocked(768, 768), blocked(768, 2304),
            kept(128, 768), kept(256, 768), kept(2, 128, 128),
        ],
        out_specs=specs,
        compiler_params=pltpu.CompilerParams(vmem_limit_bytes=40 << 20),
        name="finish",
    )(class_labels, down, up, out, qkv, pos, small, lat)


def fast_local(
    latents, valid, class_labels, group_perm, patch_weight, pos_table, class_table, ln1_gain, ln1_bias,
    qkv_weight, out_weight, ln2_gain, ln2_bias, up_weight, up_bias, down_weight, head_weight, head_bias,
    cot_latents, cot_logdet,
):
    sums = flow(
        class_labels, group_perm, cot_logdet, latents, valid, patch_weight, pos_table, ln1_gain, ln1_bias,
        ln2_gain, ln2_bias, up_bias, head_weight, head_bias[None], cot_latents, class_table,
        qkv_weight, out_weight, up_weight, down_weight,
    )
    results = list(finish(class_labels[None], *sums))
    results[1] = results[1].reshape(1)
    results[16] = results[16].reshape(96)
    return tuple(results)


def forward(latents, valid, class_rows, seq_place, weights):
    (
        patch_weight,
        pos_table,
        qkv_weight,
        out_weight,
        ln1_gain,
        ln1_bias,
        ln2_gain,
        ln2_bias,
        up_weight,
        up_bias,
        down_weight,
        head_weight,
        head_bias,
    ) = weights
    images, patch_rows, channels = latents.shape
    model_width = qkv_weight.shape[1]
    head_count = model_width // HEAD_DIM
    latent_low = latents.astype(jnp.bfloat16)
    hidden = (
        matmul(latent_low, patch_weight)
        + pos_table.astype(jnp.float32)[None]
        + class_rows[:, None, :]
    )
    own_mask = valid.astype(jnp.bfloat16)
    normed = layer_norm(
        hidden, ln1_gain[0].astype(jnp.float32), ln1_bias[0].astype(jnp.float32)
    ).astype(jnp.bfloat16)
    packed = matmul(normed, qkv_weight[0]).astype(jnp.bfloat16)
    query = packed[..., :model_width].reshape(images, patch_rows, head_count, HEAD_DIM)
    keys_own = packed[..., model_width : 2 * model_width]
    values_own = packed[..., 2 * model_width :]
    prior_keys, prior_values, prior_mask = shifted_2((keys_own, values_own, own_mask), "seq", 1)
    keys = jnp.concatenate((prior_keys, keys_own), 1).reshape(
        images, 2 * patch_rows, head_count, HEAD_DIM
    )
    values = jnp.concatenate((prior_values, values_own), 1).reshape(
        images, 2 * patch_rows, head_count, HEAD_DIM
    )
    allowed = attention_mask(jnp.concatenate((prior_mask, own_mask), 1), patch_rows, seq_place)
    logits = masked_scores(query, keys, allowed)
    row_peak = jnp.max(logits, -1, keepdims=True)
    log_total = row_peak + jnp.log(jnp.sum(jnp.exp(logits - row_peak), -1, keepdims=True))
    weights_soft = jnp.exp(logits - log_total).astype(jnp.bfloat16)
    attended = jnp.einsum(
        "bhqk,bkhd->bqhd", weights_soft, values, preferred_element_type=jnp.float32
    )
    attended = attended.astype(jnp.bfloat16).reshape(images, patch_rows, model_width)
    mid = hidden + matmul(attended, out_weight[0])
    second = layer_norm(
        mid, ln2_gain[0].astype(jnp.float32), ln2_bias[0].astype(jnp.float32)
    ).astype(jnp.bfloat16)
    preact = matmul(second, up_weight[0]) + up_bias[0].astype(jnp.float32)
    activated = jax.nn.gelu(preact, approximate=True).astype(jnp.bfloat16)
    saved = [
        (
            hidden,
            normed,
            query,
            keys,
            values,
            allowed,
            log_total,
            attended,
            mid,
            second,
            preact,
            activated,
        )
    ]
    hidden = mid + matmul(activated, down_weight[0])
    top_low = hidden.astype(jnp.bfloat16)
    head_out = matmul(top_low, head_weight) + head_bias.astype(jnp.float32)
    prior_row = shifted_2(head_out[:, patch_rows - 1, :], "seq", 1)
    shifted = jnp.concatenate((prior_row[:, None, :], head_out[:, : patch_rows - 1, :]), 1)
    shifted = shifted * valid.astype(jnp.float32)[..., None]
    alpha = shifted[..., :channels]
    shift_mean = shifted[..., channels:]
    factor = jnp.exp(-alpha)
    new_latents = (latents - shift_mean) * factor
    logdet_part = -jnp.sum(alpha, (1, 2))
    return (new_latents, logdet_part, factor, top_low, saved)


def local(
    latents,
    valid,
    class_labels,
    group_perm,
    patch_weight,
    pos_table,
    class_table,
    ln1_gain,
    ln1_bias,
    qkv_weight,
    out_weight,
    ln2_gain,
    ln2_bias,
    up_weight,
    up_bias,
    down_weight,
    head_weight,
    head_bias,
    cot_latents,
    cot_logdet,
):
    images, patch_rows, channels = latents.shape
    model_width = qkv_weight.shape[1]
    head_count = model_width // HEAD_DIM
    layer_total = qkv_weight.shape[0]
    seq_place = lax.axis_index("seq")
    picks = group_perm[:, None] == lax.iota(jnp.int32, class_labels.shape[0])[None, :]
    image_labels = jnp.sum(jnp.where(picks, class_labels[None, :], 0), 1)
    label_hot = image_labels[:, None] == lax.iota(jnp.int32, class_table.shape[0])[None, :]
    class_rows = matmul(label_hot.astype(jnp.bfloat16), class_table)
    weights = (
        patch_weight,
        pos_table,
        qkv_weight,
        out_weight,
        ln1_gain,
        ln1_bias,
        ln2_gain,
        ln2_bias,
        up_weight,
        up_bias,
        down_weight,
        head_weight,
        head_bias,
    )
    new_latents, logdet_part, factor, top_low, saved = forward(
        latents, valid, class_rows, seq_place, weights
    )
    valid_float = valid.astype(jnp.float32)
    d_alpha = -cot_latents * new_latents - cot_logdet[:, None, None]
    d_mean = -cot_latents * factor
    d_shifted = jnp.concatenate((d_alpha, d_mean), -1) * valid_float[..., None]
    next_row = shifted_2(d_shifted[:, 0, :], "seq", -1)
    d_head = jnp.concatenate((d_shifted[:, 1:, :], next_row[:, None, :]), 1).astype(jnp.bfloat16)
    head_weight_grad = outer_sum(top_low, d_head)
    head_bias_grad = jnp.sum(d_head.astype(jnp.float32), (0, 1))
    d_hidden = transposed(d_head, head_weight)
    grads_qkv, grads_out, grads_up, grads_down = ([], [], [], [])
    grads_g1, grads_b1, grads_g2, grads_b2, grads_ub = ([], [], [], [], [])
    for layer_index in reversed(range(layer_total)):
        (
            hidden,
            normed,
            query,
            keys,
            values,
            allowed,
            log_total,
            attended,
            mid,
            second,
            preact,
            activated,
        ) = saved[layer_index]
        d_down = d_hidden.astype(jnp.bfloat16)
        down_grad = outer_sum(activated, d_down)
        d_act = transposed(d_down, down_weight[layer_index])
        unused_gelu, gelu_pull = jax.vjp(lambda inner: jax.nn.gelu(inner, approximate=True), preact)
        d_pre = gelu_pull(d_act)[0].astype(jnp.bfloat16)
        up_bias_grad = jnp.sum(d_pre.astype(jnp.float32), (0, 1))
        up_grad = outer_sum(second, d_pre)
        d_second = transposed(d_pre, up_weight[layer_index])
        unused_norm, norm_pull = jax.vjp(
            layer_norm,
            mid,
            ln2_gain[layer_index].astype(jnp.float32),
            ln2_bias[layer_index].astype(jnp.float32),
        )
        d_mid_norm, ln2_gain_part, ln2_bias_part = norm_pull(d_second)
        d_mid = d_hidden + d_mid_norm
        d_proj = d_mid.astype(jnp.bfloat16)
        out_grad = outer_sum(attended, d_proj)
        d_attended = transposed(d_proj, out_weight[layer_index]).astype(jnp.bfloat16)
        d_attended = d_attended.reshape(images, patch_rows, head_count, HEAD_DIM)
        logits = masked_scores(query, keys, allowed)
        probs = jnp.exp(logits - log_total)
        d_probs = jnp.einsum(
            "bqhd,bkhd->bhqk", d_attended, values, preferred_element_type=jnp.float32
        )
        d_scores = (probs * (d_probs - jnp.sum(d_probs * probs, -1, keepdims=True))).astype(
            jnp.bfloat16
        )
        d_query = jnp.einsum(
            "bhqk,bkhd->bqhd", d_scores, keys, preferred_element_type=jnp.float32
        ) * HEAD_DIM ** (-0.5)
        d_keys = jnp.einsum(
            "bhqk,bqhd->bkhd", d_scores, query, preferred_element_type=jnp.float32
        ) * HEAD_DIM ** (-0.5)
        d_values = jnp.einsum(
            "bhqk,bqhd->bkhd",
            probs.astype(jnp.bfloat16),
            d_attended,
            preferred_element_type=jnp.float32,
        )
        d_keys = d_keys.reshape(images, 2 * patch_rows, model_width)
        d_values = d_values.reshape(images, 2 * patch_rows, model_width)
        back_keys, back_values = (
            shifted_2(d_keys[:, :patch_rows].astype(jnp.bfloat16), "seq", -1).astype(jnp.float32),
            shifted_2(d_values[:, :patch_rows].astype(jnp.bfloat16), "seq", -1).astype(jnp.float32),
        )
        d_packed = jnp.concatenate(
            (
                d_query.reshape(images, patch_rows, model_width),
                d_keys[:, patch_rows:] + back_keys,
                d_values[:, patch_rows:] + back_values,
            ),
            -1,
        ).astype(jnp.bfloat16)
        qkv_grad = outer_sum(normed, d_packed)
        d_normed = transposed(d_packed, qkv_weight[layer_index])
        unused_norm, norm_pull = jax.vjp(
            layer_norm,
            hidden,
            ln1_gain[layer_index].astype(jnp.float32),
            ln1_bias[layer_index].astype(jnp.float32),
        )
        d_input, ln1_gain_part, ln1_bias_part = norm_pull(d_normed)
        d_hidden = d_mid + d_input
        grads_qkv.insert(0, qkv_grad)
        grads_out.insert(0, out_grad)
        grads_up.insert(0, up_grad)
        grads_down.insert(0, down_grad)
        grads_g1.insert(0, ln1_gain_part)
        grads_b1.insert(0, ln1_bias_part)
        grads_g2.insert(0, ln2_gain_part)
        grads_b2.insert(0, ln2_bias_part)
        grads_ub.insert(0, up_bias_grad)
    d_embed_low = d_hidden.astype(jnp.bfloat16)
    patch_grad_part = outer_sum(latents.astype(jnp.bfloat16), d_embed_low)
    latents_grad = cot_latents * factor + transposed(d_embed_low, patch_weight)
    pos_part = jnp.sum(d_hidden, 0)
    class_part = jnp.sum(d_hidden, 1)
    logdet, class_sums = lax.psum((logdet_part, class_part), "seq")
    class_term = lax.dot_general(
        label_hot.astype(jnp.float32),
        class_sums,
        (((0,), (0,)), ((), ())),
        precision=precise,
        preferred_element_type=jnp.float32,
    )
    class_grad = lax.psum_scatter(class_term, "dp", scatter_dimension=0, tiled=True)
    pos_grad = lax.psum(pos_part, "dp")
    (
        patch_weight_grad,
        head_weight_grad,
        head_bias_grad,
        ln1_gain_grad,
        ln1_bias_grad,
        ln2_gain_grad,
        ln2_bias_grad,
        up_bias_grad,
    ) = lax.psum(
        (
            patch_grad_part,
            head_weight_grad,
            head_bias_grad,
            jnp.stack(grads_g1),
            jnp.stack(grads_b1),
            jnp.stack(grads_g2),
            jnp.stack(grads_b2),
            jnp.stack(grads_ub),
        ),
        ("dp", "seq"),
    )
    qkv_stack = jnp.stack(grads_qkv)
    out_stack = jnp.stack(grads_out)
    up_stack = jnp.stack(grads_up)
    down_stack = jnp.stack(grads_down)
    flat_parts = (
        lax.psum_scatter(eight_rows(qkv_stack), ("dp", "seq"), scatter_dimension=1, tiled=True),
        lax.psum_scatter(eight_rows(out_stack), ("dp", "seq"), scatter_dimension=1, tiled=True),
        lax.psum_scatter(eight_rows(up_stack), ("dp", "seq"), scatter_dimension=1, tiled=True),
        lax.psum_scatter(eight_rows(down_stack), ("dp", "seq"), scatter_dimension=1, tiled=True),
    )
    flat_qkv, flat_out, flat_up, flat_down = (
        lax.all_gather(
            flat_parts[0].astype(jnp.bfloat16), ("dp", "seq"), axis=1, tiled=True
        ).astype(jnp.float32),
        lax.all_gather(
            flat_parts[1].astype(jnp.bfloat16), ("dp", "seq"), axis=1, tiled=True
        ).astype(jnp.float32),
        lax.all_gather(
            flat_parts[2].astype(jnp.bfloat16), ("dp", "seq"), axis=1, tiled=True
        ).astype(jnp.float32),
        lax.all_gather(
            flat_parts[3].astype(jnp.bfloat16), ("dp", "seq"), axis=1, tiled=True
        ).astype(jnp.float32),
    )
    qkv_stack = flat_qkv.reshape(qkv_stack.shape)
    out_stack = flat_out.reshape(out_stack.shape)
    up_stack = flat_up.reshape(up_stack.shape)
    down_stack = flat_down.reshape(down_stack.shape)
    return (
        new_latents,
        logdet,
        latents_grad,
        patch_weight_grad,
        pos_grad,
        class_grad,
        ln1_gain_grad,
        ln1_bias_grad,
        qkv_stack,
        out_stack,
        ln2_gain_grad,
        ln2_bias_grad,
        up_stack,
        up_bias_grad,
        down_stack,
        head_weight_grad,
        head_bias_grad,
    )


def solution(mesh):
    in_specs = (
        P("dp", "seq", None),
        P("dp", "seq"),
        P(),
        P("dp"),
        P(),
        P("seq", None),
        P(),
        P(),
        P(),
        P(),
        P(),
        P(),
        P(),
        P(),
        P(),
        P(),
        P(),
        P(),
        P("dp", "seq", None),
        P("dp"),
    )
    out_specs = (
        P("dp", "seq", None),
        P("dp"),
        P("dp", "seq", None),
        P(),
        P("seq", None),
        P("dp", None),
        P(),
        P(),
        P(),
        P(),
        P(),
        P(),
        P(),
        P(),
        P(),
        P(),
        P(),
    )
    body = fast_local if mesh.shape["dp"] == 16 and mesh.shape["seq"] == 2 else local
    return jax.shard_map(body, mesh=mesh, in_specs=in_specs, out_specs=out_specs, check_vma=False)
```

```python
import jax
import jax.numpy as jnp
from jax import lax
from jax.experimental import pallas as pl
from jax.experimental.pallas import tpu as pltpu
from jax.sharding import PartitionSpec as P

HEAD_DIM = 64


precise = lax.Precision.HIGHEST
norm_eps = 1e-05


def shifted_2(shard, axis, by):
    size = lax.axis_size(axis)
    pairs = [(i, i + by) for i in range(size) if 0 <= i + by < size]
    return lax.ppermute(shard, axis, pairs)


def layer_norm(values, norm_gain, norm_bias):
    center = values - jnp.mean(values, -1, keepdims=True)
    spread = jnp.mean(center * center, -1, keepdims=True)
    return center * lax.rsqrt(spread + norm_eps) * norm_gain + norm_bias


def matmul(left_side, weight_mat):
    return jnp.dot(left_side, weight_mat, preferred_element_type=jnp.float32)


def outer_sum(left_side, grad_side):
    left_flat = left_side.reshape(-1, left_side.shape[-1])
    grad_flat = grad_side.reshape(-1, grad_side.shape[-1])
    return lax.dot_general(
        left_flat, grad_flat, (((0,), (0,)), ((), ())), preferred_element_type=jnp.float32
    )


def transposed(grad_side, weight_mat):
    return lax.dot_general(
        grad_side,
        weight_mat,
        (((grad_side.ndim - 1,), (1,)), ((), ())),
        preferred_element_type=jnp.float32,
    )


def eight_rows(matrix):
    return matrix.reshape(8, -1)


def attention_mask(key_valid, patch_rows, seq_place):
    query_pos = seq_place * patch_rows + lax.iota(jnp.int32, patch_rows)
    key_pos = (seq_place - 1) * patch_rows + lax.iota(jnp.int32, 2 * patch_rows)
    earlier = (key_pos[None, :] < query_pos[:, None])[None] & (key_valid[:, None, :] > 0)
    return earlier | (key_pos[None, :] == query_pos[:, None])[None]


def masked_scores(query, keys, allowed):
    logits = jnp.einsum(
        "bqhd,bkhd->bhqk", query, keys, preferred_element_type=jnp.float32
    ) * HEAD_DIM ** (-0.5)
    return jnp.where(allowed[:, None], logits, -1e30)


MESH = pl.DeviceIdType.MESH
UNITS = 24
LAST = 25
TURNS = 13
SLAB = 128
TABLE_ROWS = ((0, 384), (384, 384), (768, 256))
FINISH_ROWS = 768
AHEAD = 6
COLS = 384
STAGES = 3
CHUNK = 32
GELU_A = (2.0 / 3.141592653589793) ** 0.5
GELU_B = 0.044715
f32 = jnp.float32
bf16 = jnp.bfloat16


def flow_kernel(
    labels_sm, perm_sm, cot_logdet_sm,
    latents_ref, valid_ref, patch_ref, pos_table_ref, g1_ref, b1_ref, g2_ref, b2_ref,
    up_bias_ref, head_w_ref, head_b_ref, cot_ref,
    class_hbm, qkv_any, out_any, up_any, down_any,
    down_hbm, up_hbm, out_hbm, qkv_hbm, pos_hbm, small_hbm, latents_hbm, lines_hbm,
    stage, part, full, core_in, small_in, ab_in, c_in, send_sem, recv_sem, stage_sem, back_sem, local_sem,
    qkv_w, out_w, up_w, down_w, load_sem,
    lat_pad, cot_pad, patch_pad, head_pad, hidden, mid, xhat1, xhat2, scale1, scale2,
    keys, values, query, attended, bias, prior_mask, mask_row, probs, slope, d_hidden, d_second, d_att, d_keys, d_values,
    d_prior, d_back, row_out, row_in, grad_out, grad_in, factor, lat_out,
    lines, line_sum, line_in, line_send, line_recv, line_sem,
    lt_ref, r_ref, pos_ref, small_ref, low_top, exch_send, exch_recv, lat_sem,
):
    dp = lax.axis_index("dp")
    core = lax.axis_index("seq")
    x, y, z = dp % 2, (dp // 2) % 2, dp // 4
    side = z // 2
    inner = ((z + 1) // 2) % 2 == 1
    outer = ((z + 1) // 2) % 2 == 0
    to_core = (dp, 1 - core)
    to_x = (dp + 1 - 2 * x, core)
    to_y = (dp + 2 - 4 * y, core)
    to_mate = (dp + 4 - 8 * (z % 2), core)
    to_inner = ((dp + 12 - 8 * z + 16) % 16, core)

    def rows_at(start, count):
        return pl.ds(pl.multiple_of(start, 16), count)

    sources = [class_hbm.at[r : r + n, h * COLS : (h + 1) * COLS] for h in range(2) for r, n in TABLE_ROWS]
    targets = [part.at[3 * h + i, 0:n] for h in range(2) for i, (r, n) in enumerate(TABLE_ROWS)]
    sources += [qkv_any.at[0], out_any.at[0], up_any.at[0], down_any.at[0]]
    targets += [qkv_w, out_w, up_w, down_w]

    def load(i):
        return pltpu.make_async_copy(sources[i], targets[i], load_sem.at[i])

    for i in range(10):
        load(i).start()

    barrier = pltpu.get_barrier_semaphore()
    for target in (to_core, to_x, to_y, to_mate):
        pl.semaphore_signal(barrier, inc=1, device_id=target, device_id_type=MESH)

    @pl.when(inner)
    def _():
        pl.semaphore_signal(barrier, inc=1, device_id=to_inner, device_id_type=MESH)
        pl.semaphore_wait(barrier, 5)

    @pl.when(outer)
    def _():
        pl.semaphore_wait(barrier, 4)

    def copy(u, k, src, dst, target):
        return pltpu.make_async_remote_copy(
            src_ref=src, dst_ref=dst, send_sem=send_sem.at[u], recv_sem=recv_sem.at[k, u % TURNS],
            device_id=target, device_id_type=MESH,
        )

    def arrived(u, k, dst):
        copy(u, k, dst, dst, to_core).wait_recv()

    def added(dst, left, right):
        dst[...] = (left[...].astype(f32) + right[...].astype(f32)).astype(bf16)

    first = (x, y)
    second = (y, x)
    to_first = (to_x, to_y)
    to_second = (to_y, to_x)

    def out_rows(u, t, start, count):
        return full.at[u, rows_at(t * SLAB + start, count)]

    def part_rows(u, t, start, count):
        return part.at[u, rows_at(t * SLAB + start, count)]

    def left_index(u):
        return jnp.minimum(u // 2, 4) + jnp.minimum(jnp.maximum(u // 2 - 7, 0), 2)

    def right_index(u):
        return jnp.maximum(u // 2 - 3, 0)

    def product(u, t, half):
        rows = pl.ds(pl.multiple_of((u % 2) * 384 + t * SLAB, 128), SLAB)
        return jnp.dot(lt_ref[left_index(u), rows], r_ref[right_index(u), half], preferred_element_type=f32)

    def core_first(u):
        return pltpu.make_async_remote_copy(
            src_ref=stage.at[u % STAGES], dst_ref=core_in.at[u], send_sem=stage_sem.at[u % STAGES],
            recv_sem=recv_sem.at[0, u % TURNS], device_id=to_core, device_id_type=MESH,
        )

    def small_first():
        return pltpu.make_async_remote_copy(
            src_ref=small_ref.at[1 - core], dst_ref=small_in, send_sem=stage_sem.at[STAGES],
            recv_sem=recv_sem.at[0, LAST % TURNS], device_id=to_core, device_id_type=MESH,
        )

    def line_copy(k, src, dst, target):
        return pltpu.make_async_remote_copy(
            src_ref=src, dst_ref=dst, send_sem=line_send.at[k], recv_sem=line_recv.at[k],
            device_id=target, device_id_type=MESH,
        )

    line_steps = (
        (lines, line_in.at[0], to_core),
        (line_sum.at[0], line_in.at[1], to_x),
        (line_sum.at[1], line_in.at[2], to_y),
        (line_sum.at[2], line_in.at[3], to_mate),
        (line_sum.at[3], line_in.at[4], to_inner),
        (line_sum.at[4], line_sum.at[4], to_mate),
    )

    def line_go(k):
        return line_copy(k, *line_steps[k])

    def line_add(k):
        line_go(k).wait_recv()
        line_sum[k] = line_steps[k][0][...] + line_in[k]

    line_out = pltpu.make_async_copy(line_sum.at[4], lines_hbm, line_sem)

    def produce(u):
        @pl.when(jnp.logical_and(u >= STAGES, u < UNITS))
        def _():
            core_first(u - STAGES).wait_send()

        @pl.when(u < UNITS)
        def _():
            for t in range(3):
                stage[u % STAGES, t * SLAB : (t + 1) * SLAB] = product(u, t, 1 - core).astype(bf16)
            core_first(u).start()

        @pl.when(u == LAST)
        def _():
            small_first().start()
            line_go(0).start()

    def begin(u):
        @pl.when(u < UNITS)
        def _():
            arrived(u, 0, core_in.at[u])
            for t in range(3):
                rows = slice(t * SLAB, (t + 1) * SLAB)
                part[u, rows] = (product(u, t, core) + core_in[u, rows].astype(f32)).astype(bf16)
                if t < 2:
                    ab_first(u, t).start()
            pl.when(outer)(lambda: c_z1(u).start())

        @pl.when(u == UNITS)
        def _():
            part[UNITS, 0:256] = pos_ref[...]
            for t in range(2):
                ab_first(u, t).start()

        @pl.when(u == LAST)
        def _():
            small_first().wait_recv()
            part[LAST, 0:256] = (small_ref[core].astype(f32) + small_in[...].astype(f32)).astype(bf16)
            for t in range(2):
                ab_first(u, t).start()
            line_add(0)
            line_go(1).start()

    def ab_base(t):
        return first[t] * 64 + second[t] * 32

    def ab_first(u, t):
        return copy(u, 1, part_rows(u, t, (1 - first[t]) * 64, 64), ab_in.at[u, t, 0:64], to_first[t])

    def ab_second(u, t):
        row = first[t] * 64 + (1 - second[t]) * 32
        return copy(u, 2, part_rows(u, t, row, 32), ab_in.at[u, t, 64:96], to_second[t])

    def ab_z1(u, t):
        return copy(u, 3, part_rows(u, t, ab_base(t), 32), ab_in.at[u, t, 96:128], to_mate)

    def ab_z2(u, t):
        return copy(u, 4, part_rows(u, t, ab_base(t), 32), ab_in.at[u, t, 128:160], to_inner)

    def ab_z3(u, t):
        block = out_rows(u, t, ab_base(t), 32)
        return copy(u, 3, block, block, to_mate)

    def ab_back2(u, t):
        block = out_rows(u, t, ab_base(t), 32)
        return copy(u, 5, block, block, to_second[t])

    def ab_back1(u, t):
        block = out_rows(u, t, first[t] * 64, 64)
        return copy(u, 6, block, block, to_first[t])

    def ab1(u):
        arrived(u, 1, ab_in.at[u, :, 0:64])
        for t in range(2):
            kept = part_rows(u, t, first[t] * 64, 64)
            added(kept, kept, ab_in.at[u, t, 0:64])
            ab_second(u, t).start()

        @pl.when(u == LAST)
        def _():
            line_add(1)
            line_go(2).start()

    def ab2(u):
        arrived(u, 2, ab_in.at[u, :, 64:96])
        for t in range(2):
            kept = part_rows(u, t, ab_base(t), 32)
            added(kept, kept, ab_in.at[u, t, 64:96])
            pl.when(outer)(lambda: ab_z1(u, t).start())

        @pl.when(u == LAST)
        def _():
            line_add(2)
            pl.when(outer)(line_go(3).start)

    def ab3_inner(u):
        arrived(u, 3, ab_in.at[u, :, 96:128])
        for t in range(2):
            kept = part_rows(u, t, ab_base(t), 32)
            added(kept, kept, ab_in.at[u, t, 96:128])
            ab_z2(u, t).start()

        @pl.when(u == LAST)
        def _():
            line_add(3)
            line_go(4).start()

    def ab4_inner(u):
        arrived(u, 4, ab_in.at[u, :, 128:160])
        for t in range(2):
            added(out_rows(u, t, ab_base(t), 32), part_rows(u, t, ab_base(t), 32), ab_in.at[u, t, 128:160])
            ab_z3(u, t).start()
            ab_back2(u, t).start()

        @pl.when(u == LAST)
        def _():
            line_add(4)
            line_go(5).start()
            line_out.start()

    def ab5_outer(u):
        arrived(u, 3, full.at[u, 0:64])
        for t in range(2):
            ab_back2(u, t).start()

        @pl.when(u == LAST)
        def _():
            line_go(5).wait_recv()
            line_out.start()

    def ab6(u):
        arrived(u, 5, full.at[u, 0:64])
        for t in range(2):
            ab_back1(u, t).start()

    def place(u, h, row, count, act):
        def columns(base):
            return pl.ds(pl.multiple_of(base + h * COLS, 128), COLS)

        block, top = u // 2, (u % 2) * 384 + row

        @pl.when(block < 4)
        def _():
            act(down_hbm.at[rows_at(block * 768 + top, count), columns(0)])

        @pl.when(jnp.logical_and(block >= 4, block < 8))
        def _():
            act(up_hbm.at[rows_at(top, count), columns((block - 4) * 768)])

        @pl.when(block == 8)
        def _():
            act(out_hbm.at[rows_at(top, count), columns(0)])

        @pl.when(jnp.logical_and(block >= 9, block < 12))
        def _():
            act(qkv_hbm.at[rows_at(top, count), columns((block - 9) * 768)])

    def to_other(u, src, dst):
        return pltpu.make_async_remote_copy(
            src_ref=src, dst_ref=dst, send_sem=send_sem.at[u], recv_sem=back_sem.at[u],
            device_id=to_core, device_id_type=MESH,
        )

    def to_own(u, src, dst):
        return pltpu.make_async_copy(src, dst, local_sem.at[u])

    def both_ways(u, src, dst):
        to_other(u, src, dst).start()
        to_own(u, src, dst).start()

    def spread(u, row, count):
        place(u, core, row, count, lambda dst: both_ways(u, full.at[u, row : row + count], dst))

    def small_out(h, t):
        return small_hbm.at[pl.ds(pl.multiple_of(h * 128, 128), 128), t * COLS : (t + 1) * COLS]

    def ab7(u):
        arrived(u, 6, full.at[u, 0:128])
        spread(u, 0, 2 * SLAB)

        @pl.when(u == UNITS)
        def _():
            for t in range(2):
                to_own(
                    UNITS, full.at[UNITS, t * 128 : (t + 1) * 128], pos_hbm.at[:, t * COLS : (t + 1) * COLS]
                ).start()

        @pl.when(u == LAST)
        def _():
            for t in range(2):
                both_ways(LAST, full.at[LAST, t * 128 : (t + 1) * 128], small_out(core, t))

    far = 32 * (1 - side)
    own_end = 96 * side
    shard = z * 32
    half = shard + x * 16

    def c_z1(u):
        return copy(u, 7, part_rows(u, 2, far, 96), c_in.at[u, 0:96], to_mate)

    def c_z2(u):
        return copy(u, 8, part_rows(u, 2, (1 - side) * 64, 64), c_in.at[u, 96:160], to_inner)

    def c_z3(u):
        return copy(u, 7, part_rows(u, 2, own_end, 32), c_in.at[u, 160:192], to_mate)

    def c_x(u):
        return copy(u, 9, part_rows(u, 2, shard + (1 - x) * 16, 16), c_in.at[u, 192:208], to_x)

    def c_y(u):
        return copy(u, 10, part_rows(u, 2, half, 16), c_in.at[u, 208:224], to_y)

    def c_back_x(u):
        block = out_rows(u, 2, half, 16)
        return copy(u, 11, block, block, to_x)

    def c_z4(u):
        block = out_rows(u, 2, own_end, 32)
        return copy(u, 12, block, block, to_mate)

    def c_z5(u):
        block = out_rows(u, 2, side * 64, 64)
        return copy(u, 13, block, block, to_inner)

    def c_z6(u):
        block = out_rows(u, 2, far, 96)
        return copy(u, 12, block, block, to_mate)

    def c1_inner(u):
        arrived(u, 7, c_in.at[u, 0:96])
        kept = part_rows(u, 2, far, 96)
        added(kept, kept, c_in.at[u, 0:96])
        c_z2(u).start()

    def c2_inner(u):
        arrived(u, 8, c_in.at[u, 96:160])
        kept = part_rows(u, 2, side * 64, 64)
        added(kept, kept, c_in.at[u, 96:160])
        c_z3(u).start()
        c_x(u).start()

    def c3_outer(u):
        arrived(u, 7, c_in.at[u, 160:192])
        kept = part_rows(u, 2, shard, 32)
        added(kept, kept, c_in.at[u, 160:192])
        c_x(u).start()

    def c4(u):
        arrived(u, 9, c_in.at[u, 192:208])
        kept = part_rows(u, 2, half, 16)
        added(kept, kept, c_in.at[u, 192:208])
        c_y(u).start()

    def c5(u):
        arrived(u, 10, c_in.at[u, 208:224])
        added(out_rows(u, 2, half, 16), part_rows(u, 2, half, 16), c_in.at[u, 208:224])
        c_back_x(u).start()

    def c7(u):
        arrived(u, 11, out_rows(u, 2, shard + (1 - x) * 16, 16))
        pl.when(outer)(lambda: c_z4(u).start())

    def c8_inner(u):
        arrived(u, 12, out_rows(u, 2, own_end, 32))
        c_z5(u).start()

    def c9_inner(u):
        arrived(u, 13, out_rows(u, 2, (1 - side) * 64, 64))
        c_z6(u).start()
        spread(u, 2 * SLAB, SLAB)

    def c10_outer(u):
        arrived(u, 12, out_rows(u, 2, far, 96))
        spread(u, 2 * SLAB, SLAB)

    everyone, inners, outers = None, inner, outer
    events = [
        (1, LAST + 1, everyone, begin),
        (2, LAST + 1, everyone, ab1),
        (3, LAST + 1, everyone, ab2),
        (2, UNITS, inners, c1_inner),
        (3, UNITS, inners, c2_inner),
        (4, UNITS, outers, c3_outer),
        (4, LAST + 1, inners, ab3_inner),
        (5, LAST + 1, inners, ab4_inner),
        (6, LAST + 1, outers, ab5_outer),
        (4, UNITS, inners, c4),
        (5, UNITS, outers, c4),
        (5, UNITS, inners, c5),
        (6, UNITS, outers, c5),
        (6, UNITS, inners, c7),
        (7, UNITS, outers, c7),
        (6, LAST + 1, inners, ab6),
        (7, LAST + 1, outers, ab6),
        (7, LAST + 1, inners, ab7),
        (8, LAST + 1, outers, ab7),
        (8, UNITS, inners, c8_inner),
        (9, UNITS, inners, c9_inner),
        (10, UNITS, outers, c10_outer),
    ]

    mm_nt = (((1,), (1,)), ((), ()))
    mm_tn = (((0,), (0,)), ((), ()))

    def nt(left, right):
        return lax.dot_general(left, right, mm_nt, preferred_element_type=f32)

    def tn(left, right):
        return lax.dot_general(left, right, mm_tn, preferred_element_type=f32)

    def nn(left, right):
        return jnp.dot(left, right, preferred_element_type=f32)

    def exchange(k, src, dst):
        return pltpu.make_async_remote_copy(
            src_ref=src, dst_ref=dst, send_sem=exch_send.at[k], recv_sem=exch_recv.at[k],
            device_id=to_core, device_id_type=MESH,
        )

    chunks = [slice(r, r + CHUNK) for r in range(0, 128, CHUNK)]
    lane = lax.broadcasted_iota(jnp.int32, (128, 128), 1)
    row = lax.broadcasted_iota(jnp.int32, (128, 128), 0)
    eye = row == lane
    low_half = lane < 64
    valid_row = valid_ref[...].astype(f32)
    valid_col = jnp.sum(jnp.where(eye, valid_row, 0.0), axis=1, keepdims=True)
    mask_row[...] = jnp.broadcast_to(valid_row, (8, 128))
    lat_pad[...] = jnp.zeros((128, 128), f32)
    lat_pad[0:48] = latents_ref[0]
    lat_pad[...] = lat_pad[...].T
    cot_pad[...] = jnp.zeros((128, 128), f32)
    cot_pad[0:48] = cot_ref[0]
    cot_pad[...] = cot_pad[...].T
    patch_pad[...] = jnp.zeros((128, 768), bf16)
    patch_pad[0:48] = patch_ref[...]
    head_pad[...] = jnp.zeros((128, 768), bf16)
    head_pad[0:96] = head_w_ref[...]
    head_bias = jnp.concatenate((head_b_ref[...].astype(f32), jnp.zeros((1, 32), f32)), 1)

    @pl.when(core == 0)
    def _():
        keys[0:128] = jnp.zeros((128, 768), bf16)
        values[0:128] = jnp.zeros((128, 768), bf16)
        prior_mask[...] = jnp.zeros((8, 128), f32)
        row_in[...] = jnp.zeros((8, 128), f32)

    @pl.when(core == 1)
    def _():
        grad_in[...] = jnp.zeros((8, 128), f32)
        d_back[...] = jnp.zeros((2, 128, 768), bf16)

    @pl.when(core == 0)
    def _():
        exchange(2, mask_row, prior_mask).start()

    def normalize(src, hat, scale, gain, shift, put):
        for r in chunks:
            v = src[r]
            center = v - jnp.mean(v, -1, keepdims=True)
            inv = lax.rsqrt(jnp.mean(center * center, -1, keepdims=True) + norm_eps)
            scaled = center * inv
            hat[r] = scaled
            scale[r] = inv
            put(r, scaled * gain + shift)

    label = labels_sm[perm_sm[0]]
    hot = jnp.where(lax.broadcasted_iota(jnp.int32, (16, 1024), 1) == label, 1.0, 0.0).astype(bf16)
    for i in range(6):
        load(i).wait()
    class_row = jnp.concatenate(
        [
            sum(nn(hot[:, r : r + n], part[3 * h + i, 0:n]) for i, (r, n) in enumerate(TABLE_ROWS))
            for h in range(2)
        ],
        1,
    )[0:1]
    hidden[...] = (
        nn(lat_pad[...].astype(bf16), patch_pad[...]) + pos_table_ref[...].astype(f32) + class_row
    )

    def put_low(r, v):
        low_top[r] = v.astype(bf16)

    normalize(hidden, xhat1, scale1, g1_ref[...].astype(f32), b1_ref[...].astype(f32), put_low)
    load(6).wait()
    normed = low_top[...]
    keys[128:256] = nn(normed, qkv_w[:, 768:1536]).astype(bf16)

    @pl.when(core == 0)
    def _():
        exchange(0, keys.at[128:256], keys.at[0:128]).start()

    values[128:256] = nn(normed, qkv_w[:, 1536:2304]).astype(bf16)

    @pl.when(core == 0)
    def _():
        exchange(1, values.at[128:256], values.at[0:128]).start()

    query[...] = nn(normed, qkv_w[:, 0:768]).astype(bf16)
    lt_ref[6] = normed.astype(f32).T.astype(bf16)

    @pl.when(core == 1)
    def _():
        exchange(2, mask_row, prior_mask).wait_recv()
        exchange(0, keys.at[128:256], keys.at[0:128]).wait_recv()
        exchange(1, values.at[128:256], values.at[0:128]).wait_recv()

    bias[:, 0:128] = jnp.where(jnp.broadcast_to(prior_mask[0:1], (128, 128)) > 0.5, 0.0, -1e30)
    bias[:, 128:256] = jnp.where(((lane < row) & (valid_row > 0.5)) | eye, 0.0, -1e30)

    def columns128(p):
        return pl.ds(pl.multiple_of(p * 128, 128), 128)

    def attend(p, carried):
        cols = columns128(p)
        q_pair = query[:, cols]
        k_pair = keys[:, cols]
        v_pair = values[:, cols]
        outs = []
        for i in range(2):
            q_one = jnp.where(low_half if i == 0 else lane >= 64, q_pair, jnp.zeros_like(q_pair))
            scores = nt(q_one, k_pair) * 0.125 + bias[...]
            top = jnp.max(scores, -1, keepdims=True)
            powers = jnp.exp(scores - top)
            soft = powers * (1.0 / jnp.sum(powers, -1, keepdims=True))
            probs[2 * p + i] = soft
            outs.append(nn(soft.astype(bf16), v_pair))
        attended[:, cols] = jnp.where(low_half, outs[0], outs[1]).astype(bf16)
        return carried

    lax.fori_loop(0, 6, attend, 0)
    load(7).wait()
    mid[...] = hidden[...] + nn(attended[...], out_w[...])
    lt_ref[5] = attended[...].astype(f32).T.astype(bf16)
    normalize(mid, xhat2, scale2, g2_ref[...].astype(f32), b2_ref[...].astype(f32), put_low)
    lt_ref[4] = low_top[...].astype(f32).T.astype(bf16)
    load(8).wait()
    load(9).wait()
    d_hidden[...] = mid[...]

    def rows768(j):
        return pl.ds(pl.multiple_of(j * 768, 128), 768)

    def feed(j, carried):
        d_second[...] = nn(low_top[...], up_w[:, rows768(j)])
        shift = up_bias_ref[:, rows768(j)].astype(f32)
        for r in chunks:
            pre = d_second[r] + shift
            square = pre * pre
            bend = jnp.tanh(pre * (GELU_A + (GELU_A * GELU_B) * square))
            left = 0.5 * (1.0 + bend)
            slope[j, r] = left + 0.5 * pre * (1.0 - bend * bend) * (GELU_A + (3.0 * GELU_A * GELU_B) * square)
            d_second[r] = pre * left
        act = d_second[...]
        lt_ref[j] = act.T.astype(bf16)
        d_hidden[...] += nn(act.astype(bf16), down_w[rows768(j)])
        return carried

    lax.fori_loop(0, 4, feed, 0)
    low_top[...] = d_hidden[...].astype(bf16)
    row_out[...] = nt(low_top[...], head_pad[...]) + head_bias

    @pl.when(core == 0)
    def _():
        exchange(3, row_out.at[120:128], row_in).start()

    rolled = pltpu.roll(row_out[...], 1, 0)

    @pl.when(core == 1)
    def _():
        exchange(3, row_out.at[120:128], row_in).wait_recv()

    shifted = jnp.where(row == 0, jnp.broadcast_to(row_in[7:8], (128, 128)), rolled) * valid_col
    inside = lane < 48
    alpha = jnp.where(inside, shifted, 0.0)
    shift_mean = jnp.where(inside, pltpu.roll(shifted, 80, 1), 0.0)
    factor[...] = jnp.exp(-alpha)
    new_latents = (lat_pad[...] - shift_mean) * factor[...]
    lat_out[0] = new_latents.T
    logdet = -jnp.sum(jnp.sum(alpha, 1, keepdims=True), 0, keepdims=True)
    d_alpha = -cot_pad[...] * new_latents - cot_logdet_sm[0]
    direct = cot_pad[...] * factor[...]
    grad_out[...] = (
        jnp.where(inside, d_alpha, pltpu.roll(jnp.where(inside, -direct, 0.0), 48, 1)) * valid_col
    )

    @pl.when(core == 1)
    def _():
        exchange(4, grad_out.at[0:8], grad_in).start()

    rolled_back = pltpu.roll(grad_out[...], 127, 0)

    @pl.when(core == 0)
    def _():
        exchange(4, grad_out.at[0:8], grad_in).wait_recv()

    d_head = jnp.where(row == 127, jnp.broadcast_to(grad_in[0:1], (128, 128)), rolled_back).astype(bf16)
    head_grad = tn(d_head, low_top[...])
    head_bias_grad = jnp.sum(d_head.astype(f32), 0, keepdims=True)
    d_hidden[...] = nn(d_head, head_pad[...])
    low_top[...] = d_hidden[...].astype(bf16)
    for h in range(2):
        r_ref[0, h] = low_top[:, h * COLS : (h + 1) * COLS]

    def put(first_row, value):
        h, r = first_row // 128, first_row % 128
        for t in range(2):
            small_ref[h, t * 128 + r : t * 128 + r + value.shape[0]] = value[:, t * COLS : (t + 1) * COLS].astype(bf16)

    put(0, head_grad[0:96])

    lines[...] = jnp.zeros((16, 768), f32)
    lane1 = lax.broadcasted_iota(jnp.int32, (1, 128), 1)
    lines[8:9, 0:128] = head_bias_grad
    lines[8:9, 128:256] = jnp.where(lane1 == dp, logdet, 0.0)

    d_second[...] = jnp.zeros((128, 768), f32)

    def feed_back(j):
        d_keys[...] = nt(low_top[...], down_w[rows768(j)])
        total = jnp.zeros((1, 768), f32)
        for r in chunks:
            d_pre = (slope[j, r] * d_keys[r]).astype(bf16)
            d_att[r] = d_pre
            total += jnp.sum(d_pre.astype(f32), 0, keepdims=True)
            for h in range(2):
                r_ref[1 + j, h, r] = d_pre[:, h * COLS : (h + 1) * COLS]
        lines[pl.ds(4 + j, 1)] = total
        d_second[...] += nt(d_att[...], up_w[:, rows768(j)])

    def norm_back(grad, hat, scale, gain, base, out, line):
        gain_total = jnp.zeros((1, 768), f32)
        shift_total = jnp.zeros((1, 768), f32)
        for r in chunks:
            d = grad[r]
            scaled = hat[r]
            e = d * gain
            v = e - jnp.mean(e, -1, keepdims=True) - scaled * jnp.mean(e * scaled, -1, keepdims=True)
            out[r] = base[r] + scale[r] * v
            gain_total += jnp.sum(d * scaled, 0, keepdims=True)
            shift_total += jnp.sum(d, 0, keepdims=True)
        lines[line : line + 1] = gain_total
        lines[line + 1 : line + 2] = shift_total

    def feed_norm_back():
        norm_back(d_second, xhat2, scale2, g2_ref[...].astype(f32), d_hidden, mid, 2)
        low_top[...] = mid[...].astype(bf16)
        for h in range(2):
            r_ref[5, h] = low_top[:, h * COLS : (h + 1) * COLS]
        d_att[...] = nt(low_top[...], out_w[...]).astype(bf16)

    def attend_back(p):
        cols = columns128(p)
        q_pair = query[:, cols]
        k_pair = keys[:, cols]
        v_pair = values[:, cols]
        a_pair = d_att[:, cols]
        dq, dk, dv = [], [], []
        for i in range(2):
            own = low_half if i == 0 else lane >= 64
            a_one = jnp.where(own, a_pair, jnp.zeros_like(a_pair))
            q_one = jnp.where(own, q_pair, jnp.zeros_like(q_pair))
            soft = probs[2 * p + i]
            d_soft = nt(a_one, v_pair)
            weighted = d_soft * soft
            d_score = weighted - soft * jnp.sum(weighted, -1, keepdims=True)
            d_low = d_score.astype(bf16)
            dq.append(nn(d_low, k_pair))
            dk.append(tn(d_low, q_one))
            dv.append(tn(soft.astype(bf16), a_one))
        h, local = p // 3, pl.ds(pl.multiple_of((p % 3) * 128, 128), 128)
        r_ref[6, h, :, local] = (jnp.where(low_half, dq[0], dq[1]) * 0.125).astype(bf16)
        dk_pair = (dk[0] + dk[1]) * 0.125
        dv_pair = dv[0] + dv[1]
        d_prior[0, :, cols] = dk_pair[0:128].astype(bf16)
        d_prior[1, :, cols] = dv_pair[0:128].astype(bf16)
        d_keys[:, cols] = dk_pair[128:256]
        d_values[:, cols] = dv_pair[128:256]

    def send_prior():
        @pl.when(core == 1)
        def _():
            exchange(5, d_prior, d_back).start()

    def packed_back():
        @pl.when(core == 0)
        def _():
            exchange(5, d_prior, d_back).wait_recv()

        for h in range(2):
            cols = slice(h * COLS, (h + 1) * COLS)
            r_ref[7, h] = (d_keys[:, cols] + d_back[0, :, cols].astype(f32)).astype(bf16)
            r_ref[8, h] = (d_values[:, cols] + d_back[1, :, cols].astype(f32)).astype(bf16)
        d_second[...] = sum(
            nt(r_ref[6 + j, h], qkv_w[:, j * 768 + h * COLS : j * 768 + (h + 1) * COLS])
            for j in range(3)
            for h in range(2)
        )

    lat_copy = pltpu.make_async_copy(lat_out, latents_hbm, lat_sem)

    def embed_back():
        norm_back(d_second, xhat1, scale1, g1_ref[...].astype(f32), mid, d_hidden, 0)
        low_top[...] = d_hidden[...].astype(bf16)
        for t in range(2):
            pos_ref[t * 128 : (t + 1) * 128] = low_top[:, t * COLS : (t + 1) * COLS]
        patch_grad = tn(lat_pad[...].astype(bf16), low_top[...])
        lat_out[1] = (cot_pad[...] * factor[...] + nt(low_top[...], patch_pad[...])).T
        lat_copy.start()
        class_grad = jnp.sum(d_hidden[...], 0, keepdims=True)
        put(96, patch_grad[0:32])
        put(128, patch_grad[32:48])
        line = lax.broadcasted_iota(jnp.int32, (16, 768), 0)
        put(144, jnp.where(line == dp, class_grad, 0.0))
        put(160, jnp.zeros((96, 768), f32))

    def both(t):
        produce_now(t)

        @pl.when(jnp.logical_and(t < 8, t % 2 == 0))
        def _():
            feed_back(t // 2)

        pl.when(t == 8)(feed_norm_back)

        @pl.when(jnp.logical_and(t >= 9, t < 15))
        def _():
            attend_back(t - 9)

        pl.when(t == 14)(send_prior)
        pl.when(t == 16)(packed_back)
        pl.when(t == 18)(embed_back)

    def produce_now(t):
        pl.when(t <= LAST)(lambda: produce(t))

    def step(t, carried):
        both(t)
        for lag, count, who, event in events:
            u = t - lag
            now = jnp.logical_and(u >= 0, u < count)
            if who is not None:
                now = jnp.logical_and(now, who)
            pl.when(now)(lambda event=event, u=u: event(u))
        return carried

    lax.fori_loop(0, LAST + 9, step, 0)

    def sent(u, units, rows):
        ref = full.at[0:units, 0:rows]
        copy(u, 0, ref, ref, to_core).wait_send()

    def drain(u, carried):
        pl.when(outer)(lambda: sent(u, 3, 336))
        pl.when(inner)(lambda: sent(u, 5, 240))
        place(u, core, 0, 3 * SLAB, lambda dst: to_own(u, full.at[u], dst).wait())
        place(u, 1 - core, 0, 3 * SLAB, lambda dst: to_other(u, full.at[u], dst).wait_recv())
        return carried

    lax.fori_loop(0, UNITS, drain, 0)
    pl.when(outer)(lambda: sent(UNITS, 2, 224))
    pl.when(inner)(lambda: sent(UNITS, 2, 256))
    to_own(UNITS, pos_hbm, pos_hbm).wait()
    pl.when(outer)(lambda: sent(LAST, 2, 352))
    pl.when(inner)(lambda: sent(LAST, 2, 384))
    own_small = small_hbm.at[pl.ds(pl.multiple_of(core * 128, 128), 128)]
    other_small = small_hbm.at[pl.ds(pl.multiple_of((1 - core) * 128, 128), 128)]
    to_own(LAST, own_small, own_small).wait()
    to_other(LAST, other_small, other_small).wait_recv()
    for u in range(UNITS - STAGES, UNITS):
        core_first(u).wait_send()
    small_first().wait_send()
    lat_copy.wait()
    line_out.wait()
    for k in range(3):
        line_go(k).wait_send()
    pl.when(outer)(line_go(3).wait_send)

    @pl.when(inner)
    def _():
        line_go(4).wait_send()
        line_go(5).wait_send()

    @pl.when(core == 0)
    def _():
        exchange(2, mask_row, prior_mask).wait_send()
        exchange(0, keys.at[128:256], keys.at[0:128]).wait_send()
        exchange(1, values.at[128:256], values.at[0:128]).wait_send()
        exchange(3, row_out.at[120:128], row_in).wait_send()

    @pl.when(core == 1)
    def _():
        exchange(4, grad_out.at[0:8], grad_in).wait_send()
        exchange(5, d_prior, d_back).wait_send()


def flow(
    class_labels, group_perm, cot_logdet, latents, valid, patch_weight, pos_table, ln1_gain, ln1_bias,
    ln2_gain, ln2_bias, up_bias, head_weight, head_bias, cot_latents, class_table,
    qkv_weight, out_weight, up_weight, down_weight,
):
    smem = pl.BlockSpec(memory_space=pltpu.SMEM)
    vmem = pl.BlockSpec(memory_space=pltpu.VMEM)
    hbm = pl.BlockSpec(memory_space=pl.ANY)
    wide = (128, 768)
    return pl.pallas_call(
        flow_kernel,
        out_shape=(
            jax.ShapeDtypeStruct((3072, 768), bf16),
            jax.ShapeDtypeStruct((768, 3072), bf16),
            jax.ShapeDtypeStruct((768, 768), bf16),
            jax.ShapeDtypeStruct((768, 2304), bf16),
            jax.ShapeDtypeStruct((128, 768), bf16),
            jax.ShapeDtypeStruct((256, 768), bf16),
            jax.ShapeDtypeStruct((2, 128, 128), f32),
            jax.ShapeDtypeStruct((16, 768), f32),
        ),
        in_specs=[smem] * 3 + [vmem] * 12 + [hbm] * 5,
        out_specs=(hbm,) * 8,
        scratch_shapes=[
            pltpu.VMEM((STAGES, 3 * SLAB, COLS), bf16),
            pltpu.VMEM((LAST + 1, 3 * SLAB, COLS), bf16),
            pltpu.VMEM((LAST + 1, 3 * SLAB, COLS), bf16),
            pltpu.VMEM((UNITS, 3 * SLAB, COLS), bf16),
            pltpu.VMEM((256, COLS), bf16),
            pltpu.VMEM((LAST + 1, 2, 160, COLS), bf16),
            pltpu.VMEM((UNITS, 224, COLS), bf16),
            pltpu.SemaphoreType.DMA((LAST + 1,)),
            pltpu.SemaphoreType.DMA((14, TURNS)),
            pltpu.SemaphoreType.DMA((STAGES + 1,)),
            pltpu.SemaphoreType.DMA((LAST + 1,)),
            pltpu.SemaphoreType.DMA((LAST + 1,)),
            pltpu.VMEM((768, 2304), bf16),
            pltpu.VMEM((768, 768), bf16),
            pltpu.VMEM((768, 3072), bf16),
            pltpu.VMEM((3072, 768), bf16),
            pltpu.SemaphoreType.DMA((10,)),
            pltpu.VMEM((128, 128), f32),
            pltpu.VMEM((128, 128), f32),
            pltpu.VMEM(wide, bf16),
            pltpu.VMEM(wide, bf16),
            pltpu.VMEM(wide, f32),
            pltpu.VMEM(wide, f32),
            pltpu.VMEM(wide, f32),
            pltpu.VMEM(wide, f32),
            pltpu.VMEM((128, 1), f32),
            pltpu.VMEM((128, 1), f32),
            pltpu.VMEM((256, 768), bf16),
            pltpu.VMEM((256, 768), bf16),
            pltpu.VMEM(wide, bf16),
            pltpu.VMEM(wide, bf16),
            pltpu.VMEM((128, 256), f32),
            pltpu.VMEM((8, 128), f32),
            pltpu.VMEM((8, 128), f32),
            pltpu.VMEM((12, 128, 256), f32),
            pltpu.VMEM((4, 128, 768), f32),
            pltpu.VMEM(wide, f32),
            pltpu.VMEM(wide, f32),
            pltpu.VMEM(wide, bf16),
            pltpu.VMEM(wide, f32),
            pltpu.VMEM(wide, f32),
            pltpu.VMEM((2, 128, 768), bf16),
            pltpu.VMEM((2, 128, 768), bf16),
            pltpu.VMEM((128, 128), f32),
            pltpu.VMEM((8, 128), f32),
            pltpu.VMEM((128, 128), f32),
            pltpu.VMEM((8, 128), f32),
            pltpu.VMEM((128, 128), f32),
            pltpu.VMEM((2, 128, 128), f32),
            pltpu.VMEM((16, 768), f32),
            pltpu.VMEM((5, 16, 768), f32),
            pltpu.VMEM((5, 16, 768), f32),
            pltpu.SemaphoreType.DMA((6,)),
            pltpu.SemaphoreType.DMA((6,)),
            pltpu.SemaphoreType.DMA,
            pltpu.VMEM((7, 768, 128), bf16),
            pltpu.VMEM((9, 2, 128, COLS), bf16),
            pltpu.VMEM((256, COLS), bf16),
            pltpu.VMEM((2, 256, COLS), bf16),
            pltpu.VMEM(wide, bf16),
            pltpu.SemaphoreType.DMA((6,)),
            pltpu.SemaphoreType.DMA((6,)),
            pltpu.SemaphoreType.DMA,
        ],
        compiler_params=pltpu.CompilerParams(
            collective_id=0, has_side_effects=True, vmem_limit_bytes=62 << 20
        ),
        name="flow",
    )(
        class_labels, group_perm, cot_logdet, latents, valid, patch_weight, pos_table, ln1_gain, ln1_bias,
        ln2_gain, ln2_bias, up_bias, head_weight, head_bias, cot_latents, class_table,
        qkv_weight, out_weight, up_weight, down_weight,
    )


def finish_kernel(
    labels_ref, pos_ref, small_ref, lat_ref, line_ref, down_ref, up_ref, out_ref, qkv_ref,
    new_latents, logdet, latents_grad, patch, pos, classes, g1, b1, qkv, out, g2, b2, up, ub, down, head, hb,
    *scratch,
):
    dp = lax.axis_index("dp")
    narrow, wide, read_sem, write_sem = scratch[0:6:2], scratch[1:6:2], scratch[6], scratch[7]
    moves = []
    used = [0, 0, 0]
    for src, dst, i, rows in (
        (down_ref, down, 0, FINISH_ROWS), (up_ref, up, 2, FINISH_ROWS // 4),
        (qkv_ref, qkv, 1, FINISH_ROWS // 3), (out_ref, out, 0, FINISH_ROWS),
    ):
        for row in range(0, src.shape[0], rows):
            moves.append((src.at[row : row + rows], dst.at[0, row : row + rows], i, used[i]))
            used[i] += 1

    def read(m):
        src, dst, i, slot = moves[m]
        return pltpu.make_async_copy(src, narrow[i].at[slot], read_sem.at[m])

    def write(m):
        src, dst, i, slot = moves[m]
        return pltpu.make_async_copy(wide[i].at[slot], dst, write_sem.at[m])

    for m in range(AHEAD):
        read(m).start()
    for m in range(len(moves)):
        i, slot = moves[m][2:]
        read(m).wait()
        if m + AHEAD < len(moves):
            read(m + AHEAD).start()
        wide[i][slot] = narrow[i][slot].astype(f32)
        write(m).start()
    new_latents[0] = lat_ref[0, 0:48]
    latents_grad[0] = lat_ref[1, 0:48]
    pos[...] = pos_ref[...].astype(f32)
    patch[...] = small_ref[96:144].astype(f32)
    head[...] = small_ref[0:96].astype(f32)
    block = line_ref[...]
    for i, one in enumerate((g1, b1, g2, b2)):
        one[...] = block[i : i + 1]
    for i in range(4):
        ub[:, i * 768 : (i + 1) * 768] = block[4 + i : 5 + i]
    hb[...] = block[8:9, 0:96]
    count = labels_ref.shape[1]
    lane = lax.broadcasted_iota(jnp.int32, (1, 128), 1)
    logdet[...] = jnp.sum(jnp.where(lane == dp, block[8:9, 128:256], 0.0), 1, keepdims=True)
    by_lane = jnp.broadcast_to(labels_ref[...], (count, count)).astype(f32)
    first = lax.broadcasted_iota(jnp.int32, (count, count), 0)
    second = lax.broadcasted_iota(jnp.int32, (count, count), 1)
    by_row = jnp.sum(jnp.where(first == second, by_lane, 0.0), 1, keepdims=True)
    before = (by_lane < by_row) | ((by_lane == by_row) & (second < first))
    rank = jnp.sum(jnp.where(before, 1.0, 0.0), 1, keepdims=True)
    stored = jnp.sum(jnp.where(rank == second.astype(f32), by_row, 0.0), 0, keepdims=True)
    owned = classes.shape[0]
    wanted = (dp * owned + lax.broadcasted_iota(jnp.int32, (owned, count), 0)).astype(f32)
    hot = jnp.where(stored == wanted, 1.0, 0.0).astype(bf16)
    classes[...] = jnp.dot(hot, small_ref[144:160], preferred_element_type=f32)
    for m in range(len(moves)):
        write(m).wait()


def finish(class_labels, down, up, out, qkv, pos, small, lat, line_sums):
    count = class_labels.shape[1]
    owned = 1024 // count
    shapes = [
        (1, 48, 128), (1, 1), (1, 48, 128), (48, 768), (128, 768), (owned, 768), (1, 768), (1, 768),
        (1, 768, 2304), (1, 768, 768), (1, 768), (1, 768), (1, 768, 3072), (1, 3072), (1, 3072, 768),
        (96, 768), (1, 96),
    ]
    vmem = pl.BlockSpec(memory_space=pltpu.VMEM)
    hbm = pl.BlockSpec(memory_space=pl.ANY)
    buffers = []
    for columns, total in ((768, 3840), (2304, 768), (3072, 768)):
        rows = FINISH_ROWS * 768 // columns
        for kind in (bf16, f32):
            buffers.append(pltpu.VMEM((total // rows, rows, columns), kind))
    pieces = 3840 // FINISH_ROWS + 2304 // FINISH_ROWS + 3072 // FINISH_ROWS
    return pl.pallas_call(
        finish_kernel,
        out_shape=[jax.ShapeDtypeStruct(shape, f32) for shape in shapes],
        in_specs=[vmem] * 5 + [hbm] * 4,
        out_specs=[hbm if i in (8, 9, 12, 14) else vmem for i in range(17)],
        scratch_shapes=buffers + [pltpu.SemaphoreType.DMA((pieces,)), pltpu.SemaphoreType.DMA((pieces,))],
        compiler_params=pltpu.CompilerParams(vmem_limit_bytes=62 << 20),
        name="finish",
    )(class_labels, pos, small, lat, line_sums, down, up, out, qkv)


def fast_local(
    latents, valid, class_labels, group_perm, patch_weight, pos_table, class_table, ln1_gain, ln1_bias,
    qkv_weight, out_weight, ln2_gain, ln2_bias, up_weight, up_bias, down_weight, head_weight, head_bias,
    cot_latents, cot_logdet,
):
    sums = flow(
        class_labels, group_perm, cot_logdet, latents.swapaxes(1, 2), valid, patch_weight, pos_table, ln1_gain,
        ln1_bias, ln2_gain, ln2_bias, up_bias, head_weight.T, head_bias[None], cot_latents.swapaxes(1, 2), class_table,
        qkv_weight, out_weight, up_weight, down_weight,
    )
    results = list(finish(class_labels[None], *sums))
    results[1] = results[1].reshape(1)
    results[16] = results[16].reshape(96)
    results[0], results[2] = results[0].swapaxes(1, 2), results[2].swapaxes(1, 2)
    results[15] = results[15].T
    return tuple(results)


def forward(latents, valid, class_rows, seq_place, weights):
    (
        patch_weight,
        pos_table,
        qkv_weight,
        out_weight,
        ln1_gain,
        ln1_bias,
        ln2_gain,
        ln2_bias,
        up_weight,
        up_bias,
        down_weight,
        head_weight,
        head_bias,
    ) = weights
    images, patch_rows, channels = latents.shape
    model_width = qkv_weight.shape[1]
    head_count = model_width // HEAD_DIM
    latent_low = latents.astype(jnp.bfloat16)
    hidden = (
        matmul(latent_low, patch_weight)
        + pos_table.astype(jnp.float32)[None]
        + class_rows[:, None, :]
    )
    own_mask = valid.astype(jnp.bfloat16)
    normed = layer_norm(
        hidden, ln1_gain[0].astype(jnp.float32), ln1_bias[0].astype(jnp.float32)
    ).astype(jnp.bfloat16)
    packed = matmul(normed, qkv_weight[0]).astype(jnp.bfloat16)
    query = packed[..., :model_width].reshape(images, patch_rows, head_count, HEAD_DIM)
    keys_own = packed[..., model_width : 2 * model_width]
    values_own = packed[..., 2 * model_width :]
    prior_keys, prior_values, prior_mask = shifted_2((keys_own, values_own, own_mask), "seq", 1)
    keys = jnp.concatenate((prior_keys, keys_own), 1).reshape(
        images, 2 * patch_rows, head_count, HEAD_DIM
    )
    values = jnp.concatenate((prior_values, values_own), 1).reshape(
        images, 2 * patch_rows, head_count, HEAD_DIM
    )
    allowed = attention_mask(jnp.concatenate((prior_mask, own_mask), 1), patch_rows, seq_place)
    logits = masked_scores(query, keys, allowed)
    row_peak = jnp.max(logits, -1, keepdims=True)
    log_total = row_peak + jnp.log(jnp.sum(jnp.exp(logits - row_peak), -1, keepdims=True))
    weights_soft = jnp.exp(logits - log_total).astype(jnp.bfloat16)
    attended = jnp.einsum(
        "bhqk,bkhd->bqhd", weights_soft, values, preferred_element_type=jnp.float32
    )
    attended = attended.astype(jnp.bfloat16).reshape(images, patch_rows, model_width)
    mid = hidden + matmul(attended, out_weight[0])
    second = layer_norm(
        mid, ln2_gain[0].astype(jnp.float32), ln2_bias[0].astype(jnp.float32)
    ).astype(jnp.bfloat16)
    preact = matmul(second, up_weight[0]) + up_bias[0].astype(jnp.float32)
    activated = jax.nn.gelu(preact, approximate=True).astype(jnp.bfloat16)
    saved = [
        (
            hidden,
            normed,
            query,
            keys,
            values,
            allowed,
            log_total,
            attended,
            mid,
            second,
            preact,
            activated,
        )
    ]
    hidden = mid + matmul(activated, down_weight[0])
    top_low = hidden.astype(jnp.bfloat16)
    head_out = matmul(top_low, head_weight) + head_bias.astype(jnp.float32)
    prior_row = shifted_2(head_out[:, patch_rows - 1, :], "seq", 1)
    shifted = jnp.concatenate((prior_row[:, None, :], head_out[:, : patch_rows - 1, :]), 1)
    shifted = shifted * valid.astype(jnp.float32)[..., None]
    alpha = shifted[..., :channels]
    shift_mean = shifted[..., channels:]
    factor = jnp.exp(-alpha)
    new_latents = (latents - shift_mean) * factor
    logdet_part = -jnp.sum(alpha, (1, 2))
    return (new_latents, logdet_part, factor, top_low, saved)


def local(
    latents,
    valid,
    class_labels,
    group_perm,
    patch_weight,
    pos_table,
    class_table,
    ln1_gain,
    ln1_bias,
    qkv_weight,
    out_weight,
    ln2_gain,
    ln2_bias,
    up_weight,
    up_bias,
    down_weight,
    head_weight,
    head_bias,
    cot_latents,
    cot_logdet,
):
    images, patch_rows, channels = latents.shape
    model_width = qkv_weight.shape[1]
    head_count = model_width // HEAD_DIM
    layer_total = qkv_weight.shape[0]
    seq_place = lax.axis_index("seq")
    picks = group_perm[:, None] == lax.iota(jnp.int32, class_labels.shape[0])[None, :]
    image_labels = jnp.sum(jnp.where(picks, class_labels[None, :], 0), 1)
    label_hot = image_labels[:, None] == lax.iota(jnp.int32, class_table.shape[0])[None, :]
    class_rows = matmul(label_hot.astype(jnp.bfloat16), class_table)
    weights = (
        patch_weight,
        pos_table,
        qkv_weight,
        out_weight,
        ln1_gain,
        ln1_bias,
        ln2_gain,
        ln2_bias,
        up_weight,
        up_bias,
        down_weight,
        head_weight,
        head_bias,
    )
    new_latents, logdet_part, factor, top_low, saved = forward(
        latents, valid, class_rows, seq_place, weights
    )
    valid_float = valid.astype(jnp.float32)
    d_alpha = -cot_latents * new_latents - cot_logdet[:, None, None]
    d_mean = -cot_latents * factor
    d_shifted = jnp.concatenate((d_alpha, d_mean), -1) * valid_float[..., None]
    next_row = shifted_2(d_shifted[:, 0, :], "seq", -1)
    d_head = jnp.concatenate((d_shifted[:, 1:, :], next_row[:, None, :]), 1).astype(jnp.bfloat16)
    head_weight_grad = outer_sum(top_low, d_head)
    head_bias_grad = jnp.sum(d_head.astype(jnp.float32), (0, 1))
    d_hidden = transposed(d_head, head_weight)
    grads_qkv, grads_out, grads_up, grads_down = ([], [], [], [])
    grads_g1, grads_b1, grads_g2, grads_b2, grads_ub = ([], [], [], [], [])
    for layer_index in reversed(range(layer_total)):
        (
            hidden,
            normed,
            query,
            keys,
            values,
            allowed,
            log_total,
            attended,
            mid,
            second,
            preact,
            activated,
        ) = saved[layer_index]
        d_down = d_hidden.astype(jnp.bfloat16)
        down_grad = outer_sum(activated, d_down)
        d_act = transposed(d_down, down_weight[layer_index])
        unused_gelu, gelu_pull = jax.vjp(lambda inner: jax.nn.gelu(inner, approximate=True), preact)
        d_pre = gelu_pull(d_act)[0].astype(jnp.bfloat16)
        up_bias_grad = jnp.sum(d_pre.astype(jnp.float32), (0, 1))
        up_grad = outer_sum(second, d_pre)
        d_second = transposed(d_pre, up_weight[layer_index])
        unused_norm, norm_pull = jax.vjp(
            layer_norm,
            mid,
            ln2_gain[layer_index].astype(jnp.float32),
            ln2_bias[layer_index].astype(jnp.float32),
        )
        d_mid_norm, ln2_gain_part, ln2_bias_part = norm_pull(d_second)
        d_mid = d_hidden + d_mid_norm
        d_proj = d_mid.astype(jnp.bfloat16)
        out_grad = outer_sum(attended, d_proj)
        d_attended = transposed(d_proj, out_weight[layer_index]).astype(jnp.bfloat16)
        d_attended = d_attended.reshape(images, patch_rows, head_count, HEAD_DIM)
        logits = masked_scores(query, keys, allowed)
        probs = jnp.exp(logits - log_total)
        d_probs = jnp.einsum(
            "bqhd,bkhd->bhqk", d_attended, values, preferred_element_type=jnp.float32
        )
        d_scores = (probs * (d_probs - jnp.sum(d_probs * probs, -1, keepdims=True))).astype(
            jnp.bfloat16
        )
        d_query = jnp.einsum(
            "bhqk,bkhd->bqhd", d_scores, keys, preferred_element_type=jnp.float32
        ) * HEAD_DIM ** (-0.5)
        d_keys = jnp.einsum(
            "bhqk,bqhd->bkhd", d_scores, query, preferred_element_type=jnp.float32
        ) * HEAD_DIM ** (-0.5)
        d_values = jnp.einsum(
            "bhqk,bqhd->bkhd",
            probs.astype(jnp.bfloat16),
            d_attended,
            preferred_element_type=jnp.float32,
        )
        d_keys = d_keys.reshape(images, 2 * patch_rows, model_width)
        d_values = d_values.reshape(images, 2 * patch_rows, model_width)
        back_keys, back_values = (
            shifted_2(d_keys[:, :patch_rows].astype(jnp.bfloat16), "seq", -1).astype(jnp.float32),
            shifted_2(d_values[:, :patch_rows].astype(jnp.bfloat16), "seq", -1).astype(jnp.float32),
        )
        d_packed = jnp.concatenate(
            (
                d_query.reshape(images, patch_rows, model_width),
                d_keys[:, patch_rows:] + back_keys,
                d_values[:, patch_rows:] + back_values,
            ),
            -1,
        ).astype(jnp.bfloat16)
        qkv_grad = outer_sum(normed, d_packed)
        d_normed = transposed(d_packed, qkv_weight[layer_index])
        unused_norm, norm_pull = jax.vjp(
            layer_norm,
            hidden,
            ln1_gain[layer_index].astype(jnp.float32),
            ln1_bias[layer_index].astype(jnp.float32),
        )
        d_input, ln1_gain_part, ln1_bias_part = norm_pull(d_normed)
        d_hidden = d_mid + d_input
        grads_qkv.insert(0, qkv_grad)
        grads_out.insert(0, out_grad)
        grads_up.insert(0, up_grad)
        grads_down.insert(0, down_grad)
        grads_g1.insert(0, ln1_gain_part)
        grads_b1.insert(0, ln1_bias_part)
        grads_g2.insert(0, ln2_gain_part)
        grads_b2.insert(0, ln2_bias_part)
        grads_ub.insert(0, up_bias_grad)
    d_embed_low = d_hidden.astype(jnp.bfloat16)
    patch_grad_part = outer_sum(latents.astype(jnp.bfloat16), d_embed_low)
    latents_grad = cot_latents * factor + transposed(d_embed_low, patch_weight)
    pos_part = jnp.sum(d_hidden, 0)
    class_part = jnp.sum(d_hidden, 1)
    logdet, class_sums = lax.psum((logdet_part, class_part), "seq")
    class_term = lax.dot_general(
        label_hot.astype(jnp.float32),
        class_sums,
        (((0,), (0,)), ((), ())),
        precision=precise,
        preferred_element_type=jnp.float32,
    )
    class_grad = lax.psum_scatter(class_term, "dp", scatter_dimension=0, tiled=True)
    pos_grad = lax.psum(pos_part, "dp")
    (
        patch_weight_grad,
        head_weight_grad,
        head_bias_grad,
        ln1_gain_grad,
        ln1_bias_grad,
        ln2_gain_grad,
        ln2_bias_grad,
        up_bias_grad,
    ) = lax.psum(
        (
            patch_grad_part,
            head_weight_grad,
            head_bias_grad,
            jnp.stack(grads_g1),
            jnp.stack(grads_b1),
            jnp.stack(grads_g2),
            jnp.stack(grads_b2),
            jnp.stack(grads_ub),
        ),
        ("dp", "seq"),
    )
    qkv_stack = jnp.stack(grads_qkv)
    out_stack = jnp.stack(grads_out)
    up_stack = jnp.stack(grads_up)
    down_stack = jnp.stack(grads_down)
    flat_parts = (
        lax.psum_scatter(eight_rows(qkv_stack), ("dp", "seq"), scatter_dimension=1, tiled=True),
        lax.psum_scatter(eight_rows(out_stack), ("dp", "seq"), scatter_dimension=1, tiled=True),
        lax.psum_scatter(eight_rows(up_stack), ("dp", "seq"), scatter_dimension=1, tiled=True),
        lax.psum_scatter(eight_rows(down_stack), ("dp", "seq"), scatter_dimension=1, tiled=True),
    )
    flat_qkv, flat_out, flat_up, flat_down = (
        lax.all_gather(
            flat_parts[0].astype(jnp.bfloat16), ("dp", "seq"), axis=1, tiled=True
        ).astype(jnp.float32),
        lax.all_gather(
            flat_parts[1].astype(jnp.bfloat16), ("dp", "seq"), axis=1, tiled=True
        ).astype(jnp.float32),
        lax.all_gather(
            flat_parts[2].astype(jnp.bfloat16), ("dp", "seq"), axis=1, tiled=True
        ).astype(jnp.float32),
        lax.all_gather(
            flat_parts[3].astype(jnp.bfloat16), ("dp", "seq"), axis=1, tiled=True
        ).astype(jnp.float32),
    )
    qkv_stack = flat_qkv.reshape(qkv_stack.shape)
    out_stack = flat_out.reshape(out_stack.shape)
    up_stack = flat_up.reshape(up_stack.shape)
    down_stack = flat_down.reshape(down_stack.shape)
    return (
        new_latents,
        logdet,
        latents_grad,
        patch_weight_grad,
        pos_grad,
        class_grad,
        ln1_gain_grad,
        ln1_bias_grad,
        qkv_stack,
        out_stack,
        ln2_gain_grad,
        ln2_bias_grad,
        up_stack,
        up_bias_grad,
        down_stack,
        head_weight_grad,
        head_bias_grad,
    )


def solution(mesh):
    in_specs = (
        P("dp", "seq", None),
        P("dp", "seq"),
        P(),
        P("dp"),
        P(),
        P("seq", None),
        P(),
        P(),
        P(),
        P(),
        P(),
        P(),
        P(),
        P(),
        P(),
        P(),
        P(),
        P(),
        P("dp", "seq", None),
        P("dp"),
    )
    out_specs = (
        P("dp", "seq", None),
        P("dp"),
        P("dp", "seq", None),
        P(),
        P("seq", None),
        P("dp", None),
        P(),
        P(),
        P(),
        P(),
        P(),
        P(),
        P(),
        P(),
        P(),
        P(),
        P(),
    )
    body = fast_local if mesh.shape["dp"] == 16 and mesh.shape["seq"] == 2 else local
    return jax.shard_map(body, mesh=mesh, in_specs=in_specs, out_specs=out_specs, check_vma=False)
```

```python
import jax
import jax.numpy as jnp
from jax import lax
from jax.experimental import pallas as pl
from jax.experimental.pallas import tpu as pltpu
from jax.sharding import PartitionSpec as P

HEAD_DIM = 64


precise = lax.Precision.HIGHEST
norm_eps = 1e-05


def shifted_2(shard, axis, by):
    size = lax.axis_size(axis)
    pairs = [(i, i + by) for i in range(size) if 0 <= i + by < size]
    return lax.ppermute(shard, axis, pairs)


def layer_norm(values, norm_gain, norm_bias):
    center = values - jnp.mean(values, -1, keepdims=True)
    spread = jnp.mean(center * center, -1, keepdims=True)
    return center * lax.rsqrt(spread + norm_eps) * norm_gain + norm_bias


def matmul(left_side, weight_mat):
    return jnp.dot(left_side, weight_mat, preferred_element_type=jnp.float32)


def outer_sum(left_side, grad_side):
    left_flat = left_side.reshape(-1, left_side.shape[-1])
    grad_flat = grad_side.reshape(-1, grad_side.shape[-1])
    return lax.dot_general(
        left_flat, grad_flat, (((0,), (0,)), ((), ())), preferred_element_type=jnp.float32
    )


def transposed(grad_side, weight_mat):
    return lax.dot_general(
        grad_side,
        weight_mat,
        (((grad_side.ndim - 1,), (1,)), ((), ())),
        preferred_element_type=jnp.float32,
    )


def eight_rows(matrix):
    return matrix.reshape(8, -1)


def attention_mask(key_valid, patch_rows, seq_place):
    query_pos = seq_place * patch_rows + lax.iota(jnp.int32, patch_rows)
    key_pos = (seq_place - 1) * patch_rows + lax.iota(jnp.int32, 2 * patch_rows)
    earlier = (key_pos[None, :] < query_pos[:, None])[None] & (key_valid[:, None, :] > 0)
    return earlier | (key_pos[None, :] == query_pos[:, None])[None]


def masked_scores(query, keys, allowed):
    logits = jnp.einsum(
        "bqhd,bkhd->bhqk", query, keys, preferred_element_type=jnp.float32
    ) * HEAD_DIM ** (-0.5)
    return jnp.where(allowed[:, None], logits, -1e30)


MESH = pl.DeviceIdType.MESH
UNITS = 24
LAST = 25
TURNS = 13
STEPS = 38
DRAIN = 14
SLAB = 128
TABLE_ROWS = ((0, 384), (384, 384), (768, 256))
COLS = 384
STAGES = 3
CHUNK = 32
GELU_A = (2.0 / 3.141592653589793) ** 0.5
GELU_B = 0.044715
f32 = jnp.float32
bf16 = jnp.bfloat16


def flow_kernel(
    labels_sm, perm_sm, cot_logdet_sm,
    latents_ref, valid_ref, patch_ref, pos_table_ref, g1_ref, b1_ref, g2_ref, b2_ref,
    up_bias_ref, head_w_ref, head_b_ref, cot_ref,
    class_hbm, qkv_any, out_any, up_any, down_any,
    sums, latents_hbm, lines_hbm,
    stage, part, core_in, small_in, ab_in, c_in, send_sem, recv_sem, stage_sem, back_sem,
    qkv_w, out_w, up_w, down_w, load_sem,
    lat_pad, cot_pad, patch_pad, head_pad, hidden, mid, xhat1, xhat2, scale1, scale2,
    keys, values, query, attended, bias, prior_mask, mask_row, probs, slope, d_hidden, d_second, d_att, d_keys, d_values,
    d_prior, d_back, row_out, row_in, grad_out, grad_in, factor, lat_out,
    lines, line_sum, line_in, line_send, line_recv, line_sem,
    lt_ref, r_ref, pos_ref, small_ref, low_top, exch_send, exch_recv, lat_sem,
):
    dp = lax.axis_index("dp")
    core = lax.axis_index("seq")
    x, y, z = dp % 2, (dp // 2) % 2, dp // 4
    side = z // 2
    inner = ((z + 1) // 2) % 2 == 1
    outer = ((z + 1) // 2) % 2 == 0
    to_core = (dp, 1 - core)
    to_x = (dp + 1 - 2 * x, core)
    to_y = (dp + 2 - 4 * y, core)
    to_mate = (dp + 4 - 8 * (z % 2), core)
    to_inner = ((dp + 12 - 8 * z + 16) % 16, core)

    def rows_at(start, count):
        return pl.ds(pl.multiple_of(start, 16), count)

    sources = [class_hbm.at[r : r + n, h * COLS : (h + 1) * COLS] for h in range(2) for r, n in TABLE_ROWS]
    targets = [part.at[3 * h + i, 0:n] for h in range(2) for i, (r, n) in enumerate(TABLE_ROWS)]
    sources += [qkv_any.at[0], out_any.at[0], up_any.at[0], down_any.at[0]]
    targets += [qkv_w, out_w, up_w, down_w]

    def load(i):
        return pltpu.make_async_copy(sources[i], targets[i], load_sem.at[i])

    for i in range(10):
        load(i).start()

    barrier = pltpu.get_barrier_semaphore()
    for target in (to_core, to_x, to_y, to_mate):
        pl.semaphore_signal(barrier, inc=1, device_id=target, device_id_type=MESH)

    @pl.when(inner)
    def _():
        pl.semaphore_signal(barrier, inc=1, device_id=to_inner, device_id_type=MESH)

    def meet():
        @pl.when(inner)
        def _():
            pl.semaphore_wait(barrier, 5)

        @pl.when(outer)
        def _():
            pl.semaphore_wait(barrier, 4)

    def copy(u, k, src, dst, target):
        return pltpu.make_async_remote_copy(
            src_ref=src, dst_ref=dst, send_sem=send_sem.at[u], recv_sem=recv_sem.at[k, u % TURNS],
            device_id=target, device_id_type=MESH,
        )

    def arrived(u, k, dst):
        copy(u, k, dst, dst, to_core).wait_recv()

    def added(dst, left, right):
        dst[...] = (left[...].astype(f32) + right[...].astype(f32)).astype(bf16)

    first = (x, y)
    second = (y, x)
    to_first = (to_x, to_y)
    to_second = (to_y, to_x)

    def out_rows(u, t, start, count):
        return sums.at[u, core, rows_at(t * SLAB + start, count)]

    def part_rows(u, t, start, count):
        return part.at[u, rows_at(t * SLAB + start, count)]

    def left_index(u):
        return jnp.minimum(u // 2, 4) + jnp.minimum(jnp.maximum(u // 2 - 7, 0), 2)

    def right_index(u):
        return jnp.maximum(u // 2 - 3, 0)

    def product(u, t, half):
        rows = pl.ds(pl.multiple_of((u % 2) * 384 + t * SLAB, 128), SLAB)
        return jnp.dot(lt_ref[left_index(u), rows], r_ref[right_index(u), half], preferred_element_type=f32)

    def core_first(u):
        return pltpu.make_async_remote_copy(
            src_ref=stage.at[u % STAGES], dst_ref=core_in.at[u % TURNS], send_sem=stage_sem.at[u % STAGES],
            recv_sem=recv_sem.at[0, u % TURNS], device_id=to_core, device_id_type=MESH,
        )

    def small_first():
        return pltpu.make_async_remote_copy(
            src_ref=small_ref.at[1 - core], dst_ref=small_in, send_sem=stage_sem.at[STAGES],
            recv_sem=recv_sem.at[0, LAST % TURNS], device_id=to_core, device_id_type=MESH,
        )

    def line_copy(k, src, dst, target):
        return pltpu.make_async_remote_copy(
            src_ref=src, dst_ref=dst, send_sem=line_send.at[k], recv_sem=line_recv.at[k],
            device_id=target, device_id_type=MESH,
        )

    line_steps = (
        (lines, line_in.at[0], to_core),
        (line_sum.at[0], line_in.at[1], to_x),
        (line_sum.at[1], line_in.at[2], to_y),
        (line_sum.at[2], line_in.at[3], to_mate),
        (line_sum.at[3], line_in.at[4], to_inner),
        (line_sum.at[4], line_sum.at[4], to_mate),
    )

    def line_go(k):
        return line_copy(k, *line_steps[k])

    def line_add(k):
        line_go(k).wait_recv()
        line_sum[k] = line_steps[k][0][...] + line_in[k]

    line_out = pltpu.make_async_copy(line_sum.at[4], lines_hbm, line_sem)

    def produce(u):
        @pl.when(jnp.logical_and(u >= STAGES, u < UNITS))
        def _():
            core_first(u - STAGES).wait_send()

        @pl.when(u < UNITS)
        def _():
            for t in range(3):
                stage[u % STAGES, t * SLAB : (t + 1) * SLAB] = product(u, t, 1 - core).astype(bf16)
            core_first(u).start()

        @pl.when(u == LAST)
        def _():
            small_first().start()
            line_go(0).start()

    def begin(u):
        @pl.when(u < UNITS)
        def _():
            arrived(u, 0, core_in.at[u % TURNS])
            for t in range(3):
                rows = slice(t * SLAB, (t + 1) * SLAB)
                part[u, rows] = (product(u, t, core) + core_in[u % TURNS, rows].astype(f32)).astype(bf16)
                if t < 2:
                    ab_first(u, t).start()
            pl.when(outer)(lambda: c_z1(u).start())

        @pl.when(u == UNITS)
        def _():
            part[UNITS, 0:256] = pos_ref[...]
            for t in range(2):
                ab_first(u, t).start()

        @pl.when(u == LAST)
        def _():
            small_first().wait_recv()
            part[LAST, 0:256] = (small_ref[core].astype(f32) + small_in[...].astype(f32)).astype(bf16)
            for t in range(2):
                ab_first(u, t).start()
            line_add(0)
            line_go(1).start()

    def ab_base(t):
        return first[t] * 64 + second[t] * 32

    def ab_first(u, t):
        return copy(u, 1, part_rows(u, t, (1 - first[t]) * 64, 64), ab_in.at[u % TURNS, t, 0:64], to_first[t])

    def ab_second(u, t):
        row = first[t] * 64 + (1 - second[t]) * 32
        return copy(u, 2, part_rows(u, t, row, 32), ab_in.at[u % TURNS, t, 64:96], to_second[t])

    def ab_z1(u, t):
        return copy(u, 3, part_rows(u, t, ab_base(t), 32), ab_in.at[u % TURNS, t, 96:128], to_mate)

    def ab_z2(u, t):
        return copy(u, 4, part_rows(u, t, ab_base(t), 32), ab_in.at[u % TURNS, t, 128:160], to_inner)

    def ab_z3(u, t):
        block = out_rows(u, t, ab_base(t), 32)
        return copy(u, 3, block, block, to_mate)

    def ab_back2(u, t):
        block = out_rows(u, t, ab_base(t), 32)
        return copy(u, 5, block, block, to_second[t])

    def ab_back1(u, t):
        block = out_rows(u, t, first[t] * 64, 64)
        return copy(u, 6, block, block, to_first[t])

    def ab1(u):
        arrived(u, 1, ab_in.at[u % TURNS, :, 0:64])
        for t in range(2):
            kept = part_rows(u, t, first[t] * 64, 64)
            added(kept, kept, ab_in.at[u % TURNS, t, 0:64])
            ab_second(u, t).start()

        @pl.when(u == LAST)
        def _():
            line_add(1)
            line_go(2).start()

    def ab2(u):
        arrived(u, 2, ab_in.at[u % TURNS, :, 64:96])
        for t in range(2):
            kept = part_rows(u, t, ab_base(t), 32)
            added(kept, kept, ab_in.at[u % TURNS, t, 64:96])
            pl.when(outer)(lambda: ab_z1(u, t).start())

        @pl.when(u == LAST)
        def _():
            line_add(2)
            pl.when(outer)(line_go(3).start)

    def ab3_inner(u):
        arrived(u, 3, ab_in.at[u % TURNS, :, 96:128])
        for t in range(2):
            kept = part_rows(u, t, ab_base(t), 32)
            added(kept, kept, ab_in.at[u % TURNS, t, 96:128])
            ab_z2(u, t).start()

        @pl.when(u == LAST)
        def _():
            line_add(3)
            line_go(4).start()

    def ab4_inner(u):
        arrived(u, 4, ab_in.at[u % TURNS, :, 128:160])
        for t in range(2):
            added(out_rows(u, t, ab_base(t), 32), part_rows(u, t, ab_base(t), 32), ab_in.at[u % TURNS, t, 128:160])
            ab_z3(u, t).start()
            ab_back2(u, t).start()

        @pl.when(u == LAST)
        def _():
            line_add(4)
            line_go(5).start()
            line_out.start()

    def ab5_outer(u):
        arrived(u, 3, sums.at[u, core, 0:64])
        for t in range(2):
            ab_back2(u, t).start()

        @pl.when(u == LAST)
        def _():
            line_go(5).wait_recv()
            line_out.start()

    def ab6(u):
        arrived(u, 5, sums.at[u, core, 0:64])
        for t in range(2):
            ab_back1(u, t).start()

    def spread(u, row, count):
        block = sums.at[u, core, row : row + count]
        to_other(u, block).start()

    def to_other(u, block):
        return pltpu.make_async_remote_copy(
            src_ref=block, dst_ref=block, send_sem=send_sem.at[u], recv_sem=back_sem.at[u],
            device_id=to_core, device_id_type=MESH,
        )

    def ab7(u):
        arrived(u, 6, sums.at[u, core, 0:128])
        pl.when(u != UNITS)(lambda: spread(u, 0, 2 * SLAB))

    far = 32 * (1 - side)
    own_end = 96 * side
    shard = z * 32
    half = shard + x * 16

    def c_z1(u):
        return copy(u, 7, part_rows(u, 2, far, 96), c_in.at[u % TURNS, 0:96], to_mate)

    def c_z2(u):
        return copy(u, 8, part_rows(u, 2, (1 - side) * 64, 64), c_in.at[u % TURNS, 96:160], to_inner)

    def c_z3(u):
        return copy(u, 7, part_rows(u, 2, own_end, 32), c_in.at[u % TURNS, 160:192], to_mate)

    def c_x(u):
        return copy(u, 9, part_rows(u, 2, shard + (1 - x) * 16, 16), c_in.at[u % TURNS, 192:208], to_x)

    def c_y(u):
        return copy(u, 10, part_rows(u, 2, half, 16), c_in.at[u % TURNS, 208:224], to_y)

    def c_back_x(u):
        block = out_rows(u, 2, half, 16)
        return copy(u, 11, block, block, to_x)

    def c_z4(u):
        block = out_rows(u, 2, own_end, 32)
        return copy(u, 12, block, block, to_mate)

    def c_z5(u):
        block = out_rows(u, 2, side * 64, 64)
        return copy(u, 13, block, block, to_inner)

    def c_z6(u):
        block = out_rows(u, 2, far, 96)
        return copy(u, 12, block, block, to_mate)

    def c1_inner(u):
        arrived(u, 7, c_in.at[u % TURNS, 0:96])
        kept = part_rows(u, 2, far, 96)
        added(kept, kept, c_in.at[u % TURNS, 0:96])
        c_z2(u).start()

    def c2_inner(u):
        arrived(u, 8, c_in.at[u % TURNS, 96:160])
        kept = part_rows(u, 2, side * 64, 64)
        added(kept, kept, c_in.at[u % TURNS, 96:160])
        c_z3(u).start()
        c_x(u).start()

    def c3_outer(u):
        arrived(u, 7, c_in.at[u % TURNS, 160:192])
        kept = part_rows(u, 2, shard, 32)
        added(kept, kept, c_in.at[u % TURNS, 160:192])
        c_x(u).start()

    def c4(u):
        arrived(u, 9, c_in.at[u % TURNS, 192:208])
        kept = part_rows(u, 2, half, 16)
        added(kept, kept, c_in.at[u % TURNS, 192:208])
        c_y(u).start()

    def c5(u):
        arrived(u, 10, c_in.at[u % TURNS, 208:224])
        added(out_rows(u, 2, half, 16), part_rows(u, 2, half, 16), c_in.at[u % TURNS, 208:224])
        c_back_x(u).start()

    def c7_outer(u):
        arrived(u, 11, out_rows(u, 2, shard + (1 - x) * 16, 16))
        c_z4(u).start()

    def c8_inner(u):
        arrived(u, 11, out_rows(u, 2, shard + (1 - x) * 16, 16))
        arrived(u, 12, out_rows(u, 2, own_end, 32))
        c_z5(u).start()

    def c9_inner(u):
        arrived(u, 13, out_rows(u, 2, (1 - side) * 64, 64))
        c_z6(u).start()
        spread(u, 2 * SLAB, SLAB)

    def c10_outer(u):
        arrived(u, 12, out_rows(u, 2, far, 96))
        spread(u, 2 * SLAB, SLAB)

    def sent(u, units, rows):
        ref = part.at[0:units, 0:rows]
        copy(u, 0, ref, ref, to_core).wait_send()

    def drain(u):
        pl.when(outer)(lambda: sent(u, 3, 336))
        pl.when(inner)(lambda: sent(u, 5, 240))
        to_other(u, sums.at[u, 1 - core]).wait_recv()

    mm_nt = (((1,), (1,)), ((), ()))
    mm_tn = (((0,), (0,)), ((), ()))

    def nt(left, right):
        return lax.dot_general(left, right, mm_nt, preferred_element_type=f32)

    def tn(left, right):
        return lax.dot_general(left, right, mm_tn, preferred_element_type=f32)

    def nn(left, right):
        return jnp.dot(left, right, preferred_element_type=f32)

    def exchange(k, src, dst):
        return pltpu.make_async_remote_copy(
            src_ref=src, dst_ref=dst, send_sem=exch_send.at[k], recv_sem=exch_recv.at[k],
            device_id=to_core, device_id_type=MESH,
        )

    chunks = [slice(r, r + CHUNK) for r in range(0, 128, CHUNK)]
    lane = lax.broadcasted_iota(jnp.int32, (128, 128), 1)
    row = lax.broadcasted_iota(jnp.int32, (128, 128), 0)
    eye = row == lane
    low_half = lane < 64
    valid_row = valid_ref[...].astype(f32)
    valid_col = jnp.sum(jnp.where(eye, valid_row, 0.0), axis=1, keepdims=True)
    mask_row[...] = jnp.broadcast_to(valid_row, (8, 128))
    lat_pad[...] = jnp.zeros((128, 128), f32)
    lat_pad[0:48] = latents_ref[0]
    lat_pad[...] = lat_pad[...].T
    cot_pad[...] = jnp.zeros((128, 128), f32)
    cot_pad[0:48] = cot_ref[0]
    cot_pad[...] = cot_pad[...].T
    patch_pad[...] = jnp.zeros((128, 768), bf16)
    patch_pad[0:48] = patch_ref[...]
    head_pad[...] = jnp.zeros((128, 768), bf16)
    head_pad[0:96] = head_w_ref[...]
    head_bias = jnp.concatenate((head_b_ref[...].astype(f32), jnp.zeros((1, 32), f32)), 1)

    @pl.when(core == 0)
    def _():
        keys[0:128] = jnp.zeros((128, 768), bf16)
        values[0:128] = jnp.zeros((128, 768), bf16)
        prior_mask[...] = jnp.zeros((8, 128), f32)
        row_in[...] = jnp.zeros((8, 128), f32)

    @pl.when(core == 1)
    def _():
        grad_in[...] = jnp.zeros((8, 128), f32)
        d_back[...] = jnp.zeros((2, 128, 768), bf16)

    def normalize(src, hat, scale, gain, shift, put):
        for r in chunks:
            v = src[r]
            center = v - jnp.mean(v, -1, keepdims=True)
            inv = lax.rsqrt(jnp.mean(center * center, -1, keepdims=True) + norm_eps)
            scaled = center * inv
            hat[r] = scaled
            scale[r] = inv
            put(r, scaled * gain + shift)

    label = labels_sm[perm_sm[0]]
    hot = jnp.where(lax.broadcasted_iota(jnp.int32, (16, 1024), 1) == label, 1.0, 0.0).astype(bf16)
    for i in range(6):
        load(i).wait()
    class_row = jnp.concatenate(
        [
            sum(nn(hot[:, r : r + n], part[3 * h + i, 0:n]) for i, (r, n) in enumerate(TABLE_ROWS))
            for h in range(2)
        ],
        1,
    )[0:1]
    hidden[...] = (
        nn(lat_pad[...].astype(bf16), patch_pad[...]) + pos_table_ref[...].astype(f32) + class_row
    )

    def put_low(r, v):
        low_top[r] = v.astype(bf16)

    normalize(hidden, xhat1, scale1, g1_ref[...].astype(f32), b1_ref[...].astype(f32), put_low)
    load(6).wait()
    normed = low_top[...]
    keys[128:256] = nn(normed, qkv_w[:, 768:1536]).astype(bf16)
    meet()

    @pl.when(core == 0)
    def _():
        exchange(2, mask_row, prior_mask).start()
        exchange(0, keys.at[128:256], keys.at[0:128]).start()

    values[128:256] = nn(normed, qkv_w[:, 1536:2304]).astype(bf16)

    @pl.when(core == 0)
    def _():
        exchange(1, values.at[128:256], values.at[0:128]).start()

    query[...] = nn(normed, qkv_w[:, 0:768]).astype(bf16)
    lt_ref[6] = normed.astype(f32).T.astype(bf16)

    @pl.when(core == 1)
    def _():
        exchange(2, mask_row, prior_mask).wait_recv()
        exchange(0, keys.at[128:256], keys.at[0:128]).wait_recv()
        exchange(1, values.at[128:256], values.at[0:128]).wait_recv()

    bias[:, 0:128] = jnp.where(jnp.broadcast_to(prior_mask[0:1], (128, 128)) > 0.5, 0.0, -1e30)
    bias[:, 128:256] = jnp.where(((lane < row) & (valid_row > 0.5)) | eye, 0.0, -1e30)

    def columns128(p):
        return pl.ds(pl.multiple_of(p * 128, 128), 128)

    def attend(p):
        cols = columns128(p)
        q_pair = query[:, cols]
        k_pair = keys[:, cols]
        v_pair = values[:, cols]
        outs = []
        for i in range(2):
            q_one = jnp.where(low_half if i == 0 else lane >= 64, q_pair, jnp.zeros_like(q_pair))
            scores = nt(q_one, k_pair) * 0.125 + bias[...]
            top = jnp.max(scores, -1, keepdims=True)
            powers = jnp.exp(scores - top)
            soft = powers * (1.0 / jnp.sum(powers, -1, keepdims=True))
            probs[2 * p + i] = soft
            outs.append(nn(soft.astype(bf16), v_pair))
        attended[:, cols] = jnp.where(low_half, outs[0], outs[1]).astype(bf16)

    for p in range(6):
        attend(p)
    load(7).wait()
    mid[...] = hidden[...] + nn(attended[...], out_w[...])
    lt_ref[5] = attended[...].astype(f32).T.astype(bf16)
    normalize(mid, xhat2, scale2, g2_ref[...].astype(f32), b2_ref[...].astype(f32), put_low)
    lt_ref[4] = low_top[...].astype(f32).T.astype(bf16)
    load(8).wait()
    load(9).wait()
    d_hidden[...] = mid[...]

    def rows768(j):
        return pl.ds(pl.multiple_of(j * 768, 128), 768)

    def feed(j, carried):
        d_second[...] = nn(low_top[...], up_w[:, rows768(j)])
        shift = up_bias_ref[:, rows768(j)].astype(f32)
        for r in chunks:
            pre = d_second[r] + shift
            square = pre * pre
            bend = jnp.tanh(pre * (GELU_A + (GELU_A * GELU_B) * square))
            left = 0.5 * (1.0 + bend)
            slope[j, r] = left + 0.5 * pre * (1.0 - bend * bend) * (GELU_A + (3.0 * GELU_A * GELU_B) * square)
            d_second[r] = pre * left
        act = d_second[...]
        lt_ref[j] = act.T.astype(bf16)
        d_hidden[...] += nn(act.astype(bf16), down_w[rows768(j)])
        return carried

    lax.fori_loop(0, 4, feed, 0)
    low_top[...] = d_hidden[...].astype(bf16)
    row_out[...] = nt(low_top[...], head_pad[...]) + head_bias

    @pl.when(core == 0)
    def _():
        exchange(3, row_out.at[120:128], row_in).start()

    rolled = pltpu.roll(row_out[...], 1, 0)

    @pl.when(core == 1)
    def _():
        exchange(3, row_out.at[120:128], row_in).wait_recv()

    shifted = jnp.where(row == 0, jnp.broadcast_to(row_in[7:8], (128, 128)), rolled) * valid_col
    inside = lane < 48
    alpha = jnp.where(inside, shifted, 0.0)
    shift_mean = jnp.where(inside, pltpu.roll(shifted, 80, 1), 0.0)
    factor[...] = jnp.exp(-alpha)
    new_latents = (lat_pad[...] - shift_mean) * factor[...]
    lat_out[0] = new_latents.T
    logdet = -jnp.sum(jnp.sum(alpha, 1, keepdims=True), 0, keepdims=True)
    d_alpha = -cot_pad[...] * new_latents - cot_logdet_sm[0]
    direct = cot_pad[...] * factor[...]
    grad_out[...] = (
        jnp.where(inside, d_alpha, pltpu.roll(jnp.where(inside, -direct, 0.0), 48, 1)) * valid_col
    )

    @pl.when(core == 1)
    def _():
        exchange(4, grad_out.at[0:8], grad_in).start()

    rolled_back = pltpu.roll(grad_out[...], 127, 0)

    @pl.when(core == 0)
    def _():
        exchange(4, grad_out.at[0:8], grad_in).wait_recv()

    d_head = jnp.where(row == 127, jnp.broadcast_to(grad_in[0:1], (128, 128)), rolled_back).astype(bf16)
    head_grad = tn(d_head, low_top[...])
    head_bias_grad = jnp.sum(d_head.astype(f32), 0, keepdims=True)
    d_hidden[...] = nn(d_head, head_pad[...])
    low_top[...] = d_hidden[...].astype(bf16)
    for h in range(2):
        r_ref[0, h] = low_top[:, h * COLS : (h + 1) * COLS]

    def put(first_row, value):
        h, r = first_row // 128, first_row % 128
        for t in range(2):
            small_ref[h, t * 128 + r : t * 128 + r + value.shape[0]] = value[:, t * COLS : (t + 1) * COLS].astype(bf16)

    put(0, head_grad[0:96])

    lines[...] = jnp.zeros((16, 768), f32)
    lane1 = lax.broadcasted_iota(jnp.int32, (1, 128), 1)
    lines[8:9, 0:128] = head_bias_grad
    lines[8:9, 128:256] = jnp.where(lane1 == dp, logdet, 0.0)

    d_second[...] = jnp.zeros((128, 768), f32)

    def feed_back(j):
        d_keys[...] = nt(low_top[...], down_w[rows768(j)])
        total = jnp.zeros((1, 768), f32)
        for r in chunks:
            d_pre = (slope[j, r] * d_keys[r]).astype(bf16)
            d_att[r] = d_pre
            total += jnp.sum(d_pre.astype(f32), 0, keepdims=True)
            for h in range(2):
                r_ref[1 + j, h, r] = d_pre[:, h * COLS : (h + 1) * COLS]
        lines[pl.ds(4 + j, 1)] = total
        d_second[...] += nt(d_att[...], up_w[:, rows768(j)])

    def norm_back(grad, hat, scale, gain, base, out, line):
        gain_total = jnp.zeros((1, 768), f32)
        shift_total = jnp.zeros((1, 768), f32)
        for r in chunks:
            d = grad[r]
            scaled = hat[r]
            e = d * gain
            v = e - jnp.mean(e, -1, keepdims=True) - scaled * jnp.mean(e * scaled, -1, keepdims=True)
            out[r] = base[r] + scale[r] * v
            gain_total += jnp.sum(d * scaled, 0, keepdims=True)
            shift_total += jnp.sum(d, 0, keepdims=True)
        lines[line : line + 1] = gain_total
        lines[line + 1 : line + 2] = shift_total

    def feed_norm_back():
        norm_back(d_second, xhat2, scale2, g2_ref[...].astype(f32), d_hidden, mid, 2)
        low_top[...] = mid[...].astype(bf16)
        for h in range(2):
            r_ref[5, h] = low_top[:, h * COLS : (h + 1) * COLS]
        d_att[...] = nt(low_top[...], out_w[...]).astype(bf16)

    def attend_back(p):
        cols = columns128(p)
        q_pair = query[:, cols]
        k_pair = keys[:, cols]
        v_pair = values[:, cols]
        a_pair = d_att[:, cols]
        dq, dk, dv = [], [], []
        for i in range(2):
            own = low_half if i == 0 else lane >= 64
            a_one = jnp.where(own, a_pair, jnp.zeros_like(a_pair))
            q_one = jnp.where(own, q_pair, jnp.zeros_like(q_pair))
            soft = probs[2 * p + i]
            d_soft = nt(a_one, v_pair)
            weighted = d_soft * soft
            d_score = weighted - soft * jnp.sum(weighted, -1, keepdims=True)
            d_low = d_score.astype(bf16)
            dq.append(nn(d_low, k_pair))
            dk.append(tn(d_low, q_one))
            dv.append(tn(soft.astype(bf16), a_one))
        h, local = p // 3, pl.ds(pl.multiple_of((p % 3) * 128, 128), 128)
        r_ref[6, h, :, local] = (jnp.where(low_half, dq[0], dq[1]) * 0.125).astype(bf16)
        dk_pair = (dk[0] + dk[1]) * 0.125
        dv_pair = dv[0] + dv[1]
        d_prior[0, :, cols] = dk_pair[0:128].astype(bf16)
        d_prior[1, :, cols] = dv_pair[0:128].astype(bf16)
        d_keys[:, cols] = dk_pair[128:256]
        d_values[:, cols] = dv_pair[128:256]

    def send_prior():
        @pl.when(core == 1)
        def _():
            exchange(5, d_prior, d_back).start()

    def packed_back():
        @pl.when(core == 0)
        def _():
            exchange(5, d_prior, d_back).wait_recv()

        for h in range(2):
            cols = slice(h * COLS, (h + 1) * COLS)
            r_ref[7, h] = (d_keys[:, cols] + d_back[0, :, cols].astype(f32)).astype(bf16)
            r_ref[8, h] = (d_values[:, cols] + d_back[1, :, cols].astype(f32)).astype(bf16)
        d_second[...] = sum(
            nt(r_ref[6 + j, h], qkv_w[:, j * 768 + h * COLS : j * 768 + (h + 1) * COLS])
            for j in range(3)
            for h in range(2)
        )

    lat_copy = pltpu.make_async_copy(lat_out, latents_hbm, lat_sem)

    def embed_back():
        norm_back(d_second, xhat1, scale1, g1_ref[...].astype(f32), mid, d_hidden, 0)
        low_top[...] = d_hidden[...].astype(bf16)
        for t in range(2):
            pos_ref[t * 128 : (t + 1) * 128] = low_top[:, t * COLS : (t + 1) * COLS]
        patch_grad = tn(lat_pad[...].astype(bf16), low_top[...])
        lat_out[1] = (cot_pad[...] * factor[...] + nt(low_top[...], patch_pad[...])).T
        lat_copy.start()
        class_grad = jnp.sum(d_hidden[...], 0, keepdims=True)
        put(96, patch_grad[0:32])
        put(128, patch_grad[32:48])
        line = lax.broadcasted_iota(jnp.int32, (16, 768), 0)
        put(144, jnp.where(line == dp, class_grad, 0.0))
        put(160, jnp.zeros((96, 768), f32))

    def piece(t):
        @pl.when(jnp.logical_and(t < 8, t % 2 == 0))
        def _():
            feed_back(t // 2)

        pl.when(t == 8)(feed_norm_back)

        @pl.when(jnp.logical_and(t >= 9, t < 15))
        def _():
            attend_back(t - 9)

        pl.when(t == 14)(send_prior)
        pl.when(t == 16)(packed_back)
        pl.when(t == 18)(embed_back)

    everyone, inners, outers = None, inner, outer
    events = [
        (0, LAST + 1, everyone, produce),
        (2, UNITS, inners, c1_inner),
        (1, LAST + 1, everyone, begin),
        (7, UNITS, inners, c5),
        (9, LAST + 1, inners, ab6),
        (3, UNITS, inners, c2_inner),
        (4, LAST + 1, inners, ab3_inner),
        (0, LAST + 1, everyone, piece),
        (2, LAST + 1, everyone, ab1),
        (5, LAST + 1, inners, ab4_inner),
        (11, LAST + 1, outers, ab7),
        (5, UNITS, inners, c4),
        (8, UNITS, inners, c8_inner),
        (12, LAST + 1, inners, ab7),
        (9, UNITS, inners, c9_inner),
        (3, LAST + 1, everyone, ab2),
        (6, UNITS, outers, c5),
        (7, UNITS, outers, c7_outer),
        (4, UNITS, outers, c3_outer),
        (5, UNITS, outers, c4),
        (12, UNITS, outers, c10_outer),
        (7, LAST + 1, outers, ab5_outer),
        (8, LAST + 1, outers, ab6),
        (DRAIN, UNITS, everyone, drain),
    ]

    def step(t, carried):
        for lag, count, who, event in events:
            u = t - lag
            now = jnp.logical_and(u >= 0, u < count)
            if who is not None:
                now = jnp.logical_and(now, who)
            pl.when(now)(lambda event=event, u=u: event(u))
        return carried

    lax.fori_loop(0, STEPS, step, 0)


    def drain_more(u, carried):
        drain(u)
        return carried

    lax.fori_loop(STEPS - DRAIN, UNITS, drain_more, 0)
    pl.when(outer)(lambda: sent(UNITS, 2, 224))
    pl.when(inner)(lambda: sent(UNITS, 2, 256))
    pl.when(outer)(lambda: sent(LAST, 2, 352))
    pl.when(inner)(lambda: sent(LAST, 2, 384))
    to_other(LAST, sums.at[LAST, 1 - core, 0 : 2 * SLAB]).wait_recv()
    for u in range(UNITS - STAGES, UNITS):
        core_first(u).wait_send()
    small_first().wait_send()
    lat_copy.wait()
    line_out.wait()
    for k in range(3):
        line_go(k).wait_send()
    pl.when(outer)(line_go(3).wait_send)

    @pl.when(inner)
    def _():
        line_go(4).wait_send()
        line_go(5).wait_send()

    @pl.when(core == 0)
    def _():
        exchange(2, mask_row, prior_mask).wait_send()
        exchange(0, keys.at[128:256], keys.at[0:128]).wait_send()
        exchange(1, values.at[128:256], values.at[0:128]).wait_send()
        exchange(3, row_out.at[120:128], row_in).wait_send()

    @pl.when(core == 1)
    def _():
        exchange(4, grad_out.at[0:8], grad_in).wait_send()
        exchange(5, d_prior, d_back).wait_send()


def flow(
    class_labels, group_perm, cot_logdet, latents, valid, patch_weight, pos_table, ln1_gain, ln1_bias,
    ln2_gain, ln2_bias, up_bias, head_weight, head_bias, cot_latents, class_table,
    qkv_weight, out_weight, up_weight, down_weight,
):
    smem = pl.BlockSpec(memory_space=pltpu.SMEM)
    vmem = pl.BlockSpec(memory_space=pltpu.VMEM)
    hbm = pl.BlockSpec(memory_space=pltpu.HBM)
    wide = (128, 768)
    return pl.pallas_call(
        flow_kernel,
        out_shape=(
            pltpu.VMEM((LAST + 1, 2, 3 * SLAB, COLS), bf16),
            jax.ShapeDtypeStruct((2, 128, 128), f32),
            jax.ShapeDtypeStruct((16, 768), f32),
        ),
        in_specs=[smem] * 3 + [vmem] * 12 + [hbm] * 5,
        out_specs=(vmem, hbm, hbm),
        scratch_shapes=[
            pltpu.VMEM((STAGES, 3 * SLAB, COLS), bf16),
            pltpu.VMEM((LAST + 1, 3 * SLAB, COLS), bf16),
            pltpu.VMEM((TURNS, 3 * SLAB, COLS), bf16),
            pltpu.VMEM((256, COLS), bf16),
            pltpu.VMEM((TURNS, 2, 160, COLS), bf16),
            pltpu.VMEM((TURNS, 224, COLS), bf16),
            pltpu.SemaphoreType.DMA((LAST + 1,)),
            pltpu.SemaphoreType.DMA((14, TURNS)),
            pltpu.SemaphoreType.DMA((STAGES + 1,)),
            pltpu.SemaphoreType.DMA((LAST + 1,)),
            pltpu.VMEM((768, 2304), bf16),
            pltpu.VMEM((768, 768), bf16),
            pltpu.VMEM((768, 3072), bf16),
            pltpu.VMEM((3072, 768), bf16),
            pltpu.SemaphoreType.DMA((10,)),
            pltpu.VMEM((128, 128), f32),
            pltpu.VMEM((128, 128), f32),
            pltpu.VMEM(wide, bf16),
            pltpu.VMEM(wide, bf16),
            pltpu.VMEM(wide, f32),
            pltpu.VMEM(wide, f32),
            pltpu.VMEM(wide, f32),
            pltpu.VMEM(wide, f32),
            pltpu.VMEM((128, 1), f32),
            pltpu.VMEM((128, 1), f32),
            pltpu.VMEM((256, 768), bf16),
            pltpu.VMEM((256, 768), bf16),
            pltpu.VMEM(wide, bf16),
            pltpu.VMEM(wide, bf16),
            pltpu.VMEM((128, 256), f32),
            pltpu.VMEM((8, 128), f32),
            pltpu.VMEM((8, 128), f32),
            pltpu.VMEM((12, 128, 256), f32),
            pltpu.VMEM((4, 128, 768), f32),
            pltpu.VMEM(wide, f32),
            pltpu.VMEM(wide, f32),
            pltpu.VMEM(wide, bf16),
            pltpu.VMEM(wide, f32),
            pltpu.VMEM(wide, f32),
            pltpu.VMEM((2, 128, 768), bf16),
            pltpu.VMEM((2, 128, 768), bf16),
            pltpu.VMEM((128, 128), f32),
            pltpu.VMEM((8, 128), f32),
            pltpu.VMEM((128, 128), f32),
            pltpu.VMEM((8, 128), f32),
            pltpu.VMEM((128, 128), f32),
            pltpu.VMEM((2, 128, 128), f32),
            pltpu.VMEM((16, 768), f32),
            pltpu.VMEM((5, 16, 768), f32),
            pltpu.VMEM((5, 16, 768), f32),
            pltpu.SemaphoreType.DMA((6,)),
            pltpu.SemaphoreType.DMA((6,)),
            pltpu.SemaphoreType.DMA,
            pltpu.VMEM((7, 768, 128), bf16),
            pltpu.VMEM((9, 2, 128, COLS), bf16),
            pltpu.VMEM((256, COLS), bf16),
            pltpu.VMEM((2, 256, COLS), bf16),
            pltpu.VMEM(wide, bf16),
            pltpu.SemaphoreType.DMA((6,)),
            pltpu.SemaphoreType.DMA((6,)),
            pltpu.SemaphoreType.DMA,
        ],
        compiler_params=pltpu.CompilerParams(
            collective_id=0, has_side_effects=True, vmem_limit_bytes=46 << 20
        ),
        name="flow",
    )(
        class_labels, group_perm, cot_logdet, latents, valid, patch_weight, pos_table, ln1_gain, ln1_bias,
        ln2_gain, ln2_bias, up_bias, head_weight, head_bias, cot_latents, class_table,
        qkv_weight, out_weight, up_weight, down_weight,
    )


def finish_kernel(
    labels_ref, sums, lat_hbm, line_hbm,
    new_latents, logdet, latents_grad, patch, pos, classes, g1, b1, qkv, out, g2, b2, up, ub, down, head, hb,
    wide, write_sem, lat_ref, line_ref, pos_wide, small_wide, class_wide, in_sem, out_sem,
):
    dp = lax.axis_index("dp")
    core = lax.axis_index("seq")
    owned = classes.shape[0]
    inputs = [
        pltpu.make_async_copy(src, dst, in_sem.at[i])
        for i, (src, dst) in enumerate(
            ((lat_hbm, lat_ref), (line_hbm, line_ref))
        )
    ]
    outputs = [
        pltpu.make_async_copy(src, dst, out_sem.at[i])
        for i, (src, dst) in enumerate(
            (
                (lat_ref.at[0, 0:48], new_latents.at[0]),
                (lat_ref.at[1, 0:48], latents_grad.at[0]),
                (small_wide.at[0:96], head),
                (small_wide.at[96:144], patch),
                (pos_wide, pos),
                (class_wide, classes),
            )
        )
    ]
    def write(u):
        block, row = u // 2, (u % 2) * 384
        if block < 4:
            dst = down.at[0, block * 768 + row : block * 768 + row + 384]
        else:
            target, column = (up, block - 4) if block < 8 else (out, 0) if block == 8 else (qkv, block - 9)
            dst = target.at[0, row : row + 384, column * 768 : (column + 1) * 768]
        return pltpu.make_async_copy(wide.at[u], dst, write_sem.at[u])

    def little():
        for one in inputs:
            one.wait()
        outputs[0].start()
        outputs[1].start()
        for t in range(2):
            rows, cols = slice(t * 128, (t + 1) * 128), slice(t * COLS, (t + 1) * COLS)
            pos_wide[:, cols] = sums[UNITS, core, rows].astype(f32)
            for h in range(2):
                small_wide[h * 128 : (h + 1) * 128, cols] = sums[LAST, h, rows].astype(f32)
        for one in outputs[2:5]:
            one.start()
        block = line_ref[...]
        for i, one in enumerate((g1, b1, g2, b2)):
            one[...] = block[i : i + 1]
        for i in range(4):
            ub[:, i * 768 : (i + 1) * 768] = block[4 + i : 5 + i]
        hb[...] = block[8:9, 0:96]
        count = labels_ref.shape[1]
        lane = lax.broadcasted_iota(jnp.int32, (1, 128), 1)
        logdet[...] = jnp.sum(jnp.where(lane == dp, block[8:9, 128:256], 0.0), 1, keepdims=True)
        by_lane = jnp.broadcast_to(labels_ref[...], (count, count)).astype(f32)
        first = lax.broadcasted_iota(jnp.int32, (count, count), 0)
        second = lax.broadcasted_iota(jnp.int32, (count, count), 1)
        by_row = jnp.sum(jnp.where(first == second, by_lane, 0.0), 1, keepdims=True)
        before = (by_lane < by_row) | ((by_lane == by_row) & (second < first))
        rank = jnp.sum(jnp.where(before, 1.0, 0.0), 1, keepdims=True)
        stored = jnp.sum(jnp.where(rank == second.astype(f32), by_row, 0.0), 0, keepdims=True)
        wanted = (dp * owned + lax.broadcasted_iota(jnp.int32, (owned, count), 0)).astype(f32)
        hot = jnp.where(stored == wanted, 1.0, 0.0).astype(bf16)
        class_wide[...] = jnp.dot(hot, small_wide[144:160].astype(bf16), preferred_element_type=f32)
        outputs[5].start()

    for one in inputs:
        one.start()
    for u in range(UNITS):
        for h in range(2):
            wide[u, :, h * COLS : (h + 1) * COLS] = sums[u, h].astype(f32)
        write(u).start()
        if u == 1:
            little()
    for u in range(UNITS):
        write(u).wait()
    for one in outputs:
        one.wait()


def finish(class_labels, sums, lat, line_sums):
    count = class_labels.shape[1]
    owned = 1024 // count
    shapes = [
        (1, 48, 128), (1, 1), (1, 48, 128), (48, 768), (128, 768), (owned, 768), (1, 768), (1, 768),
        (1, 768, 2304), (1, 768, 768), (1, 768), (1, 768), (1, 768, 3072), (1, 3072), (1, 3072, 768),
        (96, 768), (1, 96),
    ]
    vmem = pl.BlockSpec(memory_space=pltpu.VMEM)
    hbm = pl.BlockSpec(memory_space=pl.ANY)
    return pl.pallas_call(
        finish_kernel,
        out_shape=[jax.ShapeDtypeStruct(shape, f32) for shape in shapes],
        in_specs=[vmem, vmem] + [pl.BlockSpec(memory_space=pltpu.HBM)] * 2,
        out_specs=[vmem if i in (1, 6, 7, 10, 11, 13, 16) else hbm for i in range(17)],
        scratch_shapes=[
            pltpu.VMEM((UNITS, 384, 768), f32),
            pltpu.SemaphoreType.DMA((UNITS,)),
            pltpu.VMEM((2, 128, 128), f32),
            pltpu.VMEM((16, 768), f32),
            pltpu.VMEM((128, 768), f32),
            pltpu.VMEM((256, 768), f32),
            pltpu.VMEM((owned, 768), f32),
            pltpu.SemaphoreType.DMA((2,)),
            pltpu.SemaphoreType.DMA((6,)),
        ],
        compiler_params=pltpu.CompilerParams(vmem_limit_bytes=34 << 20),
        name="finish",
    )(class_labels, sums, lat, line_sums)


def fast_local(
    latents, valid, class_labels, group_perm, patch_weight, pos_table, class_table, ln1_gain, ln1_bias,
    qkv_weight, out_weight, ln2_gain, ln2_bias, up_weight, up_bias, down_weight, head_weight, head_bias,
    cot_latents, cot_logdet,
):
    sums = flow(
        class_labels, group_perm, cot_logdet, latents.swapaxes(1, 2), valid, patch_weight, pos_table, ln1_gain,
        ln1_bias, ln2_gain, ln2_bias, up_bias, head_weight.T, head_bias[None], cot_latents.swapaxes(1, 2), class_table,
        qkv_weight, out_weight, up_weight, down_weight,
    )
    results = list(finish(class_labels[None], *sums))
    results[1] = results[1].reshape(1)
    results[16] = results[16].reshape(96)
    results[0], results[2] = results[0].swapaxes(1, 2), results[2].swapaxes(1, 2)
    results[15] = results[15].T
    return tuple(results)


def forward(latents, valid, class_rows, seq_place, weights):
    (
        patch_weight,
        pos_table,
        qkv_weight,
        out_weight,
        ln1_gain,
        ln1_bias,
        ln2_gain,
        ln2_bias,
        up_weight,
        up_bias,
        down_weight,
        head_weight,
        head_bias,
    ) = weights
    images, patch_rows, channels = latents.shape
    model_width = qkv_weight.shape[1]
    head_count = model_width // HEAD_DIM
    latent_low = latents.astype(jnp.bfloat16)
    hidden = (
        matmul(latent_low, patch_weight)
        + pos_table.astype(jnp.float32)[None]
        + class_rows[:, None, :]
    )
    own_mask = valid.astype(jnp.bfloat16)
    normed = layer_norm(
        hidden, ln1_gain[0].astype(jnp.float32), ln1_bias[0].astype(jnp.float32)
    ).astype(jnp.bfloat16)
    packed = matmul(normed, qkv_weight[0]).astype(jnp.bfloat16)
    query = packed[..., :model_width].reshape(images, patch_rows, head_count, HEAD_DIM)
    keys_own = packed[..., model_width : 2 * model_width]
    values_own = packed[..., 2 * model_width :]
    prior_keys, prior_values, prior_mask = shifted_2((keys_own, values_own, own_mask), "seq", 1)
    keys = jnp.concatenate((prior_keys, keys_own), 1).reshape(
        images, 2 * patch_rows, head_count, HEAD_DIM
    )
    values = jnp.concatenate((prior_values, values_own), 1).reshape(
        images, 2 * patch_rows, head_count, HEAD_DIM
    )
    allowed = attention_mask(jnp.concatenate((prior_mask, own_mask), 1), patch_rows, seq_place)
    logits = masked_scores(query, keys, allowed)
    row_peak = jnp.max(logits, -1, keepdims=True)
    log_total = row_peak + jnp.log(jnp.sum(jnp.exp(logits - row_peak), -1, keepdims=True))
    weights_soft = jnp.exp(logits - log_total).astype(jnp.bfloat16)
    attended = jnp.einsum(
        "bhqk,bkhd->bqhd", weights_soft, values, preferred_element_type=jnp.float32
    )
    attended = attended.astype(jnp.bfloat16).reshape(images, patch_rows, model_width)
    mid = hidden + matmul(attended, out_weight[0])
    second = layer_norm(
        mid, ln2_gain[0].astype(jnp.float32), ln2_bias[0].astype(jnp.float32)
    ).astype(jnp.bfloat16)
    preact = matmul(second, up_weight[0]) + up_bias[0].astype(jnp.float32)
    activated = jax.nn.gelu(preact, approximate=True).astype(jnp.bfloat16)
    saved = [
        (
            hidden,
            normed,
            query,
            keys,
            values,
            allowed,
            log_total,
            attended,
            mid,
            second,
            preact,
            activated,
        )
    ]
    hidden = mid + matmul(activated, down_weight[0])
    top_low = hidden.astype(jnp.bfloat16)
    head_out = matmul(top_low, head_weight) + head_bias.astype(jnp.float32)
    prior_row = shifted_2(head_out[:, patch_rows - 1, :], "seq", 1)
    shifted = jnp.concatenate((prior_row[:, None, :], head_out[:, : patch_rows - 1, :]), 1)
    shifted = shifted * valid.astype(jnp.float32)[..., None]
    alpha = shifted[..., :channels]
    shift_mean = shifted[..., channels:]
    factor = jnp.exp(-alpha)
    new_latents = (latents - shift_mean) * factor
    logdet_part = -jnp.sum(alpha, (1, 2))
    return (new_latents, logdet_part, factor, top_low, saved)


def local(
    latents,
    valid,
    class_labels,
    group_perm,
    patch_weight,
    pos_table,
    class_table,
    ln1_gain,
    ln1_bias,
    qkv_weight,
    out_weight,
    ln2_gain,
    ln2_bias,
    up_weight,
    up_bias,
    down_weight,
    head_weight,
    head_bias,
    cot_latents,
    cot_logdet,
):
    images, patch_rows, channels = latents.shape
    model_width = qkv_weight.shape[1]
    head_count = model_width // HEAD_DIM
    layer_total = qkv_weight.shape[0]
    seq_place = lax.axis_index("seq")
    picks = group_perm[:, None] == lax.iota(jnp.int32, class_labels.shape[0])[None, :]
    image_labels = jnp.sum(jnp.where(picks, class_labels[None, :], 0), 1)
    label_hot = image_labels[:, None] == lax.iota(jnp.int32, class_table.shape[0])[None, :]
    class_rows = matmul(label_hot.astype(jnp.bfloat16), class_table)
    weights = (
        patch_weight,
        pos_table,
        qkv_weight,
        out_weight,
        ln1_gain,
        ln1_bias,
        ln2_gain,
        ln2_bias,
        up_weight,
        up_bias,
        down_weight,
        head_weight,
        head_bias,
    )
    new_latents, logdet_part, factor, top_low, saved = forward(
        latents, valid, class_rows, seq_place, weights
    )
    valid_float = valid.astype(jnp.float32)
    d_alpha = -cot_latents * new_latents - cot_logdet[:, None, None]
    d_mean = -cot_latents * factor
    d_shifted = jnp.concatenate((d_alpha, d_mean), -1) * valid_float[..., None]
    next_row = shifted_2(d_shifted[:, 0, :], "seq", -1)
    d_head = jnp.concatenate((d_shifted[:, 1:, :], next_row[:, None, :]), 1).astype(jnp.bfloat16)
    head_weight_grad = outer_sum(top_low, d_head)
    head_bias_grad = jnp.sum(d_head.astype(jnp.float32), (0, 1))
    d_hidden = transposed(d_head, head_weight)
    grads_qkv, grads_out, grads_up, grads_down = ([], [], [], [])
    grads_g1, grads_b1, grads_g2, grads_b2, grads_ub = ([], [], [], [], [])
    for layer_index in reversed(range(layer_total)):
        (
            hidden,
            normed,
            query,
            keys,
            values,
            allowed,
            log_total,
            attended,
            mid,
            second,
            preact,
            activated,
        ) = saved[layer_index]
        d_down = d_hidden.astype(jnp.bfloat16)
        down_grad = outer_sum(activated, d_down)
        d_act = transposed(d_down, down_weight[layer_index])
        unused_gelu, gelu_pull = jax.vjp(lambda inner: jax.nn.gelu(inner, approximate=True), preact)
        d_pre = gelu_pull(d_act)[0].astype(jnp.bfloat16)
        up_bias_grad = jnp.sum(d_pre.astype(jnp.float32), (0, 1))
        up_grad = outer_sum(second, d_pre)
        d_second = transposed(d_pre, up_weight[layer_index])
        unused_norm, norm_pull = jax.vjp(
            layer_norm,
            mid,
            ln2_gain[layer_index].astype(jnp.float32),
            ln2_bias[layer_index].astype(jnp.float32),
        )
        d_mid_norm, ln2_gain_part, ln2_bias_part = norm_pull(d_second)
        d_mid = d_hidden + d_mid_norm
        d_proj = d_mid.astype(jnp.bfloat16)
        out_grad = outer_sum(attended, d_proj)
        d_attended = transposed(d_proj, out_weight[layer_index]).astype(jnp.bfloat16)
        d_attended = d_attended.reshape(images, patch_rows, head_count, HEAD_DIM)
        logits = masked_scores(query, keys, allowed)
        probs = jnp.exp(logits - log_total)
        d_probs = jnp.einsum(
            "bqhd,bkhd->bhqk", d_attended, values, preferred_element_type=jnp.float32
        )
        d_scores = (probs * (d_probs - jnp.sum(d_probs * probs, -1, keepdims=True))).astype(
            jnp.bfloat16
        )
        d_query = jnp.einsum(
            "bhqk,bkhd->bqhd", d_scores, keys, preferred_element_type=jnp.float32
        ) * HEAD_DIM ** (-0.5)
        d_keys = jnp.einsum(
            "bhqk,bqhd->bkhd", d_scores, query, preferred_element_type=jnp.float32
        ) * HEAD_DIM ** (-0.5)
        d_values = jnp.einsum(
            "bhqk,bqhd->bkhd",
            probs.astype(jnp.bfloat16),
            d_attended,
            preferred_element_type=jnp.float32,
        )
        d_keys = d_keys.reshape(images, 2 * patch_rows, model_width)
        d_values = d_values.reshape(images, 2 * patch_rows, model_width)
        back_keys, back_values = (
            shifted_2(d_keys[:, :patch_rows].astype(jnp.bfloat16), "seq", -1).astype(jnp.float32),
            shifted_2(d_values[:, :patch_rows].astype(jnp.bfloat16), "seq", -1).astype(jnp.float32),
        )
        d_packed = jnp.concatenate(
            (
                d_query.reshape(images, patch_rows, model_width),
                d_keys[:, patch_rows:] + back_keys,
                d_values[:, patch_rows:] + back_values,
            ),
            -1,
        ).astype(jnp.bfloat16)
        qkv_grad = outer_sum(normed, d_packed)
        d_normed = transposed(d_packed, qkv_weight[layer_index])
        unused_norm, norm_pull = jax.vjp(
            layer_norm,
            hidden,
            ln1_gain[layer_index].astype(jnp.float32),
            ln1_bias[layer_index].astype(jnp.float32),
        )
        d_input, ln1_gain_part, ln1_bias_part = norm_pull(d_normed)
        d_hidden = d_mid + d_input
        grads_qkv.insert(0, qkv_grad)
        grads_out.insert(0, out_grad)
        grads_up.insert(0, up_grad)
        grads_down.insert(0, down_grad)
        grads_g1.insert(0, ln1_gain_part)
        grads_b1.insert(0, ln1_bias_part)
        grads_g2.insert(0, ln2_gain_part)
        grads_b2.insert(0, ln2_bias_part)
        grads_ub.insert(0, up_bias_grad)
    d_embed_low = d_hidden.astype(jnp.bfloat16)
    patch_grad_part = outer_sum(latents.astype(jnp.bfloat16), d_embed_low)
    latents_grad = cot_latents * factor + transposed(d_embed_low, patch_weight)
    pos_part = jnp.sum(d_hidden, 0)
    class_part = jnp.sum(d_hidden, 1)
    logdet, class_sums = lax.psum((logdet_part, class_part), "seq")
    class_term = lax.dot_general(
        label_hot.astype(jnp.float32),
        class_sums,
        (((0,), (0,)), ((), ())),
        precision=precise,
        preferred_element_type=jnp.float32,
    )
    class_grad = lax.psum_scatter(class_term, "dp", scatter_dimension=0, tiled=True)
    pos_grad = lax.psum(pos_part, "dp")
    (
        patch_weight_grad,
        head_weight_grad,
        head_bias_grad,
        ln1_gain_grad,
        ln1_bias_grad,
        ln2_gain_grad,
        ln2_bias_grad,
        up_bias_grad,
    ) = lax.psum(
        (
            patch_grad_part,
            head_weight_grad,
            head_bias_grad,
            jnp.stack(grads_g1),
            jnp.stack(grads_b1),
            jnp.stack(grads_g2),
            jnp.stack(grads_b2),
            jnp.stack(grads_ub),
        ),
        ("dp", "seq"),
    )
    qkv_stack = jnp.stack(grads_qkv)
    out_stack = jnp.stack(grads_out)
    up_stack = jnp.stack(grads_up)
    down_stack = jnp.stack(grads_down)
    flat_parts = (
        lax.psum_scatter(eight_rows(qkv_stack), ("dp", "seq"), scatter_dimension=1, tiled=True),
        lax.psum_scatter(eight_rows(out_stack), ("dp", "seq"), scatter_dimension=1, tiled=True),
        lax.psum_scatter(eight_rows(up_stack), ("dp", "seq"), scatter_dimension=1, tiled=True),
        lax.psum_scatter(eight_rows(down_stack), ("dp", "seq"), scatter_dimension=1, tiled=True),
    )
    flat_qkv, flat_out, flat_up, flat_down = (
        lax.all_gather(
            flat_parts[0].astype(jnp.bfloat16), ("dp", "seq"), axis=1, tiled=True
        ).astype(jnp.float32),
        lax.all_gather(
            flat_parts[1].astype(jnp.bfloat16), ("dp", "seq"), axis=1, tiled=True
        ).astype(jnp.float32),
        lax.all_gather(
            flat_parts[2].astype(jnp.bfloat16), ("dp", "seq"), axis=1, tiled=True
        ).astype(jnp.float32),
        lax.all_gather(
            flat_parts[3].astype(jnp.bfloat16), ("dp", "seq"), axis=1, tiled=True
        ).astype(jnp.float32),
    )
    qkv_stack = flat_qkv.reshape(qkv_stack.shape)
    out_stack = flat_out.reshape(out_stack.shape)
    up_stack = flat_up.reshape(up_stack.shape)
    down_stack = flat_down.reshape(down_stack.shape)
    return (
        new_latents,
        logdet,
        latents_grad,
        patch_weight_grad,
        pos_grad,
        class_grad,
        ln1_gain_grad,
        ln1_bias_grad,
        qkv_stack,
        out_stack,
        ln2_gain_grad,
        ln2_bias_grad,
        up_stack,
        up_bias_grad,
        down_stack,
        head_weight_grad,
        head_bias_grad,
    )


def solution(mesh):
    in_specs = (
        P("dp", "seq", None),
        P("dp", "seq"),
        P(),
        P("dp"),
        P(),
        P("seq", None),
        P(),
        P(),
        P(),
        P(),
        P(),
        P(),
        P(),
        P(),
        P(),
        P(),
        P(),
        P(),
        P("dp", "seq", None),
        P("dp"),
    )
    out_specs = (
        P("dp", "seq", None),
        P("dp"),
        P("dp", "seq", None),
        P(),
        P("seq", None),
        P("dp", None),
        P(),
        P(),
        P(),
        P(),
        P(),
        P(),
        P(),
        P(),
        P(),
        P(),
        P(),
    )
    body = fast_local if mesh.shape["dp"] == 16 and mesh.shape["seq"] == 2 else local
    return jax.shard_map(body, mesh=mesh, in_specs=in_specs, out_specs=out_specs, check_vma=False)
```

```python
import jax
import jax.numpy as jnp
from jax import lax
from jax.experimental import pallas as pl
from jax.experimental.pallas import tpu as pltpu
from jax.sharding import PartitionSpec as P

HEAD_DIM = 64


precise = lax.Precision.HIGHEST
norm_eps = 1e-05


def shifted_2(shard, axis, by):
    size = lax.axis_size(axis)
    pairs = [(i, i + by) for i in range(size) if 0 <= i + by < size]
    return lax.ppermute(shard, axis, pairs)


def layer_norm(values, norm_gain, norm_bias):
    center = values - jnp.mean(values, -1, keepdims=True)
    spread = jnp.mean(center * center, -1, keepdims=True)
    return center * lax.rsqrt(spread + norm_eps) * norm_gain + norm_bias


def matmul(left_side, weight_mat):
    return jnp.dot(left_side, weight_mat, preferred_element_type=jnp.float32)


def outer_sum(left_side, grad_side):
    left_flat = left_side.reshape(-1, left_side.shape[-1])
    grad_flat = grad_side.reshape(-1, grad_side.shape[-1])
    return lax.dot_general(
        left_flat, grad_flat, (((0,), (0,)), ((), ())), preferred_element_type=jnp.float32
    )


def transposed(grad_side, weight_mat):
    return lax.dot_general(
        grad_side,
        weight_mat,
        (((grad_side.ndim - 1,), (1,)), ((), ())),
        preferred_element_type=jnp.float32,
    )


def eight_rows(matrix):
    return matrix.reshape(8, -1)


def attention_mask(key_valid, patch_rows, seq_place):
    query_pos = seq_place * patch_rows + lax.iota(jnp.int32, patch_rows)
    key_pos = (seq_place - 1) * patch_rows + lax.iota(jnp.int32, 2 * patch_rows)
    earlier = (key_pos[None, :] < query_pos[:, None])[None] & (key_valid[:, None, :] > 0)
    return earlier | (key_pos[None, :] == query_pos[:, None])[None]


def masked_scores(query, keys, allowed):
    logits = jnp.einsum(
        "bqhd,bkhd->bhqk", query, keys, preferred_element_type=jnp.float32
    ) * HEAD_DIM ** (-0.5)
    return jnp.where(allowed[:, None], logits, -1e30)


MESH = pl.DeviceIdType.MESH
UNITS = 24
LAST = 25
TURNS = 8
STEPS = 38
DRAIN = 14
SLAB = 128
LABELS = 448
TABLE_ROWS = ((0, 384), (384, 64))
COLS = 384
STAGES = 3
CHUNK = 32
GELU_A = (2.0 / 3.141592653589793) ** 0.5
GELU_B = 0.044715
f32 = jnp.float32
bf16 = jnp.bfloat16


def flow_kernel(
    labels_sm, perm_sm, cot_logdet_sm,
    latents_ref, valid_ref, patch_ref, pos_table_ref, g1_ref, b1_ref, g2_ref, b2_ref,
    up_bias_ref, head_w_ref, head_b_ref, cot_ref,
    class_hbm, qkv_any, out_any, up_any, down_any,
    sums,
    stage, part, core_in, small_in, ab_in, c_in, shared, send_sem, recv_sem, stage_sem, back_sem,
    qkv_w, out_w, up_w, down_w, load_sem,
    lat_pad, cot_pad, patch_pad, head_pad, hidden, mid, xhat1, xhat2, scale1, scale2,
    keys, values, query, attended, bias, prior_mask, mask_row, probs, slope, d_hidden, d_second, d_att, d_keys, d_values,
    d_prior, d_back, row_out, row_in, peek_out, peek_in, factor,
    lines, line_sum, line_in, line_send, line_recv,
    lt_ref, r_ref, pos_ref, small_ref, low_top, exch_send, exch_recv,
):
    dp = lax.axis_index("dp")
    core = lax.axis_index("seq")
    x, y, z = dp % 2, (dp // 2) % 2, dp // 4
    side = z // 2
    inner = ((z + 1) // 2) % 2 == 1
    outer = ((z + 1) // 2) % 2 == 0
    to_core = (dp, 1 - core)
    to_x = (dp + 1 - 2 * x, core)
    to_y = (dp + 2 - 4 * y, core)
    to_mate = (dp + 4 - 8 * (z % 2), core)
    to_inner = ((dp + 12 - 8 * z + 16) % 16, core)

    def rows_at(start, count):
        return pl.ds(pl.multiple_of(start, 16), count)

    sources = [class_hbm.at[r : r + n, h * COLS : (h + 1) * COLS] for h in range(2) for r, n in TABLE_ROWS]
    targets = [part.at[3 * h + i, 0:n] for h in range(2) for i, (r, n) in enumerate(TABLE_ROWS)]
    sources += [qkv_any.at[0], out_any.at[0]]
    targets += [qkv_w, out_w]

    def load(i):
        return pltpu.make_async_copy(sources[i], targets[i], load_sem.at[i])

    def load_feed(j):
        cols = rows = pl.ds(pl.multiple_of(j * 768, 128), 768)
        return (
            pltpu.make_async_copy(up_any.at[0, :, cols], up_w.at[:, cols], load_sem.at[6 + 2 * j]),
            pltpu.make_async_copy(down_any.at[0, rows], down_w.at[rows], load_sem.at[7 + 2 * j]),
        )

    for i in range(6):
        load(i).start()
    for j in range(4):
        for one in load_feed(j):
            one.start()

    barrier = pltpu.get_barrier_semaphore()
    for target in (to_core, to_x, to_y, to_mate):
        pl.semaphore_signal(barrier, inc=1, device_id=target, device_id_type=MESH)

    @pl.when(inner)
    def _():
        pl.semaphore_signal(barrier, inc=1, device_id=to_inner, device_id_type=MESH)

    def meet():
        @pl.when(inner)
        def _():
            pl.semaphore_wait(barrier, 5)

        @pl.when(outer)
        def _():
            pl.semaphore_wait(barrier, 4)

    def copy(u, k, src, dst, target):
        return pltpu.make_async_remote_copy(
            src_ref=src, dst_ref=dst, send_sem=send_sem.at[u], recv_sem=recv_sem.at[k, u % TURNS],
            device_id=target, device_id_type=MESH,
        )

    def arrived(u, k, dst):
        copy(u, k, dst, dst, to_core).wait_recv()

    def added(dst, left, right):
        dst[...] = (left[...].astype(f32) + right[...].astype(f32)).astype(bf16)

    first = (x, y)
    second = (y, x)
    to_first = (to_x, to_y)
    to_second = (to_y, to_x)

    def out_rows(u, t, start, count):
        return sums.at[u, core, rows_at(t * SLAB + start, count)]

    def part_rows(u, t, start, count):
        return part.at[u, rows_at(t * SLAB + start, count)]

    def left_index(u):
        return jnp.minimum(u // 2, 4) + jnp.minimum(jnp.maximum(u // 2 - 7, 0), 2)

    def right_index(u):
        return jnp.maximum(u // 2 - 3, 0)

    def product(u, t, half):
        rows = pl.ds(pl.multiple_of((u % 2) * 384 + t * SLAB, 128), SLAB)
        return jnp.dot(lt_ref[left_index(u), rows], r_ref[right_index(u), half], preferred_element_type=f32)

    def core_first(u):
        return pltpu.make_async_remote_copy(
            src_ref=stage.at[u % STAGES], dst_ref=core_in.at[u % TURNS], send_sem=stage_sem.at[u % STAGES],
            recv_sem=recv_sem.at[0, u % TURNS], device_id=to_core, device_id_type=MESH,
        )

    def small_first():
        return pltpu.make_async_remote_copy(
            src_ref=small_ref.at[1 - core], dst_ref=small_in, send_sem=stage_sem.at[STAGES],
            recv_sem=recv_sem.at[0, LAST % TURNS], device_id=to_core, device_id_type=MESH,
        )

    def line_copy(k, src, dst, target):
        return pltpu.make_async_remote_copy(
            src_ref=src, dst_ref=dst, send_sem=line_send.at[k], recv_sem=line_recv.at[k],
            device_id=target, device_id_type=MESH,
        )

    line_steps = (
        (lines, line_in.at[0], to_core),
        (line_sum.at[0], line_in.at[1], to_x),
        (line_sum.at[1], line_in.at[2], to_y),
        (line_sum.at[2], line_in.at[3], to_mate),
        (line_sum.at[3], line_in.at[4], to_inner),
        (line_sum.at[4], line_sum.at[4], to_mate),
    )

    def line_go(k):
        return line_copy(k, *line_steps[k])

    def line_add(k):
        line_go(k).wait_recv()
        line_sum[k] = line_steps[k][0][...] + line_in[k]

    def keep_lines():
        v = line_sum[4]
        for i in range(3):
            term = v.astype(bf16)
            v = v - term.astype(f32)
            for h in range(2):
                sums[LAST, h, 256 + i * 16 : 272 + i * 16] = term[:, h * COLS : (h + 1) * COLS]

    def produce(u):
        @pl.when(jnp.logical_and(u >= STAGES, u < UNITS))
        def _():
            core_first(u - STAGES).wait_send()

        @pl.when(u < UNITS)
        def _():
            for t in range(3):
                stage[u % STAGES, t * SLAB : (t + 1) * SLAB] = product(u, t, 1 - core).astype(bf16)
            core_first(u).start()

        @pl.when(u == LAST)
        def _():
            small_first().start()
            line_go(0).start()

    def begin(u):
        @pl.when(u < UNITS)
        def _():
            arrived(u, 0, core_in.at[u % TURNS])
            for t in range(3):
                rows = slice(t * SLAB, (t + 1) * SLAB)
                part[u, rows] = (product(u, t, core) + core_in[u % TURNS, rows].astype(f32)).astype(bf16)
                if t < 2:
                    ab_first(u, t).start()
            pl.when(outer)(lambda: c_z1(u).start())

        @pl.when(u == UNITS)
        def _():
            part[UNITS, 0:256] = pos_ref[...]
            for t in range(2):
                ab_first(u, t).start()

        @pl.when(u == LAST)
        def _():
            small_first().wait_recv()
            part[LAST, 0:256] = (small_ref[core].astype(f32) + small_in[...].astype(f32)).astype(bf16)
            for t in range(2):
                ab_first(u, t).start()
            line_add(0)
            line_go(1).start()

    def ab_base(t):
        return first[t] * 64 + second[t] * 32

    def ab_first(u, t):
        return copy(u, 1, part_rows(u, t, (1 - first[t]) * 64, 64), ab_in.at[u % TURNS, t, 0:64], to_first[t])

    def ab_second(u, t):
        row = first[t] * 64 + (1 - second[t]) * 32
        return copy(u, 2, part_rows(u, t, row, 32), ab_in.at[u % TURNS, t, 64:96], to_second[t])

    def ab_z1(u, t):
        return copy(u, 3, part_rows(u, t, ab_base(t), 32), ab_in.at[u % TURNS, t, 96:128], to_mate)

    def ab_z2(u, t):
        return copy(u, 4, part_rows(u, t, ab_base(t), 32), ab_in.at[u % TURNS, t, 128:160], to_inner)

    def ab_z3(u, t):
        block = out_rows(u, t, ab_base(t), 32)
        return copy(u, 3, block, block, to_mate)

    def ab_back2(u, t):
        block = out_rows(u, t, ab_base(t), 32)
        return copy(u, 5, block, block, to_second[t])

    def ab_back1(u, t):
        block = out_rows(u, t, first[t] * 64, 64)
        return copy(u, 6, block, block, to_first[t])

    def ab1(u):
        arrived(u, 1, ab_in.at[u % TURNS, :, 0:64])
        for t in range(2):
            kept = part_rows(u, t, first[t] * 64, 64)
            added(kept, kept, ab_in.at[u % TURNS, t, 0:64])
            ab_second(u, t).start()

        @pl.when(u == LAST)
        def _():
            line_add(1)
            line_go(2).start()

    def ab2(u):
        arrived(u, 2, ab_in.at[u % TURNS, :, 64:96])
        for t in range(2):
            kept = part_rows(u, t, ab_base(t), 32)
            added(kept, kept, ab_in.at[u % TURNS, t, 64:96])
            pl.when(outer)(lambda: ab_z1(u, t).start())

        @pl.when(u == LAST)
        def _():
            line_add(2)
            pl.when(outer)(line_go(3).start)

    def ab3_inner(u):
        arrived(u, 3, ab_in.at[u % TURNS, :, 96:128])
        for t in range(2):
            kept = part_rows(u, t, ab_base(t), 32)
            added(kept, kept, ab_in.at[u % TURNS, t, 96:128])
            ab_z2(u, t).start()

        @pl.when(u == LAST)
        def _():
            line_add(3)
            line_go(4).start()

    def ab4_inner(u):
        arrived(u, 4, ab_in.at[u % TURNS, :, 128:160])
        for t in range(2):
            added(out_rows(u, t, ab_base(t), 32), part_rows(u, t, ab_base(t), 32), ab_in.at[u % TURNS, t, 128:160])
            ab_z3(u, t).start()
            ab_back2(u, t).start()

        @pl.when(u == LAST)
        def _():
            line_add(4)
            line_go(5).start()
            keep_lines()

    def ab5_outer(u):
        arrived(u, 3, sums.at[u, core, 0:64])
        for t in range(2):
            ab_back2(u, t).start()

        @pl.when(u == LAST)
        def _():
            line_go(5).wait_recv()
            keep_lines()

    def ab6(u):
        arrived(u, 5, sums.at[u, core, 0:64])
        for t in range(2):
            ab_back1(u, t).start()

    def spread(u, row, count):
        block = sums.at[u, core, row : row + count]
        to_other(u, block).start()

    def to_other(u, block):
        return pltpu.make_async_remote_copy(
            src_ref=block, dst_ref=block, send_sem=send_sem.at[u], recv_sem=back_sem.at[u],
            device_id=to_core, device_id_type=MESH,
        )

    def ab7(u):
        arrived(u, 6, sums.at[u, core, 0:128])
        pl.when(u != UNITS)(lambda: spread(u, 0, 2 * SLAB))

    far = 32 * (1 - side)
    own_end = 96 * side
    shard = z * 32

    def c_z1(u):
        return copy(u, 7, part_rows(u, 2, far, 96), c_in.at[u % TURNS, 0:96], to_mate)

    def c_z2(u):
        return copy(u, 8, part_rows(u, 2, (1 - side) * 64, 64), c_in.at[u % TURNS, 96:160], to_inner)

    def c_z3(u):
        return copy(u, 7, part_rows(u, 2, own_end, 32), c_in.at[u % TURNS, 160:192], to_mate)

    def c_x(u):
        return copy(u, 9, part_rows(u, 2, shard, 32), c_in.at[u % TURNS, 192:224], to_x)

    def c_y(u):
        return copy(u, 10, shared.at[u], c_in.at[u % TURNS, 224:256], to_y)

    def c_z4(u):
        block = out_rows(u, 2, own_end, 32)
        return copy(u, 12, block, block, to_mate)

    def c_z5(u):
        block = out_rows(u, 2, side * 64, 64)
        return copy(u, 13, block, block, to_inner)

    def c_z6(u):
        block = out_rows(u, 2, far, 96)
        return copy(u, 12, block, block, to_mate)

    def c1_inner(u):
        arrived(u, 7, c_in.at[u % TURNS, 0:96])
        kept = part_rows(u, 2, far, 96)
        added(kept, kept, c_in.at[u % TURNS, 0:96])
        c_z2(u).start()

    def c2_inner(u):
        arrived(u, 8, c_in.at[u % TURNS, 96:160])
        kept = part_rows(u, 2, side * 64, 64)
        added(kept, kept, c_in.at[u % TURNS, 96:160])
        c_z3(u).start()
        c_x(u).start()

    def c3_outer(u):
        arrived(u, 7, c_in.at[u % TURNS, 160:192])
        kept = part_rows(u, 2, shard, 32)
        added(kept, kept, c_in.at[u % TURNS, 160:192])
        c_x(u).start()

    def c4(u):
        arrived(u, 9, c_in.at[u % TURNS, 192:224])
        kept = part_rows(u, 2, shard, 32)
        part_y = shared.at[u]
        added(part_y, kept, c_in.at[u % TURNS, 192:224])
        c_y(u).start()

    def c5(u):
        arrived(u, 10, c_in.at[u % TURNS, 224:256])
        added(out_rows(u, 2, shard, 32), shared.at[u], c_in.at[u % TURNS, 224:256])
        pl.when(outer)(lambda: c_z4(u).start())

    def c8_inner(u):
        arrived(u, 12, out_rows(u, 2, own_end, 32))
        c_z5(u).start()

    def c9_inner(u):
        arrived(u, 13, out_rows(u, 2, (1 - side) * 64, 64))
        c_z6(u).start()
        spread(u, 2 * SLAB, SLAB)

    def c10_outer(u):
        arrived(u, 12, out_rows(u, 2, far, 96))
        spread(u, 2 * SLAB, SLAB)

    def sent(u, units, rows):
        ref = part.at[0:units, 0:rows]
        copy(u, 0, ref, ref, to_core).wait_send()

    def drain(u):
        pl.when(outer)(lambda: sent(u, 4, 256))
        pl.when(inner)(lambda: sent(u, 4, 304))
        to_other(u, sums.at[u, 1 - core]).wait_recv()

    mm_nt = (((1,), (1,)), ((), ()))
    mm_tn = (((0,), (0,)), ((), ()))

    def nt(left, right):
        return lax.dot_general(left, right, mm_nt, preferred_element_type=f32)

    def tn(left, right):
        return lax.dot_general(left, right, mm_tn, preferred_element_type=f32)

    def nn(left, right):
        return jnp.dot(left, right, preferred_element_type=f32)

    def exchange(k, src, dst):
        return pltpu.make_async_remote_copy(
            src_ref=src, dst_ref=dst, send_sem=exch_send.at[k], recv_sem=exch_recv.at[k],
            device_id=to_core, device_id_type=MESH,
        )

    chunks = [slice(r, r + CHUNK) for r in range(0, 128, CHUNK)]
    lane = lax.broadcasted_iota(jnp.int32, (128, 128), 1)
    row = lax.broadcasted_iota(jnp.int32, (128, 128), 0)
    eye = row == lane
    low_half = lane < 64
    valid_row = valid_ref[...].astype(f32)
    valid_col = jnp.sum(jnp.where(eye, valid_row, 0.0), axis=1, keepdims=True)
    mask_row[...] = jnp.broadcast_to(valid_row, (8, 128))
    lat_pad[...] = jnp.zeros((128, 128), f32)
    lat_pad[0:48] = latents_ref[0]
    lat_pad[...] = lat_pad[...].T
    cot_pad[...] = jnp.zeros((128, 128), f32)
    cot_pad[0:48] = cot_ref[0]
    cot_pad[...] = cot_pad[...].T
    patch_pad[...] = jnp.zeros((128, 768), bf16)
    patch_pad[0:48] = patch_ref[...]
    head_pad[...] = jnp.zeros((128, 768), bf16)
    head_pad[0:96] = head_w_ref[...]
    head_bias = jnp.concatenate((head_b_ref[...].astype(f32), jnp.zeros((1, 32), f32)), 1)

    @pl.when(core == 0)
    def _():
        keys[0:128] = jnp.zeros((128, 768), bf16)
        values[0:128] = jnp.zeros((128, 768), bf16)
        prior_mask[...] = jnp.zeros((8, 128), f32)
        row_in[...] = jnp.zeros((8, 128), f32)

    @pl.when(core == 1)
    def _():
        peek_in[...] = jnp.zeros((8, 128), f32)
        d_back[...] = jnp.zeros((2, 128, 768), bf16)

    line8 = lax.broadcasted_iota(jnp.int32, (8, 128), 0)
    peek_out[...] = jnp.where(line8 == 0, lat_pad[0:1], jnp.where(line8 == 1, cot_pad[0:1], valid_row[:, 0:1]))

    def normalize(src, hat, scale, gain, shift, put):
        for r in chunks:
            v = src[r]
            center = v - jnp.mean(v, -1, keepdims=True)
            inv = lax.rsqrt(jnp.mean(center * center, -1, keepdims=True) + norm_eps)
            scaled = center * inv
            hat[r] = scaled
            scale[r] = inv
            put(r, scaled * gain + shift)

    label = labels_sm[perm_sm[0]]
    hot = jnp.where(lax.broadcasted_iota(jnp.int32, (16, LABELS), 1) == label, 1.0, 0.0).astype(bf16)
    for i in range(4):
        load(i).wait()
    class_row = jnp.concatenate(
        [
            sum(nn(hot[:, r : r + n], part[3 * h + i, 0:n]) for i, (r, n) in enumerate(TABLE_ROWS))
            for h in range(2)
        ],
        1,
    )[0:1]
    hidden[...] = (
        nn(lat_pad[...].astype(bf16), patch_pad[...]) + pos_table_ref[...].astype(f32) + class_row
    )

    def put_low(r, v):
        low_top[r] = v.astype(bf16)

    normalize(hidden, xhat1, scale1, g1_ref[...].astype(f32), b1_ref[...].astype(f32), put_low)
    load(4).wait()
    normed = low_top[...]
    keys[128:256] = nn(normed, qkv_w[:, 768:1536]).astype(bf16)
    meet()

    @pl.when(core == 1)
    def _():
        exchange(4, peek_out, peek_in).start()

    @pl.when(core == 0)
    def _():
        exchange(2, mask_row, prior_mask).start()
        exchange(0, keys.at[128:256], keys.at[0:128]).start()

    values[128:256] = nn(normed, qkv_w[:, 1536:2304]).astype(bf16)

    @pl.when(core == 0)
    def _():
        exchange(1, values.at[128:256], values.at[0:128]).start()

    query[...] = nn(normed, qkv_w[:, 0:768]).astype(bf16)
    lt_ref[6] = normed.astype(f32).T.astype(bf16)

    @pl.when(core == 1)
    def _():
        exchange(2, mask_row, prior_mask).wait_recv()
        exchange(0, keys.at[128:256], keys.at[0:128]).wait_recv()
        exchange(1, values.at[128:256], values.at[0:128]).wait_recv()

    bias[:, 0:128] = jnp.where(jnp.broadcast_to(prior_mask[0:1], (128, 128)) > 0.5, 0.0, -1e30)
    bias[:, 128:256] = jnp.where(((lane < row) & (valid_row > 0.5)) | eye, 0.0, -1e30)

    def columns128(p):
        return pl.ds(pl.multiple_of(p * 128, 128), 128)

    def attend(p):
        cols = columns128(p)
        q_pair = query[:, cols]
        k_pair = keys[:, cols]
        v_pair = values[:, cols]
        outs = []
        for i in range(2):
            q_one = jnp.where(low_half if i == 0 else lane >= 64, q_pair, jnp.zeros_like(q_pair))
            scores = nt(q_one, k_pair) * 0.125 + bias[...]
            top = jnp.max(scores, -1, keepdims=True)
            powers = jnp.exp(scores - top)
            soft = powers * (1.0 / jnp.sum(powers, -1, keepdims=True))
            probs[2 * p + i] = soft
            outs.append(nn(soft.astype(bf16), v_pair))
        attended[:, cols] = jnp.where(low_half, outs[0], outs[1]).astype(bf16)

    for p in range(6):
        attend(p)
    load(5).wait()
    mid[...] = hidden[...] + nn(attended[...], out_w[...])
    lt_ref[5] = attended[...].astype(f32).T.astype(bf16)
    normalize(mid, xhat2, scale2, g2_ref[...].astype(f32), b2_ref[...].astype(f32), put_low)
    lt_ref[4] = low_top[...].astype(f32).T.astype(bf16)
    d_hidden[...] = mid[...]

    def rows768(j):
        return pl.ds(pl.multiple_of(j * 768, 128), 768)

    def feed(j, carried):
        for one in load_feed(j):
            one.wait()
        d_second[...] = nn(low_top[...], up_w[:, rows768(j)])
        shift = up_bias_ref[:, rows768(j)].astype(f32)
        for r in chunks:
            pre = d_second[r] + shift
            square = pre * pre
            bend = jnp.tanh(pre * (GELU_A + (GELU_A * GELU_B) * square))
            left = 0.5 * (1.0 + bend)
            slope[j, r] = left + 0.5 * pre * (1.0 - bend * bend) * (GELU_A + (3.0 * GELU_A * GELU_B) * square)
            d_second[r] = pre * left
        act = d_second[...]
        lt_ref[j] = act.T.astype(bf16)
        d_hidden[...] += nn(act.astype(bf16), down_w[rows768(j)])
        return carried

    lax.fori_loop(0, 4, feed, 0)
    low_top[...] = d_hidden[...].astype(bf16)
    row_out[...] = nt(low_top[...], head_pad[...]) + head_bias

    @pl.when(core == 0)
    def _():
        exchange(3, row_out.at[120:128], row_in).start()

    def coupling(shifted, latent, cot):
        inside = lax.broadcasted_iota(jnp.int32, shifted.shape, 1) < 48
        alpha = jnp.where(inside, shifted, 0.0)
        scale = jnp.exp(-alpha)
        moved = (latent - jnp.where(inside, pltpu.roll(shifted, 80, 1), 0.0)) * scale
        d_alpha = -cot * moved - cot_logdet_sm[0]
        d_mean = pltpu.roll(jnp.where(inside, -cot * scale, 0.0), 48, 1)
        return alpha, scale, moved, jnp.where(inside, d_alpha, d_mean)

    rolled = pltpu.roll(row_out[...], 1, 0)
    d_shifted = coupling(jnp.where(row == 0, 0.0, rolled) * valid_col, lat_pad[...], cot_pad[...])[3] * valid_col

    @pl.when(core == 0)
    def _():
        exchange(4, peek_out, peek_in).wait_recv()

    def peeked(i):
        return jnp.broadcast_to(peek_in[i : i + 1], (8, 128))

    after_last = jnp.broadcast_to(row_out[127:128], (8, 128)) * peeked(2)
    d_next = coupling(after_last, peeked(0), peeked(1))[3] * peeked(2)
    d_head = jnp.where(row == 127, d_next[0:1], pltpu.roll(d_shifted, 127, 0)).astype(bf16)

    def outputs():
        @pl.when(core == 1)
        def _():
            exchange(3, row_out.at[120:128], row_in).wait_recv()

        before = jnp.where(row == 0, jnp.broadcast_to(row_in[7:8], (128, 128)), pltpu.roll(row_out[...], 1, 0))
        alpha, scale, moved = coupling(before * valid_col, lat_pad[...], cot_pad[...])[0:3]
        factor[...] = scale
        store_exact(0, moved.T[0:48])
        logdet = -jnp.sum(jnp.sum(alpha, 1, keepdims=True), 0, keepdims=True)
        lines[8:9, 128:256] = jnp.where(lax.broadcasted_iota(jnp.int32, (1, 128), 1) == dp, logdet, 0.0)

    def exact_terms(v):
        terms = []
        for i in range(3):
            terms.append(v.astype(bf16))
            v = v - terms[i].astype(f32)
        return terms

    def store_exact(h, v):
        for i, term in enumerate(exact_terms(v)):
            sums[UNITS, h, 256:304, i * 128 : (i + 1) * 128] = term

    head_grad = tn(d_head, low_top[...])
    head_bias_grad = jnp.sum(d_head.astype(f32), 0, keepdims=True)
    d_hidden[...] = nn(d_head, head_pad[...])
    low_top[...] = d_hidden[...].astype(bf16)
    for h in range(2):
        r_ref[0, h] = low_top[:, h * COLS : (h + 1) * COLS]

    def put(first_row, value):
        h, r = first_row // 128, first_row % 128
        for t in range(2):
            small_ref[h, t * 128 + r : t * 128 + r + value.shape[0]] = value[:, t * COLS : (t + 1) * COLS].astype(bf16)

    put(0, head_grad[0:96])

    lines[...] = jnp.zeros((16, 768), f32)
    lines[8:9, 0:128] = head_bias_grad

    d_second[...] = jnp.zeros((128, 768), f32)

    def feed_back(j):
        d_keys[...] = nt(low_top[...], down_w[rows768(j)])
        total = jnp.zeros((1, 768), f32)
        for r in chunks:
            d_pre = (slope[j, r] * d_keys[r]).astype(bf16)
            d_att[r] = d_pre
            total += jnp.sum(d_pre.astype(f32), 0, keepdims=True)
            for h in range(2):
                r_ref[1 + j, h, r] = d_pre[:, h * COLS : (h + 1) * COLS]
        lines[pl.ds(4 + j, 1)] = total
        d_second[...] += nt(d_att[...], up_w[:, rows768(j)])

    def norm_back(grad, hat, scale, gain, base, out, line):
        gain_total = jnp.zeros((1, 768), f32)
        shift_total = jnp.zeros((1, 768), f32)
        for r in chunks:
            d = grad[r]
            scaled = hat[r]
            e = d * gain
            v = e - jnp.mean(e, -1, keepdims=True) - scaled * jnp.mean(e * scaled, -1, keepdims=True)
            out[r] = base[r] + scale[r] * v
            gain_total += jnp.sum(d * scaled, 0, keepdims=True)
            shift_total += jnp.sum(d, 0, keepdims=True)
        lines[line : line + 1] = gain_total
        lines[line + 1 : line + 2] = shift_total

    def feed_norm_back():
        norm_back(d_second, xhat2, scale2, g2_ref[...].astype(f32), d_hidden, mid, 2)
        low_top[...] = mid[...].astype(bf16)
        for h in range(2):
            r_ref[5, h] = low_top[:, h * COLS : (h + 1) * COLS]
        d_att[...] = nt(low_top[...], out_w[...]).astype(bf16)

    def attend_back(p):
        cols = columns128(p)
        q_pair = query[:, cols]
        k_pair = keys[:, cols]
        v_pair = values[:, cols]
        a_pair = d_att[:, cols]
        dq, dk, dv = [], [], []
        for i in range(2):
            own = low_half if i == 0 else lane >= 64
            a_one = jnp.where(own, a_pair, jnp.zeros_like(a_pair))
            q_one = jnp.where(own, q_pair, jnp.zeros_like(q_pair))
            soft = probs[2 * p + i]
            d_soft = nt(a_one, v_pair)
            weighted = d_soft * soft
            d_score = weighted - soft * jnp.sum(weighted, -1, keepdims=True)
            d_low = d_score.astype(bf16)
            dq.append(nn(d_low, k_pair))
            dk.append(tn(d_low, q_one))
            dv.append(tn(soft.astype(bf16), a_one))
        h, local = p // 3, pl.ds(pl.multiple_of((p % 3) * 128, 128), 128)
        r_ref[6, h, :, local] = (jnp.where(low_half, dq[0], dq[1]) * 0.125).astype(bf16)
        dk_pair = (dk[0] + dk[1]) * 0.125
        dv_pair = dv[0] + dv[1]
        d_prior[0, :, cols] = dk_pair[0:128].astype(bf16)
        d_prior[1, :, cols] = dv_pair[0:128].astype(bf16)
        d_keys[:, cols] = dk_pair[128:256]
        d_values[:, cols] = dv_pair[128:256]

    def send_prior():
        @pl.when(core == 1)
        def _():
            exchange(5, d_prior, d_back).start()

    def packed_back():
        @pl.when(core == 0)
        def _():
            exchange(5, d_prior, d_back).wait_recv()

        for h in range(2):
            cols = slice(h * COLS, (h + 1) * COLS)
            r_ref[7, h] = (d_keys[:, cols] + d_back[0, :, cols].astype(f32)).astype(bf16)
            r_ref[8, h] = (d_values[:, cols] + d_back[1, :, cols].astype(f32)).astype(bf16)
        d_second[...] = sum(
            nt(r_ref[6 + j, h], qkv_w[:, j * 768 + h * COLS : j * 768 + (h + 1) * COLS])
            for j in range(3)
            for h in range(2)
        )

    def embed_back():
        norm_back(d_second, xhat1, scale1, g1_ref[...].astype(f32), mid, d_hidden, 0)
        low_top[...] = d_hidden[...].astype(bf16)
        for t in range(2):
            pos_ref[t * 128 : (t + 1) * 128] = low_top[:, t * COLS : (t + 1) * COLS]
        patch_grad = tn(lat_pad[...].astype(bf16), low_top[...])
        store_exact(1, (cot_pad[...] * factor[...] + nt(low_top[...], patch_pad[...])).T[0:48])
        class_grad = jnp.sum(d_hidden[...], 0, keepdims=True)
        put(96, patch_grad[0:32])
        put(128, patch_grad[32:48])
        line = lax.broadcasted_iota(jnp.int32, (16, 768), 0)
        put(144, jnp.where(line == dp, class_grad, 0.0))
        put(160, jnp.zeros((96, 768), f32))

    def piece(t):
        @pl.when(jnp.logical_and(t < 8, t % 2 == 0))
        def _():
            feed_back(t // 2)

        pl.when(t == 8)(feed_norm_back)

        @pl.when(jnp.logical_and(t >= 9, t < 15))
        def _():
            attend_back(t - 9)

        pl.when(t == 14)(send_prior)
        pl.when(t == 16)(packed_back)
        pl.when(t == 17)(outputs)
        pl.when(t == 18)(embed_back)

    everyone, inners, outers = None, inner, outer
    events = [
        (0, LAST + 1, everyone, produce),
        (8, LAST + 1, outers, ab5_outer),
        (11, LAST + 1, outers, ab7),
        (2, UNITS, inners, c1_inner),
        (1, LAST + 1, everyone, begin),
        (9, LAST + 1, inners, ab6),
        (4, LAST + 1, inners, ab3_inner),
        (0, LAST + 1, everyone, piece),
        (2, LAST + 1, everyone, ab1),
        (3, UNITS, inners, c2_inner),
        (5, LAST + 1, inners, ab4_inner),
        (8, UNITS, inners, c5),
        (5, UNITS, outers, c3_outer),
        (12, LAST + 1, inners, ab7),
        (8, UNITS, inners, c8_inner),
        (5, UNITS, inners, c4),
        (9, UNITS, inners, c9_inner),
        (9, LAST + 1, outers, ab6),
        (12, UNITS, outers, c10_outer),
        (3, LAST + 1, everyone, ab2),
        (6, UNITS, outers, c4),
        (7, UNITS, outers, c5),
        (DRAIN, UNITS, everyone, drain),
    ]

    def step(t, carried):
        for lag, count, who, event in events:
            u = t - lag
            now = jnp.logical_and(u >= 0, u < count)
            if who is not None:
                now = jnp.logical_and(now, who)
            pl.when(now)(lambda event=event, u=u: event(u))
        return carried

    lax.fori_loop(0, STEPS, step, 0)


    def drain_more(u, carried):
        drain(u)
        return carried

    lax.fori_loop(STEPS - DRAIN, UNITS, drain_more, 0)
    pl.when(outer)(lambda: sent(UNITS, 2, 224))
    pl.when(inner)(lambda: sent(UNITS, 2, 256))
    pl.when(outer)(lambda: sent(LAST, 2, 352))
    pl.when(inner)(lambda: sent(LAST, 2, 384))
    to_other(LAST, sums.at[LAST, 1 - core, 0 : 2 * SLAB]).wait_recv()
    for u in range(UNITS - STAGES, UNITS):
        core_first(u).wait_send()
    small_first().wait_send()
    for k in range(3):
        line_go(k).wait_send()
    pl.when(outer)(line_go(3).wait_send)

    @pl.when(inner)
    def _():
        line_go(4).wait_send()
        line_go(5).wait_send()

    @pl.when(core == 0)
    def _():
        exchange(2, mask_row, prior_mask).wait_send()
        exchange(0, keys.at[128:256], keys.at[0:128]).wait_send()
        exchange(1, values.at[128:256], values.at[0:128]).wait_send()
        exchange(3, row_out.at[120:128], row_in).wait_send()

    @pl.when(core == 1)
    def _():
        exchange(4, peek_out, peek_in).wait_send()
        exchange(5, d_prior, d_back).wait_send()


def flow(
    class_labels, group_perm, cot_logdet, latents, valid, patch_weight, pos_table, ln1_gain, ln1_bias,
    ln2_gain, ln2_bias, up_bias, head_weight, head_bias, cot_latents, class_table,
    qkv_weight, out_weight, up_weight, down_weight,
):
    smem = pl.BlockSpec(memory_space=pltpu.SMEM)
    vmem = pl.BlockSpec(memory_space=pltpu.VMEM)
    hbm = pl.BlockSpec(memory_space=pltpu.HBM)
    wide = (128, 768)
    return pl.pallas_call(
        flow_kernel,
        out_shape=pltpu.VMEM((LAST + 1, 2, 3 * SLAB, COLS), bf16),
        in_specs=[smem] * 3 + [vmem] * 12 + [hbm] * 5,
        out_specs=vmem,
        scratch_shapes=[
            pltpu.VMEM((STAGES, 3 * SLAB, COLS), bf16),
            pltpu.VMEM((LAST + 1, 3 * SLAB, COLS), bf16),
            pltpu.VMEM((TURNS, 3 * SLAB, COLS), bf16),
            pltpu.VMEM((256, COLS), bf16),
            pltpu.VMEM((TURNS, 2, 160, COLS), bf16),
            pltpu.VMEM((TURNS, 256, COLS), bf16),
            pltpu.VMEM((UNITS, 32, COLS), bf16),
            pltpu.SemaphoreType.DMA((LAST + 1,)),
            pltpu.SemaphoreType.DMA((14, TURNS)),
            pltpu.SemaphoreType.DMA((STAGES + 1,)),
            pltpu.SemaphoreType.DMA((LAST + 1,)),
            pltpu.VMEM((768, 2304), bf16),
            pltpu.VMEM((768, 768), bf16),
            pltpu.VMEM((768, 3072), bf16),
            pltpu.VMEM((3072, 768), bf16),
            pltpu.SemaphoreType.DMA((14,)),
            pltpu.VMEM((128, 128), f32),
            pltpu.VMEM((128, 128), f32),
            pltpu.VMEM(wide, bf16),
            pltpu.VMEM(wide, bf16),
            pltpu.VMEM(wide, f32),
            pltpu.VMEM(wide, f32),
            pltpu.VMEM(wide, f32),
            pltpu.VMEM(wide, f32),
            pltpu.VMEM((128, 1), f32),
            pltpu.VMEM((128, 1), f32),
            pltpu.VMEM((256, 768), bf16),
            pltpu.VMEM((256, 768), bf16),
            pltpu.VMEM(wide, bf16),
            pltpu.VMEM(wide, bf16),
            pltpu.VMEM((128, 256), f32),
            pltpu.VMEM((8, 128), f32),
            pltpu.VMEM((8, 128), f32),
            pltpu.VMEM((12, 128, 256), f32),
            pltpu.VMEM((4, 128, 768), f32),
            pltpu.VMEM(wide, f32),
            pltpu.VMEM(wide, f32),
            pltpu.VMEM(wide, bf16),
            pltpu.VMEM(wide, f32),
            pltpu.VMEM(wide, f32),
            pltpu.VMEM((2, 128, 768), bf16),
            pltpu.VMEM((2, 128, 768), bf16),
            pltpu.VMEM((128, 128), f32),
            pltpu.VMEM((8, 128), f32),
            pltpu.VMEM((8, 128), f32),
            pltpu.VMEM((8, 128), f32),
            pltpu.VMEM((128, 128), f32),
            pltpu.VMEM((16, 768), f32),
            pltpu.VMEM((5, 16, 768), f32),
            pltpu.VMEM((5, 16, 768), f32),
            pltpu.SemaphoreType.DMA((6,)),
            pltpu.SemaphoreType.DMA((6,)),
            pltpu.VMEM((7, 768, 128), bf16),
            pltpu.VMEM((9, 2, 128, COLS), bf16),
            pltpu.VMEM((256, COLS), bf16),
            pltpu.VMEM((2, 256, COLS), bf16),
            pltpu.VMEM(wide, bf16),
            pltpu.SemaphoreType.DMA((6,)),
            pltpu.SemaphoreType.DMA((6,)),
        ],
        compiler_params=pltpu.CompilerParams(
            collective_id=0, has_side_effects=True, vmem_limit_bytes=46 << 20
        ),
        name="flow",
    )(
        class_labels, group_perm, cot_logdet, latents, valid, patch_weight, pos_table, ln1_gain, ln1_bias,
        ln2_gain, ln2_bias, up_bias, head_weight, head_bias, cot_latents, class_table,
        qkv_weight, out_weight, up_weight, down_weight,
    )


def finish_kernel(
    labels_ref, sums,
    new_latents, logdet, latents_grad, patch, pos, classes, g1, b1, qkv, out, g2, b2, up, ub, down, head, hb,
    wide, write_sem, lat_wide, pos_wide, small_wide, class_wide, out_sem,
):
    dp = lax.axis_index("dp")
    core = lax.axis_index("seq")
    owned = classes.shape[0]
    outputs = [
        pltpu.make_async_copy(src, dst, out_sem.at[i])
        for i, (src, dst) in enumerate(
            (
                (lat_wide.at[0], new_latents.at[0]),
                (lat_wide.at[1], latents_grad.at[0]),
                (small_wide.at[0:96], head),
                (small_wide.at[96:144], patch),
                (pos_wide, pos),
                (class_wide, classes),
            )
        )
    ]
    def write(u):
        block, row = u // 2, (u % 2) * 384
        if block < 4:
            dst = down.at[0, block * 768 + row : block * 768 + row + 384]
        else:
            target, column = (up, block - 4) if block < 8 else (out, 0) if block == 8 else (qkv, block - 9)
            dst = target.at[0, row : row + 384, column * 768 : (column + 1) * 768]
        return pltpu.make_async_copy(wide.at[u], dst, write_sem.at[u])

    def little():
        for h in range(2):
            terms = [sums[UNITS, h, 256:304, i * 128 : (i + 1) * 128].astype(f32) for i in range(3)]
            lat_wide[h] = terms[0] + terms[1] + terms[2]
        outputs[0].start()
        outputs[1].start()
        for t in range(2):
            rows, cols = slice(t * 128, (t + 1) * 128), slice(t * COLS, (t + 1) * COLS)
            pos_wide[:, cols] = sums[UNITS, core, rows].astype(f32)
            for h in range(2):
                small_wide[h * 128 : (h + 1) * 128, cols] = sums[LAST, h, rows].astype(f32)
        for one in outputs[2:5]:
            one.start()
        halves = []
        for h in range(2):
            terms = [sums[LAST, h, 256 + i * 16 : 272 + i * 16].astype(f32) for i in range(3)]
            halves.append(terms[0] + terms[1] + terms[2])
        block = jnp.concatenate(halves, 1)
        for i, one in enumerate((g1, b1, g2, b2)):
            one[...] = block[i : i + 1]
        for i in range(4):
            ub[:, i * 768 : (i + 1) * 768] = block[4 + i : 5 + i]
        hb[...] = block[8:9, 0:96]
        count = labels_ref.shape[1]
        lane = lax.broadcasted_iota(jnp.int32, (1, 128), 1)
        logdet[...] = jnp.sum(jnp.where(lane == dp, block[8:9, 128:256], 0.0), 1, keepdims=True)
        by_lane = jnp.broadcast_to(labels_ref[...], (count, count)).astype(f32)
        first = lax.broadcasted_iota(jnp.int32, (count, count), 0)
        second = lax.broadcasted_iota(jnp.int32, (count, count), 1)
        by_row = jnp.sum(jnp.where(first == second, by_lane, 0.0), 1, keepdims=True)
        before = (by_lane < by_row) | ((by_lane == by_row) & (second < first))
        rank = jnp.sum(jnp.where(before, 1.0, 0.0), 1, keepdims=True)
        stored = jnp.sum(jnp.where(rank == second.astype(f32), by_row, 0.0), 0, keepdims=True)
        wanted = (dp * owned + lax.broadcasted_iota(jnp.int32, (owned, count), 0)).astype(f32)
        hot = jnp.where(stored == wanted, 1.0, 0.0).astype(bf16)
        class_wide[...] = jnp.dot(hot, small_wide[144:160].astype(bf16), preferred_element_type=f32)
        outputs[5].start()

    for u in range(UNITS):
        for h in range(2):
            wide[u, :, h * COLS : (h + 1) * COLS] = sums[u, h].astype(f32)
        write(u).start()
        if u == 1:
            little()
    for u in range(UNITS):
        write(u).wait()
    for one in outputs:
        one.wait()


def finish(class_labels, sums):
    count = class_labels.shape[1]
    owned = 1024 // count
    shapes = [
        (1, 48, 128), (1, 1), (1, 48, 128), (48, 768), (128, 768), (owned, 768), (1, 768), (1, 768),
        (1, 768, 2304), (1, 768, 768), (1, 768), (1, 768), (1, 768, 3072), (1, 3072), (1, 3072, 768),
        (96, 768), (1, 96),
    ]
    vmem = pl.BlockSpec(memory_space=pltpu.VMEM)
    hbm = pl.BlockSpec(memory_space=pl.ANY)
    return pl.pallas_call(
        finish_kernel,
        out_shape=[jax.ShapeDtypeStruct(shape, f32) for shape in shapes],
        in_specs=[vmem, vmem],
        out_specs=[vmem if i in (1, 6, 7, 10, 11, 13, 16) else hbm for i in range(17)],
        scratch_shapes=[
            pltpu.VMEM((UNITS, 384, 768), f32),
            pltpu.SemaphoreType.DMA((UNITS,)),
            pltpu.VMEM((2, 48, 128), f32),
            pltpu.VMEM((128, 768), f32),
            pltpu.VMEM((256, 768), f32),
            pltpu.VMEM((owned, 768), f32),
            pltpu.SemaphoreType.DMA((6,)),
        ],
        compiler_params=pltpu.CompilerParams(vmem_limit_bytes=34 << 20),
        name="finish",
    )(class_labels, sums)


def fast_local(
    latents, valid, class_labels, group_perm, patch_weight, pos_table, class_table, ln1_gain, ln1_bias,
    qkv_weight, out_weight, ln2_gain, ln2_bias, up_weight, up_bias, down_weight, head_weight, head_bias,
    cot_latents, cot_logdet,
):
    sums = flow(
        class_labels, group_perm, cot_logdet, latents.swapaxes(1, 2), valid, patch_weight, pos_table, ln1_gain,
        ln1_bias, ln2_gain, ln2_bias, up_bias, head_weight.T, head_bias[None], cot_latents.swapaxes(1, 2), class_table,
        qkv_weight, out_weight, up_weight, down_weight,
    )
    results = list(finish(class_labels[None], sums))
    results[1] = results[1].reshape(1)
    results[16] = results[16].reshape(96)
    results[0], results[2] = results[0].swapaxes(1, 2), results[2].swapaxes(1, 2)
    results[15] = results[15].T
    return tuple(results)


def forward(latents, valid, class_rows, seq_place, weights):
    (
        patch_weight,
        pos_table,
        qkv_weight,
        out_weight,
        ln1_gain,
        ln1_bias,
        ln2_gain,
        ln2_bias,
        up_weight,
        up_bias,
        down_weight,
        head_weight,
        head_bias,
    ) = weights
    images, patch_rows, channels = latents.shape
    model_width = qkv_weight.shape[1]
    head_count = model_width // HEAD_DIM
    latent_low = latents.astype(jnp.bfloat16)
    hidden = (
        matmul(latent_low, patch_weight)
        + pos_table.astype(jnp.float32)[None]
        + class_rows[:, None, :]
    )
    own_mask = valid.astype(jnp.bfloat16)
    normed = layer_norm(
        hidden, ln1_gain[0].astype(jnp.float32), ln1_bias[0].astype(jnp.float32)
    ).astype(jnp.bfloat16)
    packed = matmul(normed, qkv_weight[0]).astype(jnp.bfloat16)
    query = packed[..., :model_width].reshape(images, patch_rows, head_count, HEAD_DIM)
    keys_own = packed[..., model_width : 2 * model_width]
    values_own = packed[..., 2 * model_width :]
    prior_keys, prior_values, prior_mask = shifted_2((keys_own, values_own, own_mask), "seq", 1)
    keys = jnp.concatenate((prior_keys, keys_own), 1).reshape(
        images, 2 * patch_rows, head_count, HEAD_DIM
    )
    values = jnp.concatenate((prior_values, values_own), 1).reshape(
        images, 2 * patch_rows, head_count, HEAD_DIM
    )
    allowed = attention_mask(jnp.concatenate((prior_mask, own_mask), 1), patch_rows, seq_place)
    logits = masked_scores(query, keys, allowed)
    row_peak = jnp.max(logits, -1, keepdims=True)
    log_total = row_peak + jnp.log(jnp.sum(jnp.exp(logits - row_peak), -1, keepdims=True))
    weights_soft = jnp.exp(logits - log_total).astype(jnp.bfloat16)
    attended = jnp.einsum(
        "bhqk,bkhd->bqhd", weights_soft, values, preferred_element_type=jnp.float32
    )
    attended = attended.astype(jnp.bfloat16).reshape(images, patch_rows, model_width)
    mid = hidden + matmul(attended, out_weight[0])
    second = layer_norm(
        mid, ln2_gain[0].astype(jnp.float32), ln2_bias[0].astype(jnp.float32)
    ).astype(jnp.bfloat16)
    preact = matmul(second, up_weight[0]) + up_bias[0].astype(jnp.float32)
    activated = jax.nn.gelu(preact, approximate=True).astype(jnp.bfloat16)
    saved = [
        (
            hidden,
            normed,
            query,
            keys,
            values,
            allowed,
            log_total,
            attended,
            mid,
            second,
            preact,
            activated,
        )
    ]
    hidden = mid + matmul(activated, down_weight[0])
    top_low = hidden.astype(jnp.bfloat16)
    head_out = matmul(top_low, head_weight) + head_bias.astype(jnp.float32)
    prior_row = shifted_2(head_out[:, patch_rows - 1, :], "seq", 1)
    shifted = jnp.concatenate((prior_row[:, None, :], head_out[:, : patch_rows - 1, :]), 1)
    shifted = shifted * valid.astype(jnp.float32)[..., None]
    alpha = shifted[..., :channels]
    shift_mean = shifted[..., channels:]
    factor = jnp.exp(-alpha)
    new_latents = (latents - shift_mean) * factor
    logdet_part = -jnp.sum(alpha, (1, 2))
    return (new_latents, logdet_part, factor, top_low, saved)


def local(
    latents,
    valid,
    class_labels,
    group_perm,
    patch_weight,
    pos_table,
    class_table,
    ln1_gain,
    ln1_bias,
    qkv_weight,
    out_weight,
    ln2_gain,
    ln2_bias,
    up_weight,
    up_bias,
    down_weight,
    head_weight,
    head_bias,
    cot_latents,
    cot_logdet,
):
    images, patch_rows, channels = latents.shape
    model_width = qkv_weight.shape[1]
    head_count = model_width // HEAD_DIM
    layer_total = qkv_weight.shape[0]
    seq_place = lax.axis_index("seq")
    picks = group_perm[:, None] == lax.iota(jnp.int32, class_labels.shape[0])[None, :]
    image_labels = jnp.sum(jnp.where(picks, class_labels[None, :], 0), 1)
    label_hot = image_labels[:, None] == lax.iota(jnp.int32, class_table.shape[0])[None, :]
    class_rows = matmul(label_hot.astype(jnp.bfloat16), class_table)
    weights = (
        patch_weight,
        pos_table,
        qkv_weight,
        out_weight,
        ln1_gain,
        ln1_bias,
        ln2_gain,
        ln2_bias,
        up_weight,
        up_bias,
        down_weight,
        head_weight,
        head_bias,
    )
    new_latents, logdet_part, factor, top_low, saved = forward(
        latents, valid, class_rows, seq_place, weights
    )
    valid_float = valid.astype(jnp.float32)
    d_alpha = -cot_latents * new_latents - cot_logdet[:, None, None]
    d_mean = -cot_latents * factor
    d_shifted = jnp.concatenate((d_alpha, d_mean), -1) * valid_float[..., None]
    next_row = shifted_2(d_shifted[:, 0, :], "seq", -1)
    d_head = jnp.concatenate((d_shifted[:, 1:, :], next_row[:, None, :]), 1).astype(jnp.bfloat16)
    head_weight_grad = outer_sum(top_low, d_head)
    head_bias_grad = jnp.sum(d_head.astype(jnp.float32), (0, 1))
    d_hidden = transposed(d_head, head_weight)
    grads_qkv, grads_out, grads_up, grads_down = ([], [], [], [])
    grads_g1, grads_b1, grads_g2, grads_b2, grads_ub = ([], [], [], [], [])
    for layer_index in reversed(range(layer_total)):
        (
            hidden,
            normed,
            query,
            keys,
            values,
            allowed,
            log_total,
            attended,
            mid,
            second,
            preact,
            activated,
        ) = saved[layer_index]
        d_down = d_hidden.astype(jnp.bfloat16)
        down_grad = outer_sum(activated, d_down)
        d_act = transposed(d_down, down_weight[layer_index])
        unused_gelu, gelu_pull = jax.vjp(lambda inner: jax.nn.gelu(inner, approximate=True), preact)
        d_pre = gelu_pull(d_act)[0].astype(jnp.bfloat16)
        up_bias_grad = jnp.sum(d_pre.astype(jnp.float32), (0, 1))
        up_grad = outer_sum(second, d_pre)
        d_second = transposed(d_pre, up_weight[layer_index])
        unused_norm, norm_pull = jax.vjp(
            layer_norm,
            mid,
            ln2_gain[layer_index].astype(jnp.float32),
            ln2_bias[layer_index].astype(jnp.float32),
        )
        d_mid_norm, ln2_gain_part, ln2_bias_part = norm_pull(d_second)
        d_mid = d_hidden + d_mid_norm
        d_proj = d_mid.astype(jnp.bfloat16)
        out_grad = outer_sum(attended, d_proj)
        d_attended = transposed(d_proj, out_weight[layer_index]).astype(jnp.bfloat16)
        d_attended = d_attended.reshape(images, patch_rows, head_count, HEAD_DIM)
        logits = masked_scores(query, keys, allowed)
        probs = jnp.exp(logits - log_total)
        d_probs = jnp.einsum(
            "bqhd,bkhd->bhqk", d_attended, values, preferred_element_type=jnp.float32
        )
        d_scores = (probs * (d_probs - jnp.sum(d_probs * probs, -1, keepdims=True))).astype(
            jnp.bfloat16
        )
        d_query = jnp.einsum(
            "bhqk,bkhd->bqhd", d_scores, keys, preferred_element_type=jnp.float32
        ) * HEAD_DIM ** (-0.5)
        d_keys = jnp.einsum(
            "bhqk,bqhd->bkhd", d_scores, query, preferred_element_type=jnp.float32
        ) * HEAD_DIM ** (-0.5)
        d_values = jnp.einsum(
            "bhqk,bqhd->bkhd",
            probs.astype(jnp.bfloat16),
            d_attended,
            preferred_element_type=jnp.float32,
        )
        d_keys = d_keys.reshape(images, 2 * patch_rows, model_width)
        d_values = d_values.reshape(images, 2 * patch_rows, model_width)
        back_keys, back_values = (
            shifted_2(d_keys[:, :patch_rows].astype(jnp.bfloat16), "seq", -1).astype(jnp.float32),
            shifted_2(d_values[:, :patch_rows].astype(jnp.bfloat16), "seq", -1).astype(jnp.float32),
        )
        d_packed = jnp.concatenate(
            (
                d_query.reshape(images, patch_rows, model_width),
                d_keys[:, patch_rows:] + back_keys,
                d_values[:, patch_rows:] + back_values,
            ),
            -1,
        ).astype(jnp.bfloat16)
        qkv_grad = outer_sum(normed, d_packed)
        d_normed = transposed(d_packed, qkv_weight[layer_index])
        unused_norm, norm_pull = jax.vjp(
            layer_norm,
            hidden,
            ln1_gain[layer_index].astype(jnp.float32),
            ln1_bias[layer_index].astype(jnp.float32),
        )
        d_input, ln1_gain_part, ln1_bias_part = norm_pull(d_normed)
        d_hidden = d_mid + d_input
        grads_qkv.insert(0, qkv_grad)
        grads_out.insert(0, out_grad)
        grads_up.insert(0, up_grad)
        grads_down.insert(0, down_grad)
        grads_g1.insert(0, ln1_gain_part)
        grads_b1.insert(0, ln1_bias_part)
        grads_g2.insert(0, ln2_gain_part)
        grads_b2.insert(0, ln2_bias_part)
        grads_ub.insert(0, up_bias_grad)
    d_embed_low = d_hidden.astype(jnp.bfloat16)
    patch_grad_part = outer_sum(latents.astype(jnp.bfloat16), d_embed_low)
    latents_grad = cot_latents * factor + transposed(d_embed_low, patch_weight)
    pos_part = jnp.sum(d_hidden, 0)
    class_part = jnp.sum(d_hidden, 1)
    logdet, class_sums = lax.psum((logdet_part, class_part), "seq")
    class_term = lax.dot_general(
        label_hot.astype(jnp.float32),
        class_sums,
        (((0,), (0,)), ((), ())),
        precision=precise,
        preferred_element_type=jnp.float32,
    )
    class_grad = lax.psum_scatter(class_term, "dp", scatter_dimension=0, tiled=True)
    pos_grad = lax.psum(pos_part, "dp")
    (
        patch_weight_grad,
        head_weight_grad,
        head_bias_grad,
        ln1_gain_grad,
        ln1_bias_grad,
        ln2_gain_grad,
        ln2_bias_grad,
        up_bias_grad,
    ) = lax.psum(
        (
            patch_grad_part,
            head_weight_grad,
            head_bias_grad,
            jnp.stack(grads_g1),
            jnp.stack(grads_b1),
            jnp.stack(grads_g2),
            jnp.stack(grads_b2),
            jnp.stack(grads_ub),
        ),
        ("dp", "seq"),
    )
    qkv_stack = jnp.stack(grads_qkv)
    out_stack = jnp.stack(grads_out)
    up_stack = jnp.stack(grads_up)
    down_stack = jnp.stack(grads_down)
    flat_parts = (
        lax.psum_scatter(eight_rows(qkv_stack), ("dp", "seq"), scatter_dimension=1, tiled=True),
        lax.psum_scatter(eight_rows(out_stack), ("dp", "seq"), scatter_dimension=1, tiled=True),
        lax.psum_scatter(eight_rows(up_stack), ("dp", "seq"), scatter_dimension=1, tiled=True),
        lax.psum_scatter(eight_rows(down_stack), ("dp", "seq"), scatter_dimension=1, tiled=True),
    )
    flat_qkv, flat_out, flat_up, flat_down = (
        lax.all_gather(
            flat_parts[0].astype(jnp.bfloat16), ("dp", "seq"), axis=1, tiled=True
        ).astype(jnp.float32),
        lax.all_gather(
            flat_parts[1].astype(jnp.bfloat16), ("dp", "seq"), axis=1, tiled=True
        ).astype(jnp.float32),
        lax.all_gather(
            flat_parts[2].astype(jnp.bfloat16), ("dp", "seq"), axis=1, tiled=True
        ).astype(jnp.float32),
        lax.all_gather(
            flat_parts[3].astype(jnp.bfloat16), ("dp", "seq"), axis=1, tiled=True
        ).astype(jnp.float32),
    )
    qkv_stack = flat_qkv.reshape(qkv_stack.shape)
    out_stack = flat_out.reshape(out_stack.shape)
    up_stack = flat_up.reshape(up_stack.shape)
    down_stack = flat_down.reshape(down_stack.shape)
    return (
        new_latents,
        logdet,
        latents_grad,
        patch_weight_grad,
        pos_grad,
        class_grad,
        ln1_gain_grad,
        ln1_bias_grad,
        qkv_stack,
        out_stack,
        ln2_gain_grad,
        ln2_bias_grad,
        up_stack,
        up_bias_grad,
        down_stack,
        head_weight_grad,
        head_bias_grad,
    )


def solution(mesh):
    in_specs = (
        P("dp", "seq", None),
        P("dp", "seq"),
        P(),
        P("dp"),
        P(),
        P("seq", None),
        P(),
        P(),
        P(),
        P(),
        P(),
        P(),
        P(),
        P(),
        P(),
        P(),
        P(),
        P(),
        P("dp", "seq", None),
        P("dp"),
    )
    out_specs = (
        P("dp", "seq", None),
        P("dp"),
        P("dp", "seq", None),
        P(),
        P("seq", None),
        P("dp", None),
        P(),
        P(),
        P(),
        P(),
        P(),
        P(),
        P(),
        P(),
        P(),
        P(),
        P(),
    )
    body = fast_local if mesh.shape["dp"] == 16 and mesh.shape["seq"] == 2 else local
    return jax.shard_map(body, mesh=mesh, in_specs=in_specs, out_specs=out_specs, check_vma=False)
```

```python
import jax
import jax.numpy as jnp
from jax import lax
from jax.experimental import pallas as pl
from jax.experimental.pallas import tpu as pltpu
from jax.sharding import PartitionSpec as P

HEAD_DIM = 64


precise = lax.Precision.HIGHEST
norm_eps = 1e-05


def shifted_2(shard, axis, by):
    size = lax.axis_size(axis)
    pairs = [(i, i + by) for i in range(size) if 0 <= i + by < size]
    return lax.ppermute(shard, axis, pairs)


def layer_norm(values, norm_gain, norm_bias):
    center = values - jnp.mean(values, -1, keepdims=True)
    spread = jnp.mean(center * center, -1, keepdims=True)
    return center * lax.rsqrt(spread + norm_eps) * norm_gain + norm_bias


def matmul(left_side, weight_mat):
    return jnp.dot(left_side, weight_mat, preferred_element_type=jnp.float32)


def outer_sum(left_side, grad_side):
    left_flat = left_side.reshape(-1, left_side.shape[-1])
    grad_flat = grad_side.reshape(-1, grad_side.shape[-1])
    return lax.dot_general(
        left_flat, grad_flat, (((0,), (0,)), ((), ())), preferred_element_type=jnp.float32
    )


def transposed(grad_side, weight_mat):
    return lax.dot_general(
        grad_side,
        weight_mat,
        (((grad_side.ndim - 1,), (1,)), ((), ())),
        preferred_element_type=jnp.float32,
    )


def eight_rows(matrix):
    return matrix.reshape(8, -1)


def attention_mask(key_valid, patch_rows, seq_place):
    query_pos = seq_place * patch_rows + lax.iota(jnp.int32, patch_rows)
    key_pos = (seq_place - 1) * patch_rows + lax.iota(jnp.int32, 2 * patch_rows)
    earlier = (key_pos[None, :] < query_pos[:, None])[None] & (key_valid[:, None, :] > 0)
    return earlier | (key_pos[None, :] == query_pos[:, None])[None]


def masked_scores(query, keys, allowed):
    logits = jnp.einsum(
        "bqhd,bkhd->bhqk", query, keys, preferred_element_type=jnp.float32
    ) * HEAD_DIM ** (-0.5)
    return jnp.where(allowed[:, None], logits, -1e30)


MESH = pl.DeviceIdType.MESH
UNITS = 24
LAST = 25
TURNS = 8
STEPS = 38
DRAIN = 16
SLAB = 128
LABELS = 448
TABLE_ROWS = ((0, 384), (384, 64))
COLS = 384
STAGES = 3
CHUNK = 32
GELU_A = (2.0 / 3.141592653589793) ** 0.5
GELU_B = 0.044715
f32 = jnp.float32
bf16 = jnp.bfloat16


def flow_kernel(
    labels_sm, perm_sm, cot_logdet_sm,
    latents_ref, valid_ref, patch_ref, pos_table_ref, g1_ref, b1_ref, g2_ref, b2_ref,
    up_bias_ref, head_w_ref, head_b_ref, cot_ref,
    class_hbm, qkv_any, out_any, up_any, down_any,
    sums,
    stage, part, core_in, small_in, ab_in, c_in, shared,
    down_left, down_right, up_left, up_right, bulk_send, bulk_recv, send_sem, recv_sem, stage_sem, back_sem,
    qkv_w, out_w, up_w, down_w, load_sem,
    lat_pad, cot_pad, patch_pad, head_pad, hidden, mid, xhat1, xhat2, scale1, scale2,
    keys, values, query, attended, bias, prior_mask, mask_row, probs, slope, d_hidden, d_second, d_att, d_keys, d_values,
    d_prior, d_back, row_out, row_in, peek_out, peek_in, factor,
    lines, line_sum, line_in, line_send, line_recv,
    lt_ref, r_ref, pos_ref, small_ref, low_top, exch_send, exch_recv,
):
    dp = lax.axis_index("dp")
    core = lax.axis_index("seq")
    x, y, z = dp % 2, (dp // 2) % 2, dp // 4
    side = z // 2
    inner = ((z + 1) // 2) % 2 == 1
    outer = ((z + 1) // 2) % 2 == 0
    to_core = (dp, 1 - core)
    to_x = (dp + 1 - 2 * x, core)
    to_y = (dp + 2 - 4 * y, core)
    to_mate = (dp + 4 - 8 * (z % 2), core)
    to_x_other = (dp + 1 - 2 * x, 1 - core)
    to_y_other = (dp + 2 - 4 * y, 1 - core)
    to_inner = ((dp + 12 - 8 * z + 16) % 16, core)

    def rows_at(start, count):
        return pl.ds(pl.multiple_of(start, 16), count)

    sources = [class_hbm.at[r : r + n, h * COLS : (h + 1) * COLS] for h in range(2) for r, n in TABLE_ROWS]
    targets = [part.at[3 * h + i, 0:n] for h in range(2) for i, (r, n) in enumerate(TABLE_ROWS)]
    sources += [qkv_any.at[0], out_any.at[0]]
    targets += [qkv_w, out_w]

    def load(i):
        return pltpu.make_async_copy(sources[i], targets[i], load_sem.at[i])

    def load_feed(j):
        cols = rows = pl.ds(pl.multiple_of(j * 768, 128), 768)
        return (
            pltpu.make_async_copy(up_any.at[0, :, cols], up_w.at[:, cols], load_sem.at[6 + 2 * j]),
            pltpu.make_async_copy(down_any.at[0, rows], down_w.at[rows], load_sem.at[7 + 2 * j]),
        )

    for i in range(6):
        load(i).start()
    for j in range(4):
        for one in load_feed(j):
            one.start()

    barrier = pltpu.get_barrier_semaphore()
    for target in (to_core, to_x, to_y, to_mate, to_x_other, to_y_other):
        pl.semaphore_signal(barrier, inc=1, device_id=target, device_id_type=MESH)

    @pl.when(inner)
    def _():
        pl.semaphore_signal(barrier, inc=1, device_id=to_inner, device_id_type=MESH)

    def meet():
        @pl.when(inner)
        def _():
            pl.semaphore_wait(barrier, 7)

        @pl.when(outer)
        def _():
            pl.semaphore_wait(barrier, 6)

    def copy(u, k, src, dst, target):
        return pltpu.make_async_remote_copy(
            src_ref=src, dst_ref=dst, send_sem=send_sem.at[u], recv_sem=recv_sem.at[k, u % TURNS],
            device_id=target, device_id_type=MESH,
        )

    def arrived(u, k, dst):
        copy(u, k, dst, dst, to_core).wait_recv()

    def added(dst, left, right):
        dst[...] = (left[...].astype(f32) + right[...].astype(f32)).astype(bf16)

    first = (x, y)
    second = (y, x)
    to_first = (to_x, to_y)
    to_second = (to_y, to_x)

    def out_rows(u, t, start, count):
        return sums.at[u, core, rows_at(t * SLAB + start, count)]

    def part_rows(u, t, start, count):
        return part.at[u, rows_at(t * SLAB + start, count)]

    def bulk(k, src, dst, target):
        return pltpu.make_async_remote_copy(
            src_ref=src, dst_ref=dst, send_sem=bulk_send.at[k], recv_sem=bulk_recv.at[k],
            device_id=target, device_id_type=MESH,
        )

    def down_rows(i):
        return pl.ds(pl.multiple_of(i * 768, 128), 768)

    def down_left_core(i):
        return bulk(i, down_left.at[down_rows(i), 0:128], down_left.at[down_rows(i), 128:256], to_core)

    def down_left_x(i):
        return bulk(2 + i, lt_ref.at[i], down_left.at[down_rows(i), 256:384], to_x)

    def down_left_on(i):
        return bulk(4 + i, down_left.at[down_rows(i), 256:384], down_left.at[down_rows(i), 384:512], to_core)

    def down_right_go(i):
        half, target = ((1 - core, to_core), (core, to_x), (1 - core, to_x_other))[i]
        return bulk(6 + i, r_ref.at[0, half], down_right.at[128 * (i + 1) : 128 * (i + 2)], target)

    def up_left_go(i):
        first_lane, target = ((0, to_core), (0, to_y), (256, to_core))[i]
        return bulk(
            9 + i,
            up_left.at[:, first_lane : first_lane + 128],
            up_left.at[:, 128 * (i + 1) : 128 * (i + 2)],
            target,
        )

    def up_right_go(i, j):
        target = (to_core, to_y, to_y_other)[i]
        return bulk(12 + i, r_ref.at[1 + j], up_right.at[:, 128 * (i + 1) : 128 * (i + 2)], target)

    def pass_on(i):
        down_left_x(i).wait_recv()
        down_left_on(i).start()

    def begin_ab(u):
        @pl.when(u == 0)
        def _():
            for i in range(3):
                down_right_go(i).wait_recv()
                up_right_go(i, 0).wait_recv()
            up_left_go(0).wait_recv()
            up_left_go(2).wait_recv()
            down_left_core(0).wait_recv()
            down_left_on(0).wait_recv()

        @pl.when(u == 12)
        def _():
            down_left_core(1).wait_recv()
            down_left_on(1).wait_recv()

        @pl.when(u < UNITS)
        def _():
            rows = pl.ds(pl.multiple_of(u * 64, 64), 64)
            kept = part_rows(u, 0, x * 64, 64)
            kept[...] = jnp.dot(down_left[rows], down_right[...], preferred_element_type=f32).astype(bf16)
            ab_second(u, 0).start()
            rows = pl.ds(pl.multiple_of((u // 2) * 64, 64), 64)
            kept = part_rows(u, 1, y * 64, 64)
            kept[...] = jnp.dot(up_left[rows], up_right[u % 2], preferred_element_type=f32).astype(bf16)
            ab_second(u, 1).start()

    def product(u, half):
        block, rows = u // 6, pl.ds(pl.multiple_of((u % 6) * SLAB, 128), SLAB)
        return jnp.dot(lt_ref[5 + jnp.minimum(block, 1), rows], r_ref[5 + block, half], preferred_element_type=f32)

    def core_first(u):
        return pltpu.make_async_remote_copy(
            src_ref=stage.at[u % STAGES], dst_ref=core_in.at[u % TURNS], send_sem=stage_sem.at[u % STAGES],
            recv_sem=recv_sem.at[0, u % TURNS], device_id=to_core, device_id_type=MESH,
        )

    def small_first():
        return pltpu.make_async_remote_copy(
            src_ref=small_ref.at[1 - core], dst_ref=small_in, send_sem=stage_sem.at[STAGES],
            recv_sem=recv_sem.at[0, LAST % TURNS], device_id=to_core, device_id_type=MESH,
        )

    def line_copy(k, src, dst, target):
        return pltpu.make_async_remote_copy(
            src_ref=src, dst_ref=dst, send_sem=line_send.at[k], recv_sem=line_recv.at[k],
            device_id=target, device_id_type=MESH,
        )

    line_steps = (
        (lines, line_in.at[0], to_core),
        (line_sum.at[0], line_in.at[1], to_x),
        (line_sum.at[1], line_in.at[2], to_y),
        (line_sum.at[2], line_in.at[3], to_mate),
        (line_sum.at[3], line_in.at[4], to_inner),
        (line_sum.at[4], line_sum.at[4], to_mate),
    )

    def line_go(k):
        return line_copy(k, *line_steps[k])

    def line_add(k):
        line_go(k).wait_recv()
        line_sum[k] = line_steps[k][0][...] + line_in[k]

    def keep_lines():
        v = line_sum[4]
        for i in range(3):
            term = v.astype(bf16)
            v = v - term.astype(f32)
            for h in range(2):
                sums[LAST, h, 256 + i * 16 : 272 + i * 16] = term[:, h * COLS : (h + 1) * COLS]

    def produce(u):
        pl.when(u >= STAGES)(lambda: core_first(u - STAGES).wait_send())
        stage[u % STAGES] = product(u, 1 - core).astype(bf16)
        core_first(u).start()

    def begin(u):
        arrived(u, 0, core_in.at[u % TURNS])
        part[u, 2 * SLAB :] = (product(u, core) + core_in[u % TURNS].astype(f32)).astype(bf16)
        pl.when(outer)(lambda: c_z1(u).start())

    def begin_more(u):
        @pl.when(u == UNITS)
        def _():
            part[UNITS, 0:256] = pos_ref[...]
            for t in range(2):
                ab_first(u, t).start()
            small_first().start()
            line_go(0).start()

        @pl.when(u == LAST)
        def _():
            small_first().wait_recv()
            part[LAST, 0:256] = (small_ref[core].astype(f32) + small_in[...].astype(f32)).astype(bf16)
            for t in range(2):
                ab_first(u, t).start()
            line_add(0)
            line_go(1).start()

    def ab_base(t):
        return first[t] * 64 + second[t] * 32

    def ab_first(u, t):
        return copy(u, 1, part_rows(u, t, (1 - first[t]) * 64, 64), ab_in.at[u % TURNS, t, 0:64], to_first[t])

    def ab_second(u, t):
        row = first[t] * 64 + (1 - second[t]) * 32
        return copy(u, 2, part_rows(u, t, row, 32), ab_in.at[u % TURNS, t, 64:96], to_second[t])

    def ab_z1(u, t):
        return copy(u, 3, part_rows(u, t, ab_base(t), 32), ab_in.at[u % TURNS, t, 96:128], to_mate)

    def ab_z2(u, t):
        return copy(u, 4, part_rows(u, t, ab_base(t), 32), ab_in.at[u % TURNS, t, 128:160], to_inner)

    def ab_z3(u, t):
        block = out_rows(u, t, ab_base(t), 32)
        return copy(u, 3, block, block, to_mate)

    def ab_back2(u, t):
        block = out_rows(u, t, ab_base(t), 32)
        return copy(u, 5, block, block, to_second[t])

    def ab_back1(u, t):
        block = out_rows(u, t, first[t] * 64, 64)
        return copy(u, 6, block, block, to_first[t])

    def ab1(u):
        pl.when(u >= UNITS)(lambda: ab1_more(u))

    def ab1_more(u):
        arrived(u, 1, ab_in.at[u % TURNS, :, 0:64])
        for t in range(2):
            kept = part_rows(u, t, first[t] * 64, 64)
            added(kept, kept, ab_in.at[u % TURNS, t, 0:64])
            ab_second(u, t).start()

        @pl.when(u == LAST)
        def _():
            line_add(1)
            line_go(2).start()

    def ab2(u):
        arrived(u, 2, ab_in.at[u % TURNS, :, 64:96])
        for t in range(2):
            kept = part_rows(u, t, ab_base(t), 32)
            added(kept, kept, ab_in.at[u % TURNS, t, 64:96])
            pl.when(outer)(lambda: ab_z1(u, t).start())

        @pl.when(u == LAST)
        def _():
            line_add(2)
            pl.when(outer)(line_go(3).start)

    def ab3_inner(u):
        arrived(u, 3, ab_in.at[u % TURNS, :, 96:128])
        for t in range(2):
            kept = part_rows(u, t, ab_base(t), 32)
            added(kept, kept, ab_in.at[u % TURNS, t, 96:128])
            ab_z2(u, t).start()

        @pl.when(u == LAST)
        def _():
            line_add(3)
            line_go(4).start()

    def ab4_inner(u):
        arrived(u, 4, ab_in.at[u % TURNS, :, 128:160])
        for t in range(2):
            added(out_rows(u, t, ab_base(t), 32), part_rows(u, t, ab_base(t), 32), ab_in.at[u % TURNS, t, 128:160])
            ab_z3(u, t).start()
            ab_back2(u, t).start()

        @pl.when(u == LAST)
        def _():
            line_add(4)
            line_go(5).start()
            keep_lines()

    def ab5_outer(u):
        arrived(u, 3, sums.at[u, core, 0:64])
        for t in range(2):
            ab_back2(u, t).start()

        @pl.when(u == LAST)
        def _():
            line_go(5).wait_recv()
            keep_lines()

    def ab6(u):
        arrived(u, 5, sums.at[u, core, 0:64])
        for t in range(2):
            ab_back1(u, t).start()

    def spread(u, row, count):
        block = sums.at[u, core, row : row + count]
        to_other(u, block).start()

    def to_other(u, block):
        return pltpu.make_async_remote_copy(
            src_ref=block, dst_ref=block, send_sem=send_sem.at[u], recv_sem=back_sem.at[u],
            device_id=to_core, device_id_type=MESH,
        )

    def ab7(u):
        arrived(u, 6, sums.at[u, core, 0:128])
        pl.when(u != UNITS)(lambda: spread(u, 0, 2 * SLAB))

    far = 32 * (1 - side)
    own_end = 96 * side
    shard = z * 32

    def c_z1(u):
        return copy(u, 7, part_rows(u, 2, far, 96), c_in.at[u % TURNS, 0:96], to_mate)

    def c_z2(u):
        return copy(u, 8, part_rows(u, 2, (1 - side) * 64, 64), c_in.at[u % TURNS, 96:160], to_inner)

    def c_z3(u):
        return copy(u, 7, part_rows(u, 2, own_end, 32), c_in.at[u % TURNS, 160:192], to_mate)

    def c_x(u):
        return copy(u, 9, part_rows(u, 2, shard, 32), c_in.at[u % TURNS, 192:224], to_x)

    def c_y(u):
        return copy(u, 10, shared.at[u], c_in.at[u % TURNS, 224:256], to_y)

    def c_z4(u):
        block = out_rows(u, 2, own_end, 32)
        return copy(u, 12, block, block, to_mate)

    def c_z5(u):
        block = out_rows(u, 2, side * 64, 64)
        return copy(u, 13, block, block, to_inner)

    def c_z6(u):
        block = out_rows(u, 2, far, 96)
        return copy(u, 12, block, block, to_mate)

    def c1_inner(u):
        arrived(u, 7, c_in.at[u % TURNS, 0:96])
        kept = part_rows(u, 2, far, 96)
        added(kept, kept, c_in.at[u % TURNS, 0:96])
        c_z2(u).start()

    def c2_inner(u):
        arrived(u, 8, c_in.at[u % TURNS, 96:160])
        kept = part_rows(u, 2, side * 64, 64)
        added(kept, kept, c_in.at[u % TURNS, 96:160])
        c_z3(u).start()
        c_x(u).start()

    def c3_outer(u):
        arrived(u, 7, c_in.at[u % TURNS, 160:192])
        kept = part_rows(u, 2, shard, 32)
        added(kept, kept, c_in.at[u % TURNS, 160:192])
        c_x(u).start()

    def c4(u):
        arrived(u, 9, c_in.at[u % TURNS, 192:224])
        kept = part_rows(u, 2, shard, 32)
        part_y = shared.at[u]
        added(part_y, kept, c_in.at[u % TURNS, 192:224])
        c_y(u).start()

    def c5(u):
        arrived(u, 10, c_in.at[u % TURNS, 224:256])
        added(out_rows(u, 2, shard, 32), shared.at[u], c_in.at[u % TURNS, 224:256])
        pl.when(outer)(lambda: c_z4(u).start())

    def c8_inner(u):
        arrived(u, 12, out_rows(u, 2, own_end, 32))
        c_z5(u).start()

    def c9_inner(u):
        arrived(u, 13, out_rows(u, 2, (1 - side) * 64, 64))
        c_z6(u).start()
        spread(u, 2 * SLAB, SLAB)

    def c10_outer(u):
        arrived(u, 12, out_rows(u, 2, far, 96))
        spread(u, 2 * SLAB, SLAB)

    def sent(u, units, rows):
        ref = part.at[0:units, 0:rows]
        copy(u, 0, ref, ref, to_core).wait_send()

    def drain(u):
        pl.when(outer)(lambda: sent(u, 4, 224))
        pl.when(inner)(lambda: sent(u, 4, 272))
        to_other(u, sums.at[u, 1 - core]).wait_recv()

    mm_nt = (((1,), (1,)), ((), ()))
    mm_tn = (((0,), (0,)), ((), ()))

    def nt(left, right):
        return lax.dot_general(left, right, mm_nt, preferred_element_type=f32)

    def tn(left, right):
        return lax.dot_general(left, right, mm_tn, preferred_element_type=f32)

    def nn(left, right):
        return jnp.dot(left, right, preferred_element_type=f32)

    def exchange(k, src, dst):
        return pltpu.make_async_remote_copy(
            src_ref=src, dst_ref=dst, send_sem=exch_send.at[k], recv_sem=exch_recv.at[k],
            device_id=to_core, device_id_type=MESH,
        )

    chunks = [slice(r, r + CHUNK) for r in range(0, 128, CHUNK)]
    lane = lax.broadcasted_iota(jnp.int32, (128, 128), 1)
    row = lax.broadcasted_iota(jnp.int32, (128, 128), 0)
    eye = row == lane
    low_half = lane < 64
    valid_row = valid_ref[...].astype(f32)
    valid_col = jnp.sum(jnp.where(eye, valid_row, 0.0), axis=1, keepdims=True)
    mask_row[...] = jnp.broadcast_to(valid_row, (8, 128))
    lat_pad[...] = jnp.zeros((128, 128), f32)
    lat_pad[0:48] = latents_ref[0]
    lat_pad[...] = lat_pad[...].T
    cot_pad[...] = jnp.zeros((128, 128), f32)
    cot_pad[0:48] = cot_ref[0]
    cot_pad[...] = cot_pad[...].T
    patch_pad[...] = jnp.zeros((128, 768), bf16)
    patch_pad[0:48] = patch_ref[...]
    head_pad[...] = jnp.zeros((128, 768), bf16)
    head_pad[0:96] = head_w_ref[...]
    head_bias = jnp.concatenate((head_b_ref[...].astype(f32), jnp.zeros((1, 32), f32)), 1)

    @pl.when(core == 0)
    def _():
        keys[0:128] = jnp.zeros((128, 768), bf16)
        values[0:128] = jnp.zeros((128, 768), bf16)
        prior_mask[...] = jnp.zeros((8, 128), f32)
        row_in[...] = jnp.zeros((8, 128), f32)

    @pl.when(core == 1)
    def _():
        peek_in[...] = jnp.zeros((8, 128), f32)
        d_back[...] = jnp.zeros((2, 128, 768), bf16)

    line8 = lax.broadcasted_iota(jnp.int32, (8, 128), 0)
    peek_out[...] = jnp.where(line8 == 0, lat_pad[0:1], jnp.where(line8 == 1, cot_pad[0:1], valid_row[:, 0:1]))

    def normalize(src, hat, scale, gain, shift, put):
        for r in chunks:
            v = src[r]
            center = v - jnp.mean(v, -1, keepdims=True)
            inv = lax.rsqrt(jnp.mean(center * center, -1, keepdims=True) + norm_eps)
            scaled = center * inv
            hat[r] = scaled
            scale[r] = inv
            put(r, scaled * gain + shift)

    label = labels_sm[perm_sm[0]]
    hot = jnp.where(lax.broadcasted_iota(jnp.int32, (16, LABELS), 1) == label, 1.0, 0.0).astype(bf16)
    for i in range(4):
        load(i).wait()
    class_row = jnp.concatenate(
        [
            sum(nn(hot[:, r : r + n], part[3 * h + i, 0:n]) for i, (r, n) in enumerate(TABLE_ROWS))
            for h in range(2)
        ],
        1,
    )[0:1]
    hidden[...] = (
        nn(lat_pad[...].astype(bf16), patch_pad[...]) + pos_table_ref[...].astype(f32) + class_row
    )

    def put_low(r, v):
        low_top[r] = v.astype(bf16)

    normalize(hidden, xhat1, scale1, g1_ref[...].astype(f32), b1_ref[...].astype(f32), put_low)
    load(4).wait()
    normed = low_top[...]
    keys[128:256] = nn(normed, qkv_w[:, 768:1536]).astype(bf16)
    meet()

    @pl.when(core == 1)
    def _():
        exchange(4, peek_out, peek_in).start()

    @pl.when(core == 0)
    def _():
        exchange(2, mask_row, prior_mask).start()
        exchange(0, keys.at[128:256], keys.at[0:128]).start()

    values[128:256] = nn(normed, qkv_w[:, 1536:2304]).astype(bf16)

    @pl.when(core == 0)
    def _():
        exchange(1, values.at[128:256], values.at[0:128]).start()

    query[...] = nn(normed, qkv_w[:, 0:768]).astype(bf16)
    lt_ref[6] = normed.astype(f32).T.astype(bf16)

    @pl.when(core == 1)
    def _():
        exchange(2, mask_row, prior_mask).wait_recv()
        exchange(0, keys.at[128:256], keys.at[0:128]).wait_recv()
        exchange(1, values.at[128:256], values.at[0:128]).wait_recv()

    bias[:, 0:128] = jnp.where(jnp.broadcast_to(prior_mask[0:1], (128, 128)) > 0.5, 0.0, -1e30)
    bias[:, 128:256] = jnp.where(((lane < row) & (valid_row > 0.5)) | eye, 0.0, -1e30)

    def columns128(p):
        return pl.ds(pl.multiple_of(p * 128, 128), 128)

    def attend(p):
        cols = columns128(p)
        q_pair = query[:, cols]
        k_pair = keys[:, cols]
        v_pair = values[:, cols]
        outs = []
        for i in range(2):
            q_one = jnp.where(low_half if i == 0 else lane >= 64, q_pair, jnp.zeros_like(q_pair))
            scores = nt(q_one, k_pair) * 0.125 + bias[...]
            top = jnp.max(scores, -1, keepdims=True)
            powers = jnp.exp(scores - top)
            soft = powers * (1.0 / jnp.sum(powers, -1, keepdims=True))
            probs[2 * p + i] = soft
            outs.append(nn(soft.astype(bf16), v_pair))
        attended[:, cols] = jnp.where(low_half, outs[0], outs[1]).astype(bf16)

    for p in range(6):
        attend(p)
    load(5).wait()
    mid[...] = hidden[...] + nn(attended[...], out_w[...])
    lt_ref[5] = attended[...].astype(f32).T.astype(bf16)
    normalize(mid, xhat2, scale2, g2_ref[...].astype(f32), b2_ref[...].astype(f32), put_low)
    up_left[:, 0:128] = low_top[...].astype(f32).T.astype(bf16)
    for i in range(2):
        up_left_go(i).start()
    d_hidden[...] = mid[...]

    def rows768(j):
        return pl.ds(pl.multiple_of(j * 768, 128), 768)

    def feed(j, carried):
        for one in load_feed(j):
            one.wait()
        d_second[...] = nn(low_top[...], up_w[:, rows768(j)])
        shift = up_bias_ref[:, rows768(j)].astype(f32)
        for r in chunks:
            pre = d_second[r] + shift
            square = pre * pre
            bend = jnp.tanh(pre * (GELU_A + (GELU_A * GELU_B) * square))
            left = 0.5 * (1.0 + bend)
            slope[j, r] = left + 0.5 * pre * (1.0 - bend * bend) * (GELU_A + (3.0 * GELU_A * GELU_B) * square)
            d_second[r] = pre * left
        act = d_second[...]
        turned = act.T.astype(bf16)

        @pl.when(j // 2 == x)
        def _():
            down_left[down_rows(j % 2), 0:128] = turned
            down_left_core(j % 2).start()

        @pl.when(j // 2 != x)
        def _():
            lt_ref[j % 2] = turned
            pl.when(j % 2 == 0)(lambda: down_left_x(0).start())

        d_hidden[...] += nn(act.astype(bf16), down_w[rows768(j)])
        return carried

    lax.fori_loop(0, 4, feed, 0)
    low_top[...] = d_hidden[...].astype(bf16)
    row_out[...] = nt(low_top[...], head_pad[...]) + head_bias

    @pl.when(core == 0)
    def _():
        exchange(3, row_out.at[120:128], row_in).start()

    def coupling(shifted, latent, cot):
        inside = lax.broadcasted_iota(jnp.int32, shifted.shape, 1) < 48
        alpha = jnp.where(inside, shifted, 0.0)
        scale = jnp.exp(-alpha)
        moved = (latent - jnp.where(inside, pltpu.roll(shifted, 80, 1), 0.0)) * scale
        d_alpha = -cot * moved - cot_logdet_sm[0]
        d_mean = pltpu.roll(jnp.where(inside, -cot * scale, 0.0), 48, 1)
        return alpha, scale, moved, jnp.where(inside, d_alpha, d_mean)

    rolled = pltpu.roll(row_out[...], 1, 0)
    d_shifted = coupling(jnp.where(row == 0, 0.0, rolled) * valid_col, lat_pad[...], cot_pad[...])[3] * valid_col

    @pl.when(core == 0)
    def _():
        exchange(4, peek_out, peek_in).wait_recv()

    def peeked(i):
        return jnp.broadcast_to(peek_in[i : i + 1], (8, 128))

    after_last = jnp.broadcast_to(row_out[127:128], (8, 128)) * peeked(2)
    d_next = coupling(after_last, peeked(0), peeked(1))[3] * peeked(2)
    d_head = jnp.where(row == 127, d_next[0:1], pltpu.roll(d_shifted, 127, 0)).astype(bf16)

    def outputs():
        @pl.when(core == 1)
        def _():
            exchange(3, row_out.at[120:128], row_in).wait_recv()

        before = jnp.where(row == 0, jnp.broadcast_to(row_in[7:8], (128, 128)), pltpu.roll(row_out[...], 1, 0))
        alpha, scale, moved = coupling(before * valid_col, lat_pad[...], cot_pad[...])[0:3]
        factor[...] = scale
        store_exact(0, moved.T[0:48])
        logdet = -jnp.sum(jnp.sum(alpha, 1, keepdims=True), 0, keepdims=True)
        lines[8:9, 128:256] = jnp.where(lax.broadcasted_iota(jnp.int32, (1, 128), 1) == dp, logdet, 0.0)

    def exact_terms(v):
        terms = []
        for i in range(3):
            terms.append(v.astype(bf16))
            v = v - terms[i].astype(f32)
        return terms

    def store_exact(h, v):
        for i, term in enumerate(exact_terms(v)):
            sums[UNITS, h, 256:304, i * 128 : (i + 1) * 128] = term

    head_grad = tn(d_head, low_top[...])
    head_bias_grad = jnp.sum(d_head.astype(f32), 0, keepdims=True)
    d_hidden[...] = nn(d_head, head_pad[...])
    low_top[...] = d_hidden[...].astype(bf16)
    for h in range(2):
        r_ref[0, h] = low_top[:, h * COLS : (h + 1) * COLS]
    for i in range(3):
        down_right_go(i).start()
    down_left_x(1).start()
    down_right[0:128] = r_ref[0, core]

    def put(first_row, value):
        h, r = first_row // 128, first_row % 128
        for t in range(2):
            small_ref[h, t * 128 + r : t * 128 + r + value.shape[0]] = value[:, t * COLS : (t + 1) * COLS].astype(bf16)

    put(0, head_grad[0:96])

    lines[...] = jnp.zeros((16, 768), f32)
    lines[8:9, 0:128] = head_bias_grad

    d_second[...] = jnp.zeros((128, 768), f32)

    def feed_back(j):
        d_keys[...] = nt(low_top[...], down_w[rows768(j)])
        total = jnp.zeros((1, 768), f32)
        for r in chunks:
            d_pre = (slope[j, r] * d_keys[r]).astype(bf16)
            d_att[r] = d_pre
            total += jnp.sum(d_pre.astype(f32), 0, keepdims=True)
            for h in range(2):
                r_ref[1 + j, h, r] = d_pre[:, h * COLS : (h + 1) * COLS]
        near, same = j // 2 == y, j % 2 == core

        @pl.when(jnp.logical_and(near, same))
        def _():
            for h in range(2):
                up_right[h, 0:128] = r_ref[1 + j, h]

        pl.when(jnp.logical_and(near, j % 2 != core))(lambda: up_right_go(0, j).start())
        pl.when(jnp.logical_and(j // 2 != y, same))(lambda: up_right_go(1, j).start())
        pl.when(jnp.logical_and(j // 2 != y, j % 2 != core))(lambda: up_right_go(2, j).start())
        lines[pl.ds(4 + j, 1)] = total
        d_second[...] += nt(d_att[...], up_w[:, rows768(j)])

    def norm_back(grad, hat, scale, gain, base, out, line):
        gain_total = jnp.zeros((1, 768), f32)
        shift_total = jnp.zeros((1, 768), f32)
        for r in chunks:
            d = grad[r]
            scaled = hat[r]
            e = d * gain
            v = e - jnp.mean(e, -1, keepdims=True) - scaled * jnp.mean(e * scaled, -1, keepdims=True)
            out[r] = base[r] + scale[r] * v
            gain_total += jnp.sum(d * scaled, 0, keepdims=True)
            shift_total += jnp.sum(d, 0, keepdims=True)
        lines[line : line + 1] = gain_total
        lines[line + 1 : line + 2] = shift_total

    def feed_norm_back():
        norm_back(d_second, xhat2, scale2, g2_ref[...].astype(f32), d_hidden, mid, 2)
        low_top[...] = mid[...].astype(bf16)
        for h in range(2):
            r_ref[5, h] = low_top[:, h * COLS : (h + 1) * COLS]
        d_att[...] = nt(low_top[...], out_w[...]).astype(bf16)

    def attend_back(p):
        cols = columns128(p)
        q_pair = query[:, cols]
        k_pair = keys[:, cols]
        v_pair = values[:, cols]
        a_pair = d_att[:, cols]
        dq, dk, dv = [], [], []
        for i in range(2):
            own = low_half if i == 0 else lane >= 64
            a_one = jnp.where(own, a_pair, jnp.zeros_like(a_pair))
            q_one = jnp.where(own, q_pair, jnp.zeros_like(q_pair))
            soft = probs[2 * p + i]
            d_soft = nt(a_one, v_pair)
            weighted = d_soft * soft
            d_score = weighted - soft * jnp.sum(weighted, -1, keepdims=True)
            d_low = d_score.astype(bf16)
            dq.append(nn(d_low, k_pair))
            dk.append(tn(d_low, q_one))
            dv.append(tn(soft.astype(bf16), a_one))
        h, local = p // 3, pl.ds(pl.multiple_of((p % 3) * 128, 128), 128)
        r_ref[6, h, :, local] = (jnp.where(low_half, dq[0], dq[1]) * 0.125).astype(bf16)
        dk_pair = (dk[0] + dk[1]) * 0.125
        dv_pair = dv[0] + dv[1]
        d_prior[0, :, cols] = dk_pair[0:128].astype(bf16)
        d_prior[1, :, cols] = dv_pair[0:128].astype(bf16)
        d_keys[:, cols] = dk_pair[128:256]
        d_values[:, cols] = dv_pair[128:256]

    def send_prior():
        @pl.when(core == 1)
        def _():
            exchange(5, d_prior, d_back).start()

    def packed_back():
        @pl.when(core == 0)
        def _():
            exchange(5, d_prior, d_back).wait_recv()

        for h in range(2):
            cols = slice(h * COLS, (h + 1) * COLS)
            r_ref[7, h] = (d_keys[:, cols] + d_back[0, :, cols].astype(f32)).astype(bf16)
            r_ref[8, h] = (d_values[:, cols] + d_back[1, :, cols].astype(f32)).astype(bf16)
        d_second[...] = sum(
            nt(r_ref[6 + j, h], qkv_w[:, j * 768 + h * COLS : j * 768 + (h + 1) * COLS])
            for j in range(3)
            for h in range(2)
        )

    def embed_back():
        norm_back(d_second, xhat1, scale1, g1_ref[...].astype(f32), mid, d_hidden, 0)
        low_top[...] = d_hidden[...].astype(bf16)
        for t in range(2):
            pos_ref[t * 128 : (t + 1) * 128] = low_top[:, t * COLS : (t + 1) * COLS]
        patch_grad = tn(lat_pad[...].astype(bf16), low_top[...])
        store_exact(1, (cot_pad[...] * factor[...] + nt(low_top[...], patch_pad[...])).T[0:48])
        class_grad = jnp.sum(d_hidden[...], 0, keepdims=True)
        put(96, patch_grad[0:32])
        put(128, patch_grad[32:48])
        line = lax.broadcasted_iota(jnp.int32, (16, 768), 0)
        put(144, jnp.where(line == dp, class_grad, 0.0))
        put(160, jnp.zeros((96, 768), f32))

    def feed_back_all(j, carried):
        feed_back((j + 2 * (1 - y)) % 4)
        return carried

    lax.fori_loop(0, 4, feed_back_all, 0)
    pass_on(0)
    up_left_go(1).wait_recv()
    up_left_go(2).start()
    feed_norm_back()

    def piece(t):
        @pl.when(jnp.logical_and(t >= 2, t < 5))
        def _():
            attend_back(2 * t - 4)
            attend_back(2 * t - 3)

        pl.when(t == 5)(lambda: pass_on(1))
        pl.when(t == 4)(send_prior)
        pl.when(t == 6)(packed_back)
        pl.when(t == 7)(outputs)
        pl.when(t == 8)(embed_back)

    everyone, inners, outers = None, inner, outer
    events = [
        (10, LAST + 1, inners, ab7),
        (11, UNITS, inners, c9_inner),
        (2, UNITS, everyone, produce),
        (4, UNITS, inners, c1_inner),
        (8, LAST + 1, inners, ab6),
        (7, UNITS, outers, c3_outer),
        (8, UNITS, outers, c4),
        (9, UNITS, inners, c5),
        (9, UNITS, outers, c5),
        (3, UNITS, everyone, begin),
        (1, LAST + 1, everyone, begin_more),
        (7, UNITS, inners, c4),
        (5, UNITS, inners, c2_inner),
        (14, UNITS, outers, c10_outer),
        (0, LAST + 1, everyone, piece),
        (12, LAST + 1, outers, ab7),
        (5, LAST + 1, inners, ab3_inner),
        (3, LAST + 1, everyone, begin_ab),
        (3, LAST + 1, everyone, ab1),
        (6, LAST + 1, inners, ab4_inner),
        (8, LAST + 1, outers, ab5_outer),
        (9, LAST + 1, outers, ab6),
        (9, UNITS, inners, c8_inner),
        (4, LAST + 1, everyone, ab2),
        (DRAIN, UNITS, everyone, drain),
    ]

    def step(t, carried):
        for lag, count, who, event in events:
            u = t - lag
            now = jnp.logical_and(u >= 0, u < count)
            if who is not None:
                now = jnp.logical_and(now, who)
            pl.when(now)(lambda event=event, u=u: event(u))
        return carried

    lax.fori_loop(2, STEPS, step, 0)


    def drain_more(u, carried):
        drain(u)
        return carried

    lax.fori_loop(STEPS - DRAIN, UNITS, drain_more, 0)
    pl.when(outer)(lambda: sent(UNITS, 2, 224))
    pl.when(inner)(lambda: sent(UNITS, 2, 256))
    pl.when(outer)(lambda: sent(LAST, 2, 352))
    pl.when(inner)(lambda: sent(LAST, 2, 384))
    to_other(LAST, sums.at[LAST, 1 - core, 0 : 2 * SLAB]).wait_recv()
    for u in range(UNITS - STAGES, UNITS):
        core_first(u).wait_send()
    small_first().wait_send()
    for k in range(3):
        line_go(k).wait_send()
        down_right_go(k).wait_send()
        up_left_go(k).wait_send()
        up_right_go(k, 0).wait_send()
    for i in range(2):
        down_left_core(i).wait_send()
        down_left_x(i).wait_send()
        down_left_on(i).wait_send()
    pl.when(outer)(line_go(3).wait_send)

    @pl.when(inner)
    def _():
        line_go(4).wait_send()
        line_go(5).wait_send()

    @pl.when(core == 0)
    def _():
        exchange(2, mask_row, prior_mask).wait_send()
        exchange(0, keys.at[128:256], keys.at[0:128]).wait_send()
        exchange(1, values.at[128:256], values.at[0:128]).wait_send()
        exchange(3, row_out.at[120:128], row_in).wait_send()

    @pl.when(core == 1)
    def _():
        exchange(4, peek_out, peek_in).wait_send()
        exchange(5, d_prior, d_back).wait_send()


def flow(
    class_labels, group_perm, cot_logdet, latents, valid, patch_weight, pos_table, ln1_gain, ln1_bias,
    ln2_gain, ln2_bias, up_bias, head_weight, head_bias, cot_latents, class_table,
    qkv_weight, out_weight, up_weight, down_weight,
):
    smem = pl.BlockSpec(memory_space=pltpu.SMEM)
    vmem = pl.BlockSpec(memory_space=pltpu.VMEM)
    hbm = pl.BlockSpec(memory_space=pltpu.HBM)
    wide = (128, 768)
    return pl.pallas_call(
        flow_kernel,
        out_shape=pltpu.VMEM((LAST + 1, 2, 3 * SLAB, COLS), bf16),
        in_specs=[smem] * 3 + [vmem] * 12 + [hbm] * 5,
        out_specs=vmem,
        scratch_shapes=[
            pltpu.VMEM((STAGES, SLAB, COLS), bf16),
            pltpu.VMEM((LAST + 1, 3 * SLAB, COLS), bf16),
            pltpu.VMEM((TURNS, SLAB, COLS), bf16),
            pltpu.VMEM((256, COLS), bf16),
            pltpu.VMEM((TURNS, 2, 160, COLS), bf16),
            pltpu.VMEM((TURNS, 256, COLS), bf16),
            pltpu.VMEM((UNITS, 32, COLS), bf16),
            pltpu.VMEM((1536, 512), bf16),
            pltpu.VMEM((512, COLS), bf16),
            pltpu.VMEM((768, 512), bf16),
            pltpu.VMEM((2, 512, COLS), bf16),
            pltpu.SemaphoreType.DMA((15,)),
            pltpu.SemaphoreType.DMA((15,)),
            pltpu.SemaphoreType.DMA((LAST + 1,)),
            pltpu.SemaphoreType.DMA((14, TURNS)),
            pltpu.SemaphoreType.DMA((STAGES + 1,)),
            pltpu.SemaphoreType.DMA((LAST + 1,)),
            pltpu.VMEM((768, 2304), bf16),
            pltpu.VMEM((768, 768), bf16),
            pltpu.VMEM((768, 3072), bf16),
            pltpu.VMEM((3072, 768), bf16),
            pltpu.SemaphoreType.DMA((14,)),
            pltpu.VMEM((128, 128), f32),
            pltpu.VMEM((128, 128), f32),
            pltpu.VMEM(wide, bf16),
            pltpu.VMEM(wide, bf16),
            pltpu.VMEM(wide, f32),
            pltpu.VMEM(wide, f32),
            pltpu.VMEM(wide, f32),
            pltpu.VMEM(wide, f32),
            pltpu.VMEM((128, 1), f32),
            pltpu.VMEM((128, 1), f32),
            pltpu.VMEM((256, 768), bf16),
            pltpu.VMEM((256, 768), bf16),
            pltpu.VMEM(wide, bf16),
            pltpu.VMEM(wide, bf16),
            pltpu.VMEM((128, 256), f32),
            pltpu.VMEM((8, 128), f32),
            pltpu.VMEM((8, 128), f32),
            pltpu.VMEM((12, 128, 256), f32),
            pltpu.VMEM((4, 128, 768), f32),
            pltpu.VMEM(wide, f32),
            pltpu.VMEM(wide, f32),
            pltpu.VMEM(wide, bf16),
            pltpu.VMEM(wide, f32),
            pltpu.VMEM(wide, f32),
            pltpu.VMEM((2, 128, 768), bf16),
            pltpu.VMEM((2, 128, 768), bf16),
            pltpu.VMEM((128, 128), f32),
            pltpu.VMEM((8, 128), f32),
            pltpu.VMEM((8, 128), f32),
            pltpu.VMEM((8, 128), f32),
            pltpu.VMEM((128, 128), f32),
            pltpu.VMEM((16, 768), f32),
            pltpu.VMEM((5, 16, 768), f32),
            pltpu.VMEM((5, 16, 768), f32),
            pltpu.SemaphoreType.DMA((6,)),
            pltpu.SemaphoreType.DMA((6,)),
            pltpu.VMEM((7, 768, 128), bf16),
            pltpu.VMEM((9, 2, 128, COLS), bf16),
            pltpu.VMEM((256, COLS), bf16),
            pltpu.VMEM((2, 256, COLS), bf16),
            pltpu.VMEM(wide, bf16),
            pltpu.SemaphoreType.DMA((6,)),
            pltpu.SemaphoreType.DMA((6,)),
        ],
        compiler_params=pltpu.CompilerParams(
            collective_id=0, has_side_effects=True, vmem_limit_bytes=46 << 20
        ),
        name="flow",
    )(
        class_labels, group_perm, cot_logdet, latents, valid, patch_weight, pos_table, ln1_gain, ln1_bias,
        ln2_gain, ln2_bias, up_bias, head_weight, head_bias, cot_latents, class_table,
        qkv_weight, out_weight, up_weight, down_weight,
    )


def finish_kernel(
    labels_ref, sums,
    new_latents, logdet, latents_grad, patch, pos, classes, g1, b1, qkv, out, g2, b2, up, ub, down, head, hb,
    wide_down, wide_up, wide_last, write_sem, lat_wide, pos_wide, small_wide, class_wide, out_sem,
):
    dp = lax.axis_index("dp")
    core = lax.axis_index("seq")
    owned = classes.shape[0]
    outputs = [
        pltpu.make_async_copy(src, dst, out_sem.at[i])
        for i, (src, dst) in enumerate(
            (
                (lat_wide.at[0], new_latents.at[0]),
                (lat_wide.at[1], latents_grad.at[0]),
                (small_wide.at[0:96], head),
                (small_wide.at[96:144], patch),
                (pos_wide, pos),
                (class_wide, classes),
            )
        )
    ]
    writes = []

    def write(src, dst):
        writes.append(pltpu.make_async_copy(src, dst, write_sem.at[len(writes)]))
        writes[-1].start()

    def little():
        for h in range(2):
            terms = [sums[UNITS, h, 256:304, i * 128 : (i + 1) * 128].astype(f32) for i in range(3)]
            lat_wide[h] = terms[0] + terms[1] + terms[2]
        outputs[0].start()
        outputs[1].start()
        for t in range(2):
            rows, cols = slice(t * 128, (t + 1) * 128), slice(t * COLS, (t + 1) * COLS)
            pos_wide[:, cols] = sums[UNITS, core, rows].astype(f32)
            for h in range(2):
                small_wide[h * 128 : (h + 1) * 128, cols] = sums[LAST, h, rows].astype(f32)
        for one in outputs[2:5]:
            one.start()
        halves = []
        for h in range(2):
            terms = [sums[LAST, h, 256 + i * 16 : 272 + i * 16].astype(f32) for i in range(3)]
            halves.append(terms[0] + terms[1] + terms[2])
        block = jnp.concatenate(halves, 1)
        for i, one in enumerate((g1, b1, g2, b2)):
            one[...] = block[i : i + 1]
        for i in range(4):
            ub[:, i * 768 : (i + 1) * 768] = block[4 + i : 5 + i]
        hb[...] = block[8:9, 0:96]
        count = labels_ref.shape[1]
        lane = lax.broadcasted_iota(jnp.int32, (1, 128), 1)
        logdet[...] = jnp.sum(jnp.where(lane == dp, block[8:9, 128:256], 0.0), 1, keepdims=True)
        by_lane = jnp.broadcast_to(labels_ref[...], (count, count)).astype(f32)
        first = lax.broadcasted_iota(jnp.int32, (count, count), 0)
        second = lax.broadcasted_iota(jnp.int32, (count, count), 1)
        by_row = jnp.sum(jnp.where(first == second, by_lane, 0.0), 1, keepdims=True)
        before = (by_lane < by_row) | ((by_lane == by_row) & (second < first))
        rank = jnp.sum(jnp.where(before, 1.0, 0.0), 1, keepdims=True)
        stored = jnp.sum(jnp.where(rank == second.astype(f32), by_row, 0.0), 0, keepdims=True)
        wanted = (dp * owned + lax.broadcasted_iota(jnp.int32, (owned, count), 0)).astype(f32)
        hot = jnp.where(stored == wanted, 1.0, 0.0).astype(bf16)
        class_wide[...] = jnp.dot(hot, small_wide[144:160].astype(bf16), preferred_element_type=f32)
        outputs[5].start()

    for u in range(UNITS):
        block, row, turn = u // 6, (u % 6) * SLAB, 64 * (u // 2)
        for h in range(2):
            cols = slice(h * COLS, (h + 1) * COLS)
            for i in range(2):
                wide_down[1536 * i + 64 * u : 1536 * i + 64 * (u + 1), cols] = sums[
                    u, h, 64 * i : 64 * (i + 1)
                ].astype(f32)
                column = (2 * i + h) * 768 + (u % 2) * COLS
                wide_up[turn : turn + 64, column : column + COLS] = sums[
                    u, h, 128 + 64 * i : 128 + 64 * (i + 1)
                ].astype(f32)
            wide_last[block, row : row + SLAB, cols] = sums[u, h, 2 * SLAB :].astype(f32)
        target, column = (out, 0) if block == 0 else (qkv, (block - 1) * 768)
        write(wide_last.at[block, row : row + SLAB], target.at[0, row : row + SLAB, column : column + 768])
        if u % 2 == 1:
            write(wide_up.at[turn : turn + 64], up.at[0, turn : turn + 64])
        if u % 4 == 3:
            for i in range(2):
                rows = slice(1536 * i + 64 * (u - 3), 1536 * i + 64 * (u + 1))
                write(wide_down.at[rows], down.at[0, rows])
        if u == 3:
            little()
    for one in writes:
        one.wait()
    for one in outputs:
        one.wait()


def finish(class_labels, sums):
    count = class_labels.shape[1]
    owned = 1024 // count
    shapes = [
        (1, 48, 128), (1, 1), (1, 48, 128), (48, 768), (128, 768), (owned, 768), (1, 768), (1, 768),
        (1, 768, 2304), (1, 768, 768), (1, 768), (1, 768), (1, 768, 3072), (1, 3072), (1, 3072, 768),
        (96, 768), (1, 96),
    ]
    vmem = pl.BlockSpec(memory_space=pltpu.VMEM)
    hbm = pl.BlockSpec(memory_space=pl.ANY)
    return pl.pallas_call(
        finish_kernel,
        out_shape=[jax.ShapeDtypeStruct(shape, f32) for shape in shapes],
        in_specs=[vmem, vmem],
        out_specs=[vmem if i in (1, 6, 7, 10, 11, 13, 16) else hbm for i in range(17)],
        scratch_shapes=[
            pltpu.VMEM((3072, 768), f32),
            pltpu.VMEM((768, 3072), f32),
            pltpu.VMEM((4, 768, 768), f32),
            pltpu.SemaphoreType.DMA((48,)),
            pltpu.VMEM((2, 48, 128), f32),
            pltpu.VMEM((128, 768), f32),
            pltpu.VMEM((256, 768), f32),
            pltpu.VMEM((owned, 768), f32),
            pltpu.SemaphoreType.DMA((6,)),
        ],
        compiler_params=pltpu.CompilerParams(vmem_limit_bytes=34 << 20),
        name="finish",
    )(class_labels, sums)


def fast_local(
    latents, valid, class_labels, group_perm, patch_weight, pos_table, class_table, ln1_gain, ln1_bias,
    qkv_weight, out_weight, ln2_gain, ln2_bias, up_weight, up_bias, down_weight, head_weight, head_bias,
    cot_latents, cot_logdet,
):
    sums = flow(
        class_labels, group_perm, cot_logdet, latents.swapaxes(1, 2), valid, patch_weight, pos_table, ln1_gain,
        ln1_bias, ln2_gain, ln2_bias, up_bias, head_weight.T, head_bias[None], cot_latents.swapaxes(1, 2), class_table,
        qkv_weight, out_weight, up_weight, down_weight,
    )
    results = list(finish(class_labels[None], sums))
    results[1] = results[1].reshape(1)
    results[16] = results[16].reshape(96)
    results[0], results[2] = results[0].swapaxes(1, 2), results[2].swapaxes(1, 2)
    results[15] = results[15].T
    return tuple(results)


def forward(latents, valid, class_rows, seq_place, weights):
    (
        patch_weight,
        pos_table,
        qkv_weight,
        out_weight,
        ln1_gain,
        ln1_bias,
        ln2_gain,
        ln2_bias,
        up_weight,
        up_bias,
        down_weight,
        head_weight,
        head_bias,
    ) = weights
    images, patch_rows, channels = latents.shape
    model_width = qkv_weight.shape[1]
    head_count = model_width // HEAD_DIM
    latent_low = latents.astype(jnp.bfloat16)
    hidden = (
        matmul(latent_low, patch_weight)
        + pos_table.astype(jnp.float32)[None]
        + class_rows[:, None, :]
    )
    own_mask = valid.astype(jnp.bfloat16)
    normed = layer_norm(
        hidden, ln1_gain[0].astype(jnp.float32), ln1_bias[0].astype(jnp.float32)
    ).astype(jnp.bfloat16)
    packed = matmul(normed, qkv_weight[0]).astype(jnp.bfloat16)
    query = packed[..., :model_width].reshape(images, patch_rows, head_count, HEAD_DIM)
    keys_own = packed[..., model_width : 2 * model_width]
    values_own = packed[..., 2 * model_width :]
    prior_keys, prior_values, prior_mask = shifted_2((keys_own, values_own, own_mask), "seq", 1)
    keys = jnp.concatenate((prior_keys, keys_own), 1).reshape(
        images, 2 * patch_rows, head_count, HEAD_DIM
    )
    values = jnp.concatenate((prior_values, values_own), 1).reshape(
        images, 2 * patch_rows, head_count, HEAD_DIM
    )
    allowed = attention_mask(jnp.concatenate((prior_mask, own_mask), 1), patch_rows, seq_place)
    logits = masked_scores(query, keys, allowed)
    row_peak = jnp.max(logits, -1, keepdims=True)
    log_total = row_peak + jnp.log(jnp.sum(jnp.exp(logits - row_peak), -1, keepdims=True))
    weights_soft = jnp.exp(logits - log_total).astype(jnp.bfloat16)
    attended = jnp.einsum(
        "bhqk,bkhd->bqhd", weights_soft, values, preferred_element_type=jnp.float32
    )
    attended = attended.astype(jnp.bfloat16).reshape(images, patch_rows, model_width)
    mid = hidden + matmul(attended, out_weight[0])
    second = layer_norm(
        mid, ln2_gain[0].astype(jnp.float32), ln2_bias[0].astype(jnp.float32)
    ).astype(jnp.bfloat16)
    preact = matmul(second, up_weight[0]) + up_bias[0].astype(jnp.float32)
    activated = jax.nn.gelu(preact, approximate=True).astype(jnp.bfloat16)
    saved = [
        (
            hidden,
            normed,
            query,
            keys,
            values,
            allowed,
            log_total,
            attended,
            mid,
            second,
            preact,
            activated,
        )
    ]
    hidden = mid + matmul(activated, down_weight[0])
    top_low = hidden.astype(jnp.bfloat16)
    head_out = matmul(top_low, head_weight) + head_bias.astype(jnp.float32)
    prior_row = shifted_2(head_out[:, patch_rows - 1, :], "seq", 1)
    shifted = jnp.concatenate((prior_row[:, None, :], head_out[:, : patch_rows - 1, :]), 1)
    shifted = shifted * valid.astype(jnp.float32)[..., None]
    alpha = shifted[..., :channels]
    shift_mean = shifted[..., channels:]
    factor = jnp.exp(-alpha)
    new_latents = (latents - shift_mean) * factor
    logdet_part = -jnp.sum(alpha, (1, 2))
    return (new_latents, logdet_part, factor, top_low, saved)


def local(
    latents,
    valid,
    class_labels,
    group_perm,
    patch_weight,
    pos_table,
    class_table,
    ln1_gain,
    ln1_bias,
    qkv_weight,
    out_weight,
    ln2_gain,
    ln2_bias,
    up_weight,
    up_bias,
    down_weight,
    head_weight,
    head_bias,
    cot_latents,
    cot_logdet,
):
    images, patch_rows, channels = latents.shape
    model_width = qkv_weight.shape[1]
    head_count = model_width // HEAD_DIM
    layer_total = qkv_weight.shape[0]
    seq_place = lax.axis_index("seq")
    picks = group_perm[:, None] == lax.iota(jnp.int32, class_labels.shape[0])[None, :]
    image_labels = jnp.sum(jnp.where(picks, class_labels[None, :], 0), 1)
    label_hot = image_labels[:, None] == lax.iota(jnp.int32, class_table.shape[0])[None, :]
    class_rows = matmul(label_hot.astype(jnp.bfloat16), class_table)
    weights = (
        patch_weight,
        pos_table,
        qkv_weight,
        out_weight,
        ln1_gain,
        ln1_bias,
        ln2_gain,
        ln2_bias,
        up_weight,
        up_bias,
        down_weight,
        head_weight,
        head_bias,
    )
    new_latents, logdet_part, factor, top_low, saved = forward(
        latents, valid, class_rows, seq_place, weights
    )
    valid_float = valid.astype(jnp.float32)
    d_alpha = -cot_latents * new_latents - cot_logdet[:, None, None]
    d_mean = -cot_latents * factor
    d_shifted = jnp.concatenate((d_alpha, d_mean), -1) * valid_float[..., None]
    next_row = shifted_2(d_shifted[:, 0, :], "seq", -1)
    d_head = jnp.concatenate((d_shifted[:, 1:, :], next_row[:, None, :]), 1).astype(jnp.bfloat16)
    head_weight_grad = outer_sum(top_low, d_head)
    head_bias_grad = jnp.sum(d_head.astype(jnp.float32), (0, 1))
    d_hidden = transposed(d_head, head_weight)
    grads_qkv, grads_out, grads_up, grads_down = ([], [], [], [])
    grads_g1, grads_b1, grads_g2, grads_b2, grads_ub = ([], [], [], [], [])
    for layer_index in reversed(range(layer_total)):
        (
            hidden,
            normed,
            query,
            keys,
            values,
            allowed,
            log_total,
            attended,
            mid,
            second,
            preact,
            activated,
        ) = saved[layer_index]
        d_down = d_hidden.astype(jnp.bfloat16)
        down_grad = outer_sum(activated, d_down)
        d_act = transposed(d_down, down_weight[layer_index])
        unused_gelu, gelu_pull = jax.vjp(lambda inner: jax.nn.gelu(inner, approximate=True), preact)
        d_pre = gelu_pull(d_act)[0].astype(jnp.bfloat16)
        up_bias_grad = jnp.sum(d_pre.astype(jnp.float32), (0, 1))
        up_grad = outer_sum(second, d_pre)
        d_second = transposed(d_pre, up_weight[layer_index])
        unused_norm, norm_pull = jax.vjp(
            layer_norm,
            mid,
            ln2_gain[layer_index].astype(jnp.float32),
            ln2_bias[layer_index].astype(jnp.float32),
        )
        d_mid_norm, ln2_gain_part, ln2_bias_part = norm_pull(d_second)
        d_mid = d_hidden + d_mid_norm
        d_proj = d_mid.astype(jnp.bfloat16)
        out_grad = outer_sum(attended, d_proj)
        d_attended = transposed(d_proj, out_weight[layer_index]).astype(jnp.bfloat16)
        d_attended = d_attended.reshape(images, patch_rows, head_count, HEAD_DIM)
        logits = masked_scores(query, keys, allowed)
        probs = jnp.exp(logits - log_total)
        d_probs = jnp.einsum(
            "bqhd,bkhd->bhqk", d_attended, values, preferred_element_type=jnp.float32
        )
        d_scores = (probs * (d_probs - jnp.sum(d_probs * probs, -1, keepdims=True))).astype(
            jnp.bfloat16
        )
        d_query = jnp.einsum(
            "bhqk,bkhd->bqhd", d_scores, keys, preferred_element_type=jnp.float32
        ) * HEAD_DIM ** (-0.5)
        d_keys = jnp.einsum(
            "bhqk,bqhd->bkhd", d_scores, query, preferred_element_type=jnp.float32
        ) * HEAD_DIM ** (-0.5)
        d_values = jnp.einsum(
            "bhqk,bqhd->bkhd",
            probs.astype(jnp.bfloat16),
            d_attended,
            preferred_element_type=jnp.float32,
        )
        d_keys = d_keys.reshape(images, 2 * patch_rows, model_width)
        d_values = d_values.reshape(images, 2 * patch_rows, model_width)
        back_keys, back_values = (
            shifted_2(d_keys[:, :patch_rows].astype(jnp.bfloat16), "seq", -1).astype(jnp.float32),
            shifted_2(d_values[:, :patch_rows].astype(jnp.bfloat16), "seq", -1).astype(jnp.float32),
        )
        d_packed = jnp.concatenate(
            (
                d_query.reshape(images, patch_rows, model_width),
                d_keys[:, patch_rows:] + back_keys,
                d_values[:, patch_rows:] + back_values,
            ),
            -1,
        ).astype(jnp.bfloat16)
        qkv_grad = outer_sum(normed, d_packed)
        d_normed = transposed(d_packed, qkv_weight[layer_index])
        unused_norm, norm_pull = jax.vjp(
            layer_norm,
            hidden,
            ln1_gain[layer_index].astype(jnp.float32),
            ln1_bias[layer_index].astype(jnp.float32),
        )
        d_input, ln1_gain_part, ln1_bias_part = norm_pull(d_normed)
        d_hidden = d_mid + d_input
        grads_qkv.insert(0, qkv_grad)
        grads_out.insert(0, out_grad)
        grads_up.insert(0, up_grad)
        grads_down.insert(0, down_grad)
        grads_g1.insert(0, ln1_gain_part)
        grads_b1.insert(0, ln1_bias_part)
        grads_g2.insert(0, ln2_gain_part)
        grads_b2.insert(0, ln2_bias_part)
        grads_ub.insert(0, up_bias_grad)
    d_embed_low = d_hidden.astype(jnp.bfloat16)
    patch_grad_part = outer_sum(latents.astype(jnp.bfloat16), d_embed_low)
    latents_grad = cot_latents * factor + transposed(d_embed_low, patch_weight)
    pos_part = jnp.sum(d_hidden, 0)
    class_part = jnp.sum(d_hidden, 1)
    logdet, class_sums = lax.psum((logdet_part, class_part), "seq")
    class_term = lax.dot_general(
        label_hot.astype(jnp.float32),
        class_sums,
        (((0,), (0,)), ((), ())),
        precision=precise,
        preferred_element_type=jnp.float32,
    )
    class_grad = lax.psum_scatter(class_term, "dp", scatter_dimension=0, tiled=True)
    pos_grad = lax.psum(pos_part, "dp")
    (
        patch_weight_grad,
        head_weight_grad,
        head_bias_grad,
        ln1_gain_grad,
        ln1_bias_grad,
        ln2_gain_grad,
        ln2_bias_grad,
        up_bias_grad,
    ) = lax.psum(
        (
            patch_grad_part,
            head_weight_grad,
            head_bias_grad,
            jnp.stack(grads_g1),
            jnp.stack(grads_b1),
            jnp.stack(grads_g2),
            jnp.stack(grads_b2),
            jnp.stack(grads_ub),
        ),
        ("dp", "seq"),
    )
    qkv_stack = jnp.stack(grads_qkv)
    out_stack = jnp.stack(grads_out)
    up_stack = jnp.stack(grads_up)
    down_stack = jnp.stack(grads_down)
    flat_parts = (
        lax.psum_scatter(eight_rows(qkv_stack), ("dp", "seq"), scatter_dimension=1, tiled=True),
        lax.psum_scatter(eight_rows(out_stack), ("dp", "seq"), scatter_dimension=1, tiled=True),
        lax.psum_scatter(eight_rows(up_stack), ("dp", "seq"), scatter_dimension=1, tiled=True),
        lax.psum_scatter(eight_rows(down_stack), ("dp", "seq"), scatter_dimension=1, tiled=True),
    )
    flat_qkv, flat_out, flat_up, flat_down = (
        lax.all_gather(
            flat_parts[0].astype(jnp.bfloat16), ("dp", "seq"), axis=1, tiled=True
        ).astype(jnp.float32),
        lax.all_gather(
            flat_parts[1].astype(jnp.bfloat16), ("dp", "seq"), axis=1, tiled=True
        ).astype(jnp.float32),
        lax.all_gather(
            flat_parts[2].astype(jnp.bfloat16), ("dp", "seq"), axis=1, tiled=True
        ).astype(jnp.float32),
        lax.all_gather(
            flat_parts[3].astype(jnp.bfloat16), ("dp", "seq"), axis=1, tiled=True
        ).astype(jnp.float32),
    )
    qkv_stack = flat_qkv.reshape(qkv_stack.shape)
    out_stack = flat_out.reshape(out_stack.shape)
    up_stack = flat_up.reshape(up_stack.shape)
    down_stack = flat_down.reshape(down_stack.shape)
    return (
        new_latents,
        logdet,
        latents_grad,
        patch_weight_grad,
        pos_grad,
        class_grad,
        ln1_gain_grad,
        ln1_bias_grad,
        qkv_stack,
        out_stack,
        ln2_gain_grad,
        ln2_bias_grad,
        up_stack,
        up_bias_grad,
        down_stack,
        head_weight_grad,
        head_bias_grad,
    )


def solution(mesh):
    in_specs = (
        P("dp", "seq", None),
        P("dp", "seq"),
        P(),
        P("dp"),
        P(),
        P("seq", None),
        P(),
        P(),
        P(),
        P(),
        P(),
        P(),
        P(),
        P(),
        P(),
        P(),
        P(),
        P(),
        P("dp", "seq", None),
        P("dp"),
    )
    out_specs = (
        P("dp", "seq", None),
        P("dp"),
        P("dp", "seq", None),
        P(),
        P("seq", None),
        P("dp", None),
        P(),
        P(),
        P(),
        P(),
        P(),
        P(),
        P(),
        P(),
        P(),
        P(),
        P(),
    )
    body = fast_local if mesh.shape["dp"] == 16 and mesh.shape["seq"] == 2 else local
    return jax.shard_map(body, mesh=mesh, in_specs=in_specs, out_specs=out_specs, check_vma=False)
```

```python
import jax
import jax.numpy as jnp
from jax import lax
from jax.experimental import pallas as pl
from jax.experimental.pallas import tpu as pltpu
from jax.sharding import PartitionSpec as P

HEAD_DIM = 64


precise = lax.Precision.HIGHEST
norm_eps = 1e-05


def shifted_2(shard, axis, by):
    size = lax.axis_size(axis)
    pairs = [(i, i + by) for i in range(size) if 0 <= i + by < size]
    return lax.ppermute(shard, axis, pairs)


def layer_norm(values, norm_gain, norm_bias):
    center = values - jnp.mean(values, -1, keepdims=True)
    spread = jnp.mean(center * center, -1, keepdims=True)
    return center * lax.rsqrt(spread + norm_eps) * norm_gain + norm_bias


def matmul(left_side, weight_mat):
    return jnp.dot(left_side, weight_mat, preferred_element_type=jnp.float32)


def outer_sum(left_side, grad_side):
    left_flat = left_side.reshape(-1, left_side.shape[-1])
    grad_flat = grad_side.reshape(-1, grad_side.shape[-1])
    return lax.dot_general(
        left_flat, grad_flat, (((0,), (0,)), ((), ())), preferred_element_type=jnp.float32
    )


def transposed(grad_side, weight_mat):
    return lax.dot_general(
        grad_side,
        weight_mat,
        (((grad_side.ndim - 1,), (1,)), ((), ())),
        preferred_element_type=jnp.float32,
    )


def eight_rows(matrix):
    return matrix.reshape(8, -1)


def attention_mask(key_valid, patch_rows, seq_place):
    query_pos = seq_place * patch_rows + lax.iota(jnp.int32, patch_rows)
    key_pos = (seq_place - 1) * patch_rows + lax.iota(jnp.int32, 2 * patch_rows)
    earlier = (key_pos[None, :] < query_pos[:, None])[None] & (key_valid[:, None, :] > 0)
    return earlier | (key_pos[None, :] == query_pos[:, None])[None]


def masked_scores(query, keys, allowed):
    logits = jnp.einsum(
        "bqhd,bkhd->bhqk", query, keys, preferred_element_type=jnp.float32
    ) * HEAD_DIM ** (-0.5)
    return jnp.where(allowed[:, None], logits, -1e30)


MESH = pl.DeviceIdType.MESH
OUTS = 3
UNITS = 27
LAST = 28
THIRD = 18
TURNS = 8
STEPS = 44
DRAIN = 17
DRAIN_C = 18
SLAB = 128
LABELS = 448
TABLE_ROWS = ((0, 256), (256, 192))
COLS = 384
STAGES = 3
CHUNK = 32
GELU_A = (2.0 / 3.141592653589793) ** 0.5
GELU_B = 0.044715
f32 = jnp.float32
bf16 = jnp.bfloat16


def flow_kernel(
    labels_sm, perm_sm, cot_logdet_sm,
    latents_ref, valid_ref, patch_ref, pos_table_ref, g1_ref, b1_ref, g2_ref, b2_ref,
    up_bias_ref, head_w_ref, head_b_ref, cot_ref,
    class_hbm, qkv_any, out_any, up_any, down_any,
    sums,
    stage, part, part_c, out_stage, out_in, core_in, small_in, ab_in, c_in, shared,
    down_left, down_right, up_left, up_right, bulk_send, bulk_recv, send_sem, recv_sem, stage_sem, back_sem, send_c, back_c, out_send, out_recv,
    qkv_w, out_w, up_w, down_w, load_sem,
    lat_pad, cot_pad, patch_pad, head_pad, hidden, mid, xhat1, xhat2, scale1, scale2,
    keys, values, query, attended, bias, prior_mask, mask_row, probs, slope, d_hidden, d_second, d_att, d_keys, d_values,
    d_prior, d_back, row_out, row_in, peek_out, peek_in, factor,
    lines, line_sum, line_in, line_send, line_recv,
    lt_ref, r_ref, pos_ref, small_ref, low_top, exch_send, exch_recv,
):
    dp = lax.axis_index("dp")
    core = lax.axis_index("seq")
    x, y, z = dp % 2, (dp // 2) % 2, dp // 4
    side = z // 2
    inner = ((z + 1) // 2) % 2 == 1
    outer = ((z + 1) // 2) % 2 == 0
    to_core = (dp, 1 - core)
    to_x = (dp + 1 - 2 * x, core)
    to_y = (dp + 2 - 4 * y, core)
    to_mate = (dp + 4 - 8 * (z % 2), core)
    to_x_other = (dp + 1 - 2 * x, 1 - core)
    to_y_other = (dp + 2 - 4 * y, 1 - core)
    to_inner = ((dp + 12 - 8 * z + 16) % 16, core)

    def rows_at(start, count):
        return pl.ds(pl.multiple_of(start, 16), count)

    sources = [class_hbm.at[r : r + n, h * COLS : (h + 1) * COLS] for h in range(2) for r, n in TABLE_ROWS]
    targets = [part.at[3 * h + i, 0:n] for h in range(2) for i, (r, n) in enumerate(TABLE_ROWS)]
    sources += [qkv_any.at[0], out_any.at[0]]
    targets += [qkv_w, out_w]

    def load(i):
        return pltpu.make_async_copy(sources[i], targets[i], load_sem.at[i])

    def load_feed(j):
        cols = rows = pl.ds(pl.multiple_of(j * 768, 128), 768)
        return (
            pltpu.make_async_copy(up_any.at[0, :, cols], up_w.at[:, cols], load_sem.at[6 + 2 * j]),
            pltpu.make_async_copy(down_any.at[0, rows], down_w.at[rows], load_sem.at[7 + 2 * j]),
        )

    for i in range(6):
        load(i).start()
    for j in range(4):
        for one in load_feed(j):
            one.start()

    barrier = pltpu.get_barrier_semaphore()
    for target in (to_core, to_x, to_y, to_mate, to_x_other, to_y_other):
        pl.semaphore_signal(barrier, inc=1, device_id=target, device_id_type=MESH)

    @pl.when(inner)
    def _():
        pl.semaphore_signal(barrier, inc=1, device_id=to_inner, device_id_type=MESH)

    def meet():
        @pl.when(inner)
        def _():
            pl.semaphore_wait(barrier, 7)

        @pl.when(outer)
        def _():
            pl.semaphore_wait(barrier, 6)

    def copy(u, k, src, dst, target):
        return pltpu.make_async_remote_copy(
            src_ref=src, dst_ref=dst, send_sem=send_sem.at[u], recv_sem=recv_sem.at[k, u % TURNS],
            device_id=target, device_id_type=MESH,
        )

    def copy_c(u, k, src, dst, target):
        return pltpu.make_async_remote_copy(
            src_ref=src, dst_ref=dst, send_sem=send_c.at[u], recv_sem=recv_sem.at[k, u % TURNS],
            device_id=target, device_id_type=MESH,
        )

    def arrived(u, k, dst):
        pltpu.make_async_remote_copy(
            src_ref=dst, dst_ref=dst, send_sem=send_sem.at[0], recv_sem=recv_sem.at[k, u % TURNS],
            device_id=to_core, device_id_type=MESH,
        ).wait_recv()

    def added(dst, left, right):
        dst[...] = (left[...].astype(f32) + right[...].astype(f32)).astype(bf16)

    first = (x, y)
    second = (y, x)
    to_first = (to_x, to_y)
    to_second = (to_y, to_x)

    def out_rows(u, t, start, count):
        return third_rows(u, core, start, count) if t == 2 else sums.at[u, core, rows_at(t * SLAB + start, count)]

    def third_rows(u, h, start, count):
        return sums.at[LAST + 1 + u // 2, h, rows_at((u % 2) * SLAB + start, count)]

    def part_rows(u, t, start, count):
        return part_c.at[u, rows_at(start, count)] if t == 2 else part.at[u, rows_at(t * SLAB + start, count)]

    def bulk(k, src, dst, target):
        return pltpu.make_async_remote_copy(
            src_ref=src, dst_ref=dst, send_sem=bulk_send.at[k], recv_sem=bulk_recv.at[k],
            device_id=target, device_id_type=MESH,
        )

    def down_rows(i):
        return pl.ds(pl.multiple_of(i * 768, 128), 768)

    def down_left_core(i):
        return bulk(i, down_left.at[down_rows(i), 0:128], down_left.at[down_rows(i), 128:256], to_core)

    def down_left_x(i):
        return bulk(2 + i, lt_ref.at[i], down_left.at[down_rows(i), 256:384], to_x)

    def down_left_on(i):
        return bulk(4 + i, down_left.at[down_rows(i), 256:384], down_left.at[down_rows(i), 384:512], to_core)

    def down_right_go(i):
        half, target = ((1 - core, to_core), (core, to_x), (1 - core, to_x_other))[i]
        return bulk(6 + i, r_ref.at[0, half], down_right.at[128 * (i + 1) : 128 * (i + 2)], target)

    def up_left_go(i):
        first_lane, target = ((0, to_core), (0, to_y), (256, to_core))[i]
        return bulk(
            9 + i,
            up_left.at[:, first_lane : first_lane + 128],
            up_left.at[:, 128 * (i + 1) : 128 * (i + 2)],
            target,
        )

    def up_right_go(i, j):
        target = (to_core, to_y, to_y_other)[i]
        return bulk(12 + i, r_ref.at[1 + j], up_right.at[:, 128 * (i + 1) : 128 * (i + 2)], target)

    def pass_on(i):
        down_left_x(i).wait_recv()
        down_left_on(i).start()

    def begin_ab(unit):
        u = unit - OUTS

        @pl.when(u == 0)
        def _():
            for i in range(3):
                down_right_go(i).wait_recv()
                up_right_go(i, 0).wait_recv()
            up_left_go(0).wait_recv()
            up_left_go(2).wait_recv()
            down_left_core(0).wait_recv()
            down_left_on(0).wait_recv()

        @pl.when(u == 12)
        def _():
            down_left_core(1).wait_recv()
            down_left_on(1).wait_recv()

        @pl.when(jnp.logical_and(u >= 0, unit < UNITS))
        def _():
            rows = pl.ds(pl.multiple_of(u * 64, 64), 64)
            kept = part_rows(unit, 0, x * 64, 64)
            kept[...] = jnp.dot(down_left[rows], down_right[...], preferred_element_type=f32).astype(bf16)
            ab_second(unit, 0).start()
            rows = pl.ds(pl.multiple_of((u // 2) * 64, 64), 64)
            kept = part_rows(unit, 1, y * 64, 64)
            kept[...] = jnp.dot(up_left[rows], up_right[u % 2], preferred_element_type=f32).astype(bf16)
            ab_second(unit, 1).start()

    def product(u, half):
        rows = pl.ds(pl.multiple_of((u % 6) * SLAB, 128), SLAB)
        return jnp.dot(lt_ref[6, rows], r_ref[6 + u // 6, half], preferred_element_type=f32)

    def out_product(u, half):
        rows = pl.ds(pl.multiple_of(u * 256, 256), 256)
        return jnp.dot(lt_ref[5, rows], r_ref[5, half], preferred_element_type=f32)

    def out_first(u):
        return pltpu.make_async_remote_copy(
            src_ref=out_stage.at[u], dst_ref=out_in.at[u], send_sem=out_send.at[u], recv_sem=out_recv.at[u],
            device_id=to_core, device_id_type=MESH,
        )

    def core_first(u):
        return pltpu.make_async_remote_copy(
            src_ref=stage.at[u % STAGES], dst_ref=core_in.at[u % TURNS], send_sem=stage_sem.at[u % STAGES],
            recv_sem=recv_sem.at[0, u % TURNS], device_id=to_core, device_id_type=MESH,
        )

    def small_first():
        return pltpu.make_async_remote_copy(
            src_ref=small_ref.at[1 - core], dst_ref=small_in, send_sem=stage_sem.at[STAGES],
            recv_sem=recv_sem.at[0, LAST % TURNS], device_id=to_core, device_id_type=MESH,
        )

    def line_copy(k, src, dst, target):
        return pltpu.make_async_remote_copy(
            src_ref=src, dst_ref=dst, send_sem=line_send.at[k], recv_sem=line_recv.at[k],
            device_id=target, device_id_type=MESH,
        )

    line_steps = (
        (lines, line_in.at[0], to_core),
        (line_sum.at[0], line_in.at[1], to_x),
        (line_sum.at[1], line_in.at[2], to_y),
        (line_sum.at[2], line_in.at[3], to_mate),
        (line_sum.at[3], line_in.at[4], to_inner),
        (line_sum.at[4], line_sum.at[4], to_mate),
    )

    def line_go(k):
        return line_copy(k, *line_steps[k])

    def line_add(k):
        line_go(k).wait_recv()
        line_sum[k] = line_steps[k][0][...] + line_in[k]

    def keep_lines():
        v = line_sum[4]
        for i in range(3):
            term = v.astype(bf16)
            v = v - term.astype(f32)
            for h in range(2):
                sums[LAST + 1 + THIRD // 2, h, 64 + i * 16 : 80 + i * 16] = term[:, h * COLS : (h + 1) * COLS]

    def produce(u):
        pl.when(u >= STAGES)(lambda: core_first(u - STAGES).wait_send())
        stage[u % STAGES] = product(u, 1 - core).astype(bf16)
        core_first(u).start()

    def begin(u):
        arrived(u, 0, core_in.at[u % TURNS])
        part_c[u] = (product(u, core) + core_in[u % TURNS].astype(f32)).astype(bf16)
        pl.when(outer)(lambda: c_z1(u).start())

    def begin_more(u):
        @pl.when(u < OUTS)
        def _():
            out_first(u).wait_recv()
            part[u] = (out_product(u, core) + out_in[u].astype(f32)).astype(bf16)
            for t in range(2):
                ab_first(u, t).start()

        @pl.when(u == UNITS)
        def _():
            part[UNITS] = pos_ref[...]
            for t in range(2):
                ab_first(u, t).start()
            small_first().start()
            line_go(0).start()

        @pl.when(u == LAST)
        def _():
            small_first().wait_recv()
            part[LAST] = (small_ref[core].astype(f32) + small_in[...].astype(f32)).astype(bf16)
            for t in range(2):
                ab_first(u, t).start()
            line_add(0)
            line_go(1).start()

    def ab_base(t):
        return first[t] * 64 + second[t] * 32

    def ab_first(u, t):
        return copy(u, 1, part_rows(u, t, (1 - first[t]) * 64, 64), ab_in.at[u % TURNS, t, 0:64], to_first[t])

    def ab_second(u, t):
        row = first[t] * 64 + (1 - second[t]) * 32
        return copy(u, 2, part_rows(u, t, row, 32), ab_in.at[u % TURNS, t, 64:96], to_second[t])

    def ab_z1(u, t):
        return copy(u, 3, part_rows(u, t, ab_base(t), 32), ab_in.at[u % TURNS, t, 96:128], to_mate)

    def ab_z2(u, t):
        return copy(u, 4, part_rows(u, t, ab_base(t), 32), ab_in.at[u % TURNS, t, 128:160], to_inner)

    def ab_z3(u, t):
        block = out_rows(u, t, ab_base(t), 32)
        return copy(u, 3, block, block, to_mate)

    def ab_back2(u, t):
        block = out_rows(u, t, ab_base(t), 32)
        return copy(u, 5, block, block, to_second[t])

    def ab_back1(u, t):
        block = out_rows(u, t, first[t] * 64, 64)
        return copy(u, 6, block, block, to_first[t])

    def ab1(u):
        pl.when(jnp.logical_or(u < OUTS, u >= UNITS))(lambda: ab1_more(u))

    def ab1_more(u):
        arrived(u, 1, ab_in.at[u % TURNS, :, 0:64])
        for t in range(2):
            kept = part_rows(u, t, first[t] * 64, 64)
            added(kept, kept, ab_in.at[u % TURNS, t, 0:64])
            ab_second(u, t).start()

        @pl.when(u == LAST)
        def _():
            line_add(1)
            line_go(2).start()

    def ab2(u):
        arrived(u, 2, ab_in.at[u % TURNS, :, 64:96])
        for t in range(2):
            kept = part_rows(u, t, ab_base(t), 32)
            added(kept, kept, ab_in.at[u % TURNS, t, 64:96])
            pl.when(outer)(lambda: ab_z1(u, t).start())

        @pl.when(u == LAST)
        def _():
            line_add(2)
            pl.when(outer)(line_go(3).start)

    def ab3_inner(u):
        arrived(u, 3, ab_in.at[u % TURNS, :, 96:128])
        for t in range(2):
            kept = part_rows(u, t, ab_base(t), 32)
            added(kept, kept, ab_in.at[u % TURNS, t, 96:128])
            ab_z2(u, t).start()

        @pl.when(u == LAST)
        def _():
            line_add(3)
            line_go(4).start()

    def ab4_inner(u):
        arrived(u, 4, ab_in.at[u % TURNS, :, 128:160])
        for t in range(2):
            added(out_rows(u, t, ab_base(t), 32), part_rows(u, t, ab_base(t), 32), ab_in.at[u % TURNS, t, 128:160])
            ab_z3(u, t).start()
            ab_back2(u, t).start()

        @pl.when(u == LAST)
        def _():
            line_add(4)
            line_go(5).start()
            keep_lines()

    def ab5_outer(u):
        arrived(u, 3, sums.at[u, core, 0:64])
        for t in range(2):
            ab_back2(u, t).start()

        @pl.when(u == LAST)
        def _():
            line_go(5).wait_recv()
            keep_lines()

    def ab6(u):
        arrived(u, 5, sums.at[u, core, 0:64])
        for t in range(2):
            ab_back1(u, t).start()

    def to_other(u, block):
        return pltpu.make_async_remote_copy(
            src_ref=block, dst_ref=block, send_sem=send_sem.at[u], recv_sem=back_sem.at[u],
            device_id=to_core, device_id_type=MESH,
        )

    def to_other_c(u, half):
        block = third_rows(u, half, 0, SLAB)
        return pltpu.make_async_remote_copy(
            src_ref=block, dst_ref=block, send_sem=send_c.at[u], recv_sem=back_c.at[u],
            device_id=to_core, device_id_type=MESH,
        )

    def ab7(u):
        arrived(u, 6, sums.at[u, core, 0:128])
        pl.when(u != UNITS)(lambda: to_other(u, sums.at[u, core]).start())

    far = 32 * (1 - side)
    own_end = 96 * side
    shard = z * 32

    def c_z1(u):
        return copy_c(u, 7, part_rows(u, 2, far, 96), c_in.at[u % TURNS, 0:96], to_mate)

    def c_z2(u):
        return copy_c(u, 8, part_rows(u, 2, (1 - side) * 64, 64), c_in.at[u % TURNS, 96:160], to_inner)

    def c_z3(u):
        return copy_c(u, 7, part_rows(u, 2, own_end, 32), c_in.at[u % TURNS, 160:192], to_mate)

    def c_x(u):
        return copy_c(u, 9, part_rows(u, 2, shard, 32), c_in.at[u % TURNS, 192:224], to_x)

    def c_y(u):
        return copy_c(u, 10, shared.at[u], c_in.at[u % TURNS, 224:256], to_y)

    def c_z4(u):
        block = out_rows(u, 2, own_end, 32)
        return copy_c(u, 12, block, block, to_mate)

    def c_z5(u):
        block = out_rows(u, 2, side * 64, 64)
        return copy_c(u, 13, block, block, to_inner)

    def c_z6(u):
        block = out_rows(u, 2, far, 96)
        return copy_c(u, 12, block, block, to_mate)

    def c1_inner(u):
        arrived(u, 7, c_in.at[u % TURNS, 0:96])
        kept = part_rows(u, 2, far, 96)
        added(kept, kept, c_in.at[u % TURNS, 0:96])
        c_z2(u).start()

    def c2_inner(u):
        arrived(u, 8, c_in.at[u % TURNS, 96:160])
        kept = part_rows(u, 2, side * 64, 64)
        added(kept, kept, c_in.at[u % TURNS, 96:160])
        c_z3(u).start()
        c_x(u).start()

    def c3_outer(u):
        arrived(u, 7, c_in.at[u % TURNS, 160:192])
        kept = part_rows(u, 2, shard, 32)
        added(kept, kept, c_in.at[u % TURNS, 160:192])
        c_x(u).start()

    def c4(u):
        arrived(u, 9, c_in.at[u % TURNS, 192:224])
        kept = part_rows(u, 2, shard, 32)
        part_y = shared.at[u]
        added(part_y, kept, c_in.at[u % TURNS, 192:224])
        c_y(u).start()

    def c5(u):
        arrived(u, 10, c_in.at[u % TURNS, 224:256])
        added(out_rows(u, 2, shard, 32), shared.at[u], c_in.at[u % TURNS, 224:256])
        pl.when(outer)(lambda: c_z4(u).start())

    def c8_inner(u):
        arrived(u, 12, out_rows(u, 2, own_end, 32))
        c_z5(u).start()

    def c9_inner(u):
        arrived(u, 13, out_rows(u, 2, (1 - side) * 64, 64))
        c_z6(u).start()
        to_other_c(u, core).start()

    def c10_outer(u):
        arrived(u, 12, out_rows(u, 2, far, 96))
        to_other_c(u, core).start()

    def sent(sem, units, rows):
        ref = part.at[0:units, 0:rows]
        pltpu.make_async_remote_copy(
            src_ref=ref, dst_ref=ref, send_sem=sem, recv_sem=back_sem.at[0],
            device_id=to_core, device_id_type=MESH,
        ).wait_send()

    def sent_either(sem, at_outer, at_inner):
        pl.when(outer)(lambda: sent(sem, *at_outer))
        pl.when(inner)(lambda: sent(sem, *at_inner))

    def drain(u):
        pl.when(u < OUTS)(lambda: sent_either(send_sem.at[u], (4, 176), (3, 256)))
        pl.when(u >= OUTS)(lambda: sent_either(send_sem.at[u], (4, 144), (4, 160)))
        to_other(u, sums.at[u, 1 - core]).wait_recv()

    def drain_c(u):
        sent_either(send_c.at[u], (2, 160), (2, 224))
        to_other_c(u, 1 - core).wait_recv()

    mm_nt = (((1,), (1,)), ((), ()))
    mm_tn = (((0,), (0,)), ((), ()))

    def nt(left, right):
        return lax.dot_general(left, right, mm_nt, preferred_element_type=f32)

    def tn(left, right):
        return lax.dot_general(left, right, mm_tn, preferred_element_type=f32)

    def nn(left, right):
        return jnp.dot(left, right, preferred_element_type=f32)

    def exchange(k, src, dst):
        return pltpu.make_async_remote_copy(
            src_ref=src, dst_ref=dst, send_sem=exch_send.at[k], recv_sem=exch_recv.at[k],
            device_id=to_core, device_id_type=MESH,
        )

    chunks = [slice(r, r + CHUNK) for r in range(0, 128, CHUNK)]
    lane = lax.broadcasted_iota(jnp.int32, (128, 128), 1)
    row = lax.broadcasted_iota(jnp.int32, (128, 128), 0)
    eye = row == lane
    low_half = lane < 64
    valid_row = valid_ref[...].astype(f32)
    valid_col = jnp.sum(jnp.where(eye, valid_row, 0.0), axis=1, keepdims=True)
    mask_row[...] = jnp.broadcast_to(valid_row, (8, 128))
    lat_pad[...] = jnp.zeros((128, 128), f32)
    lat_pad[0:48] = latents_ref[0]
    lat_pad[...] = lat_pad[...].T
    cot_pad[...] = jnp.zeros((128, 128), f32)
    cot_pad[0:48] = cot_ref[0]
    cot_pad[...] = cot_pad[...].T
    patch_pad[...] = jnp.zeros((128, 768), bf16)
    patch_pad[0:48] = patch_ref[...]
    head_pad[...] = jnp.zeros((128, 768), bf16)
    head_pad[0:96] = head_w_ref[...]
    head_bias = jnp.concatenate((head_b_ref[...].astype(f32), jnp.zeros((1, 32), f32)), 1)

    @pl.when(core == 0)
    def _():
        keys[0:128] = jnp.zeros((128, 768), bf16)
        values[0:128] = jnp.zeros((128, 768), bf16)
        prior_mask[...] = jnp.zeros((8, 128), f32)
        row_in[...] = jnp.zeros((8, 128), f32)

    @pl.when(core == 1)
    def _():
        peek_in[...] = jnp.zeros((8, 128), f32)
        d_back[...] = jnp.zeros((2, 128, 768), bf16)

    line8 = lax.broadcasted_iota(jnp.int32, (8, 128), 0)
    peek_out[...] = jnp.where(line8 == 0, lat_pad[0:1], jnp.where(line8 == 1, cot_pad[0:1], valid_row[:, 0:1]))

    def normalize(src, hat, scale, gain, shift, put):
        for r in chunks:
            v = src[r]
            center = v - jnp.mean(v, -1, keepdims=True)
            inv = lax.rsqrt(jnp.mean(center * center, -1, keepdims=True) + norm_eps)
            scaled = center * inv
            hat[r] = scaled
            scale[r] = inv
            put(r, scaled * gain + shift)

    label = labels_sm[perm_sm[0]]
    hot = jnp.where(lax.broadcasted_iota(jnp.int32, (16, LABELS), 1) == label, 1.0, 0.0).astype(bf16)
    for i in range(4):
        load(i).wait()
    class_row = jnp.concatenate(
        [
            sum(nn(hot[:, r : r + n], part[3 * h + i, 0:n]) for i, (r, n) in enumerate(TABLE_ROWS))
            for h in range(2)
        ],
        1,
    )[0:1]
    hidden[...] = (
        nn(lat_pad[...].astype(bf16), patch_pad[...]) + pos_table_ref[...].astype(f32) + class_row
    )

    def put_low(r, v):
        low_top[r] = v.astype(bf16)

    normalize(hidden, xhat1, scale1, g1_ref[...].astype(f32), b1_ref[...].astype(f32), put_low)
    load(4).wait()
    normed = low_top[...]
    keys[128:256] = nn(normed, qkv_w[:, 768:1536]).astype(bf16)
    meet()

    @pl.when(core == 1)
    def _():
        exchange(4, peek_out, peek_in).start()

    @pl.when(core == 0)
    def _():
        exchange(2, mask_row, prior_mask).start()
        exchange(0, keys.at[128:256], keys.at[0:128]).start()

    values[128:256] = nn(normed, qkv_w[:, 1536:2304]).astype(bf16)

    @pl.when(core == 0)
    def _():
        exchange(1, values.at[128:256], values.at[0:128]).start()

    query[...] = nn(normed, qkv_w[:, 0:768]).astype(bf16)
    lt_ref[6] = normed.astype(f32).T.astype(bf16)

    @pl.when(core == 1)
    def _():
        exchange(2, mask_row, prior_mask).wait_recv()
        exchange(0, keys.at[128:256], keys.at[0:128]).wait_recv()
        exchange(1, values.at[128:256], values.at[0:128]).wait_recv()

    bias[:, 0:128] = jnp.where(jnp.broadcast_to(prior_mask[0:1], (128, 128)) > 0.5, 0.0, -1e30)
    bias[:, 128:256] = jnp.where(((lane < row) & (valid_row > 0.5)) | eye, 0.0, -1e30)

    def columns128(p):
        return pl.ds(pl.multiple_of(p * 128, 128), 128)

    def attend(p):
        cols = columns128(p)
        q_pair = query[:, cols]
        k_pair = keys[:, cols]
        v_pair = values[:, cols]
        outs = []
        for i in range(2):
            q_one = jnp.where(low_half if i == 0 else lane >= 64, q_pair, jnp.zeros_like(q_pair))
            scores = nt(q_one, k_pair) * 0.125 + bias[...]
            top = jnp.max(scores, -1, keepdims=True)
            powers = jnp.exp(scores - top)
            soft = powers * (1.0 / jnp.sum(powers, -1, keepdims=True))
            probs[2 * p + i] = soft
            outs.append(nn(soft.astype(bf16), v_pair))
        attended[:, cols] = jnp.where(low_half, outs[0], outs[1]).astype(bf16)

    for p in range(6):
        attend(p)
    load(5).wait()
    mid[...] = hidden[...] + nn(attended[...], out_w[...])
    lt_ref[5] = attended[...].astype(f32).T.astype(bf16)
    normalize(mid, xhat2, scale2, g2_ref[...].astype(f32), b2_ref[...].astype(f32), put_low)
    up_left[:, 0:128] = low_top[...].astype(f32).T.astype(bf16)
    for i in range(2):
        up_left_go(i).start()
    d_hidden[...] = mid[...]

    def rows768(j):
        return pl.ds(pl.multiple_of(j * 768, 128), 768)

    def feed(j, carried):
        for one in load_feed(j):
            one.wait()
        d_second[...] = nn(low_top[...], up_w[:, rows768(j)])
        shift = up_bias_ref[:, rows768(j)].astype(f32)
        for r in chunks:
            pre = d_second[r] + shift
            square = pre * pre
            bend = jnp.tanh(pre * (GELU_A + (GELU_A * GELU_B) * square))
            left = 0.5 * (1.0 + bend)
            slope[j, r] = left + 0.5 * pre * (1.0 - bend * bend) * (GELU_A + (3.0 * GELU_A * GELU_B) * square)
            d_second[r] = pre * left
        act = d_second[...]
        turned = act.T.astype(bf16)

        @pl.when(j // 2 == x)
        def _():
            down_left[down_rows(j % 2), 0:128] = turned
            down_left_core(j % 2).start()

        @pl.when(j // 2 != x)
        def _():
            lt_ref[j % 2] = turned
            pl.when(j % 2 == 0)(lambda: down_left_x(0).start())

        d_hidden[...] += nn(act.astype(bf16), down_w[rows768(j)])
        return carried

    lax.fori_loop(0, 4, feed, 0)
    low_top[...] = d_hidden[...].astype(bf16)
    row_out[...] = nt(low_top[...], head_pad[...]) + head_bias

    @pl.when(core == 0)
    def _():
        exchange(3, row_out.at[120:128], row_in).start()

    def coupling(shifted, latent, cot):
        inside = lax.broadcasted_iota(jnp.int32, shifted.shape, 1) < 48
        alpha = jnp.where(inside, shifted, 0.0)
        scale = jnp.exp(-alpha)
        moved = (latent - jnp.where(inside, pltpu.roll(shifted, 80, 1), 0.0)) * scale
        d_alpha = -cot * moved - cot_logdet_sm[0]
        d_mean = pltpu.roll(jnp.where(inside, -cot * scale, 0.0), 48, 1)
        return alpha, scale, moved, jnp.where(inside, d_alpha, d_mean)

    rolled = pltpu.roll(row_out[...], 1, 0)
    d_shifted = coupling(jnp.where(row == 0, 0.0, rolled) * valid_col, lat_pad[...], cot_pad[...])[3] * valid_col

    @pl.when(core == 0)
    def _():
        exchange(4, peek_out, peek_in).wait_recv()

    def peeked(i):
        return jnp.broadcast_to(peek_in[i : i + 1], (8, 128))

    after_last = jnp.broadcast_to(row_out[127:128], (8, 128)) * peeked(2)
    d_next = coupling(after_last, peeked(0), peeked(1))[3] * peeked(2)
    d_head = jnp.where(row == 127, d_next[0:1], pltpu.roll(d_shifted, 127, 0)).astype(bf16)

    def outputs():
        @pl.when(core == 1)
        def _():
            exchange(3, row_out.at[120:128], row_in).wait_recv()

        before = jnp.where(row == 0, jnp.broadcast_to(row_in[7:8], (128, 128)), pltpu.roll(row_out[...], 1, 0))
        alpha, scale, moved = coupling(before * valid_col, lat_pad[...], cot_pad[...])[0:3]
        factor[...] = scale
        store_exact(0, moved.T[0:48])
        logdet = -jnp.sum(jnp.sum(alpha, 1, keepdims=True), 0, keepdims=True)
        lines[8:9, 128:256] = jnp.where(lax.broadcasted_iota(jnp.int32, (1, 128), 1) == dp, logdet, 0.0)

    def exact_terms(v):
        terms = []
        for i in range(3):
            terms.append(v.astype(bf16))
            v = v - terms[i].astype(f32)
        return terms

    def store_exact(h, v):
        for i, term in enumerate(exact_terms(v)):
            sums[LAST + 1 + THIRD // 2, h, 0:48, i * 128 : (i + 1) * 128] = term

    head_grad = tn(d_head, low_top[...])
    head_bias_grad = jnp.sum(d_head.astype(f32), 0, keepdims=True)
    d_hidden[...] = nn(d_head, head_pad[...])
    low_top[...] = d_hidden[...].astype(bf16)
    for h in range(2):
        r_ref[0, h] = low_top[:, h * COLS : (h + 1) * COLS]
    for i in range(3):
        down_right_go(i).start()
    down_left_x(1).start()
    down_right[0:128] = r_ref[0, core]

    def put(first_row, value):
        h, r = first_row // 128, first_row % 128
        for t in range(2):
            small_ref[h, t * 128 + r : t * 128 + r + value.shape[0]] = value[:, t * COLS : (t + 1) * COLS].astype(bf16)

    put(0, head_grad[0:96])

    lines[...] = jnp.zeros((16, 768), f32)
    lines[8:9, 0:128] = head_bias_grad

    d_second[...] = jnp.zeros((128, 768), f32)

    def feed_back(j):
        d_keys[...] = nt(low_top[...], down_w[rows768(j)])
        total = jnp.zeros((1, 768), f32)
        for r in chunks:
            d_pre = (slope[j, r] * d_keys[r]).astype(bf16)
            d_att[r] = d_pre
            total += jnp.sum(d_pre.astype(f32), 0, keepdims=True)
            for h in range(2):
                r_ref[1 + j, h, r] = d_pre[:, h * COLS : (h + 1) * COLS]
        near, same = j // 2 == y, j % 2 == core

        @pl.when(jnp.logical_and(near, same))
        def _():
            for h in range(2):
                up_right[h, 0:128] = r_ref[1 + j, h]

        pl.when(jnp.logical_and(near, j % 2 != core))(lambda: up_right_go(0, j).start())
        pl.when(jnp.logical_and(j // 2 != y, same))(lambda: up_right_go(1, j).start())
        pl.when(jnp.logical_and(j // 2 != y, j % 2 != core))(lambda: up_right_go(2, j).start())
        lines[pl.ds(4 + j, 1)] = total
        d_second[...] += nt(d_att[...], up_w[:, rows768(j)])

    def norm_back(grad, hat, scale, gain, base, out, line):
        gain_total = jnp.zeros((1, 768), f32)
        shift_total = jnp.zeros((1, 768), f32)
        for r in chunks:
            d = grad[r]
            scaled = hat[r]
            e = d * gain
            v = e - jnp.mean(e, -1, keepdims=True) - scaled * jnp.mean(e * scaled, -1, keepdims=True)
            out[r] = base[r] + scale[r] * v
            gain_total += jnp.sum(d * scaled, 0, keepdims=True)
            shift_total += jnp.sum(d, 0, keepdims=True)
        lines[line : line + 1] = gain_total
        lines[line + 1 : line + 2] = shift_total

    def feed_norm_back():
        norm_back(d_second, xhat2, scale2, g2_ref[...].astype(f32), d_hidden, mid, 2)
        low_top[...] = mid[...].astype(bf16)
        for h in range(2):
            r_ref[5, h] = low_top[:, h * COLS : (h + 1) * COLS]
        d_att[...] = nt(low_top[...], out_w[...]).astype(bf16)

    def attend_back(p):
        cols = columns128(p)
        q_pair = query[:, cols]
        k_pair = keys[:, cols]
        v_pair = values[:, cols]
        a_pair = d_att[:, cols]
        dq, dk, dv = [], [], []
        for i in range(2):
            own = low_half if i == 0 else lane >= 64
            a_one = jnp.where(own, a_pair, jnp.zeros_like(a_pair))
            q_one = jnp.where(own, q_pair, jnp.zeros_like(q_pair))
            soft = probs[2 * p + i]
            d_soft = nt(a_one, v_pair)
            weighted = d_soft * soft
            d_score = weighted - soft * jnp.sum(weighted, -1, keepdims=True)
            d_low = d_score.astype(bf16)
            dq.append(nn(d_low, k_pair))
            dk.append(tn(d_low, q_one))
            dv.append(tn(soft.astype(bf16), a_one))
        h, local = p // 3, pl.ds(pl.multiple_of((p % 3) * 128, 128), 128)
        r_ref[6, h, :, local] = (jnp.where(low_half, dq[0], dq[1]) * 0.125).astype(bf16)
        dk_pair = (dk[0] + dk[1]) * 0.125
        dv_pair = dv[0] + dv[1]
        d_prior[0, :, cols] = dk_pair[0:128].astype(bf16)
        d_prior[1, :, cols] = dv_pair[0:128].astype(bf16)
        d_keys[:, cols] = dk_pair[128:256]
        d_values[:, cols] = dv_pair[128:256]

    def send_prior():
        @pl.when(core == 1)
        def _():
            exchange(5, d_prior, d_back).start()

    def packed_back():
        @pl.when(core == 0)
        def _():
            exchange(5, d_prior, d_back).wait_recv()

        for h in range(2):
            cols = slice(h * COLS, (h + 1) * COLS)
            r_ref[7, h] = (d_keys[:, cols] + d_back[0, :, cols].astype(f32)).astype(bf16)
            r_ref[8, h] = (d_values[:, cols] + d_back[1, :, cols].astype(f32)).astype(bf16)
        d_second[...] = sum(
            nt(r_ref[6 + j, h], qkv_w[:, j * 768 + h * COLS : j * 768 + (h + 1) * COLS])
            for j in range(3)
            for h in range(2)
        )

    def embed_back():
        norm_back(d_second, xhat1, scale1, g1_ref[...].astype(f32), mid, d_hidden, 0)
        low_top[...] = d_hidden[...].astype(bf16)
        for t in range(2):
            pos_ref[t * 128 : (t + 1) * 128] = low_top[:, t * COLS : (t + 1) * COLS]
        patch_grad = tn(lat_pad[...].astype(bf16), low_top[...])
        store_exact(1, (cot_pad[...] * factor[...] + nt(low_top[...], patch_pad[...])).T[0:48])
        class_grad = jnp.sum(d_hidden[...], 0, keepdims=True)
        put(96, patch_grad[0:32])
        put(128, patch_grad[32:48])
        line = lax.broadcasted_iota(jnp.int32, (16, 768), 0)
        put(144, jnp.where(line == dp, class_grad, 0.0))
        put(160, jnp.zeros((96, 768), f32))

    def feed_back_all(j, carried):
        feed_back((j + 2 * (1 - y)) % 4)
        return carried

    lax.fori_loop(0, 4, feed_back_all, 0)
    pass_on(0)
    up_left_go(1).wait_recv()
    up_left_go(2).start()
    feed_norm_back()
    for u in range(OUTS):
        out_stage[u] = out_product(u, 1 - core).astype(bf16)
        out_first(u).start()

    def piece(t):
        @pl.when(jnp.logical_and(t >= 2, t < 4))
        def _():
            for i in range(3):
                attend_back(3 * t - 6 + i)

        pl.when(t == 4)(lambda: pass_on(1))
        pl.when(t == 3)(send_prior)
        pl.when(t == 5)(packed_back)
        pl.when(t == 6)(outputs)
        pl.when(t == 7)(embed_back)

    everyone, inners, outers = None, inner, outer
    events = [
        (4, None, everyone, produce),
        (5, None, everyone, begin),
        (2, LAST + 1, everyone, begin_more),
        (9, None, inners, c4),
        (4, LAST + 1, everyone, begin_ab),
        (9, None, outers, c3_outer),
        (4, LAST + 1, everyone, ab1),
        (10, LAST + 1, outers, ab5_outer),
        (7, None, inners, c2_inner),
        (6, LAST + 1, inners, ab3_inner),
        (13, LAST + 1, outers, ab7),
        (11, None, inners, c5),
        (12, LAST + 1, inners, ab6),
        (14, None, inners, c9_inner),
        (0, LAST + 1, everyone, piece),
        (15, LAST + 1, inners, ab7),
        (5, None, inners, c1_inner),
        (7, LAST + 1, inners, ab4_inner),
        (5, LAST + 1, everyone, ab2),
        (10, None, outers, c4),
        (11, LAST + 1, outers, ab6),
        (11, None, outers, c5),
        (12, None, inners, c8_inner),
        (16, None, outers, c10_outer),
        (DRAIN, UNITS, everyone, drain),
        (DRAIN_C, None, everyone, drain_c),
    ]

    def step(t, carried):
        for lag, count, who, event in events:
            if count is None:
                turn = t - lag + 48
                u = 2 * (turn // 3) + turn % 3 - 32
                now = jnp.logical_and(turn >= 48, jnp.logical_and(turn % 3 < 2, u < THIRD))
            else:
                u = t - lag
                now = jnp.logical_and(u >= 0, u < count)
            if who is not None:
                now = jnp.logical_and(now, who)
            pl.when(now)(lambda event=event, u=u: event(u))
        return carried

    lax.fori_loop(2, STEPS, step, 0)


    def drain_more(u, carried):
        drain(u)
        return carried

    lax.fori_loop(STEPS - DRAIN, UNITS, drain_more, 0)
    for u in range(18, THIRD):
        drain_c(u)
    sent_either(send_sem.at[UNITS], (2, 224), (2, 256))
    sent_either(send_sem.at[LAST], (4, 176), (3, 256))
    to_other(LAST, sums.at[LAST, 1 - core]).wait_recv()
    for u in range(OUTS):
        out_first(u).wait_send()
    for u in range(THIRD - STAGES, THIRD):
        core_first(u).wait_send()
    small_first().wait_send()
    for k in range(3):
        line_go(k).wait_send()
        down_right_go(k).wait_send()
        up_left_go(k).wait_send()
        up_right_go(k, 0).wait_send()
    for i in range(2):
        down_left_core(i).wait_send()
        down_left_x(i).wait_send()
        down_left_on(i).wait_send()
    pl.when(outer)(line_go(3).wait_send)

    @pl.when(inner)
    def _():
        line_go(4).wait_send()
        line_go(5).wait_send()

    @pl.when(core == 0)
    def _():
        exchange(2, mask_row, prior_mask).wait_send()
        exchange(0, keys.at[128:256], keys.at[0:128]).wait_send()
        exchange(1, values.at[128:256], values.at[0:128]).wait_send()
        exchange(3, row_out.at[120:128], row_in).wait_send()

    @pl.when(core == 1)
    def _():
        exchange(4, peek_out, peek_in).wait_send()
        exchange(5, d_prior, d_back).wait_send()


def flow(
    class_labels, group_perm, cot_logdet, latents, valid, patch_weight, pos_table, ln1_gain, ln1_bias,
    ln2_gain, ln2_bias, up_bias, head_weight, head_bias, cot_latents, class_table,
    qkv_weight, out_weight, up_weight, down_weight,
):
    smem = pl.BlockSpec(memory_space=pltpu.SMEM)
    vmem = pl.BlockSpec(memory_space=pltpu.VMEM)
    hbm = pl.BlockSpec(memory_space=pltpu.HBM)
    wide = (128, 768)
    return pl.pallas_call(
        flow_kernel,
        out_shape=pltpu.VMEM((LAST + 2 + THIRD // 2, 2, 2 * SLAB, COLS), bf16),
        in_specs=[smem] * 3 + [vmem] * 12 + [hbm] * 5,
        out_specs=vmem,
        scratch_shapes=[
            pltpu.VMEM((STAGES, SLAB, COLS), bf16),
            pltpu.VMEM((LAST + 1, 2 * SLAB, COLS), bf16),
            pltpu.VMEM((THIRD, SLAB, COLS), bf16),
            pltpu.VMEM((OUTS, 2 * SLAB, COLS), bf16),
            pltpu.VMEM((OUTS, 2 * SLAB, COLS), bf16),
            pltpu.VMEM((TURNS, SLAB, COLS), bf16),
            pltpu.VMEM((256, COLS), bf16),
            pltpu.VMEM((TURNS, 2, 160, COLS), bf16),
            pltpu.VMEM((TURNS, 256, COLS), bf16),
            pltpu.VMEM((THIRD, 32, COLS), bf16),
            pltpu.VMEM((1536, 512), bf16),
            pltpu.VMEM((512, COLS), bf16),
            pltpu.VMEM((768, 512), bf16),
            pltpu.VMEM((2, 512, COLS), bf16),
            pltpu.SemaphoreType.DMA((15,)),
            pltpu.SemaphoreType.DMA((15,)),
            pltpu.SemaphoreType.DMA((LAST + 1,)),
            pltpu.SemaphoreType.DMA((14, TURNS)),
            pltpu.SemaphoreType.DMA((STAGES + 1,)),
            pltpu.SemaphoreType.DMA((LAST + 1,)),
            pltpu.SemaphoreType.DMA((THIRD,)),
            pltpu.SemaphoreType.DMA((THIRD,)),
            pltpu.SemaphoreType.DMA((OUTS,)),
            pltpu.SemaphoreType.DMA((OUTS,)),
            pltpu.VMEM((768, 2304), bf16),
            pltpu.VMEM((768, 768), bf16),
            pltpu.VMEM((768, 3072), bf16),
            pltpu.VMEM((3072, 768), bf16),
            pltpu.SemaphoreType.DMA((14,)),
            pltpu.VMEM((128, 128), f32),
            pltpu.VMEM((128, 128), f32),
            pltpu.VMEM(wide, bf16),
            pltpu.VMEM(wide, bf16),
            pltpu.VMEM(wide, f32),
            pltpu.VMEM(wide, f32),
            pltpu.VMEM(wide, f32),
            pltpu.VMEM(wide, f32),
            pltpu.VMEM((128, 1), f32),
            pltpu.VMEM((128, 1), f32),
            pltpu.VMEM((256, 768), bf16),
            pltpu.VMEM((256, 768), bf16),
            pltpu.VMEM(wide, bf16),
            pltpu.VMEM(wide, bf16),
            pltpu.VMEM((128, 256), f32),
            pltpu.VMEM((8, 128), f32),
            pltpu.VMEM((8, 128), f32),
            pltpu.VMEM((12, 128, 256), f32),
            pltpu.VMEM((4, 128, 768), f32),
            pltpu.VMEM(wide, f32),
            pltpu.VMEM(wide, f32),
            pltpu.VMEM(wide, bf16),
            pltpu.VMEM(wide, f32),
            pltpu.VMEM(wide, f32),
            pltpu.VMEM((2, 128, 768), bf16),
            pltpu.VMEM((2, 128, 768), bf16),
            pltpu.VMEM((128, 128), f32),
            pltpu.VMEM((8, 128), f32),
            pltpu.VMEM((8, 128), f32),
            pltpu.VMEM((8, 128), f32),
            pltpu.VMEM((128, 128), f32),
            pltpu.VMEM((16, 768), f32),
            pltpu.VMEM((5, 16, 768), f32),
            pltpu.VMEM((5, 16, 768), f32),
            pltpu.SemaphoreType.DMA((6,)),
            pltpu.SemaphoreType.DMA((6,)),
            pltpu.VMEM((7, 768, 128), bf16),
            pltpu.VMEM((9, 2, 128, COLS), bf16),
            pltpu.VMEM((256, COLS), bf16),
            pltpu.VMEM((2, 256, COLS), bf16),
            pltpu.VMEM(wide, bf16),
            pltpu.SemaphoreType.DMA((6,)),
            pltpu.SemaphoreType.DMA((6,)),
        ],
        compiler_params=pltpu.CompilerParams(
            collective_id=0, has_side_effects=True, vmem_limit_bytes=46 << 20
        ),
        name="flow",
    )(
        class_labels, group_perm, cot_logdet, latents, valid, patch_weight, pos_table, ln1_gain, ln1_bias,
        ln2_gain, ln2_bias, up_bias, head_weight, head_bias, cot_latents, class_table,
        qkv_weight, out_weight, up_weight, down_weight,
    )


def finish_kernel(
    labels_ref, sums,
    new_latents, logdet, latents_grad, patch, pos, classes, g1, b1, qkv, out, g2, b2, up, ub, down, head, hb,
    wide_down, wide_up, wide_last, write_sem, lat_wide, pos_wide, small_wide, class_wide, out_sem,
):
    dp = lax.axis_index("dp")
    core = lax.axis_index("seq")
    owned = classes.shape[0]
    outputs = [
        pltpu.make_async_copy(src, dst, out_sem.at[i])
        for i, (src, dst) in enumerate(
            (
                (lat_wide.at[0], new_latents.at[0]),
                (lat_wide.at[1], latents_grad.at[0]),
                (small_wide.at[0:96], head),
                (small_wide.at[96:144], patch),
                (pos_wide, pos),
                (class_wide, classes),
            )
        )
    ]
    writes = []

    def write(src, dst):
        writes.append(pltpu.make_async_copy(src, dst, write_sem.at[len(writes)]))
        writes[-1].start()

    def little():
        for h in range(2):
            terms = [sums[LAST + 1 + THIRD // 2, h, 0:48, i * 128 : (i + 1) * 128].astype(f32) for i in range(3)]
            lat_wide[h] = terms[0] + terms[1] + terms[2]
        outputs[0].start()
        outputs[1].start()
        for t in range(2):
            rows, cols = slice(t * 128, (t + 1) * 128), slice(t * COLS, (t + 1) * COLS)
            pos_wide[:, cols] = sums[UNITS, core, rows].astype(f32)
            for h in range(2):
                small_wide[h * 128 : (h + 1) * 128, cols] = sums[LAST, h, rows].astype(f32)
        for one in outputs[2:5]:
            one.start()
        halves = []
        for h in range(2):
            terms = [sums[LAST + 1 + THIRD // 2, h, 64 + i * 16 : 80 + i * 16].astype(f32) for i in range(3)]
            halves.append(terms[0] + terms[1] + terms[2])
        block = jnp.concatenate(halves, 1)
        for i, one in enumerate((g1, b1, g2, b2)):
            one[...] = block[i : i + 1]
        for i in range(4):
            ub[:, i * 768 : (i + 1) * 768] = block[4 + i : 5 + i]
        hb[...] = block[8:9, 0:96]
        count = labels_ref.shape[1]
        lane = lax.broadcasted_iota(jnp.int32, (1, 128), 1)
        logdet[...] = jnp.sum(jnp.where(lane == dp, block[8:9, 128:256], 0.0), 1, keepdims=True)
        by_lane = jnp.broadcast_to(labels_ref[...], (count, count)).astype(f32)
        first = lax.broadcasted_iota(jnp.int32, (count, count), 0)
        second = lax.broadcasted_iota(jnp.int32, (count, count), 1)
        by_row = jnp.sum(jnp.where(first == second, by_lane, 0.0), 1, keepdims=True)
        before = (by_lane < by_row) | ((by_lane == by_row) & (second < first))
        rank = jnp.sum(jnp.where(before, 1.0, 0.0), 1, keepdims=True)
        stored = jnp.sum(jnp.where(rank == second.astype(f32), by_row, 0.0), 0, keepdims=True)
        wanted = (dp * owned + lax.broadcasted_iota(jnp.int32, (owned, count), 0)).astype(f32)
        hot = jnp.where(stored == wanted, 1.0, 0.0).astype(bf16)
        class_wide[...] = jnp.dot(hot, small_wide[144:160].astype(bf16), preferred_element_type=f32)
        outputs[5].start()

    for u in range(OUTS):
        rows = slice(256 * u, 256 * (u + 1))
        for h in range(2):
            wide_last[0, rows, h * COLS : (h + 1) * COLS] = sums[u, h].astype(f32)
        write(wide_last.at[0, rows], out.at[0, rows])
    for u in range(UNITS - OUTS):
        turn = 64 * (u // 2)
        for h in range(2):
            cols = slice(h * COLS, (h + 1) * COLS)
            for i in range(2):
                wide_down[1536 * i + 64 * u : 1536 * i + 64 * (u + 1), cols] = sums[
                    u + OUTS, h, 64 * i : 64 * (i + 1)
                ].astype(f32)
                column = (2 * i + h) * 768 + (u % 2) * COLS
                wide_up[turn : turn + 64, column : column + COLS] = sums[
                    u + OUTS, h, 128 + 64 * i : 128 + 64 * (i + 1)
                ].astype(f32)
        if u % 2 == 1:
            write(wide_up.at[turn : turn + 64], up.at[0, turn : turn + 64])
        if u % 4 == 3:
            for i in range(2):
                rows = slice(1536 * i + 64 * (u - 3), 1536 * i + 64 * (u + 1))
                write(wide_down.at[rows], down.at[0, rows])
        if u == 3:
            little()
    for u in range(THIRD):
        block, row = u // 6, (u % 6) * SLAB
        for h in range(2):
            wide_last[block + 1, row : row + SLAB, h * COLS : (h + 1) * COLS] = sums[
                LAST + 1 + u // 2, h, (u % 2) * SLAB : (u % 2 + 1) * SLAB
            ].astype(f32)
        write(
            wide_last.at[block + 1, row : row + SLAB],
            qkv.at[0, row : row + SLAB, block * 768 : (block + 1) * 768],
        )
    for one in writes:
        one.wait()
    for one in outputs:
        one.wait()


def finish(class_labels, sums):
    count = class_labels.shape[1]
    owned = 1024 // count
    shapes = [
        (1, 48, 128), (1, 1), (1, 48, 128), (48, 768), (128, 768), (owned, 768), (1, 768), (1, 768),
        (1, 768, 2304), (1, 768, 768), (1, 768), (1, 768), (1, 768, 3072), (1, 3072), (1, 3072, 768),
        (96, 768), (1, 96),
    ]
    vmem = pl.BlockSpec(memory_space=pltpu.VMEM)
    hbm = pl.BlockSpec(memory_space=pl.ANY)
    return pl.pallas_call(
        finish_kernel,
        out_shape=[jax.ShapeDtypeStruct(shape, f32) for shape in shapes],
        in_specs=[vmem, vmem],
        out_specs=[vmem if i in (1, 6, 7, 10, 11, 13, 16) else hbm for i in range(17)],
        scratch_shapes=[
            pltpu.VMEM((3072, 768), f32),
            pltpu.VMEM((768, 3072), f32),
            pltpu.VMEM((4, 768, 768), f32),
            pltpu.SemaphoreType.DMA((45,)),
            pltpu.VMEM((2, 48, 128), f32),
            pltpu.VMEM((128, 768), f32),
            pltpu.VMEM((256, 768), f32),
            pltpu.VMEM((owned, 768), f32),
            pltpu.SemaphoreType.DMA((6,)),
        ],
        compiler_params=pltpu.CompilerParams(vmem_limit_bytes=34 << 20),
        name="finish",
    )(class_labels, sums)


def fast_local(
    latents, valid, class_labels, group_perm, patch_weight, pos_table, class_table, ln1_gain, ln1_bias,
    qkv_weight, out_weight, ln2_gain, ln2_bias, up_weight, up_bias, down_weight, head_weight, head_bias,
    cot_latents, cot_logdet,
):
    sums = flow(
        class_labels, group_perm, cot_logdet, latents.swapaxes(1, 2), valid, patch_weight, pos_table, ln1_gain,
        ln1_bias, ln2_gain, ln2_bias, up_bias, head_weight.T, head_bias[None], cot_latents.swapaxes(1, 2), class_table,
        qkv_weight, out_weight, up_weight, down_weight,
    )
    results = list(finish(class_labels[None], sums))
    results[1] = results[1].reshape(1)
    results[16] = results[16].reshape(96)
    results[0], results[2] = results[0].swapaxes(1, 2), results[2].swapaxes(1, 2)
    results[15] = results[15].T
    return tuple(results)


def forward(latents, valid, class_rows, seq_place, weights):
    (
        patch_weight,
        pos_table,
        qkv_weight,
        out_weight,
        ln1_gain,
        ln1_bias,
        ln2_gain,
        ln2_bias,
        up_weight,
        up_bias,
        down_weight,
        head_weight,
        head_bias,
    ) = weights
    images, patch_rows, channels = latents.shape
    model_width = qkv_weight.shape[1]
    head_count = model_width // HEAD_DIM
    latent_low = latents.astype(jnp.bfloat16)
    hidden = (
        matmul(latent_low, patch_weight)
        + pos_table.astype(jnp.float32)[None]
        + class_rows[:, None, :]
    )
    own_mask = valid.astype(jnp.bfloat16)
    normed = layer_norm(
        hidden, ln1_gain[0].astype(jnp.float32), ln1_bias[0].astype(jnp.float32)
    ).astype(jnp.bfloat16)
    packed = matmul(normed, qkv_weight[0]).astype(jnp.bfloat16)
    query = packed[..., :model_width].reshape(images, patch_rows, head_count, HEAD_DIM)
    keys_own = packed[..., model_width : 2 * model_width]
    values_own = packed[..., 2 * model_width :]
    prior_keys, prior_values, prior_mask = shifted_2((keys_own, values_own, own_mask), "seq", 1)
    keys = jnp.concatenate((prior_keys, keys_own), 1).reshape(
        images, 2 * patch_rows, head_count, HEAD_DIM
    )
    values = jnp.concatenate((prior_values, values_own), 1).reshape(
        images, 2 * patch_rows, head_count, HEAD_DIM
    )
    allowed = attention_mask(jnp.concatenate((prior_mask, own_mask), 1), patch_rows, seq_place)
    logits = masked_scores(query, keys, allowed)
    row_peak = jnp.max(logits, -1, keepdims=True)
    log_total = row_peak + jnp.log(jnp.sum(jnp.exp(logits - row_peak), -1, keepdims=True))
    weights_soft = jnp.exp(logits - log_total).astype(jnp.bfloat16)
    attended = jnp.einsum(
        "bhqk,bkhd->bqhd", weights_soft, values, preferred_element_type=jnp.float32
    )
    attended = attended.astype(jnp.bfloat16).reshape(images, patch_rows, model_width)
    mid = hidden + matmul(attended, out_weight[0])
    second = layer_norm(
        mid, ln2_gain[0].astype(jnp.float32), ln2_bias[0].astype(jnp.float32)
    ).astype(jnp.bfloat16)
    preact = matmul(second, up_weight[0]) + up_bias[0].astype(jnp.float32)
    activated = jax.nn.gelu(preact, approximate=True).astype(jnp.bfloat16)
    saved = [
        (
            hidden,
            normed,
            query,
            keys,
            values,
            allowed,
            log_total,
            attended,
            mid,
            second,
            preact,
            activated,
        )
    ]
    hidden = mid + matmul(activated, down_weight[0])
    top_low = hidden.astype(jnp.bfloat16)
    head_out = matmul(top_low, head_weight) + head_bias.astype(jnp.float32)
    prior_row = shifted_2(head_out[:, patch_rows - 1, :], "seq", 1)
    shifted = jnp.concatenate((prior_row[:, None, :], head_out[:, : patch_rows - 1, :]), 1)
    shifted = shifted * valid.astype(jnp.float32)[..., None]
    alpha = shifted[..., :channels]
    shift_mean = shifted[..., channels:]
    factor = jnp.exp(-alpha)
    new_latents = (latents - shift_mean) * factor
    logdet_part = -jnp.sum(alpha, (1, 2))
    return (new_latents, logdet_part, factor, top_low, saved)


def local(
    latents,
    valid,
    class_labels,
    group_perm,
    patch_weight,
    pos_table,
    class_table,
    ln1_gain,
    ln1_bias,
    qkv_weight,
    out_weight,
    ln2_gain,
    ln2_bias,
    up_weight,
    up_bias,
    down_weight,
    head_weight,
    head_bias,
    cot_latents,
    cot_logdet,
):
    images, patch_rows, channels = latents.shape
    model_width = qkv_weight.shape[1]
    head_count = model_width // HEAD_DIM
    layer_total = qkv_weight.shape[0]
    seq_place = lax.axis_index("seq")
    picks = group_perm[:, None] == lax.iota(jnp.int32, class_labels.shape[0])[None, :]
    image_labels = jnp.sum(jnp.where(picks, class_labels[None, :], 0), 1)
    label_hot = image_labels[:, None] == lax.iota(jnp.int32, class_table.shape[0])[None, :]
    class_rows = matmul(label_hot.astype(jnp.bfloat16), class_table)
    weights = (
        patch_weight,
        pos_table,
        qkv_weight,
        out_weight,
        ln1_gain,
        ln1_bias,
        ln2_gain,
        ln2_bias,
        up_weight,
        up_bias,
        down_weight,
        head_weight,
        head_bias,
    )
    new_latents, logdet_part, factor, top_low, saved = forward(
        latents, valid, class_rows, seq_place, weights
    )
    valid_float = valid.astype(jnp.float32)
    d_alpha = -cot_latents * new_latents - cot_logdet[:, None, None]
    d_mean = -cot_latents * factor
    d_shifted = jnp.concatenate((d_alpha, d_mean), -1) * valid_float[..., None]
    next_row = shifted_2(d_shifted[:, 0, :], "seq", -1)
    d_head = jnp.concatenate((d_shifted[:, 1:, :], next_row[:, None, :]), 1).astype(jnp.bfloat16)
    head_weight_grad = outer_sum(top_low, d_head)
    head_bias_grad = jnp.sum(d_head.astype(jnp.float32), (0, 1))
    d_hidden = transposed(d_head, head_weight)
    grads_qkv, grads_out, grads_up, grads_down = ([], [], [], [])
    grads_g1, grads_b1, grads_g2, grads_b2, grads_ub = ([], [], [], [], [])
    for layer_index in reversed(range(layer_total)):
        (
            hidden,
            normed,
            query,
            keys,
            values,
            allowed,
            log_total,
            attended,
            mid,
            second,
            preact,
            activated,
        ) = saved[layer_index]
        d_down = d_hidden.astype(jnp.bfloat16)
        down_grad = outer_sum(activated, d_down)
        d_act = transposed(d_down, down_weight[layer_index])
        unused_gelu, gelu_pull = jax.vjp(lambda inner: jax.nn.gelu(inner, approximate=True), preact)
        d_pre = gelu_pull(d_act)[0].astype(jnp.bfloat16)
        up_bias_grad = jnp.sum(d_pre.astype(jnp.float32), (0, 1))
        up_grad = outer_sum(second, d_pre)
        d_second = transposed(d_pre, up_weight[layer_index])
        unused_norm, norm_pull = jax.vjp(
            layer_norm,
            mid,
            ln2_gain[layer_index].astype(jnp.float32),
            ln2_bias[layer_index].astype(jnp.float32),
        )
        d_mid_norm, ln2_gain_part, ln2_bias_part = norm_pull(d_second)
        d_mid = d_hidden + d_mid_norm
        d_proj = d_mid.astype(jnp.bfloat16)
        out_grad = outer_sum(attended, d_proj)
        d_attended = transposed(d_proj, out_weight[layer_index]).astype(jnp.bfloat16)
        d_attended = d_attended.reshape(images, patch_rows, head_count, HEAD_DIM)
        logits = masked_scores(query, keys, allowed)
        probs = jnp.exp(logits - log_total)
        d_probs = jnp.einsum(
            "bqhd,bkhd->bhqk", d_attended, values, preferred_element_type=jnp.float32
        )
        d_scores = (probs * (d_probs - jnp.sum(d_probs * probs, -1, keepdims=True))).astype(
            jnp.bfloat16
        )
        d_query = jnp.einsum(
            "bhqk,bkhd->bqhd", d_scores, keys, preferred_element_type=jnp.float32
        ) * HEAD_DIM ** (-0.5)
        d_keys = jnp.einsum(
            "bhqk,bqhd->bkhd", d_scores, query, preferred_element_type=jnp.float32
        ) * HEAD_DIM ** (-0.5)
        d_values = jnp.einsum(
            "bhqk,bqhd->bkhd",
            probs.astype(jnp.bfloat16),
            d_attended,
            preferred_element_type=jnp.float32,
        )
        d_keys = d_keys.reshape(images, 2 * patch_rows, model_width)
        d_values = d_values.reshape(images, 2 * patch_rows, model_width)
        back_keys, back_values = (
            shifted_2(d_keys[:, :patch_rows].astype(jnp.bfloat16), "seq", -1).astype(jnp.float32),
            shifted_2(d_values[:, :patch_rows].astype(jnp.bfloat16), "seq", -1).astype(jnp.float32),
        )
        d_packed = jnp.concatenate(
            (
                d_query.reshape(images, patch_rows, model_width),
                d_keys[:, patch_rows:] + back_keys,
                d_values[:, patch_rows:] + back_values,
            ),
            -1,
        ).astype(jnp.bfloat16)
        qkv_grad = outer_sum(normed, d_packed)
        d_normed = transposed(d_packed, qkv_weight[layer_index])
        unused_norm, norm_pull = jax.vjp(
            layer_norm,
            hidden,
            ln1_gain[layer_index].astype(jnp.float32),
            ln1_bias[layer_index].astype(jnp.float32),
        )
        d_input, ln1_gain_part, ln1_bias_part = norm_pull(d_normed)
        d_hidden = d_mid + d_input
        grads_qkv.insert(0, qkv_grad)
        grads_out.insert(0, out_grad)
        grads_up.insert(0, up_grad)
        grads_down.insert(0, down_grad)
        grads_g1.insert(0, ln1_gain_part)
        grads_b1.insert(0, ln1_bias_part)
        grads_g2.insert(0, ln2_gain_part)
        grads_b2.insert(0, ln2_bias_part)
        grads_ub.insert(0, up_bias_grad)
    d_embed_low = d_hidden.astype(jnp.bfloat16)
    patch_grad_part = outer_sum(latents.astype(jnp.bfloat16), d_embed_low)
    latents_grad = cot_latents * factor + transposed(d_embed_low, patch_weight)
    pos_part = jnp.sum(d_hidden, 0)
    class_part = jnp.sum(d_hidden, 1)
    logdet, class_sums = lax.psum((logdet_part, class_part), "seq")
    class_term = lax.dot_general(
        label_hot.astype(jnp.float32),
        class_sums,
        (((0,), (0,)), ((), ())),
        precision=precise,
        preferred_element_type=jnp.float32,
    )
    class_grad = lax.psum_scatter(class_term, "dp", scatter_dimension=0, tiled=True)
    pos_grad = lax.psum(pos_part, "dp")
    (
        patch_weight_grad,
        head_weight_grad,
        head_bias_grad,
        ln1_gain_grad,
        ln1_bias_grad,
        ln2_gain_grad,
        ln2_bias_grad,
        up_bias_grad,
    ) = lax.psum(
        (
            patch_grad_part,
            head_weight_grad,
            head_bias_grad,
            jnp.stack(grads_g1),
            jnp.stack(grads_b1),
            jnp.stack(grads_g2),
            jnp.stack(grads_b2),
            jnp.stack(grads_ub),
        ),
        ("dp", "seq"),
    )
    qkv_stack = jnp.stack(grads_qkv)
    out_stack = jnp.stack(grads_out)
    up_stack = jnp.stack(grads_up)
    down_stack = jnp.stack(grads_down)
    flat_parts = (
        lax.psum_scatter(eight_rows(qkv_stack), ("dp", "seq"), scatter_dimension=1, tiled=True),
        lax.psum_scatter(eight_rows(out_stack), ("dp", "seq"), scatter_dimension=1, tiled=True),
        lax.psum_scatter(eight_rows(up_stack), ("dp", "seq"), scatter_dimension=1, tiled=True),
        lax.psum_scatter(eight_rows(down_stack), ("dp", "seq"), scatter_dimension=1, tiled=True),
    )
    flat_qkv, flat_out, flat_up, flat_down = (
        lax.all_gather(
            flat_parts[0].astype(jnp.bfloat16), ("dp", "seq"), axis=1, tiled=True
        ).astype(jnp.float32),
        lax.all_gather(
            flat_parts[1].astype(jnp.bfloat16), ("dp", "seq"), axis=1, tiled=True
        ).astype(jnp.float32),
        lax.all_gather(
            flat_parts[2].astype(jnp.bfloat16), ("dp", "seq"), axis=1, tiled=True
        ).astype(jnp.float32),
        lax.all_gather(
            flat_parts[3].astype(jnp.bfloat16), ("dp", "seq"), axis=1, tiled=True
        ).astype(jnp.float32),
    )
    qkv_stack = flat_qkv.reshape(qkv_stack.shape)
    out_stack = flat_out.reshape(out_stack.shape)
    up_stack = flat_up.reshape(up_stack.shape)
    down_stack = flat_down.reshape(down_stack.shape)
    return (
        new_latents,
        logdet,
        latents_grad,
        patch_weight_grad,
        pos_grad,
        class_grad,
        ln1_gain_grad,
        ln1_bias_grad,
        qkv_stack,
        out_stack,
        ln2_gain_grad,
        ln2_bias_grad,
        up_stack,
        up_bias_grad,
        down_stack,
        head_weight_grad,
        head_bias_grad,
    )


def solution(mesh):
    in_specs = (
        P("dp", "seq", None),
        P("dp", "seq"),
        P(),
        P("dp"),
        P(),
        P("seq", None),
        P(),
        P(),
        P(),
        P(),
        P(),
        P(),
        P(),
        P(),
        P(),
        P(),
        P(),
        P(),
        P("dp", "seq", None),
        P("dp"),
    )
    out_specs = (
        P("dp", "seq", None),
        P("dp"),
        P("dp", "seq", None),
        P(),
        P("seq", None),
        P("dp", None),
        P(),
        P(),
        P(),
        P(),
        P(),
        P(),
        P(),
        P(),
        P(),
        P(),
        P(),
    )
    body = fast_local if mesh.shape["dp"] == 16 and mesh.shape["seq"] == 2 else local
    return jax.shard_map(body, mesh=mesh, in_specs=in_specs, out_specs=out_specs, check_vma=False)
```

```python
import jax
import jax.numpy as jnp
from jax import lax
from jax.experimental import pallas as pl
from jax.experimental.pallas import tpu as pltpu
from jax.sharding import PartitionSpec as P

HEAD_DIM = 64


precise = lax.Precision.HIGHEST
norm_eps = 1e-05


def shifted_2(shard, axis, by):
    size = lax.axis_size(axis)
    pairs = [(i, i + by) for i in range(size) if 0 <= i + by < size]
    return lax.ppermute(shard, axis, pairs)


def layer_norm(values, norm_gain, norm_bias):
    center = values - jnp.mean(values, -1, keepdims=True)
    spread = jnp.mean(center * center, -1, keepdims=True)
    return center * lax.rsqrt(spread + norm_eps) * norm_gain + norm_bias


def matmul(left_side, weight_mat):
    return jnp.dot(left_side, weight_mat, preferred_element_type=jnp.float32)


def outer_sum(left_side, grad_side):
    left_flat = left_side.reshape(-1, left_side.shape[-1])
    grad_flat = grad_side.reshape(-1, grad_side.shape[-1])
    return lax.dot_general(
        left_flat, grad_flat, (((0,), (0,)), ((), ())), preferred_element_type=jnp.float32
    )


def transposed(grad_side, weight_mat):
    return lax.dot_general(
        grad_side,
        weight_mat,
        (((grad_side.ndim - 1,), (1,)), ((), ())),
        preferred_element_type=jnp.float32,
    )


def eight_rows(matrix):
    return matrix.reshape(8, -1)


def attention_mask(key_valid, patch_rows, seq_place):
    query_pos = seq_place * patch_rows + lax.iota(jnp.int32, patch_rows)
    key_pos = (seq_place - 1) * patch_rows + lax.iota(jnp.int32, 2 * patch_rows)
    earlier = (key_pos[None, :] < query_pos[:, None])[None] & (key_valid[:, None, :] > 0)
    return earlier | (key_pos[None, :] == query_pos[:, None])[None]


def masked_scores(query, keys, allowed):
    logits = jnp.einsum(
        "bqhd,bkhd->bhqk", query, keys, preferred_element_type=jnp.float32
    ) * HEAD_DIM ** (-0.5)
    return jnp.where(allowed[:, None], logits, -1e30)


MESH = pl.DeviceIdType.MESH
OUTS = 3
UNITS = 27
LAST = 28
THIRD = 18
TURNS = 8
STEPS = 44
DRAIN = 17
DRAIN_C = 18
SLAB = 128
LABELS = 448
TABLE_ROWS = ((0, 256), (256, 192))
COLS = 384
STAGES = 3
CHUNK = 32
GELU_A = (2.0 / 3.141592653589793) ** 0.5
GELU_B = 0.044715
f32 = jnp.float32
bf16 = jnp.bfloat16


def flow_kernel(
    labels_sm, perm_sm, cot_logdet_sm,
    latents_ref, valid_ref, patch_ref, pos_table_ref, g1_ref, b1_ref, g2_ref, b2_ref,
    up_bias_ref, head_w_ref, head_b_ref, cot_ref,
    class_hbm, qkv_any, out_any, up_any, down_any,
    sums,
    stage, part, part_c, out_stage, out_in, core_in, small_in, ab_in, c_in, shared,
    down_left, down_right, up_left, up_right, bulk_send, bulk_recv, send_sem, recv_sem, stage_sem, back_sem, send_c, back_c, out_send, out_recv,
    qkv_w, out_w, up_w, down_w, load_sem,
    lat_pad, cot_pad, patch_pad, head_pad, hidden, mid, xhat1, xhat2, scale1, scale2,
    keys, values, query, attended, bias, prior_mask, mask_row, probs, slope, d_hidden, d_second, d_att, d_keys, d_values,
    d_prior, d_back, row_out, row_in, peek_out, peek_in, factor,
    lines, line_sum, line_in, line_send, line_recv,
    lt_ref, r_ref, pos_ref, small_ref, low_top, exch_send, exch_recv,
):
    dp = lax.axis_index("dp")
    core = lax.axis_index("seq")
    x, y, z = dp % 2, (dp // 2) % 2, dp // 4
    side = z // 2
    inner = ((z + 1) // 2) % 2 == 1
    outer = ((z + 1) // 2) % 2 == 0
    to_core = (dp, 1 - core)
    to_x = (dp + 1 - 2 * x, core)
    to_y = (dp + 2 - 4 * y, core)
    to_mate = (dp + 4 - 8 * (z % 2), core)
    to_x_other = (dp + 1 - 2 * x, 1 - core)
    to_y_other = (dp + 2 - 4 * y, 1 - core)
    to_inner = ((dp + 12 - 8 * z + 16) % 16, core)

    def rows_at(start, count):
        return pl.ds(pl.multiple_of(start, 16), count)

    sources = [class_hbm.at[r : r + n, h * COLS : (h + 1) * COLS] for h in range(2) for r, n in TABLE_ROWS]
    targets = [part.at[3 * h + i, 0:n] for h in range(2) for i, (r, n) in enumerate(TABLE_ROWS)]
    sources += [qkv_any.at[0], out_any.at[0]]
    targets += [qkv_w, out_w]

    def load(i):
        return pltpu.make_async_copy(sources[i], targets[i], load_sem.at[i])

    def load_feed(j):
        cols = rows = pl.ds(pl.multiple_of(j * 768, 128), 768)
        return (
            pltpu.make_async_copy(up_any.at[0, :, cols], up_w.at[:, cols], load_sem.at[6 + 2 * j]),
            pltpu.make_async_copy(down_any.at[0, rows], down_w.at[rows], load_sem.at[7 + 2 * j]),
        )

    for i in range(6):
        load(i).start()
    for j in range(4):
        for one in load_feed(j):
            one.start()

    barrier = pltpu.get_barrier_semaphore()
    for target in (to_core, to_x, to_y, to_mate, to_x_other, to_y_other):
        pl.semaphore_signal(barrier, inc=1, device_id=target, device_id_type=MESH)

    @pl.when(inner)
    def _():
        pl.semaphore_signal(barrier, inc=1, device_id=to_inner, device_id_type=MESH)

    def meet():
        @pl.when(inner)
        def _():
            pl.semaphore_wait(barrier, 7)

        @pl.when(outer)
        def _():
            pl.semaphore_wait(barrier, 6)

    def copy(u, k, src, dst, target):
        return pltpu.make_async_remote_copy(
            src_ref=src, dst_ref=dst, send_sem=send_sem.at[u], recv_sem=recv_sem.at[k, u % TURNS],
            device_id=target, device_id_type=MESH,
        )

    def copy_c(u, k, src, dst, target):
        return pltpu.make_async_remote_copy(
            src_ref=src, dst_ref=dst, send_sem=send_c.at[u], recv_sem=recv_sem.at[k, u % TURNS],
            device_id=target, device_id_type=MESH,
        )

    def arrived(u, k, dst):
        pltpu.make_async_remote_copy(
            src_ref=dst, dst_ref=dst, send_sem=send_sem.at[0], recv_sem=recv_sem.at[k, u % TURNS],
            device_id=to_core, device_id_type=MESH,
        ).wait_recv()

    def added(dst, left, right):
        dst[...] = (left[...].astype(f32) + right[...].astype(f32)).astype(bf16)

    first = (x, y)
    second = (y, x)
    to_first = (to_x, to_y)
    to_second = (to_y, to_x)

    def out_rows(u, t, start, count):
        return third_rows(u, core, start, count) if t == 2 else sums.at[u, core, rows_at(t * SLAB + start, count)]

    def third_rows(u, h, start, count):
        return sums.at[LAST + 1 + u // 2, h, rows_at((u % 2) * SLAB + start, count)]

    def part_rows(u, t, start, count):
        return part_c.at[u, rows_at(start, count)] if t == 2 else part.at[u, rows_at(t * SLAB + start, count)]

    def bulk(k, src, dst, target):
        return pltpu.make_async_remote_copy(
            src_ref=src, dst_ref=dst, send_sem=bulk_send, recv_sem=bulk_recv.at[k],
            device_id=target, device_id_type=MESH,
        )

    def down_rows(i):
        return pl.ds(pl.multiple_of(i * 768, 128), 768)

    def down_left_core(i):
        return bulk(i, down_left.at[down_rows(i), 0:128], down_left.at[down_rows(i), 128:256], to_core)

    def down_left_x(i):
        return bulk(2 + i, lt_ref.at[i], down_left.at[down_rows(i), 256:384], to_x)

    def down_left_on(i):
        return bulk(4 + i, down_left.at[down_rows(i), 256:384], down_left.at[down_rows(i), 384:512], to_core)

    def down_right_go(i):
        half, target = ((1 - core, to_core), (core, to_x), (1 - core, to_x_other))[i]
        return bulk(6 + i, r_ref.at[0, half], down_right.at[128 * (i + 1) : 128 * (i + 2)], target)

    def up_left_go(i):
        first_lane, target = ((0, to_core), (0, to_y), (256, to_core))[i]
        return bulk(
            9 + i,
            up_left.at[:, first_lane : first_lane + 128],
            up_left.at[:, 128 * (i + 1) : 128 * (i + 2)],
            target,
        )

    def up_right_go(i, j):
        target = (to_core, to_y, to_y_other)[i]
        return bulk(12 + i, r_ref.at[1 + j], up_right.at[:, 128 * (i + 1) : 128 * (i + 2)], target)

    def pass_on(i):
        down_left_x(i).wait_recv()
        down_left_on(i).start()

    def begin_ab(unit):
        u = unit - OUTS

        @pl.when(u == 0)
        def _():
            for i in range(3):
                down_right_go(i).wait_recv()
                up_right_go(i, 0).wait_recv()
            up_left_go(0).wait_recv()
            up_left_go(2).wait_recv()
            down_left_core(0).wait_recv()
            down_left_on(0).wait_recv()

        @pl.when(u == 12)
        def _():
            down_left_core(1).wait_recv()
            down_left_on(1).wait_recv()

        @pl.when(jnp.logical_and(u >= 0, unit < UNITS))
        def _():
            rows = pl.ds(pl.multiple_of(u * 64, 64), 64)
            kept = part_rows(unit, 0, x * 64, 64)
            kept[...] = jnp.dot(down_left[rows], down_right[...], preferred_element_type=f32).astype(bf16)
            ab_second(unit, 0).start()
            rows = pl.ds(pl.multiple_of((u // 2) * 64, 64), 64)
            kept = part_rows(unit, 1, y * 64, 64)
            kept[...] = jnp.dot(up_left[rows], up_right[u % 2], preferred_element_type=f32).astype(bf16)
            ab_second(unit, 1).start()

    def product(u, half):
        rows = pl.ds(pl.multiple_of((u % 6) * SLAB, 128), SLAB)
        return jnp.dot(lt_ref[6, rows], r_ref[6 + u // 6, half], preferred_element_type=f32)

    def out_product(u, half):
        rows = pl.ds(pl.multiple_of(u * 256, 256), 256)
        return jnp.dot(lt_ref[5, rows], r_ref[5, half], preferred_element_type=f32)

    def out_first(u):
        return pltpu.make_async_remote_copy(
            src_ref=out_stage.at[u], dst_ref=out_in.at[u], send_sem=out_send.at[u], recv_sem=out_recv.at[u],
            device_id=to_core, device_id_type=MESH,
        )

    def core_first(u):
        return pltpu.make_async_remote_copy(
            src_ref=stage.at[u % STAGES], dst_ref=core_in.at[u % TURNS], send_sem=stage_sem.at[u % STAGES],
            recv_sem=recv_sem.at[0, u % TURNS], device_id=to_core, device_id_type=MESH,
        )

    def small_first():
        return pltpu.make_async_remote_copy(
            src_ref=small_ref.at[1 - core], dst_ref=small_in, send_sem=stage_sem.at[STAGES],
            recv_sem=recv_sem.at[0, LAST % TURNS], device_id=to_core, device_id_type=MESH,
        )

    def line_copy(k, src, dst, target):
        return pltpu.make_async_remote_copy(
            src_ref=src, dst_ref=dst, send_sem=line_send.at[k], recv_sem=line_recv.at[k],
            device_id=target, device_id_type=MESH,
        )

    line_steps = (
        (lines, line_in.at[0], to_core),
        (line_sum.at[0], line_in.at[1], to_x),
        (line_sum.at[1], line_in.at[2], to_y),
        (line_sum.at[2], line_in.at[3], to_mate),
        (line_sum.at[3], line_in.at[4], to_inner),
        (line_sum.at[4], line_sum.at[4], to_mate),
    )

    def line_go(k):
        return line_copy(k, *line_steps[k])

    def line_add(k):
        line_go(k).wait_recv()
        line_sum[k] = line_steps[k][0][...] + line_in[k]

    def keep_lines():
        v = line_sum[4]
        for i in range(3):
            term = v.astype(bf16)
            v = v - term.astype(f32)
            for h in range(2):
                sums[LAST + 1 + THIRD // 2, h, 64 + i * 16 : 80 + i * 16] = term[:, h * COLS : (h + 1) * COLS]

    def produce(u):
        pl.when(u >= STAGES)(lambda: core_first(u - STAGES).wait_send())
        stage[u % STAGES] = product(u, 1 - core).astype(bf16)
        core_first(u).start()

    def begin(u):
        arrived(u, 0, core_in.at[u % TURNS])
        part_c[u] = (product(u, core) + core_in[u % TURNS].astype(f32)).astype(bf16)
        pl.when(outer)(lambda: c_z1(u).start())

    def begin_more(u):
        @pl.when(u < OUTS)
        def _():
            out_first(u).wait_recv()
            part[u] = (out_product(u, core) + out_in[u].astype(f32)).astype(bf16)
            for t in range(2):
                ab_first(u, t).start()

        @pl.when(u == UNITS)
        def _():
            part[UNITS] = pos_ref[...]
            for t in range(2):
                ab_first(u, t).start()
            small_first().start()
            line_go(0).start()

        @pl.when(u == LAST)
        def _():
            small_first().wait_recv()
            part[LAST] = (small_ref[core].astype(f32) + small_in[...].astype(f32)).astype(bf16)
            for t in range(2):
                ab_first(u, t).start()
            line_add(0)
            line_go(1).start()

    def ab_base(t):
        return first[t] * 64 + second[t] * 32

    def ab_first(u, t):
        return copy(u, 1, part_rows(u, t, (1 - first[t]) * 64, 64), ab_in.at[u % TURNS, t, 0:64], to_first[t])

    def ab_second(u, t):
        row = first[t] * 64 + (1 - second[t]) * 32
        return copy(u, 2, part_rows(u, t, row, 32), ab_in.at[u % TURNS, t, 64:96], to_second[t])

    def ab_z1(u, t):
        return copy(u, 3, part_rows(u, t, ab_base(t), 32), ab_in.at[u % TURNS, t, 96:128], to_mate)

    def ab_z2(u, t):
        return copy(u, 4, part_rows(u, t, ab_base(t), 32), ab_in.at[u % TURNS, t, 128:160], to_inner)

    def ab_z3(u, t):
        block = out_rows(u, t, ab_base(t), 32)
        return copy(u, 3, block, block, to_mate)

    def ab_back2(u, t):
        block = out_rows(u, t, ab_base(t), 32)
        return copy(u, 5, block, block, to_second[t])

    def ab_back1(u, t):
        block = out_rows(u, t, first[t] * 64, 64)
        return copy(u, 6, block, block, to_first[t])

    def ab1(u):
        pl.when(jnp.logical_or(u < OUTS, u >= UNITS))(lambda: ab1_more(u))

    def ab1_more(u):
        arrived(u, 1, ab_in.at[u % TURNS, :, 0:64])
        for t in range(2):
            kept = part_rows(u, t, first[t] * 64, 64)
            added(kept, kept, ab_in.at[u % TURNS, t, 0:64])
            ab_second(u, t).start()

        @pl.when(u == LAST)
        def _():
            line_add(1)
            line_go(2).start()

    def ab2(u):
        arrived(u, 2, ab_in.at[u % TURNS, :, 64:96])
        for t in range(2):
            kept = part_rows(u, t, ab_base(t), 32)
            added(kept, kept, ab_in.at[u % TURNS, t, 64:96])
            pl.when(outer)(lambda: ab_z1(u, t).start())

        @pl.when(u == LAST)
        def _():
            line_add(2)
            pl.when(outer)(line_go(3).start)

    def ab3_inner(u):
        arrived(u, 3, ab_in.at[u % TURNS, :, 96:128])
        for t in range(2):
            kept = part_rows(u, t, ab_base(t), 32)
            added(kept, kept, ab_in.at[u % TURNS, t, 96:128])
            ab_z2(u, t).start()

        @pl.when(u == LAST)
        def _():
            line_add(3)
            line_go(4).start()

    def ab4_inner(u):
        arrived(u, 4, ab_in.at[u % TURNS, :, 128:160])
        for t in range(2):
            added(out_rows(u, t, ab_base(t), 32), part_rows(u, t, ab_base(t), 32), ab_in.at[u % TURNS, t, 128:160])
            ab_z3(u, t).start()
            ab_back2(u, t).start()

        @pl.when(u == LAST)
        def _():
            line_add(4)
            line_go(5).start()
            keep_lines()

    def ab5_outer(u):
        arrived(u, 3, sums.at[u, core, 0:64])
        for t in range(2):
            ab_back2(u, t).start()

        @pl.when(u == LAST)
        def _():
            line_go(5).wait_recv()
            keep_lines()

    def ab6(u):
        arrived(u, 5, sums.at[u, core, 0:64])
        for t in range(2):
            ab_back1(u, t).start()

    def to_other(u, block):
        return pltpu.make_async_remote_copy(
            src_ref=block, dst_ref=block, send_sem=send_sem.at[u], recv_sem=back_sem.at[u],
            device_id=to_core, device_id_type=MESH,
        )

    def to_other_c(u, half):
        block = third_rows(u, half, 0, SLAB)
        return pltpu.make_async_remote_copy(
            src_ref=block, dst_ref=block, send_sem=send_c.at[u], recv_sem=back_c.at[u],
            device_id=to_core, device_id_type=MESH,
        )

    def ab7(u):
        arrived(u, 6, sums.at[u, core, 0:128])
        pl.when(u != UNITS)(lambda: to_other(u, sums.at[u, core]).start())

    far = 32 * (1 - side)
    own_end = 96 * side
    shard = z * 32

    def c_z1(u):
        return copy_c(u, 7, part_rows(u, 2, far, 96), c_in.at[u % TURNS, 0:96], to_mate)

    def c_z2(u):
        return copy_c(u, 8, part_rows(u, 2, (1 - side) * 64, 64), c_in.at[u % TURNS, 96:160], to_inner)

    def c_z3(u):
        return copy_c(u, 7, part_rows(u, 2, own_end, 32), c_in.at[u % TURNS, 160:192], to_mate)

    def c_x(u):
        return copy_c(u, 9, part_rows(u, 2, shard, 32), c_in.at[u % TURNS, 192:224], to_x)

    def c_y(u):
        return copy_c(u, 10, shared.at[u], c_in.at[u % TURNS, 224:256], to_y)

    def c_z4(u):
        block = out_rows(u, 2, own_end, 32)
        return copy_c(u, 11, block, block, to_mate)

    def c_z5(u):
        block = out_rows(u, 2, side * 64, 64)
        return copy_c(u, 12, block, block, to_inner)

    def c_z6(u):
        block = out_rows(u, 2, far, 96)
        return copy_c(u, 11, block, block, to_mate)

    def c1_inner(u):
        arrived(u, 7, c_in.at[u % TURNS, 0:96])
        kept = part_rows(u, 2, far, 96)
        added(kept, kept, c_in.at[u % TURNS, 0:96])
        c_z2(u).start()

    def c2_inner(u):
        arrived(u, 8, c_in.at[u % TURNS, 96:160])
        kept = part_rows(u, 2, side * 64, 64)
        added(kept, kept, c_in.at[u % TURNS, 96:160])
        c_z3(u).start()
        c_x(u).start()

    def c3_outer(u):
        arrived(u, 7, c_in.at[u % TURNS, 160:192])
        kept = part_rows(u, 2, shard, 32)
        added(kept, kept, c_in.at[u % TURNS, 160:192])
        c_x(u).start()

    def c4(u):
        arrived(u, 9, c_in.at[u % TURNS, 192:224])
        kept = part_rows(u, 2, shard, 32)
        part_y = shared.at[u]
        added(part_y, kept, c_in.at[u % TURNS, 192:224])
        c_y(u).start()

    def c5(u):
        arrived(u, 10, c_in.at[u % TURNS, 224:256])
        added(out_rows(u, 2, shard, 32), shared.at[u], c_in.at[u % TURNS, 224:256])
        pl.when(outer)(lambda: c_z4(u).start())

    def c8_inner(u):
        arrived(u, 11, out_rows(u, 2, own_end, 32))
        c_z5(u).start()

    def c9_inner(u):
        arrived(u, 12, out_rows(u, 2, (1 - side) * 64, 64))
        c_z6(u).start()
        to_other_c(u, core).start()

    def c10_outer(u):
        arrived(u, 11, out_rows(u, 2, far, 96))
        to_other_c(u, core).start()

    def sent(sem, units, rows):
        ref = part.at[0:units, 0:rows]
        pltpu.make_async_remote_copy(
            src_ref=ref, dst_ref=ref, send_sem=sem, recv_sem=back_sem.at[0],
            device_id=to_core, device_id_type=MESH,
        ).wait_send()

    def sent_either(sem, at_outer, at_inner):
        pl.when(outer)(lambda: sent(sem, *at_outer))
        pl.when(inner)(lambda: sent(sem, *at_inner))

    def drain(u):
        pl.when(u < OUTS)(lambda: sent_either(send_sem.at[u], (4, 176), (3, 256)))
        pl.when(u >= OUTS)(lambda: sent_either(send_sem.at[u], (4, 144), (4, 160)))
        to_other(u, sums.at[u, 1 - core]).wait_recv()

    def drain_c(u):
        sent_either(send_c.at[u], (2, 160), (2, 224))
        to_other_c(u, 1 - core).wait_recv()

    mm_nt = (((1,), (1,)), ((), ()))
    mm_tn = (((0,), (0,)), ((), ()))

    def nt(left, right):
        return lax.dot_general(left, right, mm_nt, preferred_element_type=f32)

    def tn(left, right):
        return lax.dot_general(left, right, mm_tn, preferred_element_type=f32)

    def nn(left, right):
        return jnp.dot(left, right, preferred_element_type=f32)

    def exchange(k, src, dst):
        return pltpu.make_async_remote_copy(
            src_ref=src, dst_ref=dst, send_sem=exch_send.at[k], recv_sem=exch_recv.at[k],
            device_id=to_core, device_id_type=MESH,
        )

    chunks = [slice(r, r + CHUNK) for r in range(0, 128, CHUNK)]
    lane = lax.broadcasted_iota(jnp.int32, (128, 128), 1)
    row = lax.broadcasted_iota(jnp.int32, (128, 128), 0)
    eye = row == lane
    low_half = lane < 64
    valid_row = valid_ref[...].astype(f32)
    valid_col = jnp.sum(jnp.where(eye, valid_row, 0.0), axis=1, keepdims=True)
    mask_row[...] = jnp.broadcast_to(valid_row, (8, 128))
    lat_pad[...] = jnp.zeros((128, 128), f32)
    lat_pad[0:48] = latents_ref[0]
    lat_pad[...] = lat_pad[...].T
    cot_pad[...] = jnp.zeros((128, 128), f32)
    cot_pad[0:48] = cot_ref[0]
    cot_pad[...] = cot_pad[...].T
    patch_pad[...] = jnp.zeros((128, 768), bf16)
    patch_pad[0:48] = patch_ref[...]
    head_pad[...] = jnp.zeros((128, 768), bf16)
    head_pad[0:96] = head_w_ref[...]
    head_bias = jnp.concatenate((head_b_ref[...].astype(f32), jnp.zeros((1, 32), f32)), 1)

    @pl.when(core == 0)
    def _():
        keys[0:128] = jnp.zeros((128, 768), bf16)
        values[0:128] = jnp.zeros((128, 768), bf16)
        prior_mask[...] = jnp.zeros((8, 128), f32)
        row_in[...] = jnp.zeros((8, 128), f32)

    @pl.when(core == 1)
    def _():
        peek_in[...] = jnp.zeros((8, 128), f32)
        d_back[...] = jnp.zeros((2, 128, 768), bf16)

    line8 = lax.broadcasted_iota(jnp.int32, (8, 128), 0)
    peek_out[...] = jnp.where(line8 == 0, lat_pad[0:1], jnp.where(line8 == 1, cot_pad[0:1], valid_row[:, 0:1]))

    def normalize(src, hat, scale, gain, shift, put):
        for r in chunks:
            v = src[r]
            center = v - jnp.mean(v, -1, keepdims=True)
            inv = lax.rsqrt(jnp.mean(center * center, -1, keepdims=True) + norm_eps)
            scaled = center * inv
            hat[r] = scaled
            scale[r] = inv
            put(r, scaled * gain + shift)

    label = labels_sm[perm_sm[0]]
    hot = jnp.where(lax.broadcasted_iota(jnp.int32, (16, LABELS), 1) == label, 1.0, 0.0).astype(bf16)
    for i in range(4):
        load(i).wait()
    class_row = jnp.concatenate(
        [
            sum(nn(hot[:, r : r + n], part[3 * h + i, 0:n]) for i, (r, n) in enumerate(TABLE_ROWS))
            for h in range(2)
        ],
        1,
    )[0:1]
    hidden[...] = (
        nn(lat_pad[...].astype(bf16), patch_pad[...]) + pos_table_ref[...].astype(f32) + class_row
    )

    def put_low(r, v):
        low_top[r] = v.astype(bf16)

    normalize(hidden, xhat1, scale1, g1_ref[...].astype(f32), b1_ref[...].astype(f32), put_low)
    load(4).wait()
    normed = low_top[...]
    keys[128:256] = nn(normed, qkv_w[:, 768:1536]).astype(bf16)
    meet()

    @pl.when(core == 1)
    def _():
        exchange(4, peek_out, peek_in).start()

    @pl.when(core == 0)
    def _():
        exchange(2, mask_row, prior_mask).start()
        exchange(0, keys.at[128:256], keys.at[0:128]).start()

    values[128:256] = nn(normed, qkv_w[:, 1536:2304]).astype(bf16)

    @pl.when(core == 0)
    def _():
        exchange(1, values.at[128:256], values.at[0:128]).start()

    query[...] = nn(normed, qkv_w[:, 0:768]).astype(bf16)
    lt_ref[6] = normed.astype(f32).T.astype(bf16)

    @pl.when(core == 1)
    def _():
        exchange(2, mask_row, prior_mask).wait_recv()
        exchange(0, keys.at[128:256], keys.at[0:128]).wait_recv()
        exchange(1, values.at[128:256], values.at[0:128]).wait_recv()

    bias[:, 0:128] = jnp.where(jnp.broadcast_to(prior_mask[0:1], (128, 128)) > 0.5, 0.0, -1e30)
    bias[:, 128:256] = jnp.where(((lane < row) & (valid_row > 0.5)) | eye, 0.0, -1e30)

    def columns128(p):
        return pl.ds(pl.multiple_of(p * 128, 128), 128)

    def attend(p):
        cols = columns128(p)
        q_pair = query[:, cols]
        k_pair = keys[:, cols]
        v_pair = values[:, cols]
        outs = []
        for i in range(2):
            q_one = jnp.where(low_half if i == 0 else lane >= 64, q_pair, jnp.zeros_like(q_pair))
            scores = nt(q_one, k_pair) * 0.125 + bias[...]
            top = jnp.max(scores, -1, keepdims=True)
            powers = jnp.exp(scores - top)
            soft = powers * (1.0 / jnp.sum(powers, -1, keepdims=True))
            probs[2 * p + i] = soft
            outs.append(nn(soft.astype(bf16), v_pair))
        attended[:, cols] = jnp.where(low_half, outs[0], outs[1]).astype(bf16)

    for p in range(6):
        attend(p)
    load(5).wait()
    mid[...] = hidden[...] + nn(attended[...], out_w[...])
    lt_ref[5] = attended[...].astype(f32).T.astype(bf16)
    normalize(mid, xhat2, scale2, g2_ref[...].astype(f32), b2_ref[...].astype(f32), put_low)
    up_left[:, 0:128] = low_top[...].astype(f32).T.astype(bf16)
    for i in range(2):
        up_left_go(i).start()
    d_hidden[...] = mid[...]

    def rows768(j):
        return pl.ds(pl.multiple_of(j * 768, 128), 768)

    def feed(j, carried):
        for one in load_feed(j):
            one.wait()
        d_second[...] = nn(low_top[...], up_w[:, rows768(j)])
        shift = up_bias_ref[:, rows768(j)].astype(f32)
        for r in chunks:
            pre = d_second[r] + shift
            square = pre * pre
            bend = jnp.tanh(pre * (GELU_A + (GELU_A * GELU_B) * square))
            left = 0.5 * (1.0 + bend)
            slope[j, r] = left + 0.5 * pre * (1.0 - bend * bend) * (GELU_A + (3.0 * GELU_A * GELU_B) * square)
            d_second[r] = pre * left
        act = d_second[...]
        turned = act.T.astype(bf16)

        @pl.when(j // 2 == x)
        def _():
            down_left[down_rows(j % 2), 0:128] = turned
            down_left_core(j % 2).start()

        @pl.when(j // 2 != x)
        def _():
            lt_ref[j % 2] = turned
            pl.when(j % 2 == 0)(lambda: down_left_x(0).start())

        d_hidden[...] += nn(act.astype(bf16), down_w[rows768(j)])
        return carried

    lax.fori_loop(0, 4, feed, 0, unroll=True)
    low_top[...] = d_hidden[...].astype(bf16)
    row_out[...] = nt(low_top[...], head_pad[...]) + head_bias

    @pl.when(core == 0)
    def _():
        exchange(3, row_out.at[120:128], row_in).start()

    def coupling(shifted, latent, cot):
        inside = lax.broadcasted_iota(jnp.int32, shifted.shape, 1) < 48
        alpha = jnp.where(inside, shifted, 0.0)
        scale = jnp.exp(-alpha)
        moved = (latent - jnp.where(inside, pltpu.roll(shifted, 80, 1), 0.0)) * scale
        d_alpha = -cot * moved - cot_logdet_sm[0]
        d_mean = pltpu.roll(jnp.where(inside, -cot * scale, 0.0), 48, 1)
        return alpha, scale, moved, jnp.where(inside, d_alpha, d_mean)

    rolled = pltpu.roll(row_out[...], 1, 0)
    d_shifted = coupling(jnp.where(row == 0, 0.0, rolled) * valid_col, lat_pad[...], cot_pad[...])[3] * valid_col

    @pl.when(core == 0)
    def _():
        exchange(4, peek_out, peek_in).wait_recv()

    def peeked(i):
        return jnp.broadcast_to(peek_in[i : i + 1], (8, 128))

    after_last = jnp.broadcast_to(row_out[127:128], (8, 128)) * peeked(2)
    d_next = coupling(after_last, peeked(0), peeked(1))[3] * peeked(2)
    d_head = jnp.where(row == 127, d_next[0:1], pltpu.roll(d_shifted, 127, 0)).astype(bf16)

    def outputs():
        @pl.when(core == 1)
        def _():
            exchange(3, row_out.at[120:128], row_in).wait_recv()

        before = jnp.where(row == 0, jnp.broadcast_to(row_in[7:8], (128, 128)), pltpu.roll(row_out[...], 1, 0))
        alpha, scale, moved = coupling(before * valid_col, lat_pad[...], cot_pad[...])[0:3]
        factor[...] = scale
        store_exact(0, moved.T[0:48])
        logdet = -jnp.sum(jnp.sum(alpha, 1, keepdims=True), 0, keepdims=True)
        lines[8:9, 128:256] = jnp.where(lax.broadcasted_iota(jnp.int32, (1, 128), 1) == dp, logdet, 0.0)

    def exact_terms(v):
        terms = []
        for i in range(3):
            terms.append(v.astype(bf16))
            v = v - terms[i].astype(f32)
        return terms

    def store_exact(h, v):
        for i, term in enumerate(exact_terms(v)):
            sums[LAST + 1 + THIRD // 2, h, 0:48, i * 128 : (i + 1) * 128] = term

    head_grad = tn(d_head, low_top[...])
    head_bias_grad = jnp.sum(d_head.astype(f32), 0, keepdims=True)
    d_hidden[...] = nn(d_head, head_pad[...])
    low_top[...] = d_hidden[...].astype(bf16)
    for h in range(2):
        r_ref[0, h] = low_top[:, h * COLS : (h + 1) * COLS]
    for i in range(3):
        down_right_go(i).start()
    down_left_x(1).start()
    down_right[0:128] = r_ref[0, core]

    def put(first_row, value):
        h, r = first_row // 128, first_row % 128
        for t in range(2):
            small_ref[h, t * 128 + r : t * 128 + r + value.shape[0]] = value[:, t * COLS : (t + 1) * COLS].astype(bf16)

    put(0, head_grad[0:96])

    lines[...] = jnp.zeros((16, 768), f32)
    lines[8:9, 0:128] = head_bias_grad

    d_second[...] = jnp.zeros((128, 768), f32)

    def feed_back(j):
        d_keys[...] = nt(low_top[...], down_w[rows768(j)])
        total = jnp.zeros((1, 768), f32)
        for r in chunks:
            d_pre = (slope[j, r] * d_keys[r]).astype(bf16)
            d_att[r] = d_pre
            total += jnp.sum(d_pre.astype(f32), 0, keepdims=True)
            for h in range(2):
                r_ref[1 + j, h, r] = d_pre[:, h * COLS : (h + 1) * COLS]
        near, same = j // 2 == y, j % 2 == core

        @pl.when(jnp.logical_and(near, same))
        def _():
            for h in range(2):
                up_right[h, 0:128] = r_ref[1 + j, h]

        pl.when(jnp.logical_and(near, j % 2 != core))(lambda: up_right_go(0, j).start())
        pl.when(jnp.logical_and(j // 2 != y, same))(lambda: up_right_go(1, j).start())
        pl.when(jnp.logical_and(j // 2 != y, j % 2 != core))(lambda: up_right_go(2, j).start())
        lines[pl.ds(4 + j, 1)] = total
        d_second[...] += nt(d_att[...], up_w[:, rows768(j)])

    def norm_back(grad, hat, scale, gain, base, out, line):
        gain_total = jnp.zeros((1, 768), f32)
        shift_total = jnp.zeros((1, 768), f32)
        for r in chunks:
            d = grad[r]
            scaled = hat[r]
            e = d * gain
            v = e - jnp.mean(e, -1, keepdims=True) - scaled * jnp.mean(e * scaled, -1, keepdims=True)
            out[r] = base[r] + scale[r] * v
            gain_total += jnp.sum(d * scaled, 0, keepdims=True)
            shift_total += jnp.sum(d, 0, keepdims=True)
        lines[line : line + 1] = gain_total
        lines[line + 1 : line + 2] = shift_total

    def feed_norm_back():
        norm_back(d_second, xhat2, scale2, g2_ref[...].astype(f32), d_hidden, mid, 2)
        low_top[...] = mid[...].astype(bf16)
        for h in range(2):
            r_ref[5, h] = low_top[:, h * COLS : (h + 1) * COLS]
        d_att[...] = nt(low_top[...], out_w[...]).astype(bf16)

    def attend_back(p):
        cols = columns128(p)
        q_pair = query[:, cols]
        k_pair = keys[:, cols]
        v_pair = values[:, cols]
        a_pair = d_att[:, cols]
        dq, dk, dv = [], [], []
        for i in range(2):
            own = low_half if i == 0 else lane >= 64
            a_one = jnp.where(own, a_pair, jnp.zeros_like(a_pair))
            q_one = jnp.where(own, q_pair, jnp.zeros_like(q_pair))
            soft = probs[2 * p + i]
            d_soft = nt(a_one, v_pair)
            weighted = d_soft * soft
            d_score = weighted - soft * jnp.sum(weighted, -1, keepdims=True)
            d_low = d_score.astype(bf16)
            dq.append(nn(d_low, k_pair))
            dk.append(tn(d_low, q_one))
            dv.append(tn(soft.astype(bf16), a_one))
        h, local = p // 3, pl.ds(pl.multiple_of((p % 3) * 128, 128), 128)
        r_ref[6, h, :, local] = (jnp.where(low_half, dq[0], dq[1]) * 0.125).astype(bf16)
        dk_pair = (dk[0] + dk[1]) * 0.125
        dv_pair = dv[0] + dv[1]
        d_prior[0, :, cols] = dk_pair[0:128].astype(bf16)
        d_prior[1, :, cols] = dv_pair[0:128].astype(bf16)
        d_keys[:, cols] = dk_pair[128:256]
        d_values[:, cols] = dv_pair[128:256]

    def send_prior():
        @pl.when(core == 1)
        def _():
            exchange(5, d_prior, d_back).start()

    def packed_back():
        @pl.when(core == 0)
        def _():
            exchange(5, d_prior, d_back).wait_recv()

        for h in range(2):
            cols = slice(h * COLS, (h + 1) * COLS)
            r_ref[7, h] = (d_keys[:, cols] + d_back[0, :, cols].astype(f32)).astype(bf16)
            r_ref[8, h] = (d_values[:, cols] + d_back[1, :, cols].astype(f32)).astype(bf16)
        d_second[...] = sum(
            nt(r_ref[6 + j, h], qkv_w[:, j * 768 + h * COLS : j * 768 + (h + 1) * COLS])
            for j in range(3)
            for h in range(2)
        )

    def embed_back():
        norm_back(d_second, xhat1, scale1, g1_ref[...].astype(f32), mid, d_hidden, 0)
        low_top[...] = d_hidden[...].astype(bf16)
        for t in range(2):
            pos_ref[t * 128 : (t + 1) * 128] = low_top[:, t * COLS : (t + 1) * COLS]
        patch_grad = tn(lat_pad[...].astype(bf16), low_top[...])
        store_exact(1, (cot_pad[...] * factor[...] + nt(low_top[...], patch_pad[...])).T[0:48])
        class_grad = jnp.sum(d_hidden[...], 0, keepdims=True)
        put(96, patch_grad[0:32])
        put(128, patch_grad[32:48])
        line = lax.broadcasted_iota(jnp.int32, (16, 768), 0)
        put(144, jnp.where(line == dp, class_grad, 0.0))
        put(160, jnp.zeros((96, 768), f32))

    def feed_back_all(j, carried):
        feed_back((j + 2 * (1 - y)) % 4)
        return carried

    lax.fori_loop(0, 4, feed_back_all, 0)
    pass_on(0)
    up_left_go(1).wait_recv()
    up_left_go(2).start()
    feed_norm_back()
    for u in range(OUTS):
        out_stage[u] = out_product(u, 1 - core).astype(bf16)
        out_first(u).start()

    def piece(t):
        @pl.when(jnp.logical_and(t >= 2, t < 4))
        def _():
            for i in range(3):
                attend_back(3 * t - 6 + i)

        pl.when(t == 4)(lambda: pass_on(1))
        pl.when(t == 3)(send_prior)
        pl.when(t == 5)(packed_back)
        pl.when(t == 6)(outputs)
        pl.when(t == 7)(embed_back)

    everyone, inners, outers = None, inner, outer
    events = [
        (4, None, everyone, produce),
        (5, None, everyone, begin),
        (2, LAST + 1, everyone, begin_more),
        (9, None, inners, c4),
        (4, LAST + 1, everyone, begin_ab),
        (9, None, outers, c3_outer),
        (4, LAST + 1, everyone, ab1),
        (10, LAST + 1, outers, ab5_outer),
        (7, None, inners, c2_inner),
        (6, LAST + 1, inners, ab3_inner),
        (13, LAST + 1, outers, ab7),
        (11, None, inners, c5),
        (12, LAST + 1, inners, ab6),
        (14, None, inners, c9_inner),
        (0, LAST + 1, everyone, piece),
        (15, LAST + 1, inners, ab7),
        (5, None, inners, c1_inner),
        (7, LAST + 1, inners, ab4_inner),
        (5, LAST + 1, everyone, ab2),
        (10, None, outers, c4),
        (11, LAST + 1, outers, ab6),
        (11, None, outers, c5),
        (12, None, inners, c8_inner),
        (16, None, outers, c10_outer),
        (DRAIN, UNITS, everyone, drain),
        (DRAIN_C, None, everyone, drain_c),
    ]

    def step(t, carried):
        for lag, count, who, event in events:
            if count is None:
                turn = t - lag + 48
                u = 2 * (turn // 3) + turn % 3 - 32
                now = jnp.logical_and(turn >= 48, jnp.logical_and(turn % 3 < 2, u < THIRD))
            else:
                u = t - lag
                now = jnp.logical_and(u >= 0, u < count)
            if who is not None:
                now = jnp.logical_and(now, who)
            pl.when(now)(lambda event=event, u=u: event(u))
        return carried

    lax.fori_loop(2, STEPS, step, 0)


    def drain_more(u, carried):
        drain(u)
        return carried

    lax.fori_loop(STEPS - DRAIN, UNITS, drain_more, 0)
    for u in range(18, THIRD):
        drain_c(u)
    sent_either(send_sem.at[UNITS], (2, 224), (2, 256))
    sent_either(send_sem.at[LAST], (4, 176), (3, 256))
    to_other(LAST, sums.at[LAST, 1 - core]).wait_recv()
    for u in range(OUTS):
        out_first(u).wait_send()
    for u in range(THIRD - STAGES, THIRD):
        core_first(u).wait_send()
    small_first().wait_send()
    for k in range(3):
        line_go(k).wait_send()
    every = part.at[0:18, 0:192]
    bulk(0, every, every, to_core).wait_send()
    pl.when(outer)(line_go(3).wait_send)

    @pl.when(inner)
    def _():
        line_go(4).wait_send()
        line_go(5).wait_send()

    @pl.when(core == 0)
    def _():
        exchange(2, mask_row, prior_mask).wait_send()
        exchange(0, keys.at[128:256], keys.at[0:128]).wait_send()
        exchange(1, values.at[128:256], values.at[0:128]).wait_send()
        exchange(3, row_out.at[120:128], row_in).wait_send()

    @pl.when(core == 1)
    def _():
        exchange(4, peek_out, peek_in).wait_send()
        exchange(5, d_prior, d_back).wait_send()


def flow(
    class_labels, group_perm, cot_logdet, latents, valid, patch_weight, pos_table, ln1_gain, ln1_bias,
    ln2_gain, ln2_bias, up_bias, head_weight, head_bias, cot_latents, class_table,
    qkv_weight, out_weight, up_weight, down_weight,
):
    smem = pl.BlockSpec(memory_space=pltpu.SMEM)
    vmem = pl.BlockSpec(memory_space=pltpu.VMEM)
    hbm = pl.BlockSpec(memory_space=pltpu.HBM)
    wide = (128, 768)
    return pl.pallas_call(
        flow_kernel,
        out_shape=pltpu.VMEM((LAST + 2 + THIRD // 2, 2, 2 * SLAB, COLS), bf16),
        in_specs=[smem] * 3 + [vmem] * 12 + [hbm] * 5,
        out_specs=vmem,
        scratch_shapes=[
            pltpu.VMEM((STAGES, SLAB, COLS), bf16),
            pltpu.VMEM((LAST + 1, 2 * SLAB, COLS), bf16),
            pltpu.VMEM((THIRD, SLAB, COLS), bf16),
            pltpu.VMEM((OUTS, 2 * SLAB, COLS), bf16),
            pltpu.VMEM((OUTS, 2 * SLAB, COLS), bf16),
            pltpu.VMEM((TURNS, SLAB, COLS), bf16),
            pltpu.VMEM((256, COLS), bf16),
            pltpu.VMEM((TURNS, 2, 160, COLS), bf16),
            pltpu.VMEM((TURNS, 256, COLS), bf16),
            pltpu.VMEM((THIRD, 32, COLS), bf16),
            pltpu.VMEM((1536, 512), bf16),
            pltpu.VMEM((512, COLS), bf16),
            pltpu.VMEM((768, 512), bf16),
            pltpu.VMEM((2, 512, COLS), bf16),
            pltpu.SemaphoreType.DMA,
            pltpu.SemaphoreType.DMA((15,)),
            pltpu.SemaphoreType.DMA((LAST + 1,)),
            pltpu.SemaphoreType.DMA((13, TURNS)),
            pltpu.SemaphoreType.DMA((STAGES + 1,)),
            pltpu.SemaphoreType.DMA((LAST + 1,)),
            pltpu.SemaphoreType.DMA((THIRD,)),
            pltpu.SemaphoreType.DMA((THIRD,)),
            pltpu.SemaphoreType.DMA((OUTS,)),
            pltpu.SemaphoreType.DMA((OUTS,)),
            pltpu.VMEM((768, 2304), bf16),
            pltpu.VMEM((768, 768), bf16),
            pltpu.VMEM((768, 3072), bf16),
            pltpu.VMEM((3072, 768), bf16),
            pltpu.SemaphoreType.DMA((14,)),
            pltpu.VMEM((128, 128), f32),
            pltpu.VMEM((128, 128), f32),
            pltpu.VMEM(wide, bf16),
            pltpu.VMEM(wide, bf16),
            pltpu.VMEM(wide, f32),
            pltpu.VMEM(wide, f32),
            pltpu.VMEM(wide, f32),
            pltpu.VMEM(wide, f32),
            pltpu.VMEM((128, 1), f32),
            pltpu.VMEM((128, 1), f32),
            pltpu.VMEM((256, 768), bf16),
            pltpu.VMEM((256, 768), bf16),
            pltpu.VMEM(wide, bf16),
            pltpu.VMEM(wide, bf16),
            pltpu.VMEM((128, 256), f32),
            pltpu.VMEM((8, 128), f32),
            pltpu.VMEM((8, 128), f32),
            pltpu.VMEM((12, 128, 256), f32),
            pltpu.VMEM((4, 128, 768), f32),
            pltpu.VMEM(wide, f32),
            pltpu.VMEM(wide, f32),
            pltpu.VMEM(wide, bf16),
            pltpu.VMEM(wide, f32),
            pltpu.VMEM(wide, f32),
            pltpu.VMEM((2, 128, 768), bf16),
            pltpu.VMEM((2, 128, 768), bf16),
            pltpu.VMEM((128, 128), f32),
            pltpu.VMEM((8, 128), f32),
            pltpu.VMEM((8, 128), f32),
            pltpu.VMEM((8, 128), f32),
            pltpu.VMEM((128, 128), f32),
            pltpu.VMEM((16, 768), f32),
            pltpu.VMEM((5, 16, 768), f32),
            pltpu.VMEM((5, 16, 768), f32),
            pltpu.SemaphoreType.DMA((6,)),
            pltpu.SemaphoreType.DMA((6,)),
            pltpu.VMEM((7, 768, 128), bf16),
            pltpu.VMEM((9, 2, 128, COLS), bf16),
            pltpu.VMEM((256, COLS), bf16),
            pltpu.VMEM((2, 256, COLS), bf16),
            pltpu.VMEM(wide, bf16),
            pltpu.SemaphoreType.DMA((6,)),
            pltpu.SemaphoreType.DMA((6,)),
        ],
        compiler_params=pltpu.CompilerParams(
            collective_id=0, has_side_effects=True, vmem_limit_bytes=46 << 20
        ),
        name="flow",
    )(
        class_labels, group_perm, cot_logdet, latents, valid, patch_weight, pos_table, ln1_gain, ln1_bias,
        ln2_gain, ln2_bias, up_bias, head_weight, head_bias, cot_latents, class_table,
        qkv_weight, out_weight, up_weight, down_weight,
    )


def finish_kernel(
    labels_ref, sums,
    new_latents, logdet, latents_grad, patch, pos, classes, g1, b1, qkv, out, g2, b2, up, ub, down, head, hb,
    wide_down, wide_up, wide_last, write_sem, lat_wide, pos_wide, small_wide, class_wide, out_sem,
):
    dp = lax.axis_index("dp")
    core = lax.axis_index("seq")
    owned = classes.shape[0]
    outputs = [
        pltpu.make_async_copy(src, dst, out_sem.at[i])
        for i, (src, dst) in enumerate(
            (
                (lat_wide.at[0], new_latents.at[0]),
                (lat_wide.at[1], latents_grad.at[0]),
                (small_wide.at[0:96], head),
                (small_wide.at[96:144], patch),
                (pos_wide, pos),
                (class_wide, classes),
            )
        )
    ]
    def write(k, src, dst):
        pltpu.make_async_copy(src, dst, write_sem.at[k]).start()

    def little():
        for h in range(2):
            terms = [sums[LAST + 1 + THIRD // 2, h, 0:48, i * 128 : (i + 1) * 128].astype(f32) for i in range(3)]
            lat_wide[h] = terms[0] + terms[1] + terms[2]
        outputs[0].start()
        outputs[1].start()
        for t in range(2):
            rows, cols = slice(t * 128, (t + 1) * 128), slice(t * COLS, (t + 1) * COLS)
            pos_wide[:, cols] = sums[UNITS, core, rows].astype(f32)
            for h in range(2):
                small_wide[h * 128 : (h + 1) * 128, cols] = sums[LAST, h, rows].astype(f32)
        for one in outputs[2:5]:
            one.start()
        halves = []
        for h in range(2):
            terms = [sums[LAST + 1 + THIRD // 2, h, 64 + i * 16 : 80 + i * 16].astype(f32) for i in range(3)]
            halves.append(terms[0] + terms[1] + terms[2])
        block = jnp.concatenate(halves, 1)
        for i, one in enumerate((g1, b1, g2, b2)):
            one[...] = block[i : i + 1]
        for i in range(4):
            ub[:, i * 768 : (i + 1) * 768] = block[4 + i : 5 + i]
        hb[...] = block[8:9, 0:96]
        count = labels_ref.shape[1]
        lane = lax.broadcasted_iota(jnp.int32, (1, 128), 1)
        logdet[...] = jnp.sum(jnp.where(lane == dp, block[8:9, 128:256], 0.0), 1, keepdims=True)
        by_lane = jnp.broadcast_to(labels_ref[...], (count, count)).astype(f32)
        first = lax.broadcasted_iota(jnp.int32, (count, count), 0)
        second = lax.broadcasted_iota(jnp.int32, (count, count), 1)
        by_row = jnp.sum(jnp.where(first == second, by_lane, 0.0), 1, keepdims=True)
        before = (by_lane < by_row) | ((by_lane == by_row) & (second < first))
        rank = jnp.sum(jnp.where(before, 1.0, 0.0), 1, keepdims=True)
        stored = jnp.sum(jnp.where(rank == second.astype(f32), by_row, 0.0), 0, keepdims=True)
        wanted = (dp * owned + lax.broadcasted_iota(jnp.int32, (owned, count), 0)).astype(f32)
        hot = jnp.where(stored == wanted, 1.0, 0.0).astype(bf16)
        class_wide[...] = jnp.dot(hot, small_wide[144:160].astype(bf16), preferred_element_type=f32)
        outputs[5].start()

    for u in range(OUTS):
        rows = slice(256 * u, 256 * (u + 1))
        for h in range(2):
            wide_last[0, rows, h * COLS : (h + 1) * COLS] = sums[u, h].astype(f32)
        write(0, wide_last.at[0, rows], out.at[0, rows])
    for u in range(UNITS - OUTS):
        turn = 64 * (u // 2)
        for h in range(2):
            cols = slice(h * COLS, (h + 1) * COLS)
            for i in range(2):
                wide_down[1536 * i + 64 * u : 1536 * i + 64 * (u + 1), cols] = sums[
                    u + OUTS, h, 64 * i : 64 * (i + 1)
                ].astype(f32)
                column = (2 * i + h) * 768 + (u % 2) * COLS
                wide_up[turn : turn + 64, column : column + COLS] = sums[
                    u + OUTS, h, 128 + 64 * i : 128 + 64 * (i + 1)
                ].astype(f32)
        if u % 2 == 1:
            write(1, wide_up.at[turn : turn + 64], up.at[0, turn : turn + 64])
        if u % 4 == 3:
            for i in range(2):
                rows = slice(1536 * i + 64 * (u - 3), 1536 * i + 64 * (u + 1))
                write(2, wide_down.at[rows], down.at[0, rows])
        if u == 3:
            little()
    for u in range(THIRD):
        block, row = u // 6, (u % 6) * SLAB
        for h in range(2):
            wide_last[block + 1, row : row + SLAB, h * COLS : (h + 1) * COLS] = sums[
                LAST + 1 + u // 2, h, (u % 2) * SLAB : (u % 2 + 1) * SLAB
            ].astype(f32)
        write(
            0,
            wide_last.at[block + 1, row : row + SLAB],
            qkv.at[0, row : row + SLAB, block * 768 : (block + 1) * 768],
        )
    for k, buffer in enumerate((wide_last, wide_up, wide_down)):
        pltpu.make_async_copy(buffer, buffer, write_sem.at[k]).wait()
    for one in outputs:
        one.wait()


def finish(class_labels, sums):
    count = class_labels.shape[1]
    owned = 1024 // count
    shapes = [
        (1, 48, 128), (1, 1), (1, 48, 128), (48, 768), (128, 768), (owned, 768), (1, 768), (1, 768),
        (1, 768, 2304), (1, 768, 768), (1, 768), (1, 768), (1, 768, 3072), (1, 3072), (1, 3072, 768),
        (96, 768), (1, 96),
    ]
    vmem = pl.BlockSpec(memory_space=pltpu.VMEM)
    hbm = pl.BlockSpec(memory_space=pl.ANY)
    return pl.pallas_call(
        finish_kernel,
        out_shape=[jax.ShapeDtypeStruct(shape, f32) for shape in shapes],
        in_specs=[vmem, vmem],
        out_specs=[vmem if i in (1, 6, 7, 10, 11, 13, 16) else hbm for i in range(17)],
        scratch_shapes=[
            pltpu.VMEM((3072, 768), f32),
            pltpu.VMEM((768, 3072), f32),
            pltpu.VMEM((4, 768, 768), f32),
            pltpu.SemaphoreType.DMA((3,)),
            pltpu.VMEM((2, 48, 128), f32),
            pltpu.VMEM((128, 768), f32),
            pltpu.VMEM((256, 768), f32),
            pltpu.VMEM((owned, 768), f32),
            pltpu.SemaphoreType.DMA((6,)),
        ],
        compiler_params=pltpu.CompilerParams(vmem_limit_bytes=34 << 20),
        name="finish",
    )(class_labels, sums)


def fast_local(
    latents, valid, class_labels, group_perm, patch_weight, pos_table, class_table, ln1_gain, ln1_bias,
    qkv_weight, out_weight, ln2_gain, ln2_bias, up_weight, up_bias, down_weight, head_weight, head_bias,
    cot_latents, cot_logdet,
):
    sums = flow(
        class_labels, group_perm, cot_logdet, latents.swapaxes(1, 2), valid, patch_weight, pos_table, ln1_gain,
        ln1_bias, ln2_gain, ln2_bias, up_bias, head_weight.T, head_bias[None], cot_latents.swapaxes(1, 2), class_table,
        qkv_weight, out_weight, up_weight, down_weight,
    )
    results = list(finish(class_labels[None], sums))
    results[1] = results[1].reshape(1)
    results[16] = results[16].reshape(96)
    results[0], results[2] = results[0].swapaxes(1, 2), results[2].swapaxes(1, 2)
    results[15] = results[15].T
    return tuple(results)


def forward(latents, valid, class_rows, seq_place, weights):
    (
        patch_weight,
        pos_table,
        qkv_weight,
        out_weight,
        ln1_gain,
        ln1_bias,
        ln2_gain,
        ln2_bias,
        up_weight,
        up_bias,
        down_weight,
        head_weight,
        head_bias,
    ) = weights
    images, patch_rows, channels = latents.shape
    model_width = qkv_weight.shape[1]
    head_count = model_width // HEAD_DIM
    latent_low = latents.astype(jnp.bfloat16)
    hidden = (
        matmul(latent_low, patch_weight)
        + pos_table.astype(jnp.float32)[None]
        + class_rows[:, None, :]
    )
    own_mask = valid.astype(jnp.bfloat16)
    normed = layer_norm(
        hidden, ln1_gain[0].astype(jnp.float32), ln1_bias[0].astype(jnp.float32)
    ).astype(jnp.bfloat16)
    packed = matmul(normed, qkv_weight[0]).astype(jnp.bfloat16)
    query = packed[..., :model_width].reshape(images, patch_rows, head_count, HEAD_DIM)
    keys_own = packed[..., model_width : 2 * model_width]
    values_own = packed[..., 2 * model_width :]
    prior_keys, prior_values, prior_mask = shifted_2((keys_own, values_own, own_mask), "seq", 1)
    keys = jnp.concatenate((prior_keys, keys_own), 1).reshape(
        images, 2 * patch_rows, head_count, HEAD_DIM
    )
    values = jnp.concatenate((prior_values, values_own), 1).reshape(
        images, 2 * patch_rows, head_count, HEAD_DIM
    )
    allowed = attention_mask(jnp.concatenate((prior_mask, own_mask), 1), patch_rows, seq_place)
    logits = masked_scores(query, keys, allowed)
    row_peak = jnp.max(logits, -1, keepdims=True)
    log_total = row_peak + jnp.log(jnp.sum(jnp.exp(logits - row_peak), -1, keepdims=True))
    weights_soft = jnp.exp(logits - log_total).astype(jnp.bfloat16)
    attended = jnp.einsum(
        "bhqk,bkhd->bqhd", weights_soft, values, preferred_element_type=jnp.float32
    )
    attended = attended.astype(jnp.bfloat16).reshape(images, patch_rows, model_width)
    mid = hidden + matmul(attended, out_weight[0])
    second = layer_norm(
        mid, ln2_gain[0].astype(jnp.float32), ln2_bias[0].astype(jnp.float32)
    ).astype(jnp.bfloat16)
    preact = matmul(second, up_weight[0]) + up_bias[0].astype(jnp.float32)
    activated = jax.nn.gelu(preact, approximate=True).astype(jnp.bfloat16)
    saved = [
        (
            hidden,
            normed,
            query,
            keys,
            values,
            allowed,
            log_total,
            attended,
            mid,
            second,
            preact,
            activated,
        )
    ]
    hidden = mid + matmul(activated, down_weight[0])
    top_low = hidden.astype(jnp.bfloat16)
    head_out = matmul(top_low, head_weight) + head_bias.astype(jnp.float32)
    prior_row = shifted_2(head_out[:, patch_rows - 1, :], "seq", 1)
    shifted = jnp.concatenate((prior_row[:, None, :], head_out[:, : patch_rows - 1, :]), 1)
    shifted = shifted * valid.astype(jnp.float32)[..., None]
    alpha = shifted[..., :channels]
    shift_mean = shifted[..., channels:]
    factor = jnp.exp(-alpha)
    new_latents = (latents - shift_mean) * factor
    logdet_part = -jnp.sum(alpha, (1, 2))
    return (new_latents, logdet_part, factor, top_low, saved)


def local(
    latents,
    valid,
    class_labels,
    group_perm,
    patch_weight,
    pos_table,
    class_table,
    ln1_gain,
    ln1_bias,
    qkv_weight,
    out_weight,
    ln2_gain,
    ln2_bias,
    up_weight,
    up_bias,
    down_weight,
    head_weight,
    head_bias,
    cot_latents,
    cot_logdet,
):
    images, patch_rows, channels = latents.shape
    model_width = qkv_weight.shape[1]
    head_count = model_width // HEAD_DIM
    layer_total = qkv_weight.shape[0]
    seq_place = lax.axis_index("seq")
    picks = group_perm[:, None] == lax.iota(jnp.int32, class_labels.shape[0])[None, :]
    image_labels = jnp.sum(jnp.where(picks, class_labels[None, :], 0), 1)
    label_hot = image_labels[:, None] == lax.iota(jnp.int32, class_table.shape[0])[None, :]
    class_rows = matmul(label_hot.astype(jnp.bfloat16), class_table)
    weights = (
        patch_weight,
        pos_table,
        qkv_weight,
        out_weight,
        ln1_gain,
        ln1_bias,
        ln2_gain,
        ln2_bias,
        up_weight,
        up_bias,
        down_weight,
        head_weight,
        head_bias,
    )
    new_latents, logdet_part, factor, top_low, saved = forward(
        latents, valid, class_rows, seq_place, weights
    )
    valid_float = valid.astype(jnp.float32)
    d_alpha = -cot_latents * new_latents - cot_logdet[:, None, None]
    d_mean = -cot_latents * factor
    d_shifted = jnp.concatenate((d_alpha, d_mean), -1) * valid_float[..., None]
    next_row = shifted_2(d_shifted[:, 0, :], "seq", -1)
    d_head = jnp.concatenate((d_shifted[:, 1:, :], next_row[:, None, :]), 1).astype(jnp.bfloat16)
    head_weight_grad = outer_sum(top_low, d_head)
    head_bias_grad = jnp.sum(d_head.astype(jnp.float32), (0, 1))
    d_hidden = transposed(d_head, head_weight)
    grads_qkv, grads_out, grads_up, grads_down = ([], [], [], [])
    grads_g1, grads_b1, grads_g2, grads_b2, grads_ub = ([], [], [], [], [])
    for layer_index in reversed(range(layer_total)):
        (
            hidden,
            normed,
            query,
            keys,
            values,
            allowed,
            log_total,
            attended,
            mid,
            second,
            preact,
            activated,
        ) = saved[layer_index]
        d_down = d_hidden.astype(jnp.bfloat16)
        down_grad = outer_sum(activated, d_down)
        d_act = transposed(d_down, down_weight[layer_index])
        unused_gelu, gelu_pull = jax.vjp(lambda inner: jax.nn.gelu(inner, approximate=True), preact)
        d_pre = gelu_pull(d_act)[0].astype(jnp.bfloat16)
        up_bias_grad = jnp.sum(d_pre.astype(jnp.float32), (0, 1))
        up_grad = outer_sum(second, d_pre)
        d_second = transposed(d_pre, up_weight[layer_index])
        unused_norm, norm_pull = jax.vjp(
            layer_norm,
            mid,
            ln2_gain[layer_index].astype(jnp.float32),
            ln2_bias[layer_index].astype(jnp.float32),
        )
        d_mid_norm, ln2_gain_part, ln2_bias_part = norm_pull(d_second)
        d_mid = d_hidden + d_mid_norm
        d_proj = d_mid.astype(jnp.bfloat16)
        out_grad = outer_sum(attended, d_proj)
        d_attended = transposed(d_proj, out_weight[layer_index]).astype(jnp.bfloat16)
        d_attended = d_attended.reshape(images, patch_rows, head_count, HEAD_DIM)
        logits = masked_scores(query, keys, allowed)
        probs = jnp.exp(logits - log_total)
        d_probs = jnp.einsum(
            "bqhd,bkhd->bhqk", d_attended, values, preferred_element_type=jnp.float32
        )
        d_scores = (probs * (d_probs - jnp.sum(d_probs * probs, -1, keepdims=True))).astype(
            jnp.bfloat16
        )
        d_query = jnp.einsum(
            "bhqk,bkhd->bqhd", d_scores, keys, preferred_element_type=jnp.float32
        ) * HEAD_DIM ** (-0.5)
        d_keys = jnp.einsum(
            "bhqk,bqhd->bkhd", d_scores, query, preferred_element_type=jnp.float32
        ) * HEAD_DIM ** (-0.5)
        d_values = jnp.einsum(
            "bhqk,bqhd->bkhd",
            probs.astype(jnp.bfloat16),
            d_attended,
            preferred_element_type=jnp.float32,
        )
        d_keys = d_keys.reshape(images, 2 * patch_rows, model_width)
        d_values = d_values.reshape(images, 2 * patch_rows, model_width)
        back_keys, back_values = (
            shifted_2(d_keys[:, :patch_rows].astype(jnp.bfloat16), "seq", -1).astype(jnp.float32),
            shifted_2(d_values[:, :patch_rows].astype(jnp.bfloat16), "seq", -1).astype(jnp.float32),
        )
        d_packed = jnp.concatenate(
            (
                d_query.reshape(images, patch_rows, model_width),
                d_keys[:, patch_rows:] + back_keys,
                d_values[:, patch_rows:] + back_values,
            ),
            -1,
        ).astype(jnp.bfloat16)
        qkv_grad = outer_sum(normed, d_packed)
        d_normed = transposed(d_packed, qkv_weight[layer_index])
        unused_norm, norm_pull = jax.vjp(
            layer_norm,
            hidden,
            ln1_gain[layer_index].astype(jnp.float32),
            ln1_bias[layer_index].astype(jnp.float32),
        )
        d_input, ln1_gain_part, ln1_bias_part = norm_pull(d_normed)
        d_hidden = d_mid + d_input
        grads_qkv.insert(0, qkv_grad)
        grads_out.insert(0, out_grad)
        grads_up.insert(0, up_grad)
        grads_down.insert(0, down_grad)
        grads_g1.insert(0, ln1_gain_part)
        grads_b1.insert(0, ln1_bias_part)
        grads_g2.insert(0, ln2_gain_part)
        grads_b2.insert(0, ln2_bias_part)
        grads_ub.insert(0, up_bias_grad)
    d_embed_low = d_hidden.astype(jnp.bfloat16)
    patch_grad_part = outer_sum(latents.astype(jnp.bfloat16), d_embed_low)
    latents_grad = cot_latents * factor + transposed(d_embed_low, patch_weight)
    pos_part = jnp.sum(d_hidden, 0)
    class_part = jnp.sum(d_hidden, 1)
    logdet, class_sums = lax.psum((logdet_part, class_part), "seq")
    class_term = lax.dot_general(
        label_hot.astype(jnp.float32),
        class_sums,
        (((0,), (0,)), ((), ())),
        precision=precise,
        preferred_element_type=jnp.float32,
    )
    class_grad = lax.psum_scatter(class_term, "dp", scatter_dimension=0, tiled=True)
    pos_grad = lax.psum(pos_part, "dp")
    (
        patch_weight_grad,
        head_weight_grad,
        head_bias_grad,
        ln1_gain_grad,
        ln1_bias_grad,
        ln2_gain_grad,
        ln2_bias_grad,
        up_bias_grad,
    ) = lax.psum(
        (
            patch_grad_part,
            head_weight_grad,
            head_bias_grad,
            jnp.stack(grads_g1),
            jnp.stack(grads_b1),
            jnp.stack(grads_g2),
            jnp.stack(grads_b2),
            jnp.stack(grads_ub),
        ),
        ("dp", "seq"),
    )
    qkv_stack = jnp.stack(grads_qkv)
    out_stack = jnp.stack(grads_out)
    up_stack = jnp.stack(grads_up)
    down_stack = jnp.stack(grads_down)
    flat_parts = (
        lax.psum_scatter(eight_rows(qkv_stack), ("dp", "seq"), scatter_dimension=1, tiled=True),
        lax.psum_scatter(eight_rows(out_stack), ("dp", "seq"), scatter_dimension=1, tiled=True),
        lax.psum_scatter(eight_rows(up_stack), ("dp", "seq"), scatter_dimension=1, tiled=True),
        lax.psum_scatter(eight_rows(down_stack), ("dp", "seq"), scatter_dimension=1, tiled=True),
    )
    flat_qkv, flat_out, flat_up, flat_down = (
        lax.all_gather(
            flat_parts[0].astype(jnp.bfloat16), ("dp", "seq"), axis=1, tiled=True
        ).astype(jnp.float32),
        lax.all_gather(
            flat_parts[1].astype(jnp.bfloat16), ("dp", "seq"), axis=1, tiled=True
        ).astype(jnp.float32),
        lax.all_gather(
            flat_parts[2].astype(jnp.bfloat16), ("dp", "seq"), axis=1, tiled=True
        ).astype(jnp.float32),
        lax.all_gather(
            flat_parts[3].astype(jnp.bfloat16), ("dp", "seq"), axis=1, tiled=True
        ).astype(jnp.float32),
    )
    qkv_stack = flat_qkv.reshape(qkv_stack.shape)
    out_stack = flat_out.reshape(out_stack.shape)
    up_stack = flat_up.reshape(up_stack.shape)
    down_stack = flat_down.reshape(down_stack.shape)
    return (
        new_latents,
        logdet,
        latents_grad,
        patch_weight_grad,
        pos_grad,
        class_grad,
        ln1_gain_grad,
        ln1_bias_grad,
        qkv_stack,
        out_stack,
        ln2_gain_grad,
        ln2_bias_grad,
        up_stack,
        up_bias_grad,
        down_stack,
        head_weight_grad,
        head_bias_grad,
    )


def solution(mesh):
    in_specs = (
        P("dp", "seq", None),
        P("dp", "seq"),
        P(),
        P("dp"),
        P(),
        P("seq", None),
        P(),
        P(),
        P(),
        P(),
        P(),
        P(),
        P(),
        P(),
        P(),
        P(),
        P(),
        P(),
        P("dp", "seq", None),
        P("dp"),
    )
    out_specs = (
        P("dp", "seq", None),
        P("dp"),
        P("dp", "seq", None),
        P(),
        P("seq", None),
        P("dp", None),
        P(),
        P(),
        P(),
        P(),
        P(),
        P(),
        P(),
        P(),
        P(),
        P(),
        P(),
    )
    body = fast_local if mesh.shape["dp"] == 16 and mesh.shape["seq"] == 2 else local
    return jax.shard_map(body, mesh=mesh, in_specs=in_specs, out_specs=out_specs, check_vma=False)
```
